32 devices in a mesh: slides: 16 (over z, x, core), branch: 2 (over y).
Axes of the slice: x: 2, y: 2, z: 4, core: 2. Of those that a mesh axis runs over, the one named last changes fastest.
Arguments:
- tokens: bfloat16 [32768, 768], P(('slides', 'branch')), may hold values from -6 to 6
- cotangent: bfloat16 [32768, 768], P(('slides', 'branch')), may hold values from -6 to 6
- first_gain: bfloat16 [768], P('branch'), may hold values from 0.25 to 1.75
- first_shift: bfloat16 [768], P('branch'), may hold values from -1.5 to 1.5
- joint_weight: bfloat16 [768, 2304], P('slides', 'branch'), may hold values from -0.21875 to 0.21875
- joint_bias: bfloat16 [1536], P('branch'), may hold values from -1.5 to 1.5
- output_weight: bfloat16 [768, 768], P('slides', 'branch'), may hold values from -1.75 to 1.75
- output_bias: bfloat16 [768], P('branch'), may hold values from -1.5 to 1.5
- second_gain: bfloat16 [768], P('branch'), may hold values from 0.25 to 1.75
- second_shift: bfloat16 [768], P('branch'), may hold values from -1.5 to 1.5
- expand_weight: bfloat16 [768, 3072], P('slides', 'branch'), may hold values from -0.21875 to 0.21875
- expand_bias: bfloat16 [3072], P('branch'), may hold values from -1.5 to 1.5
- reduce_weight: bfloat16 [3072, 768], P('slides', 'branch'), may hold values from -0.109375 to 0.109375
- reduce_bias: bfloat16 [768], P('branch'), may hold values from -1.5 to 1.5
- block_owner: int32 [16, 2], P('slides'), may hold values from 0 to 1, as said below
- tile_count: int32 [16, 2], P('slides'), may hold values from 1 to 1024
Outputs:
- output: bfloat16 [32768, 768], P(('slides', 'branch'))
- tokens_delta: float32 [32768, 768], P(('slides', 'branch'))
- first_gain_delta: float32 [768], P('branch')
- first_shift_delta: float32 [768], P('branch')
- joint_weight_delta: float32 [768, 2304], P('slides', 'branch')
- joint_bias_delta: float32 [1536], P('branch')
- output_weight_delta: float32 [768, 768], P('slides', 'branch')
- output_bias_delta: float32 [768], P('branch')
- second_gain_delta: float32 [768], P('branch')
- second_shift_delta: float32 [768], P('branch')
- expand_weight_delta: float32 [768, 3072], P('slides', 'branch')
- expand_bias_delta: float32 [3072], P('branch')
- reduce_weight_delta: float32 [3072, 768], P('slides', 'branch')
- reduce_bias_delta: float32 [768], P('branch')
The draws below stay inside these ranges and needn't reach their ends.
Inputs may be any that keep to these rules, and one draw needn't show every extreme that they name: `block_owner`: each row starts at 0 and rises by 0 or 1 from one block to the next, so a slide covers whole consecutive blocks of 1024 positions. `tile_count`: live tiles stand at the start of each block of 1024 positions; the rest of the block is padding.
All inputs are finite; a program needn't handle non-finite values.
Results may differ from the reference program's by a relative error of at most 0.0092.
Values may be sent and summed in bfloat16 or wider, within the bound.
No kernel may reach another device: no remote copies, remote signals or barrier semaphores. Data moves between devices by JAX's collectives and lax.ppermute only.
A program may use at most 320 MiB of HBM per device.

```python
import math
import jax
import jax.numpy as jnp
import numpy as np
from jax import lax

D = 768
HEADS = 16
HEAD_DIM = 48
FF = 3072
SEG_BASE = 1024
BRANCHES = 5
SEQ = 2048
TOKENS = 32768
BLOCKS = 2
N_SLIDES = 16
N_BRANCH = 2


def draw_block_owner(key, part):
    steps = jax.random.randint(jax.random.fold_in(key, 71), (N_SLIDES, BLOCKS), 0, 2, dtype=jnp.int32)
    steps = steps.at[0, :].set(1)
    steps = steps.at[:, 0].set(0)
    return jnp.cumsum(steps, axis=1).astype(jnp.int32)


def set_ends(values, stream_key, smallest, high):
    shape = values.shape
    index_at = [jax.random.randint(jax.random.fold_in(stream_key, axis), (), 0, shape[axis]) for axis in range(len(shape))]
    values = values.at[tuple(index_at)].set(smallest)
    longest = shape.index(max(shape))
    index_at[longest] = (index_at[longest] + 1) % shape[longest]
    return values.at[tuple(index_at)].set(high)


def block_scale(key, dims, shards, smallest, largest):
    def one(axis_at, shards_of):
        steps = jax.random.uniform(jax.random.fold_in(jax.random.fold_in(key, 6), axis_at), (shards_of,), jnp.float32, smallest / len(shards), largest / len(shards))
        return jnp.repeat(jnp.exp(steps), dims[axis_at] // shards_of).reshape((-1,) + (1,) * (len(dims) - axis_at - 1))

    loudness = one(*shards[0])
    for cut in shards[1:]:
        loudness = loudness * one(*cut)
    return loudness


def bell_draw(stream_key, shape, spread, most, pieces=(), kind=jnp.bfloat16):
    level = block_scale(stream_key, shape, pieces, -0.22, 0.18) if pieces else 1.0
    array = jax.random.normal(stream_key, shape, jnp.float32) * spread * level
    return jnp.minimum(jnp.maximum(array, -most), most).astype(kind)


def setup_inputs(seed: int = 0) -> dict:
    streams_of = jax.random.split(jax.random.key(seed), 17)
    tokens = bell_draw(streams_of[0], (TOKENS, D), 1.0, 6.0, ((0, 32),))
    cotangent = bell_draw(streams_of[1], (TOKENS, D), 1.0, 6.0, ((0, 32),))
    first_gain = jnp.clip(1.0 + 0.15 * jax.random.normal(streams_of[2], (D,), jnp.float32), 0.25, 1.75).astype(jnp.bfloat16)
    first_shift = bell_draw(streams_of[3], (D,), 0.3, 1.5, ((0, 2),))
    joint_weight = bell_draw(streams_of[4], (D, 3 * D), D ** -0.5, 0.21875, ((0, 16), (1, 2)))
    joint_bias = bell_draw(streams_of[5], (2 * D,), 0.3, 1.5, ((0, 2),))
    output_weight = bell_draw(streams_of[6], (D, D), (D // 64) ** -0.5, 1.75, ((0, 16), (1, 2)))
    output_bias = bell_draw(streams_of[7], (D,), 0.3, 1.5, ((0, 2),))
    second_gain = jnp.clip(1.0 + 0.15 * jax.random.normal(streams_of[8], (D,), jnp.float32), 0.25, 1.75).astype(jnp.bfloat16)
    second_shift = bell_draw(streams_of[9], (D,), 0.3, 1.5, ((0, 2),))
    expand_weight = bell_draw(streams_of[10], (D, FF), D ** -0.5, 0.21875, ((0, 16), (1, 2)))
    expand_bias = bell_draw(streams_of[11], (FF,), 0.3, 1.5, ((0, 2),))
    reduce_weight = bell_draw(streams_of[12], (FF, D), FF ** -0.5, 0.109375, ((0, 16), (1, 2)))
    reduce_bias = bell_draw(streams_of[13], (D,), 0.3, 1.5, ((0, 2),))
    block_owner = draw_block_owner(jax.random.fold_in(streams_of[16], 71), 0)
    tile_count = set_ends(jax.random.randint(streams_of[15], (N_SLIDES, BLOCKS), 1, SEG_BASE + 1), jax.random.fold_in(streams_of[15], 1), 1, SEG_BASE).astype(jnp.int32)
    return dict(tokens=tokens, cotangent=cotangent, first_gain=first_gain, first_shift=first_shift, joint_weight=joint_weight, joint_bias=joint_bias, output_weight=output_weight, output_bias=output_bias, second_gain=second_gain, second_shift=second_shift, expand_weight=expand_weight, expand_bias=expand_bias, reduce_weight=reduce_weight, reduce_bias=reduce_bias, block_owner=block_owner, tile_count=tile_count)


EPSILON = 1e-05
NEGATIVE = -1e+30

@jax.custom_vjp
def low(v):
    return lax.optimization_barrier(v.astype(jnp.bfloat16)).astype(jnp.float32)

@jax.custom_vjp
def low_back(v):
    return v

def low_keep(v):
    return (low(v), None)

def low_pass(kept, grad):
    return (grad,)

def back_keep(v):
    return (v, None)

def back_low(kept, grad):
    return (low(grad),)
low.defvjp(low_keep, low_pass)
low_back.defvjp(back_keep, back_low)

def matmul(left, right):
    return jnp.dot(left, right, precision=lax.Precision.HIGHEST, preferred_element_type=jnp.float32)

def normalize(values, gain, shift):
    centred = values - lax.optimization_barrier(jnp.mean(values, axis=-1, keepdims=True))
    scaled = centred * lax.rsqrt(lax.optimization_barrier(jnp.mean(centred * centred, axis=-1, keepdims=True)) + EPSILON)
    return scaled * gain + shift

def gelu_value(values):
    return 0.5 * values * (1.0 + lax.erf(values * (1.0 / math.sqrt(2.0))))

def pick_rows(table, stride, head_count):
    shaped = table.reshape((table.shape[0] // stride, stride) + table.shape[1:])
    if table.ndim == 1:
        return shaped[:, np.arange(head_count) % stride]
    return shaped[:, np.arange(head_count) % stride, np.arange(head_count)]

def put_rows(picked, stride, head_count, canvas):
    shaped = canvas.reshape((canvas.shape[0] // stride, stride) + canvas.shape[1:])
    return shaped.at[:, np.arange(head_count) % stride, np.arange(head_count)].set(picked).reshape(canvas.shape)

def branch_attention(queries, key_copies, value_copies, owner_pos, live_pos, branch_level):
    stride = 2 ** branch_level
    seg_width = min(SEG_BASE * stride, SEQ)
    seg_keys = seg_width // stride
    segments = SEQ // seg_width
    shard_len = SEQ // N_BRANCH
    span = min(seg_width, shard_len)
    query_rows = span // stride
    block_count = SEQ // span
    block_ids = np.arange(block_count)
    shard_of = block_ids * span // shard_len
    seg_of = block_ids * span // seg_width
    positions = jnp.arange(SEQ, dtype=jnp.int32)

    def key_copy_blocks(copies):
        picked = jax.vmap(lambda table: pick_rows(table, stride, HEADS))(copies)
        shaped = picked.reshape((copies.shape[0], segments, seg_keys) + picked.shape[2:])
        return shaped[shard_of, seg_of]

    def key_blocks(table):
        picked = pick_rows(table, stride, HEADS)
        return picked.reshape((segments, seg_keys) + picked.shape[1:])[seg_of]

    def query_blocks(table):
        picked = pick_rows(table, stride, HEADS)
        return picked.reshape((block_count, query_rows) + picked.shape[1:])

    def block_pass(blocks_in):
        query_blk, key_blk, value_blk, qpos_blk, qowner_blk, kpos_blk, kowner_blk, klive_blk = blocks_in
        raw = jnp.einsum('qhd,khd->hqk', query_blk, key_blk, precision=lax.Precision.HIGHEST)
        scores = low_back(raw * HEAD_DIM ** (-0.5))
        qpos_t = qpos_blk.T
        qowner_t = qowner_blk.T
        kpos_t = kpos_blk.T
        kowner_t = kowner_blk.T
        klive_t = klive_blk.T
        allowed = (qowner_t[:, :, None] == kowner_t[:, None, :]) & (klive_t[:, None, :] | (qpos_t[:, :, None] == kpos_t[:, None, :]))
        masked = jnp.where(allowed, scores, NEGATIVE)
        norm_log = jax.nn.logsumexp(masked, axis=-1)
        probs = low(jnp.exp(masked - norm_log[..., None]))
        result = jnp.einsum('hqk,khd->qhd', probs, value_blk, precision=lax.Precision.HIGHEST)
        return (low_back(result), norm_log.T)
    results, norm_logs = lax.map(jax.checkpoint(block_pass), (query_blocks(queries), key_copy_blocks(key_copies), key_copy_blocks(value_copies), query_blocks(positions), query_blocks(owner_pos), key_blocks(positions), key_blocks(owner_pos), key_blocks(live_pos)))
    branch_out = put_rows(results.reshape((SEQ // stride, HEADS, HEAD_DIM)), stride, HEADS, jnp.zeros((SEQ, HEADS, HEAD_DIM), jnp.float32))
    branch_log = put_rows(norm_logs.reshape((SEQ // stride, HEADS)), stride, HEADS, jnp.full((SEQ, HEADS), NEGATIVE, jnp.float32))
    return (branch_out, branch_log)

def layer(group_tokens, weights, owner_pos, live_pos):
    first_gain, first_shift, joint_weight, joint_bias, output_weight, output_bias, second_gain, second_shift, expand_weight, expand_bias, reduce_weight, reduce_bias = weights
    hidden_one = low(normalize(group_tokens, first_gain, first_shift))
    joint_rows = matmul(hidden_one, joint_weight)
    queries = low_back(low(joint_rows[:, :D] + joint_bias[:D])).reshape(SEQ, HEADS, HEAD_DIM)
    keys_rows = low_back(low(joint_rows[:, D:2 * D])).reshape(SEQ, HEADS, HEAD_DIM)
    values_rows = low_back(low(joint_rows[:, 2 * D:] + joint_bias[D:])).reshape(SEQ, HEADS, HEAD_DIM)
    key_copies = jnp.stack([low_back(keys_rows) for copy_index in range(N_BRANCH)])
    value_copies = jnp.stack([low_back(values_rows) for copy_index in range(N_BRANCH)])
    outputs = []
    logs_all = []
    for branch_level in range(BRANCHES):
        branch_out, branch_log = branch_attention(queries, key_copies, value_copies, owner_pos, live_pos, branch_level)
        outputs.append(branch_out)
        logs_all.append(branch_log)
    stacked = jnp.stack(logs_all)
    total_log = jax.nn.logsumexp(stacked, axis=0)
    mixed = lax.optimization_barrier(jnp.sum(jnp.exp(stacked - total_log)[..., None] * jnp.stack(outputs), axis=0))
    attended = low(mixed.reshape(SEQ, D))
    middle = group_tokens + low_back(matmul(attended, output_weight)) + output_bias
    hidden_two = low(normalize(middle, second_gain, second_shift))
    expanded = low_back(matmul(hidden_two, expand_weight) + expand_bias)
    activated = low(gelu_value(expanded))
    return middle + low_back(matmul(activated, reduce_weight)) + reduce_bias

def reference(tokens, cotangent, first_gain, first_shift, joint_weight, joint_bias, output_weight, output_bias, second_gain, second_shift, expand_weight, expand_bias, reduce_weight, reduce_bias, block_owner, tile_count):
    params = tuple((member.astype(jnp.float32) for member in (first_gain, first_shift, joint_weight, joint_bias, output_weight, output_bias, second_gain, second_shift, expand_weight, expand_bias, reduce_weight, reduce_bias)))
    rows_in = tokens.astype(jnp.float32).reshape(N_SLIDES, SEQ, D)
    rows_back = cotangent.astype(jnp.float32).reshape(N_SLIDES, SEQ, D)
    within = jnp.arange(SEG_BASE, dtype=jnp.int32)

    def group_step(totals, members):
        group_in, group_back, owner_row, count_row = members
        owner_pos = jnp.broadcast_to(owner_row[:, None], (BLOCKS, SEG_BASE)).reshape(SEQ)
        live_pos = (within[None, :] < count_row[:, None]).reshape(SEQ)

        def forward(group_tokens, *weights):
            return layer(group_tokens, weights, owner_pos, live_pos)
        result, pullback = jax.vjp(forward, group_in, *params)
        gradients = pullback(group_back)
        totals = tuple((total + gradient for total, gradient in zip(totals, gradients[1:])))
        return (totals, (result.astype(jnp.bfloat16), gradients[0]))
    initial = tuple((jnp.zeros_like(member) for member in params))
    totals, (results, token_grads) = lax.scan(group_step, initial, (rows_in, rows_back, block_owner.astype(jnp.int32), tile_count.astype(jnp.int32)))
    return (results.reshape(TOKENS, D), token_grads.reshape(TOKENS, D), totals[0], totals[1], totals[2], totals[3], totals[4], totals[5], totals[6], totals[7], totals[8], totals[9], totals[10], totals[11])
```

```python
import functools
import math

import jax
import jax.numpy as jnp
import numpy as np
from jax import lax
from jax.experimental import pallas as pl
from jax.experimental.pallas import tpu as pltpu
from jax.sharding import PartitionSpec as P

HEADS = 16
SEG_BASE = 1024
BRANCHES = 5
RESIDUES = 2 ** (BRANCHES - 1)
EPSILON = 1e-05
NEGATIVE = -1e30
WINDOW = 256
LANES = 128
VMEM_LIMIT = 60 * 1024 * 1024
NESTED = [int(format(j, "04b")[::-1], 2) for j in range(RESIDUES)]
LEVELS = [BRANCHES - 1 if j == 0 else BRANCHES - 2 - int(math.log2(j)) for j in range(RESIDUES)]

BF16 = jnp.bfloat16
F32 = jnp.float32


def standardize(values):
    centred = values - jnp.mean(values, axis=-1, keepdims=True)
    inverse = lax.rsqrt(jnp.mean(centred * centred, axis=-1, keepdims=True) + EPSILON)
    return (centred * inverse, inverse)


def norm_back(upstream, normed, inverse, gain):
    scaled = upstream * gain
    return inverse * (
        scaled
        - jnp.mean(scaled, axis=-1, keepdims=True)
        - normed * jnp.mean(scaled * normed, axis=-1, keepdims=True)
    )


def gelu_pair(values):
    cumulative = 0.5 * (1.0 + lax.erf(values * (1.0 / math.sqrt(2.0))))
    density = jnp.exp(-0.5 * values * values) * (1.0 / math.sqrt(2.0 * math.pi))
    return values * cumulative, cumulative + values * density


def dot_nn(left, right):
    return lax.dot_general(left, right, (((1,), (0,)), ((), ())), preferred_element_type=F32)


def dot_nt(left, right):
    return lax.dot_general(left, right, (((1,), (1,)), ((), ())), preferred_element_type=F32)


def dot_tn(left, right):
    return lax.dot_general(left, right, (((0,), (0,)), ((), ())), preferred_element_type=F32)


def head_view(width, head_dim):
    head = pl.program_id(0)
    tile = jnp.minimum(lax.div(head * head_dim, LANES), width // LANES - WINDOW // LANES)
    lanes = pl.ds(pl.multiple_of(tile * LANES, LANES), WINDOW)
    lane = lax.broadcasted_iota(jnp.int32, (1, WINDOW), 1) + tile * LANES
    mask = (lane >= head * head_dim) & (lane < (head + 1) * head_dim)
    order = [jnp.bitwise_xor(jnp.int32(code), head) for code in NESTED]
    return head, lanes, mask, order


def own_rows(ref, lanes, order, lead=()):
    return jnp.concatenate([ref[(*lead, code, slice(None), lanes)] for code in order], axis=0)


def key_rows(own_ref, far_ref, lanes, order):
    own = [
        own_ref[d, code, :, lanes] for d in range(own_ref.shape[0]) for code in order
    ]
    far = [
        far_ref[d, lax.div(code, 2), :, lanes]
        for d in range(far_ref.shape[0])
        for code in order[: RESIDUES // 2]
    ]
    return jnp.concatenate(own, axis=0), jnp.concatenate(far, axis=0)


def biased_scores(raw, bias_ref, first, rows, block, scale):
    keys = raw.shape[1]
    bias = bias_ref[0]
    pieces = []
    step = min(LANES, rows)
    for start in range(first, first + rows, step):
        part = raw[start - first : start - first + step] * scale
        added = []
        counts = []
        cut = start
        while cut < start + step:
            level = LEVELS[cut // block]
            stop = cut
            while stop < start + step and LEVELS[stop // block] == level:
                stop += block
            added.append(part[cut - start : stop - start] + bias[level : level + 1, :keys])
            counts.append(jnp.full((stop - cut, 1), math.log2(1.0 + level), F32))
            cut = stop
        whole = added[0] if len(added) == 1 else jnp.concatenate(added, axis=0)
        count = counts[0] if len(counts) == 1 else jnp.concatenate(counts, axis=0)
        here = part[:, start : start + step] + count
        eye = lax.broadcasted_iota(jnp.int32, (step, step), 0) == lax.broadcasted_iota(
            jnp.int32, (step, step), 1
        )
        here = jnp.where(eye, here, whole[:, start : start + step])
        sides = [whole[:, :start]] if start else []
        sides.append(here)
        if start + step < keys:
            sides.append(whole[:, start + step :])
        pieces.append(jnp.concatenate(sides, axis=1) if len(sides) > 1 else here)
    return pieces[0] if len(pieces) == 1 else jnp.concatenate(pieces, axis=0)


def put_rows(ref, value, lanes, mask, order, first, block):
    for at in range(value.shape[0] // block):
        code = order[first // block + at]
        fresh = value[at * block : (at + 1) * block].astype(ref.dtype)
        ref[code, :, lanes] = jnp.where(mask, fresh, ref[code, :, lanes])


def forward_kernel(rows, chunk, head_dim, q_ref, k_ref, v_ref, kx_ref, vx_ref, bias_ref, o_ref, t_ref):
    block = rows // RESIDUES
    head, lanes, mask, order = head_view(q_ref.shape[-1], head_dim)
    scale = head_dim ** (-0.5) * math.log2(math.e)
    queries = jnp.where(mask, own_rows(q_ref, lanes, order), jnp.zeros((), BF16))
    own_k, far_k = key_rows(k_ref, kx_ref, lanes, order)
    own_v, far_v = key_rows(v_ref, vx_ref, lanes, order)
    both_k = jnp.concatenate([own_k, far_k], axis=0)
    both_v = jnp.concatenate([own_v, far_v], axis=0)
    lane = lax.broadcasted_iota(jnp.int32, (1, LANES), 1)
    for first in range(0, rows, chunk):
        far = first < rows // 2
        raw = dot_nt(queries[first : first + chunk], both_k if far else own_k)
        scores = biased_scores(raw, bias_ref, first, chunk, block, scale)
        highest = jnp.max(scores, axis=1, keepdims=True)
        weights = jnp.exp2(scores - highest)
        total = jnp.sum(weights, axis=1, keepdims=True)
        mixed = dot_nn(weights.astype(BF16), both_v if far else own_v) * (1.0 / total)
        put_rows(o_ref, mixed, lanes, mask, order, first, block)
        total_log = highest + jnp.log2(total)
        for at in range(chunk // block):
            code = order[first // block + at]
            t_ref[code] = jnp.where(
                lane == head, total_log[at * block : (at + 1) * block], t_ref[code]
            )


def backward_kernel(
    rows, chunk, head_dim,
    q_ref, k_ref, v_ref, kx_ref, vx_ref, bias_ref, o_ref, g_ref, t_ref,
    dq_ref, dk_ref, dv_ref, dkx_ref, dvx_ref,
    p_own, s_own, p_far, s_far,
):
    block = rows // RESIDUES
    head, lanes, mask, order = head_view(q_ref.shape[-1], head_dim)
    natural = head_dim ** (-0.5)
    scale = natural * math.log2(math.e)
    zero = jnp.zeros((), BF16)
    queries = jnp.where(mask, own_rows(q_ref, lanes, order), zero)
    upstream = jnp.where(mask, own_rows(g_ref, lanes, order), zero)
    mixed = own_rows(o_ref, lanes, order)
    own_k, far_k = key_rows(k_ref, kx_ref, lanes, order)
    own_v, far_v = key_rows(v_ref, vx_ref, lanes, order)
    both_k = jnp.concatenate([own_k, far_k], axis=0)
    both_v = jnp.concatenate([own_v, far_v], axis=0)
    lane = lax.broadcasted_iota(jnp.int32, (1, LANES), 1)
    own_keys = own_k.shape[0]
    for first in range(0, rows, chunk):
        far = first < rows // 2
        span = slice(first, first + chunk)
        raw = dot_nt(queries[span], both_k if far else own_k)
        scores = biased_scores(raw, bias_ref, first, chunk, block, scale)
        logs = jnp.concatenate(
            [t_ref[order[j]] for j in range(first // block, (first + chunk) // block)], axis=0
        )
        total_log = jnp.sum(jnp.where(lane == head, logs, 0.0), axis=1, keepdims=True)
        inner = jnp.sum(
            upstream[span].astype(F32) * mixed[span].astype(F32), axis=1, keepdims=True
        )
        probs = jnp.exp2(scores - total_log)
        prob_grad = dot_nt(upstream[span], both_v if far else own_v)
        score_grad = (probs * (prob_grad - inner)).astype(BF16)
        probs = probs.astype(BF16)
        query_grad = dot_nn(score_grad, both_k if far else own_k) * natural
        put_rows(dq_ref, query_grad, lanes, mask, order, first, block)
        p_own[span] = probs[:, :own_keys]
        s_own[span] = score_grad[:, :own_keys]
        if far:
            p_far[span] = probs[:, own_keys:]
            s_far[span] = score_grad[:, own_keys:]
    half = rows // 2
    value_grad = dot_tn(p_own[...], upstream)
    key_grad = dot_tn(s_own[...], queries) * natural
    for d in range(k_ref.shape[0]):
        put_rows(dk_ref.at[d], key_grad[d * rows : (d + 1) * rows], lanes, mask, order, 0, block)
        put_rows(dv_ref.at[d], value_grad[d * rows : (d + 1) * rows], lanes, mask, order, 0, block)
    value_far = dot_tn(p_far[...], upstream[:half])
    key_far = dot_tn(s_far[...], queries[:half]) * natural
    halves = [lax.div(code, 2) for code in order]
    for d in range(kx_ref.shape[0]):
        put_rows(dkx_ref.at[d], key_far[d * half : (d + 1) * half], lanes, mask, halves, 0, block)
        put_rows(dvx_ref.at[d], value_far[d * half : (d + 1) * half], lanes, mask, halves, 0, block)


def whole_spec(shape):
    zeros = (0,) * len(shape)
    return pl.BlockSpec(shape, lambda h: zeros)


def bias_spec(bias):
    return pl.BlockSpec((1,) + bias.shape[1:], lambda h: (h, 0, 0))


def attend(q, k, v, kx, vx, bias, head_dim):
    blocks, block, width = q.shape
    rows = blocks * block
    chunk = min(256, rows // 2)
    pairs = HEADS * rows * (k.shape[0] * rows + kx.shape[0] * rows // 4)
    return pl.pallas_call(
        functools.partial(forward_kernel, rows, chunk, head_dim),
        grid=(HEADS,),
        in_specs=[whole_spec(m.shape) for m in (q, k, v, kx, vx)] + [bias_spec(bias)],
        out_specs=[whole_spec(q.shape), whole_spec((blocks, block, LANES))],
        out_shape=[
            jax.ShapeDtypeStruct(q.shape, BF16),
            jax.ShapeDtypeStruct((blocks, block, LANES), F32),
        ],
        compiler_params=pltpu.CompilerParams(vmem_limit_bytes=VMEM_LIMIT),
        cost_estimate=pl.CostEstimate(
            flops=4 * pairs * LANES, transcendentals=pairs, bytes_accessed=10 * rows * width
        ),
        name="attend",
    )(q, k, v, kx, vx, bias)


def attend_back(q, k, v, kx, vx, bias, o, g, t, head_dim):
    blocks, block, width = q.shape
    rows = blocks * block
    chunk = min(256, rows // 2)
    far_keys = kx.shape[0] * rows // 2
    pairs = HEADS * rows * (k.shape[0] * rows + kx.shape[0] * rows // 4)
    outs = [q, k, v, kx, vx]
    return pl.pallas_call(
        functools.partial(backward_kernel, rows, chunk, head_dim),
        grid=(HEADS,),
        in_specs=[whole_spec(m.shape) for m in (q, k, v, kx, vx)]
        + [bias_spec(bias)]
        + [whole_spec(m.shape) for m in (o, g, t)],
        out_specs=[whole_spec(m.shape) for m in outs],
        out_shape=[jax.ShapeDtypeStruct(m.shape, BF16) for m in outs],
        scratch_shapes=[
            pltpu.VMEM((rows, k.shape[0] * rows), BF16),
            pltpu.VMEM((rows, k.shape[0] * rows), BF16),
            pltpu.VMEM((rows // 2, far_keys), BF16),
            pltpu.VMEM((rows // 2, far_keys), BF16),
        ],
        compiler_params=pltpu.CompilerParams(vmem_limit_bytes=VMEM_LIMIT),
        cost_estimate=pl.CostEstimate(
            flops=10 * pairs * LANES, transcendentals=pairs, bytes_accessed=20 * rows * width
        ),
        name="attend_back",
    )(q, k, v, kx, vx, bias, o, g, t)


def head_positions(rows):
    block = rows // RESIDUES
    code = np.array(NESTED)[None, :, None] ^ np.arange(HEADS)[:, None, None]
    return (np.arange(block)[None, None, :] * RESIDUES + code).reshape(HEADS, rows)


def key_bias(rows, own_starts, far_starts, own_count, far_count, same):
    block = rows // RESIDUES
    places = head_positions(rows)
    level = np.arange(8)[:, None]
    blocks = np.array(LEVELS)[np.arange(rows) // block][None, :]
    own_times = np.log2(1.0 + np.minimum(level, blocks)).astype(np.float32)
    with np.errstate(divide="ignore"):
        far_times = np.log2(np.minimum(level, blocks)[:, : rows // 2]).astype(np.float32)
    far_times = np.maximum(far_times, np.float32(NEGATIVE))
    parts = []
    for start in own_starts:
        live = start + jnp.asarray(places) < own_count
        parts.append(jnp.where(live[:, None, :], own_times[None], NEGATIVE))
    for start in far_starts:
        live = (start + jnp.asarray(places[:, : rows // 2]) < far_count) & same
        parts.append(jnp.where(live[:, None, :], far_times[None], NEGATIVE))
    return jnp.concatenate(parts, axis=2)


def parity_lanes(width, head_dim):
    return (np.arange(width) // head_dim) % 2 == 1


def half_of(table, odd):
    split = table.reshape(RESIDUES // 2, 2, *table.shape[1:])
    return jnp.where(odd, split[:, 1], split[:, 0])


def add_half(total, half, odd):
    split = total.reshape(RESIDUES // 2, 2, *total.shape[1:]).astype(F32)
    half = half.astype(F32)
    both = jnp.stack(
        [split[:, 0] + jnp.where(odd, 0.0, half), split[:, 1] + jnp.where(odd, half, 0.0)], axis=1
    )
    return both.reshape(total.shape)


def swap_pairs(value):
    return lax.ppermute(value, "branch", [(0, 1), (1, 0)])


def gather_columns(shard, branches):
    if branches != 2:
        return lax.all_gather(shard, "branch", axis=shard.ndim - 1, tiled=True)
    other = swap_pairs(shard)
    first = lax.axis_index("branch") == 0
    return jnp.concatenate(
        [jnp.where(first, shard, other), jnp.where(first, other, shard)], axis=-1
    )


def scatter_columns(total, branches):
    if branches != 2:
        return lax.psum_scatter(
            total, "branch", scatter_dimension=total.ndim - 1, tiled=True
        ).astype(F32)
    half = total.shape[-1] // 2
    at = lax.axis_index("branch")
    keep = lax.dynamic_slice_in_dim(total, at * half, half, total.ndim - 1)
    away = lax.dynamic_slice_in_dim(total, (1 - at) * half, half, total.ndim - 1)
    return keep.astype(F32) + swap_pairs(away).astype(F32)


def weight_sum(partial, branches):
    low = lax.psum_scatter(partial.astype(BF16), "slides", scatter_dimension=0, tiled=True)
    return scatter_columns(low, branches)


def on_device(
    tokens,
    cotangent,
    first_gain,
    first_shift,
    joint_weight,
    joint_bias,
    output_weight,
    output_bias,
    second_gain,
    second_shift,
    expand_weight,
    expand_bias,
    reduce_weight,
    reduce_bias,
    block_owner,
    tile_count,
):
    rows, width = tokens.shape
    branches = lax.axis_size("branch")
    head_dim = width // HEADS
    block = rows // RESIDUES
    mates = SEG_BASE // rows
    at = lax.axis_index("branch")
    segment = lax.div(at, mates)
    within = at - segment * mates
    odd = parity_lanes(width, head_dim)

    def residues_first(table):
        return table.reshape(block, RESIDUES, width).swapaxes(0, 1).reshape(rows, width)

    def positions_first(table):
        return table.reshape(RESIDUES, block, width).swapaxes(0, 1).reshape(rows, width)

    joint_full = lax.all_gather(gather_columns(joint_weight, branches), "slides", axis=0, tiled=True)
    output_full = lax.all_gather(gather_columns(output_weight, branches), "slides", axis=0, tiled=True)
    expand_full = lax.all_gather(gather_columns(expand_weight, branches), "slides", axis=0, tiled=True)
    reduce_full = lax.all_gather(gather_columns(reduce_weight, branches), "slides", axis=0, tiled=True)
    parameters = (
        first_gain, first_shift, joint_bias, output_bias,
        second_gain, second_shift, expand_bias, reduce_bias,
    )
    packed = lax.all_gather(jnp.concatenate(parameters), "branch", axis=0, tiled=False)
    vectors = []
    cut = 0
    for member in parameters:
        size = member.shape[0]
        vectors.append(packed[:, cut : cut + size].reshape(-1).astype(F32))
        cut += size
    gain_one, shift_one, bias_joint, bias_output, gain_two, shift_two, bias_expand, bias_reduce = vectors

    owners = block_owner.reshape(-1)
    counts = tile_count.reshape(-1)
    own_count = jnp.where(segment == 0, counts[0], counts[1])
    far_count = jnp.where(segment == 0, counts[1], counts[0])
    own_starts = [lax.rem(within + d, mates) * rows for d in range(mates)]
    far_starts = [d * rows for d in range(mates)]
    bias = key_bias(rows, own_starts, far_starts, own_count, far_count, owners[0] == owners[1])

    tokens_f = residues_first(tokens).astype(F32)
    upstream_low = residues_first(cotangent)
    normed_one, inverse_one = standardize(tokens_f)
    hidden_one = (normed_one * gain_one + shift_one).astype(BF16)
    joint_rows = jnp.dot(hidden_one, joint_full, preferred_element_type=F32)
    shape = (RESIDUES, block, width)
    q = (joint_rows[:, :width] + bias_joint[:width]).astype(BF16).reshape(shape)
    k = joint_rows[:, width : 2 * width].astype(BF16).reshape(shape)
    v = (joint_rows[:, 2 * width :] + bias_joint[width:]).astype(BF16).reshape(shape)
    if mates == 1 and branches == 2:
        k_own, v_own = k[None], v[None]
        k_far, v_far = swap_pairs(half_of(k, odd))[None], swap_pairs(half_of(v, odd))[None]
    else:
        k_all = lax.all_gather(k, "branch", axis=0)
        v_all = lax.all_gather(v, "branch", axis=0)
        own_at = [segment * mates + lax.rem(within + d, mates) for d in range(mates)]
        far_at = [(1 - segment) * mates + d for d in range(mates)]
        k_own = jnp.stack([lax.dynamic_index_in_dim(k_all, d, 0, False) for d in own_at])
        v_own = jnp.stack([lax.dynamic_index_in_dim(v_all, d, 0, False) for d in own_at])
        k_far = jnp.stack([half_of(lax.dynamic_index_in_dim(k_all, d, 0, False), odd) for d in far_at])
        v_far = jnp.stack([half_of(lax.dynamic_index_in_dim(v_all, d, 0, False), odd) for d in far_at])
    attended, total_log = attend(q, k_own, v_own, k_far, v_far, bias, head_dim)
    attended_rows = attended.reshape(rows, width)
    middle = tokens_f + jnp.dot(attended_rows, output_full, preferred_element_type=F32) + bias_output
    normed_two, inverse_two = standardize(middle)
    hidden_two = (normed_two * gain_two + shift_two).astype(BF16)
    expanded = jnp.dot(hidden_two, expand_full, preferred_element_type=F32) + bias_expand
    activated, slope = gelu_pair(expanded)
    activated = activated.astype(BF16)
    output = middle + jnp.dot(activated, reduce_full, preferred_element_type=F32) + bias_reduce
    output = positions_first(output.astype(BF16))

    upstream = upstream_low.astype(F32)
    reduce_bias_part = jnp.sum(upstream, axis=0)
    reduce_weight_part = dot_tn(activated, upstream_low)
    reduce_sum = weight_sum(reduce_weight_part, branches)
    activated_grad = dot_nt(upstream_low, reduce_full)
    expanded_grad = (activated_grad * slope).astype(BF16)
    expand_bias_part = jnp.sum(expanded_grad.astype(F32), axis=0)
    expand_weight_part = dot_tn(hidden_two, expanded_grad)
    expand_sum = weight_sum(expand_weight_part, branches)
    hidden_two_grad = dot_nt(expanded_grad, expand_full)
    second_gain_part = jnp.sum(hidden_two_grad * normed_two, axis=0)
    second_shift_part = jnp.sum(hidden_two_grad, axis=0)
    middle_grad = upstream + norm_back(hidden_two_grad, normed_two, inverse_two, gain_two)
    output_bias_part = jnp.sum(middle_grad, axis=0)
    middle_low = middle_grad.astype(BF16)
    output_weight_part = dot_tn(attended_rows, middle_low)
    output_sum = weight_sum(output_weight_part, branches)
    mixed_grad = dot_nt(middle_low, output_full).astype(BF16).reshape(shape)

    dq, dk_own, dv_own, dk_far, dv_far = attend_back(
        q, k_own, v_own, k_far, v_far, bias, attended, mixed_grad, total_log, head_dim
    )
    if mates == 1 and branches == 2:
        key_sum = add_half(dk_own[0], swap_pairs(dk_far[0]), odd)
        value_sum = add_half(dv_own[0], swap_pairs(dv_far[0]), odd)
    else:

        def spread(own, far):
            canvas = jnp.zeros((branches, *shape), BF16)
            for d, index in enumerate(own_at):
                canvas = lax.dynamic_update_index_in_dim(canvas, own[d], index, 0)
            for d, index in enumerate(far_at):
                full = add_half(jnp.zeros(shape, F32), far[d], odd).astype(BF16)
                canvas = lax.dynamic_update_index_in_dim(canvas, full, index, 0)
            return lax.psum_scatter(canvas, "branch", scatter_dimension=0, tiled=True)[0]

        key_sum = spread(dk_own, dk_far)
        value_sum = spread(dv_own, dv_far)
    query_low = dq.reshape(rows, width)
    value_low = value_sum.astype(BF16).reshape(rows, width)
    joint_grad = jnp.concatenate(
        [query_low, key_sum.astype(BF16).reshape(rows, width), value_low], axis=1
    )
    joint_bias_part = jnp.concatenate(
        [jnp.sum(query_low.astype(F32), axis=0), jnp.sum(value_low.astype(F32), axis=0)]
    )
    joint_weight_part = dot_tn(hidden_one, joint_grad)
    joint_sum = weight_sum(joint_weight_part, branches)
    hidden_one_grad = dot_nt(joint_grad, joint_full)
    first_gain_part = jnp.sum(hidden_one_grad * normed_one, axis=0)
    first_shift_part = jnp.sum(hidden_one_grad, axis=0)
    tokens_grad = middle_grad + norm_back(hidden_one_grad, normed_one, inverse_one, gain_one)
    tokens_grad = positions_first(tokens_grad)

    partial_vectors = (
        first_gain_part, first_shift_part, joint_bias_part, output_bias_part,
        second_gain_part, second_shift_part, expand_bias_part, reduce_bias_part,
    )
    summed = lax.psum(jnp.concatenate(partial_vectors), ("slides", "branch"))
    mine = []
    cut = 0
    for member in partial_vectors:
        size = member.shape[0]
        share = size // branches
        mine.append(lax.dynamic_slice_in_dim(summed, cut + at * share, share))
        cut += size
    return (
        output,
        tokens_grad,
        mine[0],
        mine[1],
        joint_sum,
        mine[2],
        output_sum,
        mine[3],
        mine[4],
        mine[5],
        expand_sum,
        mine[6],
        reduce_sum,
        mine[7],
    )


def solution(mesh):
    rows = P(("slides", "branch"), None)
    matrix = P("slides", "branch")
    vector = P("branch")
    placed = (
        rows, rows, vector, vector, matrix, vector, matrix, vector,
        vector, vector, matrix, vector, matrix, vector, P("slides", None), P("slides", None),
    )
    given = (
        rows, rows, vector, vector, matrix, vector, matrix, vector,
        vector, vector, matrix, vector, matrix, vector,
    )
    return jax.shard_map(on_device, mesh=mesh, in_specs=placed, out_specs=given, check_vma=False)
```

```python
import functools
import math

import jax
import jax.numpy as jnp
import numpy as np
from jax import lax
from jax.experimental import pallas as pl
from jax.experimental.pallas import tpu as pltpu
from jax.sharding import PartitionSpec as P

HEADS = 16
SEG_BASE = 1024
BRANCHES = 5
RESIDUES = 2 ** (BRANCHES - 1)
EPSILON = 1e-05
NEGATIVE = -1e30
WINDOW = 256
LANES = 128
VMEM_LIMIT = 60 * 1024 * 1024
NESTED = [int(format(j, "04b")[::-1], 2) for j in range(RESIDUES)]
LEVELS = [BRANCHES - 1 if j == 0 else BRANCHES - 2 - int(math.log2(j)) for j in range(RESIDUES)]

BF16 = jnp.bfloat16
F32 = jnp.float32


def standardize(values):
    centred = values - jnp.mean(values, axis=-1, keepdims=True)
    inverse = lax.rsqrt(jnp.mean(centred * centred, axis=-1, keepdims=True) + EPSILON)
    return (centred * inverse, inverse)


def norm_back(upstream, normed, inverse, gain):
    scaled = upstream * gain
    return inverse * (
        scaled
        - jnp.mean(scaled, axis=-1, keepdims=True)
        - normed * jnp.mean(scaled * normed, axis=-1, keepdims=True)
    )


def gelu_pair(values):
    cumulative = 0.5 * (1.0 + lax.erf(values * (1.0 / math.sqrt(2.0))))
    density = jnp.exp(-0.5 * values * values) * (1.0 / math.sqrt(2.0 * math.pi))
    return values * cumulative, cumulative + values * density


def dot_nn(left, right):
    return lax.dot_general(left, right, (((1,), (0,)), ((), ())), preferred_element_type=F32)


def dot_nt(left, right):
    return lax.dot_general(left, right, (((1,), (1,)), ((), ())), preferred_element_type=F32)


def dot_tn(left, right):
    return lax.dot_general(left, right, (((0,), (0,)), ((), ())), preferred_element_type=F32)


def head_view(width, head_dim):
    head = pl.program_id(0)
    tile = jnp.minimum(lax.div(head * head_dim, LANES), width // LANES - WINDOW // LANES)
    lanes = pl.ds(pl.multiple_of(tile * LANES, LANES), WINDOW)
    lane = lax.broadcasted_iota(jnp.int32, (1, WINDOW), 1) + tile * LANES
    mask = (lane >= head * head_dim) & (lane < (head + 1) * head_dim)
    order = [jnp.bitwise_xor(jnp.int32(code), head) for code in NESTED]
    return head, lanes, mask, order


def own_rows(ref, lanes, order, lead=()):
    return jnp.concatenate([ref[(*lead, code, slice(None), lanes)] for code in order], axis=0)


def key_rows(own_ref, far_ref, lanes, order):
    found = [own_ref[d, code, :, lanes] for d in range(own_ref.shape[0]) for code in order]
    if far_ref is not None:
        found += [
            far_ref[d, lax.div(code, 2), :, lanes]
            for d in range(far_ref.shape[0])
            for code in order[: RESIDUES // 2]
        ]
    return jnp.concatenate(found, axis=0)


def keep_results(earlier, results):
    @pl.when(pl.program_id(0) == 0)
    def _():
        for before, after in zip(earlier, results):
            after[...] = before[...]


def biased_scores(raw, bias_ref, first, rows, block, scale):
    keys = raw.shape[1]
    bias = bias_ref[0]
    pieces = []
    step = min(LANES, rows)
    for start in range(first, first + rows, step):
        part = raw[start - first : start - first + step] * scale
        added = []
        counts = []
        cut = start
        while cut < start + step:
            level = LEVELS[cut // block]
            stop = cut
            while stop < start + step and LEVELS[stop // block] == level:
                stop += block
            added.append(part[cut - start : stop - start] + bias[level : level + 1, :keys])
            counts.append(jnp.full((stop - cut, 1), math.log2(1.0 + level), F32))
            cut = stop
        whole = added[0] if len(added) == 1 else jnp.concatenate(added, axis=0)
        count = counts[0] if len(counts) == 1 else jnp.concatenate(counts, axis=0)
        here = part[:, start : start + step] + count
        eye = lax.broadcasted_iota(jnp.int32, (step, step), 0) == lax.broadcasted_iota(
            jnp.int32, (step, step), 1
        )
        here = jnp.where(eye, here, whole[:, start : start + step])
        sides = [whole[:, :start]] if start else []
        sides.append(here)
        if start + step < keys:
            sides.append(whole[:, start + step :])
        pieces.append(jnp.concatenate(sides, axis=1) if len(sides) > 1 else here)
    return pieces[0] if len(pieces) == 1 else jnp.concatenate(pieces, axis=0)


def put_rows(ref, value, lanes, mask, order, first, block):
    for at in range(value.shape[0] // block):
        code = order[first // block + at]
        fresh = value[at * block : (at + 1) * block].astype(ref.dtype)
        ref[code, :, lanes] = jnp.where(mask, fresh, ref[code, :, lanes])


def forward_kernel(rows, chunk, head_dim, far, *refs):
    q_ref, k_ref, v_ref = refs[:3]
    kx_ref, vx_ref = refs[3:5] if far else (None, None)
    bias_ref = refs[5 if far else 3]
    o_ref, t_ref = refs[-2:]
    block = rows // RESIDUES
    if far:
        keep_results(refs[6:8], refs[-2:])
    head, lanes, mask, order = head_view(q_ref.shape[-1], head_dim)
    scale = head_dim ** (-0.5) * math.log2(math.e)
    mine = order[: RESIDUES // 2] if far else order[RESIDUES // 2 :]
    queries = jnp.where(mask, own_rows(q_ref, lanes, mine), jnp.zeros((), BF16))
    keys = key_rows(k_ref, kx_ref, lanes, order)
    values = key_rows(v_ref, vx_ref, lanes, order)
    lane = lax.broadcasted_iota(jnp.int32, (1, LANES), 1)
    start = 0 if far else rows // 2
    for first in range(start, start + rows // 2, chunk):
        raw = dot_nt(queries[first - start : first - start + chunk], keys)
        scores = biased_scores(raw, bias_ref, first, chunk, block, scale)
        highest = jnp.max(scores, axis=1, keepdims=True)
        weights = jnp.exp2(scores - highest)
        total = jnp.sum(weights, axis=1, keepdims=True)
        mixed = dot_nn(weights.astype(BF16), values) * (1.0 / total)
        put_rows(o_ref, mixed, lanes, mask, order, first, block)
        total_log = highest + jnp.log2(total)
        for at in range(chunk // block):
            code = order[first // block + at]
            t_ref[code] = jnp.where(
                lane == head, total_log[at * block : (at + 1) * block], t_ref[code]
            )


def backward_kernel(rows, chunk, head_dim, far, *refs):
    q_ref, k_ref, v_ref = refs[:3]
    kx_ref, vx_ref = refs[3:5] if far else (None, None)
    bias_ref, o_ref, g_ref, t_ref = refs[5:9] if far else refs[3:7]
    if far:
        dq_ref, dk_ref, dv_ref, dkx_ref, dvx_ref, probs_ref, grads_ref = refs[9:]
    else:
        before, dq_ref, dk_ref, dv_ref, probs_ref, grads_ref = refs[7:]
        keep_results([before], [dq_ref])
    block = rows // RESIDUES
    half = rows // 2
    head, lanes, mask, order = head_view(q_ref.shape[-1], head_dim)
    mine = order[: RESIDUES // 2] if far else order[RESIDUES // 2 :]
    natural = head_dim ** (-0.5)
    scale = natural * math.log2(math.e)
    zero = jnp.zeros((), BF16)
    queries = jnp.where(mask, own_rows(q_ref, lanes, mine), zero)
    upstream = jnp.where(mask, own_rows(g_ref, lanes, mine), zero)
    mixed = own_rows(o_ref, lanes, mine)
    logs = jnp.concatenate([t_ref[code] for code in mine], axis=0)
    keys = key_rows(k_ref, kx_ref, lanes, order)
    values = key_rows(v_ref, vx_ref, lanes, order)
    lane = lax.broadcasted_iota(jnp.int32, (1, LANES), 1)
    start = 0 if far else half
    for first in range(start, start + half, chunk):
        span = slice(first - start, first - start + chunk)
        raw = dot_nt(queries[span], keys)
        scores = biased_scores(raw, bias_ref, first, chunk, block, scale)
        total_log = jnp.sum(jnp.where(lane == head, logs[span], 0.0), axis=1, keepdims=True)
        inner = jnp.sum(
            upstream[span].astype(F32) * mixed[span].astype(F32), axis=1, keepdims=True
        )
        probs = jnp.exp2(scores - total_log)
        prob_grad = dot_nt(upstream[span], values)
        score_grad = (probs * (prob_grad - inner)).astype(BF16)
        probs_ref[span] = probs.astype(BF16)
        grads_ref[span] = score_grad
        query_grad = dot_nn(score_grad, keys) * natural
        put_rows(dq_ref, query_grad, lanes, mask, order, first, block)
    value_grad = dot_tn(probs_ref[...], upstream)
    key_grad = dot_tn(grads_ref[...], queries) * natural
    for d in range(k_ref.shape[0]):
        part = slice(d * rows, (d + 1) * rows)
        put_rows(dk_ref.at[d], key_grad[part], lanes, mask, order, 0, block)
        put_rows(dv_ref.at[d], value_grad[part], lanes, mask, order, 0, block)
    if far:
        halves = [lax.div(code, 2) for code in order]
        for d in range(kx_ref.shape[0]):
            part = slice(k_ref.shape[0] * rows + d * half, k_ref.shape[0] * rows + (d + 1) * half)
            put_rows(dkx_ref.at[d], key_grad[part], lanes, mask, halves, 0, block)
            put_rows(dvx_ref.at[d], value_grad[part], lanes, mask, halves, 0, block)


def whole_spec(shape):
    zeros = (0,) * len(shape)
    return pl.BlockSpec(shape, lambda h: zeros)


def bias_spec(bias):
    return pl.BlockSpec((1,) + bias.shape[1:], lambda h: (h, 0, 0))


def attention_call(kernel, name, head_dim, far, ins, outs, scratch, matmuls):
    q, k = ins[0], ins[1]
    blocks, block, width = q.shape
    rows = blocks * block
    chunk = min(256, rows // 2)
    keys = k.shape[0] * rows + (ins[3].shape[0] * rows // 2 if far else 0)
    pairs = HEADS * rows // 2 * keys
    bias = 5 if far else 3
    return pl.pallas_call(
        functools.partial(kernel, rows, chunk, head_dim, far),
        grid=(HEADS,),
        in_specs=[bias_spec(m) if i == bias else whole_spec(m.shape) for i, m in enumerate(ins)],
        out_specs=[whole_spec(m.shape) for m in outs],
        out_shape=outs,
        scratch_shapes=[pltpu.VMEM((rows // 2, keys), BF16)] * scratch,
        compiler_params=pltpu.CompilerParams(vmem_limit_bytes=VMEM_LIMIT),
        cost_estimate=pl.CostEstimate(
            flops=2 * matmuls * pairs * LANES,
            transcendentals=pairs,
            bytes_accessed=8 * rows * width,
        ),
        name=name,
    )(*ins)


def like(*members):
    return [jax.ShapeDtypeStruct(m.shape, m.dtype) for m in members]


def attend(q, k, v, bias, head_dim):
    outs = like(q) + [jax.ShapeDtypeStruct((*q.shape[:2], LANES), F32)]
    return attention_call(forward_kernel, "attend_own", head_dim, False, (q, k, v, bias), outs, 0, 2)


def attend_far(q, k, v, kx, vx, bias, o, t, head_dim):
    ins = (q, k, v, kx, vx, bias, o, t)
    return attention_call(forward_kernel, "attend_far", head_dim, True, ins, like(o, t), 0, 2)


def attend_far_back(q, k, v, kx, vx, bias, o, g, t, head_dim):
    ins = (q, k, v, kx, vx, bias, o, g, t)
    return attention_call(
        backward_kernel, "attend_far_back", head_dim, True, ins, like(q, k, v, kx, vx), 2, 5
    )


def attend_back(q, k, v, bias, o, g, t, dq, head_dim):
    ins = (q, k, v, bias, o, g, t, dq)
    return attention_call(
        backward_kernel, "attend_own_back", head_dim, False, ins, like(q, k, v), 2, 5
    )


def head_positions(rows):
    block = rows // RESIDUES
    code = np.array(NESTED)[None, :, None] ^ np.arange(HEADS)[:, None, None]
    return (np.arange(block)[None, None, :] * RESIDUES + code).reshape(HEADS, rows)


def key_bias(rows, own_starts, far_starts, own_count, far_count, same):
    block = rows // RESIDUES
    places = head_positions(rows)
    level = np.arange(8)[:, None]
    blocks = np.array(LEVELS)[np.arange(rows) // block][None, :]
    own_times = np.log2(1.0 + np.minimum(level, blocks)).astype(np.float32)
    with np.errstate(divide="ignore"):
        far_times = np.log2(np.minimum(level, blocks)[:, : rows // 2]).astype(np.float32)
    far_times = np.maximum(far_times, np.float32(NEGATIVE))
    parts = []
    for start in own_starts:
        live = start + jnp.asarray(places) < own_count
        parts.append(jnp.where(live[:, None, :], own_times[None], NEGATIVE))
    for start in far_starts:
        live = (start + jnp.asarray(places[:, : rows // 2]) < far_count) & same
        parts.append(jnp.where(live[:, None, :], far_times[None], NEGATIVE))
    return jnp.concatenate(parts, axis=2)


def parity_lanes(width, head_dim):
    return (np.arange(width) // head_dim) % 2 == 1


def half_of(table, odd):
    split = table.reshape(RESIDUES // 2, 2, *table.shape[1:])
    return jnp.where(odd, split[:, 1], split[:, 0])


def add_half(total, half, odd):
    split = total.reshape(RESIDUES // 2, 2, *total.shape[1:]).astype(F32)
    half = half.astype(F32)
    both = jnp.stack(
        [split[:, 0] + jnp.where(odd, 0.0, half), split[:, 1] + jnp.where(odd, half, 0.0)], axis=1
    )
    return both.reshape(total.shape)


def swap_pairs(value):
    return lax.ppermute(value, "branch", [(0, 1), (1, 0)])


def gather_columns(shard, branches):
    if branches != 2:
        return lax.all_gather(shard, "branch", axis=shard.ndim - 1, tiled=True)
    other = swap_pairs(shard)
    first = lax.axis_index("branch") == 0
    return jnp.concatenate(
        [jnp.where(first, shard, other), jnp.where(first, other, shard)], axis=-1
    )


def scatter_columns(total, branches):
    if branches != 2:
        return lax.psum_scatter(
            total, "branch", scatter_dimension=total.ndim - 1, tiled=True
        ).astype(F32)
    half = total.shape[-1] // 2
    at = lax.axis_index("branch")
    keep = lax.dynamic_slice_in_dim(total, at * half, half, total.ndim - 1)
    away = lax.dynamic_slice_in_dim(total, (1 - at) * half, half, total.ndim - 1)
    return keep.astype(F32) + swap_pairs(away).astype(F32)


def weight_sum(partial, branches):
    low = lax.psum_scatter(partial, "slides", scatter_dimension=0, tiled=True)
    return scatter_columns(low, branches)


def flip(value, bit):
    return lax.ppermute(value, "slides", [(i, i ^ bit) for i in range(lax.axis_size("slides"))])


def shifted(value, step):
    size = lax.axis_size("slides")
    return lax.ppermute(value, "slides", [(i, (i + 4 * step) % size) for i in range(size)])


def place_kernel(depth, columns, *refs):
    spot = refs[0]
    pieces, full, sems = refs[1:5], refs[5], refs[6]
    outer, near, core, branch = spot[0], spot[1], spot[2], spot[3]
    copies = []
    for index, piece in enumerate(pieces):
        group, other_core = index % 2, index // 2
        rounds, width = piece.shape[2], piece.shape[4]
        for one in range(2):
            for two in range(2):
                far_branch, far_near = (one, two) if group == 0 else (two, one)
                for step in range(rounds):
                    shard = (
                        lax.rem(outer - step + rounds, rounds) * 4
                        + jnp.bitwise_xor(near, far_near) * 2
                        + jnp.bitwise_xor(core, other_core)
                    )
                    row = pl.multiple_of(shard * depth, 16)
                    offset = 0 if group == 0 else columns - width
                    column = jnp.bitwise_xor(branch, far_branch) * columns + offset
                    copies.append(
                        pltpu.make_async_copy(
                            piece.at[one, two, step],
                            full.at[
                                pl.ds(row, depth), pl.ds(pl.multiple_of(column, LANES), width)
                            ],
                            sems.at[len(copies)],
                        )
                    )
    for copy in copies:
        copy.start()
    for copy in copies:
        copy.wait()


def gather_matrix(shard, branches):
    size = lax.axis_size("slides")
    depth, columns = shard.shape
    if branches != 2 or size % 4 or depth % 16 or columns % LANES:
        return lax.all_gather(gather_columns(shard, branches), "slides", axis=0, tiled=True)
    held = [shard] + [shifted(shard, step) for step in range(1, size // 4)]
    half = columns // 2 // LANES * LANES
    first = jnp.stack([m[:, :half] for m in held])
    second = jnp.stack([m[:, half:] for m in held])
    first, second = jnp.stack([first, flip(first, 2)]), jnp.stack([second, swap_pairs(second)])
    first, second = jnp.stack([first, swap_pairs(first)]), jnp.stack([second, flip(second, 2)])
    pieces = (first, second, flip(first, 1), flip(second, 1))
    slide = lax.axis_index("slides")
    spot = jnp.stack(
        [
            lax.div(slide, 4),
            lax.rem(lax.div(slide, 2), 2),
            lax.rem(slide, 2),
            lax.axis_index("branch"),
        ]
    )
    return pl.pallas_call(
        functools.partial(place_kernel, depth, columns),
        in_specs=[pl.BlockSpec(memory_space=pltpu.SMEM)]
        + [pl.BlockSpec(memory_space=pl.ANY)] * len(pieces),
        out_specs=pl.BlockSpec(memory_space=pl.ANY),
        out_shape=jax.ShapeDtypeStruct((size * depth, branches * columns), shard.dtype),
        scratch_shapes=[pltpu.SemaphoreType.DMA((2 * branches * size,))],
        name="place",
    )(spot.astype(jnp.int32), *pieces)


def pick(table, index, axis):
    return lax.dynamic_index_in_dim(table, index, axis, keepdims=False)


def sum_matrix(partial, branches):
    size = lax.axis_size("slides")
    if branches != 2 or size % 4 or partial.shape[0] % (16 * size):
        return weight_sum(partial, branches)
    slide, at = lax.axis_index("slides"), lax.axis_index("branch")
    outer, near, core = lax.div(slide, 4), lax.rem(lax.div(slide, 2), 2), lax.rem(slide, 2)
    rounds = size // 4
    depth, columns = partial.shape[0] // size, partial.shape[1] // 2
    parts = partial.reshape(rounds, 2, 2, depth, 2, columns)

    def both(keep, sent):
        return (keep.astype(F32) + sent.astype(F32)).astype(BF16)

    parts = both(pick(parts, core, 2), flip(pick(parts, 1 - core, 2), 1))
    half = depth // 2
    first, second = parts[:, :, :half], parts[:, :, half:]
    first, second = (
        both(pick(first, at, 3), swap_pairs(pick(first, 1 - at, 3))),
        both(pick(second, near, 1), flip(pick(second, 1 - near, 1), 2)),
    )
    first, second = (
        both(pick(first, near, 1), flip(pick(first, 1 - near, 1), 2)),
        both(pick(second, at, 2), swap_pairs(pick(second, 1 - at, 2))),
    )
    joined = jnp.concatenate([first, second], axis=1)
    total = pick(joined, outer, 0).astype(F32)
    for step in range(1, rounds):
        total += shifted(pick(joined, lax.rem(outer + step, rounds), 0), step).astype(F32)
    return total


def sum_vector(partial, branches):
    size = lax.axis_size("slides")
    if branches != 2 or size % 4:
        return lax.psum(partial, ("slides", "branch"))
    total = partial.reshape(-1, LANES)
    total += flip(total, 1)
    total += swap_pairs(total)
    total += flip(total, 2)
    held = [shifted(total, step) for step in range(1, size // 4)]
    return sum(held, total).reshape(-1)


def on_device(
    tokens,
    cotangent,
    first_gain,
    first_shift,
    joint_weight,
    joint_bias,
    output_weight,
    output_bias,
    second_gain,
    second_shift,
    expand_weight,
    expand_bias,
    reduce_weight,
    reduce_bias,
    block_owner,
    tile_count,
):
    rows, width = tokens.shape
    branches = lax.axis_size("branch")
    head_dim = width // HEADS
    block = rows // RESIDUES
    mates = SEG_BASE // rows
    at = lax.axis_index("branch")
    segment = lax.div(at, mates)
    within = at - segment * mates
    odd = parity_lanes(width, head_dim)

    def residues_first(table):
        return table.reshape(block, RESIDUES, width).swapaxes(0, 1).reshape(rows, width)

    def positions_first(table):
        return table.reshape(RESIDUES, block, width).swapaxes(0, 1).reshape(rows, width)

    joint_full = gather_matrix(joint_weight, branches)
    output_full = lax.all_gather(gather_columns(output_weight, branches), "slides", axis=0, tiled=True)
    expand_full = lax.all_gather(gather_columns(expand_weight, branches), "slides", axis=0, tiled=True)
    reduce_full = lax.all_gather(gather_columns(reduce_weight, branches), "slides", axis=0, tiled=True)
    parameters = (
        first_gain, first_shift, joint_bias, output_bias,
        second_gain, second_shift, expand_bias, reduce_bias,
    )
    packed = lax.all_gather(jnp.concatenate(parameters), "branch", axis=0, tiled=False)
    vectors = []
    cut = 0
    for member in parameters:
        size = member.shape[0]
        vectors.append(packed[:, cut : cut + size].reshape(-1).astype(F32))
        cut += size
    gain_one, shift_one, bias_joint, bias_output, gain_two, shift_two, bias_expand, bias_reduce = vectors

    owners = block_owner.reshape(-1)
    counts = tile_count.reshape(-1)
    own_count = jnp.where(segment == 0, counts[0], counts[1])
    far_count = jnp.where(segment == 0, counts[1], counts[0])
    own_starts = [lax.rem(within + d, mates) * rows for d in range(mates)]
    far_starts = [d * rows for d in range(mates)]
    bias = key_bias(rows, own_starts, far_starts, own_count, far_count, owners[0] == owners[1])

    tokens_f = residues_first(tokens).astype(F32)
    upstream_low = residues_first(cotangent)
    normed_one, inverse_one = standardize(tokens_f)
    hidden_one = (normed_one * gain_one + shift_one).astype(BF16)
    joint_rows = jnp.dot(hidden_one, joint_full, preferred_element_type=F32)
    shape = (RESIDUES, block, width)
    q = (joint_rows[:, :width] + bias_joint[:width]).astype(BF16).reshape(shape)
    k = joint_rows[:, width : 2 * width].astype(BF16).reshape(shape)
    v = (joint_rows[:, 2 * width :] + bias_joint[width:]).astype(BF16).reshape(shape)
    if mates == 1 and branches == 2:
        k_own, v_own = k[None], v[None]
        k_far, v_far = swap_pairs(half_of(k, odd))[None], swap_pairs(half_of(v, odd))[None]
    else:
        k_all = lax.all_gather(k, "branch", axis=0)
        v_all = lax.all_gather(v, "branch", axis=0)
        own_at = [segment * mates + lax.rem(within + d, mates) for d in range(mates)]
        far_at = [(1 - segment) * mates + d for d in range(mates)]
        k_own = jnp.stack([lax.dynamic_index_in_dim(k_all, d, 0, False) for d in own_at])
        v_own = jnp.stack([lax.dynamic_index_in_dim(v_all, d, 0, False) for d in own_at])
        k_far = jnp.stack([half_of(lax.dynamic_index_in_dim(k_all, d, 0, False), odd) for d in far_at])
        v_far = jnp.stack([half_of(lax.dynamic_index_in_dim(v_all, d, 0, False), odd) for d in far_at])
    own_bias = bias[:, :, : mates * rows]
    attended, total_log = attend(q, k_own, v_own, own_bias, head_dim)
    attended, total_log = attend_far(
        q, k_own, v_own, k_far, v_far, bias, attended, total_log, head_dim
    )
    attended_rows = attended.reshape(rows, width)
    middle = tokens_f + jnp.dot(attended_rows, output_full, preferred_element_type=F32) + bias_output
    normed_two, inverse_two = standardize(middle)
    hidden_two = (normed_two * gain_two + shift_two).astype(BF16)
    expanded = jnp.dot(hidden_two, expand_full, preferred_element_type=F32) + bias_expand
    activated, slope = gelu_pair(expanded)
    activated = activated.astype(BF16)
    output = middle + jnp.dot(activated, reduce_full, preferred_element_type=F32) + bias_reduce
    output = positions_first(output.astype(BF16))

    upstream = upstream_low.astype(F32)
    reduce_bias_part = jnp.sum(upstream, axis=0)
    reduce_weight_part = dot_tn(activated, upstream_low).astype(BF16)
    activated_grad = dot_nt(upstream_low, reduce_full)
    expanded_grad = (activated_grad * slope).astype(BF16)
    expand_bias_part = jnp.sum(expanded_grad.astype(F32), axis=0)
    expand_weight_part = dot_tn(hidden_two, expanded_grad).astype(BF16)
    hidden_two_grad = dot_nt(expanded_grad, expand_full)
    second_gain_part = jnp.sum(hidden_two_grad * normed_two, axis=0)
    second_shift_part = jnp.sum(hidden_two_grad, axis=0)
    middle_grad = upstream + norm_back(hidden_two_grad, normed_two, inverse_two, gain_two)
    output_bias_part = jnp.sum(middle_grad, axis=0)
    middle_low = middle_grad.astype(BF16)
    output_weight_part = dot_tn(attended_rows, middle_low).astype(BF16)
    mixed_grad = dot_nt(middle_low, output_full).astype(BF16).reshape(shape)

    mixed_grad, reduce_weight_part, expand_weight_part, output_weight_part = (
        lax.optimization_barrier(
            (mixed_grad, reduce_weight_part, expand_weight_part, output_weight_part)
        )
    )
    reduce_sum = weight_sum(reduce_weight_part, branches)
    expand_sum = weight_sum(expand_weight_part, branches)
    output_sum = weight_sum(output_weight_part, branches)

    dq, dk_first, dv_first, dk_far, dv_far = attend_far_back(
        q, k_own, v_own, k_far, v_far, bias, attended, mixed_grad, total_log, head_dim
    )
    dq, dk_own, dv_own = attend_back(
        q, k_own, v_own, own_bias, attended, mixed_grad, total_log, dq, head_dim
    )
    dk_own = dk_own.astype(F32) + dk_first.astype(F32)
    dv_own = dv_own.astype(F32) + dv_first.astype(F32)
    if mates == 1 and branches == 2:
        key_sum = add_half(dk_own[0], swap_pairs(dk_far[0]), odd)
        value_sum = add_half(dv_own[0], swap_pairs(dv_far[0]), odd)
    else:

        def spread(own, far):
            canvas = jnp.zeros((branches, *shape), BF16)
            for d, index in enumerate(own_at):
                canvas = lax.dynamic_update_index_in_dim(canvas, own[d].astype(BF16), index, 0)
            for d, index in enumerate(far_at):
                full = add_half(jnp.zeros(shape, F32), far[d], odd).astype(BF16)
                canvas = lax.dynamic_update_index_in_dim(canvas, full, index, 0)
            return lax.psum_scatter(canvas, "branch", scatter_dimension=0, tiled=True)[0]

        key_sum = spread(dk_own, dk_far)
        value_sum = spread(dv_own, dv_far)
    query_low = dq.reshape(rows, width)
    value_low = value_sum.astype(BF16).reshape(rows, width)
    joint_grad = jnp.concatenate(
        [query_low, key_sum.astype(BF16).reshape(rows, width), value_low], axis=1
    )
    joint_bias_part = jnp.concatenate(
        [jnp.sum(query_low.astype(F32), axis=0), jnp.sum(value_low.astype(F32), axis=0)]
    )
    joint_weight_part = dot_tn(hidden_one, joint_grad).astype(BF16)
    joint_sum = sum_matrix(joint_weight_part, branches)
    hidden_one_grad = dot_nt(joint_grad, joint_full)
    first_gain_part = jnp.sum(hidden_one_grad * normed_one, axis=0)
    first_shift_part = jnp.sum(hidden_one_grad, axis=0)
    tokens_grad = middle_grad + norm_back(hidden_one_grad, normed_one, inverse_one, gain_one)
    tokens_grad = positions_first(tokens_grad)

    partial_vectors = (
        first_gain_part, first_shift_part, joint_bias_part, output_bias_part,
        second_gain_part, second_shift_part, expand_bias_part, reduce_bias_part,
    )
    summed = sum_vector(jnp.concatenate(partial_vectors), branches)
    mine = []
    cut = 0
    for member in partial_vectors:
        size = member.shape[0]
        share = size // branches
        mine.append(lax.dynamic_slice_in_dim(summed, cut + at * share, share))
        cut += size
    return (
        output,
        tokens_grad,
        mine[0],
        mine[1],
        joint_sum,
        mine[2],
        output_sum,
        mine[3],
        mine[4],
        mine[5],
        expand_sum,
        mine[6],
        reduce_sum,
        mine[7],
    )


def solution(mesh):
    rows = P(("slides", "branch"), None)
    matrix = P("slides", "branch")
    vector = P("branch")
    placed = (
        rows, rows, vector, vector, matrix, vector, matrix, vector,
        vector, vector, matrix, vector, matrix, vector, P("slides", None), P("slides", None),
    )
    given = (
        rows, rows, vector, vector, matrix, vector, matrix, vector,
        vector, vector, matrix, vector, matrix, vector,
    )
    return jax.shard_map(on_device, mesh=mesh, in_specs=placed, out_specs=given, check_vma=False)
```

```python
import functools
import math

import jax
import jax.numpy as jnp
import numpy as np
from jax import lax
from jax.experimental import pallas as pl
from jax.experimental.pallas import tpu as pltpu
from jax.sharding import PartitionSpec as P

HEADS = 16
SEG_BASE = 1024
BRANCHES = 5
RESIDUES = 2 ** (BRANCHES - 1)
EPSILON = 1e-05
NEGATIVE = -1e30
WINDOW = 256
LANES = 128
VMEM_LIMIT = 60 * 1024 * 1024
NESTED = [int(format(j, "04b")[::-1], 2) for j in range(RESIDUES)]
LEVELS = [BRANCHES - 1 if j == 0 else BRANCHES - 2 - int(math.log2(j)) for j in range(RESIDUES)]

BF16 = jnp.bfloat16
F32 = jnp.float32


def standardize(values):
    centred = values - jnp.mean(values, axis=-1, keepdims=True)
    inverse = lax.rsqrt(jnp.mean(centred * centred, axis=-1, keepdims=True) + EPSILON)
    return (centred * inverse, inverse)


def norm_back(upstream, normed, inverse, gain):
    scaled = upstream * gain
    return inverse * (
        scaled
        - jnp.mean(scaled, axis=-1, keepdims=True)
        - normed * jnp.mean(scaled * normed, axis=-1, keepdims=True)
    )


def gelu_pair(values):
    cumulative = 0.5 * (1.0 + lax.erf(values * (1.0 / math.sqrt(2.0))))
    density = jnp.exp(-0.5 * values * values) * (1.0 / math.sqrt(2.0 * math.pi))
    return values * cumulative, cumulative + values * density


def dot_nn(left, right):
    return lax.dot_general(left, right, (((1,), (0,)), ((), ())), preferred_element_type=F32)


def dot_nt(left, right):
    return lax.dot_general(left, right, (((1,), (1,)), ((), ())), preferred_element_type=F32)


def dot_tn(left, right):
    return lax.dot_general(left, right, (((0,), (0,)), ((), ())), preferred_element_type=F32)


def head_view(width, head_dim):
    head = pl.program_id(0)
    tile = jnp.minimum(lax.div(head * head_dim, LANES), width // LANES - WINDOW // LANES)
    lanes = pl.ds(pl.multiple_of(tile * LANES, LANES), WINDOW)
    lane = lax.broadcasted_iota(jnp.int32, (1, WINDOW), 1) + tile * LANES
    mask = (lane >= head * head_dim) & (lane < (head + 1) * head_dim)
    order = [jnp.bitwise_xor(jnp.int32(code), head) for code in NESTED]
    return head, lanes, mask, order


def own_rows(ref, lanes, order, lead=()):
    return jnp.concatenate([ref[(*lead, code, slice(None), lanes)] for code in order], axis=0)


def key_rows(own_ref, far_ref, lanes, order):
    found = [own_ref[d, code, :, lanes] for d in range(own_ref.shape[0]) for code in order]
    if far_ref is not None:
        found += [
            far_ref[d, lax.div(code, 2), :, lanes]
            for d in range(far_ref.shape[0])
            for code in order[: RESIDUES // 2]
        ]
    return jnp.concatenate(found, axis=0)


def keep_results(earlier, results):
    @pl.when(pl.program_id(0) == 0)
    def _():
        for before, after in zip(earlier, results):
            after[...] = before[...]


def biased_scores(raw, bias_ref, first, rows, block, scale):
    keys = raw.shape[1]
    bias = bias_ref[0]
    pieces = []
    step = min(LANES, rows)
    for start in range(first, first + rows, step):
        part = raw[start - first : start - first + step] * scale
        added = []
        counts = []
        cut = start
        while cut < start + step:
            level = LEVELS[cut // block]
            stop = cut
            while stop < start + step and LEVELS[stop // block] == level:
                stop += block
            added.append(part[cut - start : stop - start] + bias[level : level + 1, :keys])
            counts.append(jnp.full((stop - cut, 1), math.log2(1.0 + level), F32))
            cut = stop
        whole = added[0] if len(added) == 1 else jnp.concatenate(added, axis=0)
        count = counts[0] if len(counts) == 1 else jnp.concatenate(counts, axis=0)
        here = part[:, start : start + step] + count
        eye = lax.broadcasted_iota(jnp.int32, (step, step), 0) == lax.broadcasted_iota(
            jnp.int32, (step, step), 1
        )
        here = jnp.where(eye, here, whole[:, start : start + step])
        sides = [whole[:, :start]] if start else []
        sides.append(here)
        if start + step < keys:
            sides.append(whole[:, start + step :])
        pieces.append(jnp.concatenate(sides, axis=1) if len(sides) > 1 else here)
    return pieces[0] if len(pieces) == 1 else jnp.concatenate(pieces, axis=0)


def put_rows(ref, value, lanes, mask, order, first, block):
    for at in range(value.shape[0] // block):
        code = order[first // block + at]
        fresh = value[at * block : (at + 1) * block].astype(ref.dtype)
        ref[code, :, lanes] = jnp.where(mask, fresh, ref[code, :, lanes])


def forward_kernel(rows, chunk, head_dim, far, *refs):
    q_ref, k_ref, v_ref = refs[:3]
    kx_ref, vx_ref = refs[3:5] if far else (None, None)
    bias_ref = refs[5 if far else 3]
    o_ref, t_ref = refs[-2:]
    block = rows // RESIDUES
    if far:
        keep_results(refs[6:8], refs[-2:])
    head, lanes, mask, order = head_view(q_ref.shape[-1], head_dim)
    scale = head_dim ** (-0.5) * math.log2(math.e)
    mine = order[: RESIDUES // 2] if far else order[RESIDUES // 2 :]
    queries = jnp.where(mask, own_rows(q_ref, lanes, mine), jnp.zeros((), BF16))
    keys = key_rows(k_ref, kx_ref, lanes, order)
    values = key_rows(v_ref, vx_ref, lanes, order)
    lane = lax.broadcasted_iota(jnp.int32, (1, LANES), 1)
    start = 0 if far else rows // 2
    for first in range(start, start + rows // 2, chunk):
        raw = dot_nt(queries[first - start : first - start + chunk], keys)
        scores = biased_scores(raw, bias_ref, first, chunk, block, scale)
        highest = jnp.max(scores, axis=1, keepdims=True)
        weights = jnp.exp2(scores - highest)
        total = jnp.sum(weights, axis=1, keepdims=True)
        mixed = dot_nn(weights.astype(BF16), values) * (1.0 / total)
        put_rows(o_ref, mixed, lanes, mask, order, first, block)
        total_log = highest + jnp.log2(total)
        for at in range(chunk // block):
            code = order[first // block + at]
            t_ref[code] = jnp.where(
                lane == head, total_log[at * block : (at + 1) * block], t_ref[code]
            )


def backward_kernel(rows, chunk, head_dim, far, *refs):
    q_ref, k_ref, v_ref = refs[:3]
    kx_ref, vx_ref = refs[3:5] if far else (None, None)
    bias_ref, o_ref, g_ref, t_ref = refs[5:9] if far else refs[3:7]
    if far:
        dq_ref, dk_ref, dv_ref, dkx_ref, dvx_ref, probs_ref, grads_ref = refs[9:]
    else:
        before, dq_ref, dk_ref, dv_ref, probs_ref, grads_ref = refs[7:]
        keep_results([before], [dq_ref])
    block = rows // RESIDUES
    half = rows // 2
    head, lanes, mask, order = head_view(q_ref.shape[-1], head_dim)
    mine = order[: RESIDUES // 2] if far else order[RESIDUES // 2 :]
    natural = head_dim ** (-0.5)
    scale = natural * math.log2(math.e)
    zero = jnp.zeros((), BF16)
    queries = jnp.where(mask, own_rows(q_ref, lanes, mine), zero)
    upstream = jnp.where(mask, own_rows(g_ref, lanes, mine), zero)
    mixed = own_rows(o_ref, lanes, mine)
    logs = jnp.concatenate([t_ref[code] for code in mine], axis=0)
    keys = key_rows(k_ref, kx_ref, lanes, order)
    values = key_rows(v_ref, vx_ref, lanes, order)
    lane = lax.broadcasted_iota(jnp.int32, (1, LANES), 1)
    start = 0 if far else half
    for first in range(start, start + half, chunk):
        span = slice(first - start, first - start + chunk)
        raw = dot_nt(queries[span], keys)
        scores = biased_scores(raw, bias_ref, first, chunk, block, scale)
        total_log = jnp.sum(jnp.where(lane == head, logs[span], 0.0), axis=1, keepdims=True)
        inner = jnp.sum(
            upstream[span].astype(F32) * mixed[span].astype(F32), axis=1, keepdims=True
        )
        probs = jnp.exp2(scores - total_log)
        prob_grad = dot_nt(upstream[span], values)
        score_grad = (probs * (prob_grad - inner)).astype(BF16)
        probs_ref[span] = probs.astype(BF16)
        grads_ref[span] = score_grad
        query_grad = dot_nn(score_grad, keys) * natural
        put_rows(dq_ref, query_grad, lanes, mask, order, first, block)
    value_grad = dot_tn(probs_ref[...], upstream)
    key_grad = dot_tn(grads_ref[...], queries) * natural
    for d in range(k_ref.shape[0]):
        part = slice(d * rows, (d + 1) * rows)
        put_rows(dk_ref.at[d], key_grad[part], lanes, mask, order, 0, block)
        put_rows(dv_ref.at[d], value_grad[part], lanes, mask, order, 0, block)
    if far:
        halves = [lax.div(code, 2) for code in order]
        for d in range(kx_ref.shape[0]):
            part = slice(k_ref.shape[0] * rows + d * half, k_ref.shape[0] * rows + (d + 1) * half)
            put_rows(dkx_ref.at[d], key_grad[part], lanes, mask, halves, 0, block)
            put_rows(dvx_ref.at[d], value_grad[part], lanes, mask, halves, 0, block)


def whole_spec(shape):
    zeros = (0,) * len(shape)
    return pl.BlockSpec(shape, lambda h: zeros)


def bias_spec(bias):
    return pl.BlockSpec((1,) + bias.shape[1:], lambda h: (h, 0, 0))


def attention_call(kernel, name, head_dim, far, ins, outs, scratch, matmuls):
    q, k = ins[0], ins[1]
    blocks, block, width = q.shape
    rows = blocks * block
    chunk = min(256, rows // 2)
    keys = k.shape[0] * rows + (ins[3].shape[0] * rows // 2 if far else 0)
    pairs = HEADS * rows // 2 * keys
    bias = 5 if far else 3
    return pl.pallas_call(
        functools.partial(kernel, rows, chunk, head_dim, far),
        grid=(HEADS,),
        in_specs=[bias_spec(m) if i == bias else whole_spec(m.shape) for i, m in enumerate(ins)],
        out_specs=[whole_spec(m.shape) for m in outs],
        out_shape=outs,
        scratch_shapes=[pltpu.VMEM((rows // 2, keys), BF16)] * scratch,
        compiler_params=pltpu.CompilerParams(vmem_limit_bytes=VMEM_LIMIT),
        cost_estimate=pl.CostEstimate(
            flops=2 * matmuls * pairs * LANES,
            transcendentals=pairs,
            bytes_accessed=8 * rows * width,
        ),
        name=name,
    )(*ins)


def like(*members):
    return [jax.ShapeDtypeStruct(m.shape, m.dtype) for m in members]


def attend(q, k, v, bias, head_dim):
    outs = like(q) + [jax.ShapeDtypeStruct((*q.shape[:2], LANES), F32)]
    return attention_call(forward_kernel, "attend_own", head_dim, False, (q, k, v, bias), outs, 0, 2)


def attend_far(q, k, v, kx, vx, bias, o, t, head_dim):
    ins = (q, k, v, kx, vx, bias, o, t)
    return attention_call(forward_kernel, "attend_far", head_dim, True, ins, like(o, t), 0, 2)


def attend_far_back(q, k, v, kx, vx, bias, o, g, t, head_dim):
    ins = (q, k, v, kx, vx, bias, o, g, t)
    return attention_call(
        backward_kernel, "attend_far_back", head_dim, True, ins, like(q, k, v, kx, vx), 2, 5
    )


def attend_back(q, k, v, bias, o, g, t, dq, head_dim):
    ins = (q, k, v, bias, o, g, t, dq)
    return attention_call(
        backward_kernel, "attend_own_back", head_dim, False, ins, like(q, k, v), 2, 5
    )


def feed_forward_kernel(blocks, *refs):
    tokens_ref, attended_ref, cotangent_ref, small_ref, wide_ref, packed_ref = refs[:6]
    output_ref, active_ref, expanded_ref, hidden_ref, low_ref, grad_ref, mixed_ref, sums_ref, wide_sums_ref = refs[6:15]
    reduce_w, expand_w, output_w, sems = refs[15:]
    width = tokens_ref.shape[-1]
    depth = output_w.shape[1]

    @pl.when(pl.program_id(0) == 0)
    def _():
        cut = reduce_w.shape[1]
        copies = [
            pltpu.make_async_copy(
                packed_ref.at[:, pl.ds(cut + blocks * depth, depth)], output_w, sems.at[0]
            )
        ]
        for i in range(blocks):
            copies.append(
                pltpu.make_async_copy(
                    packed_ref.at[:, pl.ds(cut + i * depth, depth)], expand_w.at[i], sems.at[i + 1]
                )
            )
        copies.append(
            pltpu.make_async_copy(
                packed_ref.at[:, pl.ds(0, cut)], reduce_w, sems.at[blocks + 1]
            )
        )
        for copy in copies:
            copy.start()
        for copy in copies:
            copy.wait()
        sums_ref[...] = jnp.zeros_like(sums_ref)
        wide_sums_ref[...] = jnp.zeros_like(wide_sums_ref)

    bias_output, gain, shift, bias_reduce = (small_ref[i : i + 1] for i in range(4))
    project = output_w[...].reshape(width, width)
    middle = tokens_ref[...].astype(F32) + dot_nn(attended_ref[...], project) + bias_output
    normed, inverse = standardize(middle)
    hidden = (normed * gain + shift).astype(BF16)
    hidden_ref[...] = hidden
    cotangent = cotangent_ref[...]
    output = middle + bias_reduce
    hidden_grad = jnp.zeros(middle.shape, F32)
    shrink_all = reduce_w[...].reshape(blocks * width, width)
    for i in range(blocks):
        span = slice(i * width, (i + 1) * width)
        grow = expand_w[i].reshape(width, width)
        shrink = shrink_all[span]
        active, slope = gelu_pair(dot_nn(hidden, grow) + wide_ref[:, span])
        active = active.astype(BF16)
        active_ref[:, span] = active
        output += dot_nn(active, shrink)
        expanded = (dot_nt(cotangent, shrink) * slope).astype(BF16)
        expanded_ref[:, span] = expanded
        wide_sums_ref[:, span] += jnp.sum(expanded.astype(F32), axis=0, keepdims=True)
        hidden_grad += dot_nt(expanded, grow)
    output_ref[...] = output.astype(BF16)
    upstream = cotangent.astype(F32)
    middle_grad = upstream + norm_back(hidden_grad, normed, inverse, gain)
    grad_ref[...] = middle_grad
    low = middle_grad.astype(BF16)
    low_ref[...] = low
    mixed_ref[...] = dot_nt(low, project).astype(BF16)
    for i, part in enumerate((hidden_grad * normed, hidden_grad, middle_grad, upstream)):
        sums_ref[i : i + 1] += jnp.sum(part, axis=0, keepdims=True)


def feed_forward(tokens, attended, cotangent, small, wide, packed):
    rows, width = tokens.shape
    ff = wide.shape[1]
    blocks = ff // width
    shards = packed.shape[0]
    tile = min(rows, 256)
    narrow_spec = pl.BlockSpec((tile, width), lambda r: (r, 0))
    wide_spec = pl.BlockSpec((tile, ff), lambda r: (r, 0))
    return pl.pallas_call(
        functools.partial(feed_forward_kernel, blocks),
        grid=(rows // tile,),
        in_specs=[narrow_spec] * 3
        + [whole_spec(small.shape), whole_spec(wide.shape), pl.BlockSpec(memory_space=pl.ANY)],
        out_specs=[
            narrow_spec, wide_spec, wide_spec, narrow_spec, narrow_spec, narrow_spec, narrow_spec,
            whole_spec((4, width)), whole_spec((1, ff)),
        ],
        out_shape=[
            jax.ShapeDtypeStruct((rows, width), BF16),
            jax.ShapeDtypeStruct((rows, ff), BF16),
            jax.ShapeDtypeStruct((rows, ff), BF16),
            jax.ShapeDtypeStruct((rows, width), BF16),
            jax.ShapeDtypeStruct((rows, width), BF16),
            jax.ShapeDtypeStruct((rows, width), F32),
            jax.ShapeDtypeStruct((rows, width), BF16),
            jax.ShapeDtypeStruct((4, width), F32),
            jax.ShapeDtypeStruct((1, ff), F32),
        ],
        scratch_shapes=[
            pltpu.VMEM((shards, ff // shards, width), BF16),
            pltpu.VMEM((blocks, shards, width // shards, width), BF16),
            pltpu.VMEM((shards, width // shards, width), BF16),
            pltpu.SemaphoreType.DMA((blocks + 2,)),
        ],
        compiler_params=pltpu.CompilerParams(vmem_limit_bytes=VMEM_LIMIT),
        cost_estimate=pl.CostEstimate(
            flops=2 * rows * width * (4 * ff + 2 * width),
            transcendentals=2 * rows * ff,
            bytes_accessed=2 * packed.size + 20 * rows * width,
        ),
        name="feed_forward",
    )(tokens, attended, cotangent, small, wide, packed)


def weight_kernel(left_ref, right_ref, *refs):
    out_ref = refs[-1]
    product = dot_tn(left_ref[...], right_ref[...])
    out_ref[...] = product.astype(BF16).reshape(out_ref.shape)


def packed_gradient(left, right, before, shape, depth, first):
    rows, features = left.shape
    width = shape[-1]
    columns = right.shape[1] // width
    step = min(384, features)
    many = step // depth if depth < step else 1
    block = (many, depth, width) if depth < step else (1, step, width)
    tall = block[1]
    inner = depth // tall

    def out_map(i, g):
        return (g, first // tall + i, 0) if depth < step else (0, first // tall + i * inner + g, 0)

    before = [] if before is None else [before]
    return pl.pallas_call(
        weight_kernel,
        grid=(columns, features // step),
        in_specs=[
            pl.BlockSpec((rows, step), lambda i, g: (0, g)),
            pl.BlockSpec((rows, width), lambda i, g: (0, i)),
        ]
        + [pl.BlockSpec(memory_space=pl.ANY)] * len(before),
        out_specs=pl.BlockSpec(block, out_map),
        out_shape=jax.ShapeDtypeStruct(shape, BF16),
        input_output_aliases={2: 0} if before else {},
        compiler_params=pltpu.CompilerParams(vmem_limit_bytes=VMEM_LIMIT),
        cost_estimate=pl.CostEstimate(
            flops=2 * rows * features * right.shape[1],
            transcendentals=0,
            bytes_accessed=2 * (left.size + right.size + features * right.shape[1]),
        ),
        name="weight_gradient",
    )(left, right, *before)


def head_positions(rows):
    block = rows // RESIDUES
    code = np.array(NESTED)[None, :, None] ^ np.arange(HEADS)[:, None, None]
    return (np.arange(block)[None, None, :] * RESIDUES + code).reshape(HEADS, rows)


def key_bias(rows, own_starts, far_starts, own_count, far_count, same):
    block = rows // RESIDUES
    places = head_positions(rows)
    level = np.arange(8)[:, None]
    blocks = np.array(LEVELS)[np.arange(rows) // block][None, :]
    own_times = np.log2(1.0 + np.minimum(level, blocks)).astype(np.float32)
    with np.errstate(divide="ignore"):
        far_times = np.log2(np.minimum(level, blocks)[:, : rows // 2]).astype(np.float32)
    far_times = np.maximum(far_times, np.float32(NEGATIVE))
    parts = []
    for start in own_starts:
        live = start + jnp.asarray(places) < own_count
        parts.append(jnp.where(live[:, None, :], own_times[None], NEGATIVE))
    for start in far_starts:
        live = (start + jnp.asarray(places[:, : rows // 2]) < far_count) & same
        parts.append(jnp.where(live[:, None, :], far_times[None], NEGATIVE))
    return jnp.concatenate(parts, axis=2)


def parity_lanes(width, head_dim):
    return (np.arange(width) // head_dim) % 2 == 1


def half_of(table, odd):
    split = table.reshape(RESIDUES // 2, 2, *table.shape[1:])
    return jnp.where(odd, split[:, 1], split[:, 0])


def add_half(total, half, odd):
    split = total.reshape(RESIDUES // 2, 2, *total.shape[1:]).astype(F32)
    half = half.astype(F32)
    both = jnp.stack(
        [split[:, 0] + jnp.where(odd, 0.0, half), split[:, 1] + jnp.where(odd, half, 0.0)], axis=1
    )
    return both.reshape(total.shape)


def swap_pairs(value):
    return lax.ppermute(value, "branch", [(0, 1), (1, 0)])


def gather_columns(shard, branches):
    if branches != 2:
        return lax.all_gather(shard, "branch", axis=shard.ndim - 1, tiled=True)
    other = swap_pairs(shard)
    first = lax.axis_index("branch") == 0
    return jnp.concatenate(
        [jnp.where(first, shard, other), jnp.where(first, other, shard)], axis=-1
    )


def scatter_columns(total, branches):
    if branches != 2:
        return lax.psum_scatter(
            total, "branch", scatter_dimension=total.ndim - 1, tiled=True
        ).astype(F32)
    half = total.shape[-1] // 2
    at = lax.axis_index("branch")
    keep = lax.dynamic_slice_in_dim(total, at * half, half, total.ndim - 1)
    away = lax.dynamic_slice_in_dim(total, (1 - at) * half, half, total.ndim - 1)
    return keep.astype(F32) + swap_pairs(away).astype(F32)


def weight_sum(partial, branches):
    low = lax.psum_scatter(partial, "slides", scatter_dimension=0, tiled=True)
    return scatter_columns(low, branches)


def pack_rows(reduce_part, expand_part, output_part):
    width = output_part.shape[-1]
    blocks = expand_part.shape[-1] // width
    return jnp.concatenate(
        [reduce_part]
        + [expand_part[..., i * width : (i + 1) * width] for i in range(blocks)]
        + [output_part],
        axis=-2,
    )


def unpack_rows(packed, width, ff):
    blocks = ff // width
    depth = packed.shape[-2] // (2 * blocks + 1)
    cut = blocks * depth
    expand = [packed[..., cut + i * depth : cut + (i + 1) * depth, :] for i in range(blocks)]
    return packed[..., :cut, :], jnp.concatenate(expand, axis=-1), packed[..., 2 * cut :, :]


def gather_packed(reduce_weight, expand_weight, output_weight, branches):
    size = lax.axis_size("slides")
    shard = pack_rows(
        gather_columns(reduce_weight, branches),
        gather_columns(expand_weight, branches),
        gather_columns(output_weight, branches),
    )
    packed = lax.all_gather(shard, "slides", axis=0, tiled=False)
    if output_weight.shape[0] % 16 == 0:
        return packed
    parts = unpack_rows(packed, shard.shape[-1], size * reduce_weight.shape[0])
    return pack_rows(*(m.reshape(1, -1, m.shape[-1]) for m in parts))


def sum_packed(packed, branches, width, ff):
    size = lax.axis_size("slides")
    if packed.shape[0] != size:
        parts = unpack_rows(packed, width, ff)
        packed = pack_rows(*(m.reshape(size, -1, m.shape[-1]) for m in parts))
    rows = packed.shape[1]
    low = lax.psum_scatter(packed.reshape(size * rows, width), "slides", scatter_dimension=0, tiled=True)
    parts = unpack_rows(low, width, ff)
    return [scatter_columns(part, branches) for part in parts]


def flip(value, bit):
    return lax.ppermute(value, "slides", [(i, i ^ bit) for i in range(lax.axis_size("slides"))])


def shifted(value, step):
    size = lax.axis_size("slides")
    return lax.ppermute(value, "slides", [(i, (i + 4 * step) % size) for i in range(size)])


def place_kernel(depth, columns, *refs):
    spot, pieces, full = refs[0], refs[1:5], refs[5]
    outer, near, core, branch = spot[0], spot[1], spot[2], spot[3]
    for index, piece in enumerate(pieces):
        group, other_core = index % 2, index // 2
        rounds, width = piece.shape[2], piece.shape[4]
        for one in range(2):
            for two in range(2):
                far_branch, far_near = (one, two) if group == 0 else (two, one)
                offset = 0 if group == 0 else columns - width
                column = jnp.bitwise_xor(branch, far_branch) * columns + offset
                lanes = pl.ds(pl.multiple_of(column, LANES), width)
                for step in range(rounds):
                    shard = (
                        lax.rem(outer - step + rounds, rounds) * 4
                        + jnp.bitwise_xor(near, far_near) * 2
                        + jnp.bitwise_xor(core, other_core)
                    )
                    row = pl.multiple_of(shard * depth, 16)
                    full[pl.ds(row, depth), lanes] = piece[one, two, step]


def gather_matrix(shard, branches):
    size = lax.axis_size("slides")
    depth, columns = shard.shape
    if branches != 2 or size % 4 or depth % 16 or columns % LANES:
        return lax.all_gather(gather_columns(shard, branches), "slides", axis=0, tiled=True)
    held = [shard] + [shifted(shard, step) for step in range(1, size // 4)]
    half = columns // 2 // LANES * LANES
    first = jnp.stack([m[:, :half] for m in held])
    second = jnp.stack([m[:, half:] for m in held])
    first, second = jnp.stack([first, flip(first, 2)]), jnp.stack([second, swap_pairs(second)])
    first, second = jnp.stack([first, swap_pairs(first)]), jnp.stack([second, flip(second, 2)])
    pieces = (first, second, flip(first, 1), flip(second, 1))
    slide = lax.axis_index("slides")
    spot = jnp.stack(
        [
            lax.div(slide, 4),
            lax.rem(lax.div(slide, 2), 2),
            lax.rem(slide, 2),
            lax.axis_index("branch"),
        ]
    )
    return pl.pallas_call(
        functools.partial(place_kernel, depth, columns),
        in_specs=[pl.BlockSpec(memory_space=pltpu.SMEM)]
        + [pl.BlockSpec(memory_space=pltpu.VMEM)] * len(pieces),
        out_specs=pl.BlockSpec(memory_space=pltpu.VMEM),
        out_shape=jax.ShapeDtypeStruct((size * depth, branches * columns), shard.dtype),
        compiler_params=pltpu.CompilerParams(vmem_limit_bytes=VMEM_LIMIT),
        name="place",
    )(spot.astype(jnp.int32), *pieces)


def pick(table, index, axis):
    return lax.dynamic_index_in_dim(table, index, axis, keepdims=False)


def sum_matrix(partial, branches):
    size = lax.axis_size("slides")
    if branches != 2 or size % 4 or partial.shape[0] % (16 * size):
        return weight_sum(partial, branches)
    slide, at = lax.axis_index("slides"), lax.axis_index("branch")
    outer, near, core = lax.div(slide, 4), lax.rem(lax.div(slide, 2), 2), lax.rem(slide, 2)
    rounds = size // 4
    depth, columns = partial.shape[0] // size, partial.shape[1] // 2
    parts = partial.reshape(rounds, 2, 2, depth, 2, columns)

    def both(keep, sent):
        return (keep.astype(F32) + sent.astype(F32)).astype(BF16)

    parts = both(pick(parts, core, 2), flip(pick(parts, 1 - core, 2), 1))
    half = depth // 2
    first, second = parts[:, :, :half], parts[:, :, half:]
    first, second = (
        both(pick(first, at, 3), swap_pairs(pick(first, 1 - at, 3))),
        both(pick(second, near, 1), flip(pick(second, 1 - near, 1), 2)),
    )
    first, second = (
        both(pick(first, near, 1), flip(pick(first, 1 - near, 1), 2)),
        both(pick(second, at, 2), swap_pairs(pick(second, 1 - at, 2))),
    )
    joined = jnp.concatenate([first, second], axis=1)
    total = pick(joined, outer, 0).astype(F32)
    for step in range(1, rounds):
        total += shifted(pick(joined, lax.rem(outer + step, rounds), 0), step).astype(F32)
    return total


def sum_vector(partial, branches):
    size = lax.axis_size("slides")
    if branches != 2 or size % 4:
        return lax.psum(partial, ("slides", "branch"))
    total = partial.reshape(-1, LANES)
    total += flip(total, 1)
    total += swap_pairs(total)
    total += flip(total, 2)
    held = [shifted(total, step) for step in range(1, size // 4)]
    return sum(held, total).reshape(-1)


def on_device(
    tokens,
    cotangent,
    first_gain,
    first_shift,
    joint_weight,
    joint_bias,
    output_weight,
    output_bias,
    second_gain,
    second_shift,
    expand_weight,
    expand_bias,
    reduce_weight,
    reduce_bias,
    block_owner,
    tile_count,
):
    rows, width = tokens.shape
    branches = lax.axis_size("branch")
    head_dim = width // HEADS
    block = rows // RESIDUES
    mates = SEG_BASE // rows
    at = lax.axis_index("branch")
    segment = lax.div(at, mates)
    within = at - segment * mates
    odd = parity_lanes(width, head_dim)

    def residues_first(table):
        return table.reshape(block, RESIDUES, width).swapaxes(0, 1).reshape(rows, width)

    def positions_first(table):
        return table.reshape(RESIDUES, block, width).swapaxes(0, 1).reshape(rows, width)

    joint_full = gather_matrix(joint_weight, branches)
    packed_weights = gather_packed(reduce_weight, expand_weight, output_weight, branches)
    parameters = (
        first_gain, first_shift, joint_bias, output_bias,
        second_gain, second_shift, expand_bias, reduce_bias,
    )
    packed = lax.all_gather(jnp.concatenate(parameters), "branch", axis=0, tiled=False)
    vectors = []
    cut = 0
    for member in parameters:
        size = member.shape[0]
        vectors.append(packed[:, cut : cut + size].reshape(-1).astype(F32))
        cut += size
    gain_one, shift_one, bias_joint, bias_output, gain_two, shift_two, bias_expand, bias_reduce = vectors

    owners = block_owner.reshape(-1)
    counts = tile_count.reshape(-1)
    own_count = jnp.where(segment == 0, counts[0], counts[1])
    far_count = jnp.where(segment == 0, counts[1], counts[0])
    own_starts = [lax.rem(within + d, mates) * rows for d in range(mates)]
    far_starts = [d * rows for d in range(mates)]
    bias = key_bias(rows, own_starts, far_starts, own_count, far_count, owners[0] == owners[1])

    tokens_low = residues_first(tokens)
    tokens_f = tokens_low.astype(F32)
    upstream_low = residues_first(cotangent)
    normed_one, inverse_one = standardize(tokens_f)
    hidden_one = (normed_one * gain_one + shift_one).astype(BF16)
    joint_rows = jnp.dot(hidden_one, joint_full, preferred_element_type=F32)
    shape = (RESIDUES, block, width)
    q = (joint_rows[:, :width] + bias_joint[:width]).astype(BF16).reshape(shape)
    k = joint_rows[:, width : 2 * width].astype(BF16).reshape(shape)
    v = (joint_rows[:, 2 * width :] + bias_joint[width:]).astype(BF16).reshape(shape)
    if mates == 1 and branches == 2:
        k_own, v_own = k[None], v[None]
        k_far, v_far = swap_pairs(half_of(k, odd))[None], swap_pairs(half_of(v, odd))[None]
    else:
        k_all = lax.all_gather(k, "branch", axis=0)
        v_all = lax.all_gather(v, "branch", axis=0)
        own_at = [segment * mates + lax.rem(within + d, mates) for d in range(mates)]
        far_at = [(1 - segment) * mates + d for d in range(mates)]
        k_own = jnp.stack([lax.dynamic_index_in_dim(k_all, d, 0, False) for d in own_at])
        v_own = jnp.stack([lax.dynamic_index_in_dim(v_all, d, 0, False) for d in own_at])
        k_far = jnp.stack([half_of(lax.dynamic_index_in_dim(k_all, d, 0, False), odd) for d in far_at])
        v_far = jnp.stack([half_of(lax.dynamic_index_in_dim(v_all, d, 0, False), odd) for d in far_at])
    own_bias = bias[:, :, : mates * rows]
    attended, total_log = attend(q, k_own, v_own, own_bias, head_dim)
    attended, total_log = attend_far(
        q, k_own, v_own, k_far, v_far, bias, attended, total_log, head_dim
    )
    attended_rows = attended.reshape(rows, width)
    ff = bias_expand.shape[0]
    small = jnp.stack([bias_output, gain_two, shift_two, bias_reduce])
    (
        output, activated, expanded_grad, hidden_two, middle_low, middle_grad, mixed_grad, sums, wide_sums,
    ) = feed_forward(
        tokens_low, attended_rows, upstream_low, small, bias_expand.reshape(1, ff), packed_weights
    )
    output = positions_first(output)
    second_gain_part, second_shift_part, output_bias_part, reduce_bias_part = sums
    expand_bias_part = wide_sums.reshape(-1)
    shards = packed_weights.shape[0]
    packed_grads = packed_gradient(
        activated, upstream_low, None, packed_weights.shape, ff // shards, 0
    )
    packed_grads = packed_gradient(
        hidden_two, expanded_grad, packed_grads, packed_weights.shape, width // shards, ff // shards
    )
    packed_grads = packed_gradient(
        attended_rows, middle_low, packed_grads, packed_weights.shape, width // shards, 2 * ff // shards
    )
    mixed_grad, packed_grads = lax.optimization_barrier((mixed_grad.reshape(shape), packed_grads))
    reduce_sum, expand_sum, output_sum = sum_packed(packed_grads, branches, width, ff)

    dq, dk_first, dv_first, dk_far, dv_far = attend_far_back(
        q, k_own, v_own, k_far, v_far, bias, attended, mixed_grad, total_log, head_dim
    )
    dq, dk_own, dv_own = attend_back(
        q, k_own, v_own, own_bias, attended, mixed_grad, total_log, dq, head_dim
    )
    dk_own = dk_own.astype(F32) + dk_first.astype(F32)
    dv_own = dv_own.astype(F32) + dv_first.astype(F32)
    if mates == 1 and branches == 2:
        key_sum = add_half(dk_own[0], swap_pairs(dk_far[0]), odd)
        value_sum = add_half(dv_own[0], swap_pairs(dv_far[0]), odd)
    else:

        def spread(own, far):
            canvas = jnp.zeros((branches, *shape), BF16)
            for d, index in enumerate(own_at):
                canvas = lax.dynamic_update_index_in_dim(canvas, own[d].astype(BF16), index, 0)
            for d, index in enumerate(far_at):
                full = add_half(jnp.zeros(shape, F32), far[d], odd).astype(BF16)
                canvas = lax.dynamic_update_index_in_dim(canvas, full, index, 0)
            return lax.psum_scatter(canvas, "branch", scatter_dimension=0, tiled=True)[0]

        key_sum = spread(dk_own, dk_far)
        value_sum = spread(dv_own, dv_far)
    query_low = dq.reshape(rows, width)
    value_low = value_sum.astype(BF16).reshape(rows, width)
    joint_grad = jnp.concatenate(
        [query_low, key_sum.astype(BF16).reshape(rows, width), value_low], axis=1
    )
    joint_bias_part = jnp.concatenate(
        [jnp.sum(query_low.astype(F32), axis=0), jnp.sum(value_low.astype(F32), axis=0)]
    )
    joint_weight_part = dot_tn(hidden_one, joint_grad).astype(BF16)
    joint_sum = sum_matrix(joint_weight_part, branches)
    hidden_one_grad = dot_nt(joint_grad, joint_full)
    first_gain_part = jnp.sum(hidden_one_grad * normed_one, axis=0)
    first_shift_part = jnp.sum(hidden_one_grad, axis=0)
    tokens_grad = middle_grad + norm_back(hidden_one_grad, normed_one, inverse_one, gain_one)
    tokens_grad = positions_first(tokens_grad)

    partial_vectors = (
        first_gain_part, first_shift_part, joint_bias_part, output_bias_part,
        second_gain_part, second_shift_part, expand_bias_part, reduce_bias_part,
    )
    summed = sum_vector(jnp.concatenate(partial_vectors), branches)
    mine = []
    cut = 0
    for member in partial_vectors:
        size = member.shape[0]
        share = size // branches
        mine.append(lax.dynamic_slice_in_dim(summed, cut + at * share, share))
        cut += size
    return (
        output,
        tokens_grad,
        mine[0],
        mine[1],
        joint_sum,
        mine[2],
        output_sum,
        mine[3],
        mine[4],
        mine[5],
        expand_sum,
        mine[6],
        reduce_sum,
        mine[7],
    )


def solution(mesh):
    rows = P(("slides", "branch"), None)
    matrix = P("slides", "branch")
    vector = P("branch")
    placed = (
        rows, rows, vector, vector, matrix, vector, matrix, vector,
        vector, vector, matrix, vector, matrix, vector, P("slides", None), P("slides", None),
    )
    given = (
        rows, rows, vector, vector, matrix, vector, matrix, vector,
        vector, vector, matrix, vector, matrix, vector,
    )
    return jax.shard_map(on_device, mesh=mesh, in_specs=placed, out_specs=given, check_vma=False)
```

```python
import functools
import math

import jax
import jax.numpy as jnp
import ml_dtypes
import numpy as np
from jax import lax
from jax.experimental import pallas as pl
from jax.experimental.pallas import tpu as pltpu
from jax.sharding import PartitionSpec as P

HEADS = 16
SEG_BASE = 1024
BRANCHES = 5
RESIDUES = 2 ** (BRANCHES - 1)
EPSILON = 1e-05
NEGATIVE = -1e30
LANES = 128
EXTRA = 32
TIMES, LIVE, FIXED = 0, 12, 13
UNROLL = 2
PIECE = 512
VMEM_LIMIT = 60 * 1024 * 1024

BF16 = jnp.bfloat16
F32 = jnp.float32


def standardize(values):
    centred = values - jnp.mean(values, axis=-1, keepdims=True)
    inverse = lax.rsqrt(jnp.mean(centred * centred, axis=-1, keepdims=True) + EPSILON)
    return (centred * inverse, inverse)


def norm_back(upstream, normed, inverse, gain):
    scaled = upstream * gain
    return inverse * (
        scaled
        - jnp.mean(scaled, axis=-1, keepdims=True)
        - normed * jnp.mean(scaled * normed, axis=-1, keepdims=True)
    )


def gelu_pair(values):
    cumulative = 0.5 * (1.0 + lax.erf(values * (1.0 / math.sqrt(2.0))))
    density = jnp.exp(-0.5 * values * values) * (1.0 / math.sqrt(2.0 * math.pi))
    return values * cumulative, cumulative + values * density


def dot_nn(left, right):
    return lax.dot_general(left, right, (((1,), (0,)), ((), ())), preferred_element_type=F32)


def dot_nt(left, right):
    return lax.dot_general(left, right, (((1,), (1,)), ((), ())), preferred_element_type=F32)


def dot_tn(left, right):
    return lax.dot_general(left, right, (((0,), (0,)), ((), ())), preferred_element_type=F32)


def thirds(value):
    first = value.astype(BF16)
    rest = value - first.astype(F32)
    second = rest.astype(BF16)
    return first, second, (rest - second.astype(F32)).astype(BF16)


class HeadView:
    def __init__(self, head, far, refs, head_dim):
        half = refs["q"].shape[-1] // 2
        same = lax.rem(head, 2)
        same = same if far else 1 - same
        self.half = half
        self.rows = pl.ds(pl.multiple_of(head * head_dim, 16), head_dim)
        self.same = pl.ds(pl.multiple_of(same * half, LANES), half)
        self.other = pl.ds(pl.multiple_of((1 - same) * half, LANES), half)
        self.devices = refs["k"].shape[0]
        self.head = head
        self.far = far
        extras = [
            refs["same"][head] if far else refs["plain"][same],
            refs["plain"][1 - same],
        ]
        if far:
            extras.append(refs["far"][head])
        self.extra = jnp.concatenate(extras, axis=1)

    def gathered(self, own_ref, far_ref):
        found = [own_ref[d, self.rows, self.same] for d in range(self.devices)]
        found += [own_ref[d, self.rows, self.other] for d in range(self.devices)]
        if self.far:
            found += [far_ref[d, self.rows, :] for d in range(far_ref.shape[0])]
        return jnp.concatenate(found, axis=1)

    def spread(self, value, own_ref, far_ref, before_ref=None):
        half = self.half
        for d in range(self.devices):
            for lanes, at in ((self.same, d), (self.other, self.devices + d)):
                part = value[:, at * half : (at + 1) * half]
                if before_ref is not None:
                    part = part + before_ref[d, self.rows, lanes].astype(F32)
                own_ref[d, self.rows, lanes] = part.astype(BF16)
        if self.far:
            for d in range(far_ref.shape[0]):
                at = 2 * self.devices + d
                far_ref[d, self.rows, :] = value[:, at * half : (at + 1) * half].astype(BF16)


def with_self(scores, own, first):
    half = scores.shape[1]
    if first >= half:
        return scores
    eye = lax.broadcasted_iota(jnp.int32, (LANES, LANES), 0) == lax.broadcasted_iota(
        jnp.int32, (LANES, LANES), 1
    )
    bands = []
    for row in range(0, min(scores.shape[0], half - first), LANES):
        at = first + row
        band = scores[row : row + LANES]
        here = jnp.where(eye, own[:, at : at + LANES], band[:, at : at + LANES])
        sides = [band[:, :at]] if at else []
        sides.append(here)
        if at + LANES < half:
            sides.append(band[:, at + LANES :])
        bands.append(jnp.concatenate(sides, axis=1))
    if half - first < scores.shape[0]:
        bands.append(scores[half - first :])
    return jnp.concatenate(bands, axis=0)


def head_scores(view, refs, keys, head_dim, constant):
    scale = head_dim ** (-0.5) * math.log2(math.e)
    scaled = refs["q"][view.rows, view.same].astype(F32) * scale
    high = scaled.astype(BF16)
    low = (scaled - high.astype(F32)).astype(BF16)
    half = view.half
    if view.far:
        extra = refs["query"][view.head]
        own = refs["self"][view.head]
    else:
        row = lax.broadcasted_iota(jnp.int32, (EXTRA, half), 0)
        extra = jnp.where(row == LIVE, 1.0, 0.0).astype(BF16)
        own = jnp.zeros((1, half), F32)
    own = own + jnp.sum(scaled * keys[:, :half].astype(F32), axis=0, keepdims=True)
    if constant is not None:
        row = lax.broadcasted_iota(jnp.int32, (EXTRA, half), 0)
        filled = extra.astype(F32)
        for i, part in enumerate(thirds(constant)):
            filled = jnp.where(row == FIXED + i, part.astype(F32), filled)
        extra = filled.astype(BF16)
        own = own + constant
    left = jnp.concatenate([keys, keys, view.extra], axis=0)
    right = jnp.concatenate([high, low, extra], axis=0)

    def scores(at):
        return with_self(dot_tn(left[:, at : at + PIECE], right), own, at)

    return scores


def forward_kernel(head_dim, far, names, count, *refs):
    o_ref, t_ref = refs[len(names) :]
    refs = dict(zip(names, refs))
    if far:
        o_ref[...] = refs["o"][...]
        t_ref[...] = refs["t"][...]

    @pl.loop(0, count, unroll=UNROLL)
    def _(head):
        view = HeadView(head, far, refs, head_dim)
        keys = view.gathered(refs["k"], refs.get("kx"))
        values = view.gathered(refs["v"], refs.get("vx"))
        scores = head_scores(view, refs, keys, head_dim, None)
        parts = [scores(at) for at in range(0, keys.shape[1], PIECE)]
        highest = functools.reduce(
            jnp.maximum, [jnp.max(part, axis=0, keepdims=True) for part in parts]
        )
        mixed, total = 0.0, 0.0
        for i, part in enumerate(parts):
            weights = jnp.exp2(part - highest)
            total += jnp.sum(weights, axis=0, keepdims=True)
            mixed += dot_nn(values[:, i * PIECE : (i + 1) * PIECE], weights.astype(BF16))
        mixed *= 1.0 / total
        o_ref[view.rows, view.same] = mixed.astype(BF16)
        t_ref[head, :, view.same] = highest + jnp.log2(total)


def backward_kernel(head_dim, far, names, count, *refs):
    results = refs[len(names) :]
    refs = dict(zip(names, refs))
    dq_ref, dk_ref, dv_ref = results[:3]
    dkx_ref, dvx_ref = results[3:] if far else (None, None)
    natural = head_dim ** (-0.5)
    if not far:
        dq_ref[...] = refs["dq"][...]

    @pl.loop(0, count, unroll=UNROLL)
    def _(head):
        view = HeadView(head, far, refs, head_dim)
        keys = view.gathered(refs["k"], refs.get("kx"))
        values = view.gathered(refs["v"], refs.get("vx"))
        queries = refs["q"][view.rows, view.same]
        upstream = refs["g"][view.rows, view.same]
        mixed = refs["o"][view.rows, view.same]
        total_log = refs["t"][head, :, view.same]
        scores = head_scores(view, refs, keys, head_dim, -total_log)
        inner = -jnp.sum(upstream.astype(F32) * mixed.astype(F32), axis=0, keepdims=True)
        row = lax.broadcasted_iota(jnp.int32, (16, view.half), 0)
        filled = jnp.zeros((16, view.half), F32)
        for i, part in enumerate(thirds(inner)):
            filled = jnp.where(row == i, part.astype(F32), filled)
        row = lax.broadcasted_iota(jnp.int32, (16, keys.shape[1]), 0)
        ones = jnp.where(row < 3, 1.0, 0.0).astype(BF16)
        left = jnp.concatenate([values, ones], axis=0)
        right = jnp.concatenate([upstream, filled.astype(BF16)], axis=0)
        query_grad, key_parts, value_parts = 0.0, [], []
        for at in range(0, keys.shape[1], PIECE):
            span = slice(at, at + PIECE)
            part = scores(at)
            prob_grad = dot_tn(left[:, span], right)
            probs = jnp.exp2(part)
            score_grad = (probs * prob_grad).astype(BF16)
            value_parts.append(dot_nt(upstream, probs.astype(BF16)))
            key_parts.append(dot_nt(queries, score_grad) * natural)
            query_grad += dot_nn(keys[:, span], score_grad)
        query_grad *= natural
        value_grad = jnp.concatenate(value_parts, axis=1)
        key_grad = jnp.concatenate(key_parts, axis=1)
        dq_ref[view.rows, view.same] = query_grad.astype(BF16)
        view.spread(value_grad, dv_ref, dvx_ref, refs.get("dv"))
        view.spread(key_grad, dk_ref, dkx_ref, refs.get("dk"))


def whole_spec(shape):
    zeros = (0,) * len(shape)
    return pl.BlockSpec(shape, lambda *_: zeros)


def like(*members):
    return [jax.ShapeDtypeStruct(m.shape, m.dtype) for m in members]


def attention_call(kernel, name, head_dim, far, ins, outs, matmuls):
    width, rows = ins["q"].shape
    keys = ins["k"].shape[0] * rows + (ins["kx"].shape[0] * rows // 2 if far else 0)
    pairs = HEADS * rows // 2 * keys
    return pl.pallas_call(
        functools.partial(kernel, head_dim, far, tuple(ins), HEADS),
        in_specs=[pl.BlockSpec(memory_space=pltpu.VMEM)] * len(ins),
        out_specs=[pl.BlockSpec(memory_space=pltpu.VMEM)] * len(outs),
        out_shape=outs,
        compiler_params=pltpu.CompilerParams(vmem_limit_bytes=VMEM_LIMIT),
        cost_estimate=pl.CostEstimate(
            flops=2 * matmuls * pairs * LANES,
            transcendentals=pairs,
            bytes_accessed=8 * rows * width,
        ),
        name=name,
    )(*ins.values())


def attend(q, k, v, extras, head_dim):
    ins = dict(q=q, k=k, v=v, plain=extras["plain"])
    outs = like(q) + [jax.ShapeDtypeStruct((HEADS, 1, q.shape[1]), F32)]
    return attention_call(forward_kernel, "attend_own", head_dim, False, ins, outs, 2)


def attend_far(q, k, v, kx, vx, extras, o, t, head_dim):
    ins = dict(q=q, k=k, v=v, kx=kx, vx=vx, o=o, t=t, **extras)
    return attention_call(forward_kernel, "attend_far", head_dim, True, ins, like(o, t), 2)


def attend_far_back(q, k, v, kx, vx, extras, o, g, t, head_dim):
    ins = dict(q=q, k=k, v=v, kx=kx, vx=vx, o=o, g=g, t=t, **extras)
    outs = like(q, k, v, kx, vx)
    return attention_call(backward_kernel, "attend_far_back", head_dim, True, ins, outs, 5)


def attend_back(q, k, v, extras, o, g, t, dq, dk, dv, head_dim):
    ins = dict(q=q, k=k, v=v, o=o, g=g, t=t, dq=dq, dk=dk, dv=dv, plain=extras["plain"])
    return attention_call(backward_kernel, "attend_own_back", head_dim, False, ins, like(q, k, v), 5)


def feed_forward_kernel(blocks, *refs):
    tokens_ref, attended_ref, cotangent_ref, small_ref, wide_ref, packed_ref = refs[:6]
    output_ref, active_ref, expanded_ref, hidden_ref, low_ref, grad_ref, mixed_ref, sums_ref, wide_sums_ref = refs[6:15]
    reduce_w, expand_w, output_w, sems = refs[15:]
    width = tokens_ref.shape[-1]
    depth = output_w.shape[1]

    @pl.when(pl.program_id(0) == 0)
    def _():
        cut = reduce_w.shape[1]
        copies = [
            pltpu.make_async_copy(
                packed_ref.at[:, pl.ds(cut + blocks * depth, depth)], output_w, sems.at[0]
            )
        ]
        for i in range(blocks):
            copies.append(
                pltpu.make_async_copy(
                    packed_ref.at[:, pl.ds(cut + i * depth, depth)], expand_w.at[i], sems.at[i + 1]
                )
            )
        copies.append(
            pltpu.make_async_copy(
                packed_ref.at[:, pl.ds(0, cut)], reduce_w, sems.at[blocks + 1]
            )
        )
        for copy in copies:
            copy.start()
        for copy in copies:
            copy.wait()
        sums_ref[...] = jnp.zeros_like(sums_ref)
        wide_sums_ref[...] = jnp.zeros_like(wide_sums_ref)

    bias_output, gain, shift, bias_reduce = (small_ref[i : i + 1] for i in range(4))
    project = output_w[...].reshape(width, width)
    middle = tokens_ref[...].astype(F32) + dot_tn(attended_ref[...], project) + bias_output
    normed, inverse = standardize(middle)
    hidden = (normed * gain + shift).astype(BF16)
    hidden_ref[...] = hidden
    cotangent = cotangent_ref[...]
    output = middle + bias_reduce
    hidden_grad = jnp.zeros(middle.shape, F32)
    shrink_all = reduce_w[...].reshape(blocks * width, width)
    for i in range(blocks):
        span = slice(i * width, (i + 1) * width)
        grow = expand_w[i].reshape(width, width)
        shrink = shrink_all[span]
        active, slope = gelu_pair(dot_nn(hidden, grow) + wide_ref[:, span])
        active = active.astype(BF16)
        active_ref[:, span] = active
        output += dot_nn(active, shrink)
        expanded = (dot_nt(cotangent, shrink) * slope).astype(BF16)
        expanded_ref[:, span] = expanded
        wide_sums_ref[:, span] += jnp.sum(expanded.astype(F32), axis=0, keepdims=True)
        hidden_grad += dot_nt(expanded, grow)
    output_ref[...] = output.astype(BF16)
    upstream = cotangent.astype(F32)
    middle_grad = upstream + norm_back(hidden_grad, normed, inverse, gain)
    grad_ref[...] = middle_grad
    low = middle_grad.astype(BF16)
    low_ref[...] = low
    mixed_ref[...] = dot_nt(project, low).astype(BF16)
    for i, part in enumerate((hidden_grad * normed, hidden_grad, middle_grad, upstream)):
        sums_ref[i : i + 1] += jnp.sum(part, axis=0, keepdims=True)


def feed_forward(tokens, attended, cotangent, small, wide, packed):
    rows, width = tokens.shape
    ff = wide.shape[1]
    blocks = ff // width
    shards = packed.shape[0]
    tile = min(rows, 256)
    narrow_spec = pl.BlockSpec((tile, width), lambda r: (r, 0))
    wide_spec = pl.BlockSpec((tile, ff), lambda r: (r, 0))
    turned_spec = pl.BlockSpec((width, tile), lambda r: (0, r))
    return pl.pallas_call(
        functools.partial(feed_forward_kernel, blocks),
        grid=(rows // tile,),
        in_specs=[narrow_spec, turned_spec, narrow_spec]
        + [whole_spec(small.shape), whole_spec(wide.shape), pl.BlockSpec(memory_space=pl.ANY)],
        out_specs=[
            narrow_spec, wide_spec, wide_spec, narrow_spec, narrow_spec, narrow_spec, turned_spec,
            whole_spec((4, width)), whole_spec((1, ff)),
        ],
        out_shape=[
            jax.ShapeDtypeStruct((rows, width), BF16),
            jax.ShapeDtypeStruct((rows, ff), BF16),
            jax.ShapeDtypeStruct((rows, ff), BF16),
            jax.ShapeDtypeStruct((rows, width), BF16),
            jax.ShapeDtypeStruct((rows, width), BF16),
            jax.ShapeDtypeStruct((rows, width), F32),
            jax.ShapeDtypeStruct((width, rows), BF16),
            jax.ShapeDtypeStruct((4, width), F32),
            jax.ShapeDtypeStruct((1, ff), F32),
        ],
        scratch_shapes=[
            pltpu.VMEM((shards, ff // shards, width), BF16),
            pltpu.VMEM((blocks, shards, width // shards, width), BF16),
            pltpu.VMEM((shards, width // shards, width), BF16),
            pltpu.SemaphoreType.DMA((blocks + 2,)),
        ],
        compiler_params=pltpu.CompilerParams(vmem_limit_bytes=VMEM_LIMIT),
        cost_estimate=pl.CostEstimate(
            flops=2 * rows * width * (4 * ff + 2 * width),
            transcendentals=2 * rows * ff,
            bytes_accessed=2 * packed.size + 20 * rows * width,
        ),
        name="feed_forward",
    )(tokens, attended, cotangent, small, wide, packed)


def weight_kernel(turned, left_ref, right_ref, *refs):
    out_ref = refs[-1]
    product = (dot_nn if turned else dot_tn)(left_ref[...], right_ref[...])
    out_ref[...] = product.astype(BF16).reshape(out_ref.shape)


def packed_gradient(left, right, before, shape, depth, first, turned=False):
    rows, features = left.shape[::-1] if turned else left.shape
    width = shape[-1]
    columns = right.shape[1] // width
    step = min(384, features)
    many = step // depth if depth < step else 1
    block = (many, depth, width) if depth < step else (1, step, width)
    tall = block[1]
    inner = depth // tall

    def out_map(i, g):
        return (g, first // tall + i, 0) if depth < step else (0, first // tall + i * inner + g, 0)

    before = [] if before is None else [before]
    return pl.pallas_call(
        functools.partial(weight_kernel, turned),
        grid=(columns, features // step),
        in_specs=[
            pl.BlockSpec((step, rows), lambda i, g: (g, 0))
            if turned
            else pl.BlockSpec((rows, step), lambda i, g: (0, g)),
            pl.BlockSpec((rows, width), lambda i, g: (0, i)),
        ]
        + [pl.BlockSpec(memory_space=pl.ANY)] * len(before),
        out_specs=pl.BlockSpec(block, out_map),
        out_shape=jax.ShapeDtypeStruct(shape, BF16),
        input_output_aliases={2: 0} if before else {},
        compiler_params=pltpu.CompilerParams(vmem_limit_bytes=VMEM_LIMIT),
        cost_estimate=pl.CostEstimate(
            flops=2 * rows * features * right.shape[1],
            transcendentals=0,
            bytes_accessed=2 * (left.size + right.size + features * right.shape[1]),
        ),
        name="weight_gradient",
    )(left, right, *before)


def level_table():
    head = np.arange(HEADS)[:, None]
    residue = 2 * np.arange(RESIDUES // 2)[None, :] + head % 2
    return sum((residue % 2**b == head % 2**b).astype(int) for b in range(1, BRANCHES))


def log_rows(times):
    parts = np.log2(times).astype(np.float32)
    rows = []
    for _ in range(3):
        low = parts.astype(ml_dtypes.bfloat16)
        rows.append(low)
        parts = parts - low.astype(np.float32)
    return np.stack(rows, axis=2).reshape(times.shape[0], -1, times.shape[2])


def attention_extras(rows, own_starts, far_starts, own_count, far_count, same):
    half, block = rows // 2, rows // RESIDUES
    levels = level_table()
    level = np.arange(1, BRANCHES)[None, :, None]
    lower = np.minimum(level, levels[:, None, :])

    def repeat(table, devices):
        return np.tile(np.repeat(table, block, axis=-1), devices)

    rank = np.arange(half)
    place = [(rank % block) * RESIDUES + 2 * (rank // block) + parity for parity in range(2)]

    def liveness(starts, count, allowed):
        live = [
            jnp.stack([(start + jnp.asarray(place[p]) < count) & allowed for p in range(2)])
            for start in starts
        ]
        return jnp.where(jnp.concatenate(live, axis=1), 0.0, NEGATIVE).astype(BF16)

    def built(times, live):
        count, _, keys = times.shape
        fixed = np.zeros((count, EXTRA, keys), ml_dtypes.bfloat16)
        fixed[:, TIMES:LIVE] = times
        fixed[:, FIXED : FIXED + 3] = 1
        row = np.arange(EXTRA)[None, :, None]
        return jnp.where(row == LIVE, live[:, None], jnp.asarray(fixed))

    own_live = liveness(own_starts, own_count, True)
    far_live = liveness(far_starts, far_count, same)
    by_head = np.arange(HEADS) % 2
    none = np.zeros((2, LIVE, half * len(own_starts)), ml_dtypes.bfloat16)

    def per_head(live):
        return jnp.where(by_head[:, None] == 1, live[1], live[0])

    query = np.zeros((HEADS, EXTRA, half), ml_dtypes.bfloat16)
    spread = np.repeat(levels, block, axis=1)
    for one in range(1, BRANCHES):
        query[:, 3 * (one - 1) : 3 * one] = (spread == one)[:, None, :]
    query[:, LIVE] = 1
    return {
        "plain": built(none, own_live),
        "same": built(repeat(log_rows(1.0 + lower), len(own_starts)), per_head(own_live)),
        "far": built(repeat(log_rows(lower), len(far_starts)), per_head(far_live)),
        "query": jnp.asarray(query),
        "self": jnp.asarray(np.log2(1.0 + spread).astype(np.float32))[:, None],
    }


def half_of(table, odd):
    half = table.shape[-1] // 2
    return jnp.where(odd, table[..., half:], table[..., :half])


def add_half(total, part, odd):
    part = part.astype(F32)
    both = jnp.concatenate([jnp.where(odd, 0.0, part), jnp.where(odd, part, 0.0)], axis=-1)
    return total.astype(F32) + both


def swap_pairs(value):
    return lax.ppermute(value, "branch", [(0, 1), (1, 0)])


def gather_columns(shard, branches):
    if branches != 2:
        return lax.all_gather(shard, "branch", axis=shard.ndim - 1, tiled=True)
    other = swap_pairs(shard)
    first = lax.axis_index("branch") == 0
    return jnp.concatenate(
        [jnp.where(first, shard, other), jnp.where(first, other, shard)], axis=-1
    )


def scatter_columns(total, branches):
    if branches != 2:
        return lax.psum_scatter(
            total, "branch", scatter_dimension=total.ndim - 1, tiled=True
        ).astype(F32)
    half = total.shape[-1] // 2
    at = lax.axis_index("branch")
    keep = lax.dynamic_slice_in_dim(total, at * half, half, total.ndim - 1)
    away = lax.dynamic_slice_in_dim(total, (1 - at) * half, half, total.ndim - 1)
    return keep.astype(F32) + swap_pairs(away).astype(F32)


def weight_sum(partial, branches):
    low = lax.psum_scatter(partial, "slides", scatter_dimension=0, tiled=True)
    return scatter_columns(low, branches)


def pack_rows(reduce_part, expand_part, output_part):
    width = output_part.shape[-1]
    blocks = expand_part.shape[-1] // width
    return jnp.concatenate(
        [reduce_part]
        + [expand_part[..., i * width : (i + 1) * width] for i in range(blocks)]
        + [output_part],
        axis=-2,
    )


def unpack_rows(packed, width, ff):
    blocks = ff // width
    depth = packed.shape[-2] // (2 * blocks + 1)
    cut = blocks * depth
    expand = [packed[..., cut + i * depth : cut + (i + 1) * depth, :] for i in range(blocks)]
    return packed[..., :cut, :], jnp.concatenate(expand, axis=-1), packed[..., 2 * cut :, :]


def join_columns(own, other):
    first = lax.axis_index("branch") == 0
    return jnp.concatenate(
        [jnp.where(first, own, other), jnp.where(first, other, own)], axis=-1
    )


def gather_packed(reduce_weight, expand_weight, output_weight, vectors, branches):
    size = lax.axis_size("slides")
    width = output_weight.shape[1] * branches
    sizes = [m.shape[0] for m in vectors]
    cuts = np.cumsum([0] + sizes)
    if branches == 2:
        columns = width // 2
        narrow = jnp.concatenate([reduce_weight, output_weight], axis=0)
        small = jnp.concatenate([m.reshape(-1, columns) for m in vectors], axis=0)
        narrow_other, expand_other, small_other = (
            swap_pairs(narrow), swap_pairs(expand_weight), swap_pairs(small),
        )
        both = join_columns(narrow, narrow_other)
        cut = reduce_weight.shape[0]
        shard = pack_rows(both[:cut], join_columns(expand_weight, expand_other), both[cut:])
        first = lax.axis_index("branch") == 0
        halves = [jnp.where(first, small, small_other), jnp.where(first, small_other, small)]
        at = cuts // columns
        whole = [
            jnp.concatenate(
                [half[row : row + 1] for half in halves for row in range(at[i], at[i + 1])], axis=1
            )
            for i in range(len(sizes))
        ]
    else:
        shard = pack_rows(
            gather_columns(reduce_weight, branches),
            gather_columns(expand_weight, branches),
            gather_columns(output_weight, branches),
        )
        table = lax.all_gather(jnp.concatenate(vectors), "branch", axis=0, tiled=False)
        whole = [table[:, cuts[i] : cuts[i + 1]].reshape(1, -1) for i in range(len(sizes))]
    whole = [m.astype(F32) for m in whole]
    packed = lax.all_gather(shard, "slides", axis=0, tiled=False)
    if output_weight.shape[0] % 16 == 0:
        return packed, whole
    parts = unpack_rows(packed, shard.shape[-1], size * reduce_weight.shape[0])
    return pack_rows(*(m.reshape(1, -1, m.shape[-1]) for m in parts)), whole


def sum_packed(packed, branches, width, ff):
    size = lax.axis_size("slides")
    if packed.shape[0] != size:
        parts = unpack_rows(packed, width, ff)
        packed = pack_rows(*(m.reshape(size, -1, m.shape[-1]) for m in parts))
    rows = packed.shape[1]
    low = lax.psum_scatter(packed.reshape(size * rows, width), "slides", scatter_dimension=0, tiled=True)
    parts = unpack_rows(low, width, ff)
    if branches != 2:
        return [scatter_columns(part, branches) for part in parts]
    at = lax.axis_index("branch")
    columns = width // 2
    depth = parts[2].shape[0]

    def half(index):
        grown = lax.dynamic_slice_in_dim(parts[1], index * (ff // 2), ff // 2, 1)
        pieces = [lax.dynamic_slice_in_dim(parts[i], index * columns, columns, 1) for i in (0, 2)]
        pieces += [grown[:, i : i + columns] for i in range(0, ff // 2, columns)]
        return jnp.concatenate(pieces, axis=0)

    total = half(at).astype(F32) + swap_pairs(half(1 - at)).astype(F32)
    cut = parts[0].shape[0]
    tail = [
        total[row : row + depth] for row in range(cut + depth, total.shape[0], depth)
    ]
    return total[:cut], jnp.concatenate(tail, axis=1), total[cut : cut + depth]


def flip(value, bit):
    return lax.ppermute(value, "slides", [(i, i ^ bit) for i in range(lax.axis_size("slides"))])


def shifted(value, step):
    size = lax.axis_size("slides")
    return lax.ppermute(value, "slides", [(i, (i + 4 * step) % size) for i in range(size)])


def place_kernel(depth, columns, *refs):
    spot, pieces, full = refs[0], refs[1:5], refs[5]
    outer, near, core, branch = spot[0], spot[1], spot[2], spot[3]
    for index, piece in enumerate(pieces):
        group, other_core = index % 2, index // 2
        rounds, width = piece.shape[2], piece.shape[4]
        for one in range(2):
            for two in range(2):
                far_branch, far_near = (one, two) if group == 0 else (two, one)
                offset = 0 if group == 0 else columns - width
                column = jnp.bitwise_xor(branch, far_branch) * columns + offset
                lanes = pl.ds(pl.multiple_of(column, LANES), width)
                for step in range(rounds):
                    shard = (
                        lax.rem(outer - step + rounds, rounds) * 4
                        + jnp.bitwise_xor(near, far_near) * 2
                        + jnp.bitwise_xor(core, other_core)
                    )
                    row = pl.multiple_of(shard * depth, 16)
                    full[pl.ds(row, depth), lanes] = piece[one, two, step]


def gather_matrix(shard, later, branches):
    size = lax.axis_size("slides")
    depth, columns = shard.shape
    if branches != 2 or size % 4 or depth % 16 or columns % LANES:
        full = lax.all_gather(gather_columns(shard, branches), "slides", axis=0, tiled=True)
        return full, later
    held = [shard] + [shifted(shard, step) for step in range(1, size // 4)]
    held[1], later = lax.optimization_barrier((held[1], later))
    half = columns // 2 // LANES * LANES
    first = jnp.stack([m[:, :half] for m in held])
    second = jnp.stack([m[:, half:] for m in held])
    first, second = jnp.stack([first, flip(first, 2)]), jnp.stack([second, swap_pairs(second)])
    first, second = jnp.stack([first, swap_pairs(first)]), jnp.stack([second, flip(second, 2)])
    pieces = (first, second, flip(first, 1), flip(second, 1))
    slide = lax.axis_index("slides")
    spot = jnp.stack(
        [
            lax.div(slide, 4),
            lax.rem(lax.div(slide, 2), 2),
            lax.rem(slide, 2),
            lax.axis_index("branch"),
        ]
    )
    full = pl.pallas_call(
        functools.partial(place_kernel, depth, columns),
        in_specs=[pl.BlockSpec(memory_space=pltpu.SMEM)]
        + [pl.BlockSpec(memory_space=pltpu.VMEM)] * len(pieces),
        out_specs=pl.BlockSpec(memory_space=pltpu.VMEM),
        out_shape=jax.ShapeDtypeStruct((size * depth, branches * columns), shard.dtype),
        compiler_params=pltpu.CompilerParams(vmem_limit_bytes=VMEM_LIMIT),
        name="place",
    )(spot.astype(jnp.int32), *pieces)
    return full, later


def pick(table, index, axis):
    return lax.dynamic_index_in_dim(table, index, axis, keepdims=False)


def split_kernel(core_ref, left_ref, right_ref, keep_ref, send_ref, product_ref):
    depth = product_ref.shape[1]
    product_ref[...] = dot_nt(left_ref[...], right_ref[...]).astype(BF16).reshape(product_ref.shape)
    core = core_ref[0]
    for pair in range(product_ref.shape[0] // 2):
        at = (0, pair // 2, pair % 2)
        keep_ref[at] = product_ref[2 * pair + core]
        send_ref[at] = product_ref[2 * pair + 1 - core]


def sum_product(left, right, branches):
    size = lax.axis_size("slides")
    features, rows = left.shape
    depth, columns = features // size, right.shape[0] // branches
    step = 384
    if branches != 2 or size % 8 or depth % 16 or step % (4 * depth) or columns % step:
        return weight_sum(dot_nt(left, right).astype(BF16), branches)
    slide, at = lax.axis_index("slides"), lax.axis_index("branch")
    outer, near, core = lax.div(slide, 4), lax.rem(lax.div(slide, 2), 2), lax.rem(slide, 2)
    rounds, many, wide = size // 4, step // depth, columns // step
    block = pl.BlockSpec(
        (1, many // 4, 2, depth, step), lambda g, j: (j // wide, g, 0, 0, j % wide)
    )
    keep, send = pl.pallas_call(
        split_kernel,
        grid=(features // step, 2 * wide),
        in_specs=[
            pl.BlockSpec(memory_space=pltpu.SMEM),
            pl.BlockSpec((step, rows), lambda g, j: (g, 0)),
            pl.BlockSpec((step, rows), lambda g, j: (j, 0)),
        ],
        out_specs=[block, block],
        out_shape=[jax.ShapeDtypeStruct((2, rounds, 2, depth, columns), BF16)] * 2,
        scratch_shapes=[pltpu.VMEM((many, depth, step), BF16)],
        compiler_params=pltpu.CompilerParams(vmem_limit_bytes=VMEM_LIMIT),
        cost_estimate=pl.CostEstimate(
            flops=4 * rows * features * columns,
            transcendentals=0,
            bytes_accessed=2 * (left.size + right.size + 2 * features * columns),
        ),
        name="joint_gradient",
    )(core.reshape(1), left, right)

    def both(kept, sent):
        return (kept.astype(F32) + sent.astype(F32)).astype(BF16)

    total = both(keep, flip(send, 1))
    low, high = total[:, : rounds // 2], total[:, rounds // 2 :]
    low, high = (
        both(pick(low, at, 0), swap_pairs(pick(low, 1 - at, 0))),
        both(pick(high, near, 2), flip(pick(high, 1 - near, 2), 2)),
    )
    low, high = (
        both(pick(low, near, 1), flip(pick(low, 1 - near, 1), 2)),
        both(pick(high, at, 0), swap_pairs(pick(high, 1 - at, 0))),
    )
    joined = jnp.concatenate([low, high], axis=0)
    total = pick(joined, outer, 0).astype(F32)
    for step in range(1, rounds):
        total += shifted(pick(joined, lax.rem(outer + step, rounds), 0), step).astype(F32)
    return total


def sum_vector(partial, branches):
    size = lax.axis_size("slides")
    if branches != 2 or size % 4:
        return lax.psum(partial, ("slides", "branch"))
    total = partial.reshape(-1, LANES)
    total += flip(total, 1)
    total += swap_pairs(total)
    total += flip(total, 2)
    held = [shifted(total, step) for step in range(1, size // 4)]
    return sum(held, total).reshape(-1)


def on_device(
    tokens,
    cotangent,
    first_gain,
    first_shift,
    joint_weight,
    joint_bias,
    output_weight,
    output_bias,
    second_gain,
    second_shift,
    expand_weight,
    expand_bias,
    reduce_weight,
    reduce_bias,
    block_owner,
    tile_count,
):
    rows, width = tokens.shape
    branches = lax.axis_size("branch")
    head_dim = width // HEADS
    block = rows // RESIDUES
    mates = SEG_BASE // rows
    at = lax.axis_index("branch")
    segment = lax.div(at, mates)
    within = at - segment * mates
    odd = ((np.arange(width) // head_dim) % 2 == 1)[:, None]

    def residues_first(table):
        return table.reshape(block, RESIDUES // 2, 2, width).transpose(2, 1, 0, 3).reshape(rows, width)

    def positions_first(table):
        return table.reshape(2, RESIDUES // 2, block, width).transpose(2, 1, 0, 3).reshape(rows, width)

    parameters = (
        first_gain, first_shift, joint_bias, output_bias,
        second_gain, second_shift, expand_bias, reduce_bias,
    )
    joint_full, later = gather_matrix(
        joint_weight, (reduce_weight, expand_weight, output_weight, parameters), branches
    )
    packed_weights, vectors = gather_packed(*later, branches)
    gain_one, shift_one, bias_joint, bias_output, gain_two, shift_two, bias_expand, bias_reduce = vectors
    bias_joint = bias_joint.reshape(-1)

    owners = block_owner.reshape(-1)
    counts = tile_count.reshape(-1)
    own_count = jnp.where(segment == 0, counts[0], counts[1])
    far_count = jnp.where(segment == 0, counts[1], counts[0])
    own_starts = [lax.rem(within + d, mates) * rows for d in range(mates)]
    far_starts = [d * rows for d in range(mates)]
    extras = attention_extras(
        rows, own_starts, far_starts, own_count, far_count, owners[0] == owners[1]
    )

    tokens_low = residues_first(tokens)
    tokens_f = tokens_low.astype(F32)
    upstream_low = residues_first(cotangent)
    normed_one, inverse_one = standardize(tokens_f)
    hidden_one = (normed_one * gain_one + shift_one).astype(BF16)
    hidden_turned = hidden_one.T
    joint_rows = dot_tn(joint_full, hidden_turned)
    q = (joint_rows[:width] + bias_joint[:width, None]).astype(BF16)
    k = joint_rows[width : 2 * width].astype(BF16)
    v = (joint_rows[2 * width :] + bias_joint[width:, None]).astype(BF16)
    if mates == 1 and branches == 2:
        k_own, v_own = k[None], v[None]
        k_far, v_far = swap_pairs(half_of(k, odd))[None], swap_pairs(half_of(v, odd))[None]
    else:
        k_all = lax.all_gather(k, "branch", axis=0)
        v_all = lax.all_gather(v, "branch", axis=0)
        own_at = [segment * mates + lax.rem(within + d, mates) for d in range(mates)]
        far_at = [(1 - segment) * mates + d for d in range(mates)]
        k_own = jnp.stack([lax.dynamic_index_in_dim(k_all, d, 0, False) for d in own_at])
        v_own = jnp.stack([lax.dynamic_index_in_dim(v_all, d, 0, False) for d in own_at])
        k_far = jnp.stack([half_of(lax.dynamic_index_in_dim(k_all, d, 0, False), odd) for d in far_at])
        v_far = jnp.stack([half_of(lax.dynamic_index_in_dim(v_all, d, 0, False), odd) for d in far_at])
    attended, total_log = attend(q, k_own, v_own, extras, head_dim)
    attended, total_log = attend_far(
        q, k_own, v_own, k_far, v_far, extras, attended, total_log, head_dim
    )
    ff = bias_expand.shape[1]
    small = jnp.concatenate([bias_output, gain_two, shift_two, bias_reduce], axis=0)
    (
        output, activated, expanded_grad, hidden_two, middle_low, middle_grad, mixed_grad, sums, wide_sums,
    ) = feed_forward(
        tokens_low, attended, upstream_low, small, bias_expand, packed_weights
    )
    output = positions_first(output)
    second_gain_part, second_shift_part, output_bias_part, reduce_bias_part = sums
    expand_bias_part = wide_sums.reshape(-1)
    shards = packed_weights.shape[0]
    packed_grads = packed_gradient(
        activated, upstream_low, None, packed_weights.shape, ff // shards, 0
    )
    packed_grads = packed_gradient(
        hidden_two, expanded_grad, packed_grads, packed_weights.shape, width // shards, ff // shards
    )
    packed_grads = packed_gradient(
        attended, middle_low, packed_grads, packed_weights.shape, width // shards, 2 * ff // shards, True
    )
    mixed_grad, packed_grads = lax.optimization_barrier((mixed_grad, packed_grads))
    reduce_sum, expand_sum, output_sum = sum_packed(packed_grads, branches, width, ff)

    dq, dk_first, dv_first, dk_far, dv_far = attend_far_back(
        q, k_own, v_own, k_far, v_far, extras, attended, mixed_grad, total_log, head_dim
    )
    dq, dk_own, dv_own = attend_back(
        q, k_own, v_own, extras, attended, mixed_grad, total_log, dq, dk_first, dv_first, head_dim
    )
    if mates == 1 and branches == 2:
        key_sum = add_half(dk_own[0], swap_pairs(dk_far[0]), odd)
        value_sum = add_half(dv_own[0], swap_pairs(dv_far[0]), odd)
    else:

        def spread(own, far):
            canvas = jnp.zeros((branches, width, rows), BF16)
            for d, index in enumerate(own_at):
                canvas = lax.dynamic_update_index_in_dim(canvas, own[d], index, 0)
            for d, index in enumerate(far_at):
                full = add_half(jnp.zeros((width, rows), F32), far[d], odd).astype(BF16)
                canvas = lax.dynamic_update_index_in_dim(canvas, full, index, 0)
            return lax.psum_scatter(canvas, "branch", scatter_dimension=0, tiled=True)[0]

        key_sum = spread(dk_own, dk_far)
        value_sum = spread(dv_own, dv_far)
    value_low = value_sum.astype(BF16)
    joint_grad = jnp.concatenate([dq, key_sum.astype(BF16), value_low], axis=0)
    joint_bias_part = jnp.concatenate(
        [jnp.sum(dq.astype(F32), axis=1), jnp.sum(value_low.astype(F32), axis=1)]
    )
    joint_sum = sum_product(hidden_turned, joint_grad, branches)
    hidden_one_grad = lax.dot_general(
        joint_grad, joint_full, (((0,), (1,)), ((), ())), preferred_element_type=F32
    )
    first_gain_part = jnp.sum(hidden_one_grad * normed_one, axis=0)
    first_shift_part = jnp.sum(hidden_one_grad, axis=0)
    tokens_grad = middle_grad + norm_back(hidden_one_grad, normed_one, inverse_one, gain_one)
    tokens_grad = positions_first(tokens_grad)

    partial_vectors = (
        first_gain_part, first_shift_part, joint_bias_part, output_bias_part,
        second_gain_part, second_shift_part, expand_bias_part, reduce_bias_part,
    )
    summed = sum_vector(jnp.concatenate(partial_vectors), branches)
    mine = []
    cut = 0
    for member in partial_vectors:
        size = member.shape[0]
        share = size // branches
        mine.append(lax.dynamic_slice_in_dim(summed, cut + at * share, share))
        cut += size
    return (
        output,
        tokens_grad,
        mine[0],
        mine[1],
        joint_sum,
        mine[2],
        output_sum,
        mine[3],
        mine[4],
        mine[5],
        expand_sum,
        mine[6],
        reduce_sum,
        mine[7],
    )


def solution(mesh):
    rows = P(("slides", "branch"), None)
    matrix = P("slides", "branch")
    vector = P("branch")
    placed = (
        rows, rows, vector, vector, matrix, vector, matrix, vector,
        vector, vector, matrix, vector, matrix, vector, P("slides", None), P("slides", None),
    )
    given = (
        rows, rows, vector, vector, matrix, vector, matrix, vector,
        vector, vector, matrix, vector, matrix, vector,
    )
    return jax.shard_map(on_device, mesh=mesh, in_specs=placed, out_specs=given, check_vma=False)
```

```python
import functools
import math

import jax
import jax.numpy as jnp
import ml_dtypes
import numpy as np
from jax import lax
from jax.experimental import pallas as pl
from jax.experimental.pallas import tpu as pltpu
from jax.sharding import PartitionSpec as P

HEADS = 16
SEG_BASE = 1024
BRANCHES = 5
RESIDUES = 2 ** (BRANCHES - 1)
EPSILON = 1e-05
NEGATIVE = -1e30
LANES = 128
EXTRA = 32
TIMES, LIVE, FIXED = 0, 12, 13
UNROLL = 2
PIECE = 512
VMEM_LIMIT = 60 * 1024 * 1024

BF16 = jnp.bfloat16
F32 = jnp.float32


def standardize(values):
    centred = values - jnp.mean(values, axis=-1, keepdims=True)
    inverse = lax.rsqrt(jnp.mean(centred * centred, axis=-1, keepdims=True) + EPSILON)
    return (centred * inverse, inverse)


def norm_back(upstream, normed, inverse, gain):
    scaled = upstream * gain
    return inverse * (
        scaled
        - jnp.mean(scaled, axis=-1, keepdims=True)
        - normed * jnp.mean(scaled * normed, axis=-1, keepdims=True)
    )


def gelu_pair(values):
    cumulative = 0.5 * (1.0 + lax.erf(values * (1.0 / math.sqrt(2.0))))
    density = jnp.exp(-0.5 * values * values) * (1.0 / math.sqrt(2.0 * math.pi))
    return values * cumulative, cumulative + values * density


def dot_nn(left, right):
    return lax.dot_general(left, right, (((1,), (0,)), ((), ())), preferred_element_type=F32)


def dot_nt(left, right):
    return lax.dot_general(left, right, (((1,), (1,)), ((), ())), preferred_element_type=F32)


def dot_tn(left, right):
    return lax.dot_general(left, right, (((0,), (0,)), ((), ())), preferred_element_type=F32)


def thirds(value):
    first = value.astype(BF16)
    rest = value - first.astype(F32)
    second = rest.astype(BF16)
    return first, second, (rest - second.astype(F32)).astype(BF16)


class HeadView:
    def __init__(self, head, far, refs, head_dim):
        half = refs["q"].shape[-1] // 2
        same = lax.rem(head, 2)
        same = same if far else 1 - same
        self.half = half
        self.rows = pl.ds(pl.multiple_of(head * head_dim, 16), head_dim)
        self.same = pl.ds(pl.multiple_of(same * half, LANES), half)
        self.other = pl.ds(pl.multiple_of((1 - same) * half, LANES), half)
        self.devices = refs["k"].shape[0]
        self.head = head
        self.far = far
        extras = [
            refs["same"][head] if far else refs["plain"][same],
            refs["plain"][1 - same],
        ]
        if far:
            extras.append(refs["far"][head])
        self.extra = jnp.concatenate(extras, axis=1)

    def gathered(self, own_ref, far_ref):
        found = [own_ref[d, self.rows, self.same] for d in range(self.devices)]
        found += [own_ref[d, self.rows, self.other] for d in range(self.devices)]
        if self.far:
            found += [far_ref[d, self.rows, :] for d in range(far_ref.shape[0])]
        return jnp.concatenate(found, axis=1)

    def spread(self, value, own_ref, far_ref, before_ref=None):
        half = self.half
        for d in range(self.devices):
            for lanes, at in ((self.same, d), (self.other, self.devices + d)):
                part = value[:, at * half : (at + 1) * half]
                if before_ref is not None:
                    part = part + before_ref[d, self.rows, lanes].astype(F32)
                own_ref[d, self.rows, lanes] = part.astype(BF16)
        if self.far:
            for d in range(far_ref.shape[0]):
                at = 2 * self.devices + d
                far_ref[d, self.rows, :] = value[:, at * half : (at + 1) * half].astype(BF16)


def with_self(scores, own, first):
    half = scores.shape[1]
    if first >= half:
        return scores
    eye = lax.broadcasted_iota(jnp.int32, (LANES, LANES), 0) == lax.broadcasted_iota(
        jnp.int32, (LANES, LANES), 1
    )
    bands = []
    for row in range(0, min(scores.shape[0], half - first), LANES):
        at = first + row
        band = scores[row : row + LANES]
        here = jnp.where(eye, own[:, at : at + LANES], band[:, at : at + LANES])
        sides = [band[:, :at]] if at else []
        sides.append(here)
        if at + LANES < half:
            sides.append(band[:, at + LANES :])
        bands.append(jnp.concatenate(sides, axis=1))
    if half - first < scores.shape[0]:
        bands.append(scores[half - first :])
    return jnp.concatenate(bands, axis=0)


def head_scores(view, refs, keys, head_dim, constant):
    scale = head_dim ** (-0.5) * math.log2(math.e)
    scaled = refs["q"][view.rows, view.same].astype(F32) * scale
    high = scaled.astype(BF16)
    low = (scaled - high.astype(F32)).astype(BF16)
    half = view.half
    if view.far:
        extra = refs["query"][view.head]
        own = refs["self"][view.head]
    else:
        row = lax.broadcasted_iota(jnp.int32, (EXTRA, half), 0)
        extra = jnp.where(row == LIVE, 1.0, 0.0).astype(BF16)
        own = jnp.zeros((1, half), F32)
    own = own + jnp.sum(scaled * keys[:, :half].astype(F32), axis=0, keepdims=True)
    if constant is not None:
        row = lax.broadcasted_iota(jnp.int32, (EXTRA, half), 0)
        filled = extra.astype(F32)
        for i, part in enumerate(thirds(constant)):
            filled = jnp.where(row == FIXED + i, part.astype(F32), filled)
        extra = filled.astype(BF16)
        own = own + constant
    left = jnp.concatenate([keys, keys, view.extra], axis=0)
    right = jnp.concatenate([high, low, extra], axis=0)

    def scores(at):
        return with_self(dot_tn(left[:, at : at + PIECE], right), own, at)

    return scores


def forward_kernel(head_dim, far, names, count, *refs):
    o_ref, t_ref = refs[len(names) :]
    refs = dict(zip(names, refs))
    if far:
        o_ref[...] = refs["o"][...]
        t_ref[...] = refs["t"][...]

    @pl.loop(0, count, unroll=UNROLL)
    def _(head):
        view = HeadView(head, far, refs, head_dim)
        keys = view.gathered(refs["k"], refs.get("kx"))
        values = view.gathered(refs["v"], refs.get("vx"))
        scores = head_scores(view, refs, keys, head_dim, None)
        parts = [scores(at) for at in range(0, keys.shape[1], PIECE)]
        highest = functools.reduce(
            jnp.maximum, [jnp.max(part, axis=0, keepdims=True) for part in parts]
        )
        mixed, total = 0.0, 0.0
        for i, part in enumerate(parts):
            weights = jnp.exp2(part - highest)
            total += jnp.sum(weights, axis=0, keepdims=True)
            mixed += dot_nn(values[:, i * PIECE : (i + 1) * PIECE], weights.astype(BF16))
        mixed *= 1.0 / total
        o_ref[view.rows, view.same] = mixed.astype(BF16)
        t_ref[head, :, view.same] = highest + jnp.log2(total)


def backward_kernel(head_dim, far, names, count, *refs):
    results = refs[len(names) :]
    refs = dict(zip(names, refs))
    dq_ref, dk_ref, dv_ref = results[:3]
    dkx_ref, dvx_ref = results[3:] if far else (None, None)
    natural = head_dim ** (-0.5)
    if not far:
        dq_ref[...] = refs["dq"][...]

    @pl.loop(0, count, unroll=UNROLL)
    def _(head):
        view = HeadView(head, far, refs, head_dim)
        keys = view.gathered(refs["k"], refs.get("kx"))
        values = view.gathered(refs["v"], refs.get("vx"))
        queries = refs["q"][view.rows, view.same]
        upstream = refs["g"][view.rows, view.same]
        mixed = refs["o"][view.rows, view.same]
        total_log = refs["t"][head, :, view.same]
        scores = head_scores(view, refs, keys, head_dim, -total_log)
        inner = -jnp.sum(upstream.astype(F32) * mixed.astype(F32), axis=0, keepdims=True)
        row = lax.broadcasted_iota(jnp.int32, (16, view.half), 0)
        filled = jnp.zeros((16, view.half), F32)
        for i, part in enumerate(thirds(inner)):
            filled = jnp.where(row == i, part.astype(F32), filled)
        row = lax.broadcasted_iota(jnp.int32, (16, keys.shape[1]), 0)
        ones = jnp.where(row < 3, 1.0, 0.0).astype(BF16)
        left = jnp.concatenate([values, ones], axis=0)
        right = jnp.concatenate([upstream, filled.astype(BF16)], axis=0)
        query_grad, key_parts, value_parts = 0.0, [], []
        for at in range(0, keys.shape[1], PIECE):
            span = slice(at, at + PIECE)
            part = scores(at)
            prob_grad = dot_tn(left[:, span], right)
            probs = jnp.exp2(part)
            score_grad = (probs * prob_grad).astype(BF16)
            value_parts.append(dot_nt(upstream, probs.astype(BF16)))
            key_parts.append(dot_nt(queries, score_grad) * natural)
            query_grad += dot_nn(keys[:, span], score_grad)
        query_grad *= natural
        value_grad = jnp.concatenate(value_parts, axis=1)
        key_grad = jnp.concatenate(key_parts, axis=1)
        dq_ref[view.rows, view.same] = query_grad.astype(BF16)
        view.spread(value_grad, dv_ref, dvx_ref, refs.get("dv"))
        view.spread(key_grad, dk_ref, dkx_ref, refs.get("dk"))


def whole_spec(shape):
    zeros = (0,) * len(shape)
    return pl.BlockSpec(shape, lambda *_: zeros)


def like(*members):
    return [jax.ShapeDtypeStruct(m.shape, m.dtype) for m in members]


def attention_call(kernel, name, head_dim, far, ins, outs, matmuls):
    width, rows = ins["q"].shape
    keys = ins["k"].shape[0] * rows + (ins["kx"].shape[0] * rows // 2 if far else 0)
    pairs = HEADS * rows // 2 * keys
    return pl.pallas_call(
        functools.partial(kernel, head_dim, far, tuple(ins), HEADS),
        in_specs=[pl.BlockSpec(memory_space=pltpu.VMEM)] * len(ins),
        out_specs=[pl.BlockSpec(memory_space=pltpu.VMEM)] * len(outs),
        out_shape=outs,
        compiler_params=pltpu.CompilerParams(vmem_limit_bytes=VMEM_LIMIT),
        cost_estimate=pl.CostEstimate(
            flops=2 * matmuls * pairs * LANES,
            transcendentals=pairs,
            bytes_accessed=8 * rows * width,
        ),
        name=name,
    )(*ins.values())


def attend(q, k, v, extras, head_dim):
    ins = dict(q=q, k=k, v=v, plain=extras["plain"])
    outs = like(q) + [jax.ShapeDtypeStruct((HEADS, 1, q.shape[1]), F32)]
    return attention_call(forward_kernel, "attend_own", head_dim, False, ins, outs, 2)


def attend_far(q, k, v, kx, vx, extras, o, t, head_dim):
    ins = dict(q=q, k=k, v=v, kx=kx, vx=vx, o=o, t=t, **extras)
    return attention_call(forward_kernel, "attend_far", head_dim, True, ins, like(o, t), 2)


def attend_far_back(q, k, v, kx, vx, extras, o, g, t, head_dim):
    ins = dict(q=q, k=k, v=v, kx=kx, vx=vx, o=o, g=g, t=t, **extras)
    outs = like(q, k, v, kx, vx)
    return attention_call(backward_kernel, "attend_far_back", head_dim, True, ins, outs, 5)


def attend_back(q, k, v, extras, o, g, t, dq, dk, dv, head_dim):
    ins = dict(q=q, k=k, v=v, o=o, g=g, t=t, dq=dq, dk=dk, dv=dv, plain=extras["plain"])
    return attention_call(backward_kernel, "attend_own_back", head_dim, False, ins, like(q, k, v), 5)


def residue_rows(block):
    order = [2 * i + parity for parity in range(2) for i in range(RESIDUES // 2)]
    return [
        (i * block, pl.ds(residue, block, stride=RESIDUES)) for i, residue in enumerate(order)
    ]


def stripes(rows, width):
    return pltpu.VMEM((width // LANES, rows, LANES), F32)


def fill_stripes(ref, value):
    for c in range(ref.shape[0]):
        ref[c] = value[:, c * LANES : (c + 1) * LANES]


def read_stripes(ref, rows):
    return jnp.concatenate([ref[c, rows, :] for c in range(ref.shape[0])], axis=1)


def write_stripes(ref, rows, value):
    for c in range(ref.shape[0]):
        ref[c, rows, :] = value[:, c * LANES : (c + 1) * LANES]


def place_pieces(spot, pieces, full, depth, columns):
    outer, near, core, branch = spot[0], spot[1], spot[2], spot[3]
    for index, piece in enumerate(pieces):
        group, other_core = index % 2, index // 2
        rounds, width = piece.shape[2], piece.shape[4]
        for one in range(2):
            for two in range(2):
                far_branch, far_near = (one, two) if group == 0 else (two, one)
                offset = 0 if group == 0 else columns - width
                column = jnp.bitwise_xor(branch, far_branch) * columns + offset
                lanes = pl.ds(pl.multiple_of(column, LANES), width)
                for step in range(rounds):
                    shard = (
                        lax.rem(outer - step + rounds, rounds) * 4
                        + jnp.bitwise_xor(near, far_near) * 2
                        + jnp.bitwise_xor(core, other_core)
                    )
                    row = pl.multiple_of(shard * depth, 16)
                    full[pl.ds(row, depth), lanes] = piece[one, two, step]


def project_kernel(head_dim, placed, *refs):
    tokens_ref, norm_ref, bias_ref = refs[:3]
    outs, wide_ref, hidden_ref = refs[-10:-2], refs[-2], refs[-1]
    full_ref, ordered_ref, turned_ref = outs[:3]
    rows, width = tokens_ref.shape
    block = rows // RESIDUES
    if placed is None:
        full_ref[...] = refs[3][...]
    else:
        place_pieces(refs[3], refs[4:8], full_ref, *placed)
    fill_stripes(wide_ref, tokens_ref[...].astype(F32))
    gain, shift = norm_ref[0:1], norm_ref[1:2]
    for first, natural in residue_rows(block):
        span = slice(first, first + block)
        values = read_stripes(wide_ref, natural)
        ordered_ref[span] = values.astype(BF16)
        hidden_ref[span] = (standardize(values)[0] * gain + shift).astype(BF16)
    turned_ref[...] = hidden_ref[...].T
    ones = jnp.where(lax.broadcasted_iota(jnp.int32, (16, LANES), 0) == 0, 1.0, 0.0).astype(BF16)
    odd = lax.rem(lax.div(lax.broadcasted_iota(jnp.int32, (width, 1), 0), head_dim), 2) == 1
    half = rows // 2
    for i in range(3):
        product = dot_tn(full_ref[:, i * width : (i + 1) * width], turned_ref[...])
        if i != 1:
            at = i // 2 * width
            column = dot_tn(bias_ref[:, at : at + width], ones)
            product += jnp.concatenate([column] * (rows // LANES), axis=1)
        low = product.astype(BF16)
        outs[3 + i][...] = low
        if i:
            outs[5 + i][...] = jnp.where(odd, low[:, half:], low[:, :half])


def project(tokens, norms, bias, full, pieces, spot, placed, head_dim):
    rows, width = tokens.shape
    ins = [tokens, norms, bias] + ([full] if placed is None else [spot, *pieces])
    specs = [pl.BlockSpec(memory_space=pltpu.VMEM)] * len(ins)
    if placed is not None:
        specs[3] = pl.BlockSpec(memory_space=pltpu.SMEM)
    turned = jax.ShapeDtypeStruct((width, rows), BF16)
    part = jax.ShapeDtypeStruct((width, rows // 2), BF16)
    outs = [
        jax.ShapeDtypeStruct((width, 3 * width), BF16), jax.ShapeDtypeStruct((rows, width), BF16),
        turned, turned, turned, turned, part, part,
    ]
    return pl.pallas_call(
        functools.partial(project_kernel, head_dim, placed),
        in_specs=specs,
        out_specs=[pl.BlockSpec(memory_space=pltpu.VMEM)] * len(outs),
        out_shape=outs,
        scratch_shapes=[stripes(rows, width), pltpu.VMEM((rows, width), BF16)],
        compiler_params=pltpu.CompilerParams(vmem_limit_bytes=VMEM_LIMIT),
        cost_estimate=pl.CostEstimate(
            flops=6 * rows * width * width,
            transcendentals=0,
            bytes_accessed=12 * width * width + 16 * rows * width,
        ),
        name="project",
    )(*ins)


def finish_kernel(weight_ref, grad_ref, tokens_ref, middle_ref, norm_ref, out_ref, sums_ref, natural_ref):
    step, count = pl.program_id(0), pl.num_programs(0)
    tile, width = tokens_ref.shape
    block = out_ref.shape[0] // RESIDUES

    @pl.when(step == 0)
    def _():
        sums_ref[...] = jnp.zeros_like(sums_ref)

    grad = dot_nn(weight_ref[...], grad_ref[...]).T
    normed, inverse = standardize(tokens_ref[...].astype(F32))
    sums_ref[0:1] += jnp.sum(grad * normed, axis=0, keepdims=True)
    sums_ref[1:2] += jnp.sum(grad, axis=0, keepdims=True)
    total = middle_ref[...] + norm_back(grad, normed, inverse, norm_ref[0:1])
    many = tile // block
    half = RESIDUES // 2
    for i in range(many):
        place = step * many + i
        residue = 2 * lax.rem(place, half) + lax.div(place, half)
        natural = pl.ds(residue, block, stride=RESIDUES)
        write_stripes(natural_ref, natural, total[i * block : (i + 1) * block])

    @pl.when(step == count - 1)
    def _():
        out_ref[...] = read_stripes(natural_ref, slice(None))


def finish(weight, grad, tokens, middle, norms):
    rows, width = tokens.shape
    tile = min(rows, 256)
    narrow_spec = pl.BlockSpec((tile, width), lambda r: (r, 0))
    return pl.pallas_call(
        finish_kernel,
        grid=(rows // tile,),
        in_specs=[
            whole_spec(weight.shape),
            pl.BlockSpec((grad.shape[0], tile), lambda r: (0, r)),
            narrow_spec,
            narrow_spec,
            whole_spec(norms.shape),
        ],
        out_specs=[whole_spec((rows, width)), whole_spec((2, width))],
        out_shape=[
            jax.ShapeDtypeStruct((rows, width), F32),
            jax.ShapeDtypeStruct((2, width), F32),
        ],
        scratch_shapes=[stripes(rows, width)],
        compiler_params=pltpu.CompilerParams(vmem_limit_bytes=VMEM_LIMIT),
        cost_estimate=pl.CostEstimate(
            flops=6 * rows * width * width,
            transcendentals=0,
            bytes_accessed=6 * width * width + 16 * rows * width,
        ),
        name="finish",
    )(weight, grad, tokens, middle, norms)


def feed_forward_kernel(blocks, *refs):
    tokens_ref, attended_ref, natural_ref, small_ref, wide_ref, packed_ref = refs[:6]
    (
        output_ref, ordered_ref, active_ref, expanded_ref, hidden_ref, low_ref, grad_ref, mixed_ref,
        sums_ref, wide_sums_ref,
    ) = refs[6:16]
    reduce_w, expand_w, output_w, cotangent_scr, output_scr, sems = refs[16:]
    tile, width = tokens_ref.shape
    depth = output_w.shape[1]
    step, count = pl.program_id(0), pl.num_programs(0)
    block = natural_ref.shape[0] // RESIDUES
    halves, columns = packed_ref.shape[1], packed_ref.shape[3]

    @pl.when(step == 0)
    def _():
        cut = reduce_w.shape[1]
        local = blocks // halves * width // columns
        moves = []
        for y in range(halves):
            lanes = pl.ds(y * columns, columns)
            moves.append((y, cut + local * depth, depth, output_w.at[:, :, lanes]))
        for y in range(halves):
            for i in range(local):
                at = (y * local + i) * columns
                target = expand_w.at[at // width, :, :, pl.ds(at % width, columns)]
                moves.append((y, cut + i * depth, depth, target))
        for y in range(halves):
            lanes = pl.ds(y * columns, columns)
            moves.append((y, 0, cut, reduce_w.at[:, :, lanes]))
        copies = [
            pltpu.make_async_copy(packed_ref.at[:, y, pl.ds(at, size)], target, sems.at[i])
            for i, (y, at, size, target) in enumerate(moves)
        ]
        for copy in copies:
            copy.start()
        fill_stripes(cotangent_scr, natural_ref[...].astype(F32))
        sums_ref[...] = jnp.zeros_like(sums_ref)
        wide_sums_ref[...] = jnp.zeros_like(wide_sums_ref)
        for copy in copies:
            copy.wait()

    many, half = tile // block, RESIDUES // 2
    strided = []
    for i in range(many):
        place = step * many + i
        residue = 2 * lax.rem(place, half) + lax.div(place, half)
        strided.append(pl.ds(residue, block, stride=RESIDUES))
    bias_output, gain, shift, bias_reduce = (small_ref[i : i + 1] for i in range(4))
    project = output_w[...].reshape(width, width)
    middle = tokens_ref[...].astype(F32) + dot_tn(attended_ref[...], project) + bias_output
    normed, inverse = standardize(middle)
    hidden = (normed * gain + shift).astype(BF16)
    hidden_ref[...] = hidden
    upstream = jnp.concatenate([read_stripes(cotangent_scr, natural) for natural in strided], axis=0)
    cotangent = upstream.astype(BF16)
    ordered_ref[...] = cotangent
    output = middle + bias_reduce
    hidden_grad = jnp.zeros(middle.shape, F32)
    shrink_all = reduce_w[...].reshape(blocks * width, width)
    for i in range(blocks):
        span = slice(i * width, (i + 1) * width)
        grow = expand_w[i].reshape(width, width)
        shrink = shrink_all[span]
        active, slope = gelu_pair(dot_nn(hidden, grow) + wide_ref[:, span])
        active = active.astype(BF16)
        active_ref[:, span] = active
        output += dot_nn(active, shrink)
        expanded = (dot_nt(cotangent, shrink) * slope).astype(BF16)
        expanded_ref[:, span] = expanded
        wide_sums_ref[:, span] += jnp.sum(expanded.astype(F32), axis=0, keepdims=True)
        hidden_grad += dot_nt(expanded, grow)
    for i, natural in enumerate(strided):
        write_stripes(output_scr, natural, output[i * block : (i + 1) * block])
    middle_grad = upstream + norm_back(hidden_grad, normed, inverse, gain)
    grad_ref[...] = middle_grad
    low = middle_grad.astype(BF16)
    low_ref[...] = low
    mixed_ref[...] = dot_nt(project, low).astype(BF16)
    for i, part in enumerate((hidden_grad * normed, hidden_grad, middle_grad, upstream)):
        sums_ref[i : i + 1] += jnp.sum(part, axis=0, keepdims=True)

    @pl.when(step == count - 1)
    def _():
        output_ref[...] = read_stripes(output_scr, slice(None)).astype(BF16)


def feed_forward(tokens, attended, cotangent, small, wide, packed):
    rows, width = tokens.shape
    ff = wide.shape[1]
    blocks = ff // width
    shards, halves = packed.shape[:2]
    tile = min(rows, 256)
    narrow_spec = pl.BlockSpec((tile, width), lambda r: (r, 0))
    wide_spec = pl.BlockSpec((tile, ff), lambda r: (r, 0))
    turned_spec = pl.BlockSpec((width, tile), lambda r: (0, r))
    natural_spec = whole_spec((rows, width))
    narrow, grown = (jax.ShapeDtypeStruct((rows, n), BF16) for n in (width, ff))
    return pl.pallas_call(
        functools.partial(feed_forward_kernel, blocks),
        grid=(rows // tile,),
        in_specs=[
            narrow_spec, turned_spec, natural_spec, whole_spec(small.shape), whole_spec(wide.shape),
            pl.BlockSpec(memory_space=pl.ANY),
        ],
        out_specs=[
            natural_spec, narrow_spec, wide_spec, wide_spec, narrow_spec, narrow_spec, narrow_spec,
            turned_spec, whole_spec((4, width)), whole_spec((1, ff)),
        ],
        out_shape=[
            narrow, narrow, grown, grown, narrow, narrow,
            jax.ShapeDtypeStruct((rows, width), F32),
            jax.ShapeDtypeStruct((width, rows), BF16),
            jax.ShapeDtypeStruct((4, width), F32),
            jax.ShapeDtypeStruct((1, ff), F32),
        ],
        scratch_shapes=[
            pltpu.VMEM((shards, ff // shards, width), BF16),
            pltpu.VMEM((blocks, shards, width // shards, width), BF16),
            pltpu.VMEM((shards, width // shards, width), BF16),
            stripes(rows, width),
            stripes(rows, width),
            pltpu.SemaphoreType.DMA((2 * halves + blocks * halves,)),
        ],
        compiler_params=pltpu.CompilerParams(vmem_limit_bytes=VMEM_LIMIT),
        cost_estimate=pl.CostEstimate(
            flops=2 * rows * width * (4 * ff + 2 * width),
            transcendentals=2 * rows * ff,
            bytes_accessed=2 * packed.size + 20 * rows * width,
        ),
        name="feed_forward",
    )(tokens, attended, cotangent, small, wide, packed)


def weight_kernel(turned, left_ref, right_ref, *refs):
    out_ref = refs[-1]
    product = (dot_nn if turned else dot_tn)(left_ref[...], right_ref[...])
    out_ref[...] = product.astype(BF16).reshape(out_ref.shape)


def packed_gradient(left, right, before, shape, depth, first, turned=False):
    rows, features = left.shape[::-1] if turned else left.shape
    width = shape[-1]
    columns = right.shape[1] // width
    step = min(384, features)
    many = step // depth if depth < step else 1
    block = (many, depth, width) if depth < step else (1, step, width)
    tall = block[1]
    inner = depth // tall

    def out_map(i, g):
        return (g, first // tall + i, 0) if depth < step else (0, first // tall + i * inner + g, 0)

    before = [] if before is None else [before]
    return pl.pallas_call(
        functools.partial(weight_kernel, turned),
        grid=(columns, features // step),
        in_specs=[
            pl.BlockSpec((step, rows), lambda i, g: (g, 0))
            if turned
            else pl.BlockSpec((rows, step), lambda i, g: (0, g)),
            pl.BlockSpec((rows, width), lambda i, g: (0, i)),
        ]
        + [pl.BlockSpec(memory_space=pl.ANY)] * len(before),
        out_specs=pl.BlockSpec(block, out_map),
        out_shape=jax.ShapeDtypeStruct(shape, BF16),
        input_output_aliases={2: 0} if before else {},
        compiler_params=pltpu.CompilerParams(vmem_limit_bytes=VMEM_LIMIT),
        cost_estimate=pl.CostEstimate(
            flops=2 * rows * features * right.shape[1],
            transcendentals=0,
            bytes_accessed=2 * (left.size + right.size + features * right.shape[1]),
        ),
        name="weight_gradient",
    )(left, right, *before)


def level_table():
    head = np.arange(HEADS)[:, None]
    residue = 2 * np.arange(RESIDUES // 2)[None, :] + head % 2
    return sum((residue % 2**b == head % 2**b).astype(int) for b in range(1, BRANCHES))


def log_rows(times):
    parts = np.log2(times).astype(np.float32)
    rows = []
    for _ in range(3):
        low = parts.astype(ml_dtypes.bfloat16)
        rows.append(low)
        parts = parts - low.astype(np.float32)
    return np.stack(rows, axis=2).reshape(times.shape[0], -1, times.shape[2])


def attention_extras(rows, own_starts, far_starts, own_count, far_count, same):
    half, block = rows // 2, rows // RESIDUES
    levels = level_table()
    level = np.arange(1, BRANCHES)[None, :, None]
    lower = np.minimum(level, levels[:, None, :])

    def repeat(table, devices):
        return np.tile(np.repeat(table, block, axis=-1), devices)

    rank = np.arange(half)
    place = [(rank % block) * RESIDUES + 2 * (rank // block) + parity for parity in range(2)]

    def liveness(starts, count, allowed):
        live = [
            jnp.stack([(start + jnp.asarray(place[p]) < count) & allowed for p in range(2)])
            for start in starts
        ]
        return jnp.where(jnp.concatenate(live, axis=1), 0.0, NEGATIVE).astype(BF16)

    def built(times, live):
        count, _, keys = times.shape
        fixed = np.zeros((count, EXTRA, keys), ml_dtypes.bfloat16)
        fixed[:, TIMES:LIVE] = times
        fixed[:, FIXED : FIXED + 3] = 1
        row = np.arange(EXTRA)[None, :, None]
        return jnp.where(row == LIVE, live[:, None], jnp.asarray(fixed))

    own_live = liveness(own_starts, own_count, True)
    far_live = liveness(far_starts, far_count, same)
    by_head = np.arange(HEADS) % 2
    none = np.zeros((2, LIVE, half * len(own_starts)), ml_dtypes.bfloat16)

    def per_head(live):
        return jnp.where(by_head[:, None] == 1, live[1], live[0])

    query = np.zeros((HEADS, EXTRA, half), ml_dtypes.bfloat16)
    spread = np.repeat(levels, block, axis=1)
    for one in range(1, BRANCHES):
        query[:, 3 * (one - 1) : 3 * one] = (spread == one)[:, None, :]
    query[:, LIVE] = 1
    return {
        "plain": built(none, own_live),
        "same": built(repeat(log_rows(1.0 + lower), len(own_starts)), per_head(own_live)),
        "far": built(repeat(log_rows(lower), len(far_starts)), per_head(far_live)),
        "query": jnp.asarray(query),
        "self": jnp.asarray(np.log2(1.0 + spread).astype(np.float32))[:, None],
    }


def half_of(table, odd):
    half = table.shape[-1] // 2
    return jnp.where(odd, table[..., half:], table[..., :half])


def add_half(total, part, odd):
    part = part.astype(F32)
    both = jnp.concatenate([jnp.where(odd, 0.0, part), jnp.where(odd, part, 0.0)], axis=-1)
    return total.astype(F32) + both


def swap_pairs(value):
    return lax.ppermute(value, "branch", [(0, 1), (1, 0)])


def gather_columns(shard, branches):
    if branches != 2:
        return lax.all_gather(shard, "branch", axis=shard.ndim - 1, tiled=True)
    other = swap_pairs(shard)
    first = lax.axis_index("branch") == 0
    return jnp.concatenate(
        [jnp.where(first, shard, other), jnp.where(first, other, shard)], axis=-1
    )


def scatter_columns(total, branches):
    if branches != 2:
        return lax.psum_scatter(
            total, "branch", scatter_dimension=total.ndim - 1, tiled=True
        ).astype(F32)
    half = total.shape[-1] // 2
    at = lax.axis_index("branch")
    keep = lax.dynamic_slice_in_dim(total, at * half, half, total.ndim - 1)
    away = lax.dynamic_slice_in_dim(total, (1 - at) * half, half, total.ndim - 1)
    return keep.astype(F32) + swap_pairs(away).astype(F32)


def weight_sum(partial, branches):
    low = lax.psum_scatter(partial, "slides", scatter_dimension=0, tiled=True)
    return scatter_columns(low, branches)


def pack_rows(reduce_part, expand_part, output_part):
    width = output_part.shape[-1]
    blocks = expand_part.shape[-1] // width
    return jnp.concatenate(
        [reduce_part]
        + [expand_part[..., i * width : (i + 1) * width] for i in range(blocks)]
        + [output_part],
        axis=-2,
    )


def unpack_rows(packed, width, ff):
    blocks = ff // width
    depth = packed.shape[-2] // (2 * blocks + 1)
    cut = blocks * depth
    expand = [packed[..., cut + i * depth : cut + (i + 1) * depth, :] for i in range(blocks)]
    return packed[..., :cut, :], jnp.concatenate(expand, axis=-1), packed[..., 2 * cut :, :]


def join_columns(own, other):
    first = lax.axis_index("branch") == 0
    return jnp.concatenate(
        [jnp.where(first, own, other), jnp.where(first, other, own)], axis=-1
    )


def gather_packed(reduce_weight, expand_weight, output_weight, branches):
    size = lax.axis_size("slides")
    shard = pack_rows(reduce_weight, expand_weight, output_weight)
    packed = lax.all_gather(shard, ("slides", "branch"), axis=0, tiled=False)
    packed = packed.reshape(size, branches, *shard.shape)
    if branches == 2 and output_weight.shape[0] % 16 == 0:
        return packed
    ff = size * reduce_weight.shape[0]
    parts = unpack_rows(packed, shard.shape[1], ff // branches)
    parts = [m.transpose(0, 2, 1, 3).reshape(1, -1, branches * m.shape[-1]) for m in parts]
    return pack_rows(*parts)[None]


def gather_vectors(vectors, branches, rows_of):
    cuts = np.cumsum([0] + [m.shape[0] for m in vectors])
    if branches != 2:
        table = lax.all_gather(jnp.concatenate(vectors), "branch", axis=0, tiled=False)
        return [table[:, a:b].reshape(1, -1) for a, b in zip(cuts, cuts[1:])]
    own, other = rows_of
    columns = own.shape[1]
    first = lax.axis_index("branch") == 0
    halves = [jnp.where(first, own, other), jnp.where(first, other, own)]
    at = cuts // columns
    return [
        jnp.concatenate(
            [half[row : row + 1] for half in halves for row in range(at[i], at[i + 1])], axis=1
        )
        for i in range(len(vectors))
    ]


def sum_packed(packed, branches, width, ff):
    size = lax.axis_size("slides")
    if packed.shape[0] != size:
        parts = unpack_rows(packed, width, ff)
        packed = pack_rows(*(m.reshape(size, -1, m.shape[-1]) for m in parts))
    rows = packed.shape[1]
    low = lax.psum_scatter(packed.reshape(size * rows, width), "slides", scatter_dimension=0, tiled=True)
    parts = unpack_rows(low, width, ff)
    if branches != 2:
        return [scatter_columns(part, branches) for part in parts]
    at = lax.axis_index("branch")
    columns = width // 2
    depth = parts[2].shape[0]

    def half(index):
        grown = lax.dynamic_slice_in_dim(parts[1], index * (ff // 2), ff // 2, 1)
        pieces = [lax.dynamic_slice_in_dim(parts[i], index * columns, columns, 1) for i in (0, 2)]
        pieces += [grown[:, i : i + columns] for i in range(0, ff // 2, columns)]
        return jnp.concatenate(pieces, axis=0)

    total = half(at).astype(F32) + swap_pairs(half(1 - at)).astype(F32)
    cut = parts[0].shape[0]
    tail = [
        total[row : row + depth] for row in range(cut + depth, total.shape[0], depth)
    ]
    return total[:cut], jnp.concatenate(tail, axis=1), total[cut : cut + depth]


def flip(value, bit):
    return lax.ppermute(value, "slides", [(i, i ^ bit) for i in range(lax.axis_size("slides"))])


def shifted(value, step):
    size = lax.axis_size("slides")
    return lax.ppermute(value, "slides", [(i, (i + 4 * step) % size) for i in range(size)])


def gather_pieces(shard, small):
    size = lax.axis_size("slides")
    depth, columns = shard.shape
    held = [shard] + [shifted(shard, step) for step in range(1, size // 4)]
    half = columns // 2 // LANES * LANES
    first = jnp.stack([m[:, :half] for m in held])
    second = jnp.stack([m[:, half:] for m in held])
    first, second, small = lax.optimization_barrier((first, second, small))
    other = swap_pairs(small)
    first, second = jnp.stack([first, flip(first, 2)]), jnp.stack([second, swap_pairs(second)])
    first, second = jnp.stack([first, swap_pairs(first)]), jnp.stack([second, flip(second, 2)])
    pieces = (first, second, flip(first, 1), flip(second, 1))
    slide = lax.axis_index("slides")
    spot = jnp.stack(
        [
            lax.div(slide, 4),
            lax.rem(lax.div(slide, 2), 2),
            lax.rem(slide, 2),
            lax.axis_index("branch"),
        ]
    )
    return pieces, spot.astype(jnp.int32), other


def pick(table, index, axis):
    return lax.dynamic_index_in_dim(table, index, axis, keepdims=False)


def split_kernel(core_ref, left_ref, right_ref, keep_ref, send_ref, product_ref):
    product_ref[...] = dot_nt(left_ref[...], right_ref[...]).astype(BF16).reshape(product_ref.shape)
    core = core_ref[0]
    for pair in range(product_ref.shape[0] // 2):
        at = (0, pair // 2, pair % 2)
        keep_ref[at] = product_ref[2 * pair + core]
        send_ref[at] = product_ref[2 * pair + 1 - core]


def split_product(left, right, core):
    size = lax.axis_size("slides")
    features, rows = left.shape
    depth, columns = features // size, right.shape[0] // 2
    step = 384
    wide = columns // step
    block = pl.BlockSpec((1, size // 4, 2, depth, step), lambda j: (j // wide, 0, 0, 0, j % wide))
    return pl.pallas_call(
        split_kernel,
        grid=(2 * wide,),
        in_specs=[
            pl.BlockSpec(memory_space=pltpu.SMEM),
            whole_spec(left.shape),
            pl.BlockSpec((step, rows), lambda j: (j, 0)),
        ],
        out_specs=[block, block],
        out_shape=[jax.ShapeDtypeStruct((2, size // 4, 2, depth, columns), BF16)] * 2,
        scratch_shapes=[pltpu.VMEM((size, depth, step), BF16)],
        compiler_params=pltpu.CompilerParams(vmem_limit_bytes=VMEM_LIMIT),
        cost_estimate=pl.CostEstimate(
            flops=4 * rows * features * columns,
            transcendentals=0,
            bytes_accessed=2 * (left.size + right.size + 2 * features * columns),
        ),
        name="joint_gradient",
    )(core.reshape(1), left, right)


def sum_tree(kept, sent, vector_of, near, outer, at):
    rounds = kept.shape[1]

    def both(one, two):
        return (one.astype(F32) + two.astype(F32)).astype(BF16)

    arrived = flip(sent, 1)
    vector = vector_of().reshape(-1, LANES)
    vector += flip(vector, 1)
    total = both(kept, arrived)
    low, high = total[:, : rounds // 2], total[:, rounds // 2 :]
    away, off, vector = lax.optimization_barrier(
        (pick(low, 1 - at, 0), pick(high, 1 - near, 2), vector)
    )
    low, high = both(pick(low, at, 0), swap_pairs(away)), both(pick(high, near, 2), flip(off, 2))
    vector += swap_pairs(vector)
    away, off, vector = lax.optimization_barrier(
        (pick(low, 1 - near, 1), pick(high, 1 - at, 0), vector)
    )
    low, high = both(pick(low, near, 1), flip(away, 2)), both(pick(high, at, 0), swap_pairs(off))
    vector += flip(vector, 2)
    joined = jnp.concatenate([low, high], axis=0)
    total = pick(joined, outer, 0).astype(F32)
    sends = [pick(joined, lax.rem(outer + step, rounds), 0) for step in range(1, rounds)]
    sends, vector = lax.optimization_barrier((sends, vector))
    result = vector
    for step, part in enumerate(sends):
        total += shifted(part, step + 1).astype(F32)
        result += shifted(vector, step + 1)
    return total, result.reshape(-1)


def on_device(
    tokens,
    cotangent,
    first_gain,
    first_shift,
    joint_weight,
    joint_bias,
    output_weight,
    output_bias,
    second_gain,
    second_shift,
    expand_weight,
    expand_bias,
    reduce_weight,
    reduce_bias,
    block_owner,
    tile_count,
):
    rows, width = tokens.shape
    branches = lax.axis_size("branch")
    head_dim = width // HEADS
    block = rows // RESIDUES
    mates = SEG_BASE // rows
    at = lax.axis_index("branch")
    segment = lax.div(at, mates)
    within = at - segment * mates
    odd = ((np.arange(width) // head_dim) % 2 == 1)[:, None]

    parameters = (
        first_gain, first_shift, joint_bias, output_bias,
        second_gain, second_shift, expand_bias, reduce_bias,
    )
    packed_weights = gather_packed(reduce_weight, expand_weight, output_weight, branches)
    depth = joint_weight.shape[0]
    slides = lax.axis_size("slides")
    trees = branches == 2 and slides % 8 == 0 and depth % 16 == 0
    if trees:
        small = jnp.concatenate([m.reshape(-1, width // 2) for m in parameters], axis=0)
        pieces, spot, other = gather_pieces(joint_weight, small)
        vectors = gather_vectors(parameters, branches, (small, other))
        joint_full, placed = None, joint_weight.shape
    else:
        joint_full = lax.all_gather(
            gather_columns(joint_weight, branches), "slides", axis=0, tiled=True
        )
        vectors = gather_vectors(parameters, branches, None)
        pieces, spot, placed = (), None, None
    bias_joint = jnp.pad(vectors[2], ((0, 15), (0, 0)))
    gain_one, shift_one, _, bias_output, gain_two, shift_two, bias_expand, bias_reduce = (
        m.astype(F32) for m in vectors
    )
    norms = jnp.concatenate([gain_one, shift_one], axis=0)

    owners = block_owner.reshape(-1)
    counts = tile_count.reshape(-1)
    own_count = jnp.where(segment == 0, counts[0], counts[1])
    far_count = jnp.where(segment == 0, counts[1], counts[0])
    own_starts = [lax.rem(within + d, mates) * rows for d in range(mates)]
    far_starts = [d * rows for d in range(mates)]
    extras = attention_extras(
        rows, own_starts, far_starts, own_count, far_count, owners[0] == owners[1]
    )

    joint_full, tokens_low, hidden_turned, q, k, v, k_half, v_half = project(
        tokens, norms, bias_joint, joint_full, pieces, spot, placed, head_dim
    )
    if mates == 1 and branches == 2:
        k_own, v_own = k[None], v[None]
        k_far, v_far = swap_pairs(k_half)[None], swap_pairs(v_half)[None]
    else:
        own_at = [segment * mates + lax.rem(within + d, mates) for d in range(mates)]
        far_at = [(1 - segment) * mates + d for d in range(mates)]

        def chosen(table, indices):
            whole = lax.all_gather(table, "branch", axis=0)
            return jnp.stack([lax.dynamic_index_in_dim(whole, d, 0, False) for d in indices])

        k_own, v_own = chosen(k, own_at), chosen(v, own_at)
        k_far, v_far = chosen(k_half, far_at), chosen(v_half, far_at)
    attended, total_log = attend(q, k_own, v_own, extras, head_dim)
    attended, total_log = attend_far(
        q, k_own, v_own, k_far, v_far, extras, attended, total_log, head_dim
    )
    ff = bias_expand.shape[1]
    small = jnp.concatenate([bias_output, gain_two, shift_two, bias_reduce], axis=0)
    (
        output, upstream_low, activated, expanded_grad, hidden_two, middle_low, middle_grad, mixed_grad,
        sums, wide_sums,
    ) = feed_forward(tokens_low, attended, cotangent, small, bias_expand, packed_weights)
    second_gain_part, second_shift_part, output_bias_part, reduce_bias_part = sums
    expand_bias_part = wide_sums.reshape(-1)
    shards = slides if packed_weights.shape[0] > 1 else 1
    shape = (shards, (2 * ff + width) // shards, width)
    packed_grads = packed_gradient(activated, upstream_low, None, shape, ff // shards, 0)
    packed_grads = packed_gradient(
        hidden_two, expanded_grad, packed_grads, shape, width // shards, ff // shards
    )
    packed_grads = packed_gradient(
        attended, middle_low, packed_grads, shape, width // shards, 2 * ff // shards, True
    )
    mixed_grad, packed_grads = lax.optimization_barrier((mixed_grad, packed_grads))
    reduce_sum, expand_sum, output_sum = sum_packed(packed_grads, branches, width, ff)

    dq, dk_first, dv_first, dk_far, dv_far = attend_far_back(
        q, k_own, v_own, k_far, v_far, extras, attended, mixed_grad, total_log, head_dim
    )
    dq, dk_own, dv_own = attend_back(
        q, k_own, v_own, extras, attended, mixed_grad, total_log, dq, dk_first, dv_first, head_dim
    )
    if mates == 1 and branches == 2:
        key_sum = add_half(dk_own[0], swap_pairs(dk_far[0]), odd)
        value_sum = add_half(dv_own[0], swap_pairs(dv_far[0]), odd)
    else:

        def spread(own, far):
            canvas = jnp.zeros((branches, width, rows), BF16)
            for d, index in enumerate(own_at):
                canvas = lax.dynamic_update_index_in_dim(canvas, own[d], index, 0)
            for d, index in enumerate(far_at):
                full = add_half(jnp.zeros((width, rows), F32), far[d], odd).astype(BF16)
                canvas = lax.dynamic_update_index_in_dim(canvas, full, index, 0)
            return lax.psum_scatter(canvas, "branch", scatter_dimension=0, tiled=True)[0]

        key_sum = spread(dk_own, dk_far)
        value_sum = spread(dv_own, dv_far)
    value_low = value_sum.astype(BF16)
    joint_grad = jnp.concatenate([dq, key_sum.astype(BF16), value_low], axis=0)
    joint_bias_part = jnp.concatenate(
        [jnp.sum(dq.astype(F32), axis=1), jnp.sum(value_low.astype(F32), axis=1)]
    )
    finished = {}

    def vector_parts():
        tokens_grad, first_sums = finish(joint_full, joint_grad, tokens_low, middle_grad, norms)
        finished["tokens"] = tokens_grad
        finished["parts"] = (
            first_sums[0], first_sums[1], joint_bias_part, output_bias_part,
            second_gain_part, second_shift_part, expand_bias_part, reduce_bias_part,
        )
        return jnp.concatenate(finished["parts"])

    if trees:
        slide = lax.axis_index("slides")
        kept, sent = split_product(hidden_turned, joint_grad, lax.rem(slide, 2))
        joint_sum, summed = sum_tree(
            kept, sent, vector_parts, lax.rem(lax.div(slide, 2), 2), lax.div(slide, 4), at
        )
    else:
        joint_sum = weight_sum(dot_nt(hidden_turned, joint_grad).astype(BF16), branches)
        summed = lax.psum(vector_parts(), ("slides", "branch"))
    tokens_grad, partial_vectors = finished["tokens"], finished["parts"]
    mine = []
    cut = 0
    for member in partial_vectors:
        size = member.shape[0]
        share = size // branches
        mine.append(lax.dynamic_slice_in_dim(summed, cut + at * share, share))
        cut += size
    return (
        output,
        tokens_grad,
        mine[0],
        mine[1],
        joint_sum,
        mine[2],
        output_sum,
        mine[3],
        mine[4],
        mine[5],
        expand_sum,
        mine[6],
        reduce_sum,
        mine[7],
    )


def solution(mesh):
    rows = P(("slides", "branch"), None)
    matrix = P("slides", "branch")
    vector = P("branch")
    placed = (
        rows, rows, vector, vector, matrix, vector, matrix, vector,
        vector, vector, matrix, vector, matrix, vector, P("slides", None), P("slides", None),
    )
    given = (
        rows, rows, vector, vector, matrix, vector, matrix, vector,
        vector, vector, matrix, vector, matrix, vector,
    )
    return jax.shard_map(on_device, mesh=mesh, in_specs=placed, out_specs=given, check_vma=False)
```

```python
import functools
import math

import jax
import jax.numpy as jnp
import ml_dtypes
import numpy as np
from jax import lax
from jax.experimental import pallas as pl
from jax.experimental.pallas import tpu as pltpu
from jax.sharding import PartitionSpec as P

HEADS = 16
SEG_BASE = 1024
BRANCHES = 5
RESIDUES = 2 ** (BRANCHES - 1)
EPSILON = 1e-05
NEGATIVE = -1e30
LANES = 128
EXTRA = 32
TIMES, LIVE, FIXED = 0, 12, 13
UNROLL = 2
PIECE = 512
VMEM_LIMIT = 60 * 1024 * 1024
FEED_FORWARD_VMEM = 63 * 1024 * 1024

BF16 = jnp.bfloat16
F32 = jnp.float32


def standardize(values):
    centred = values - jnp.mean(values, axis=-1, keepdims=True)
    inverse = lax.rsqrt(jnp.mean(centred * centred, axis=-1, keepdims=True) + EPSILON)
    return (centred * inverse, inverse)


def norm_back(upstream, normed, inverse, gain):
    scaled = upstream * gain
    return inverse * (
        scaled
        - jnp.mean(scaled, axis=-1, keepdims=True)
        - normed * jnp.mean(scaled * normed, axis=-1, keepdims=True)
    )


def gelu_pair(values):
    cumulative = 0.5 * (1.0 + lax.erf(values * (1.0 / math.sqrt(2.0))))
    density = jnp.exp(-0.5 * values * values) * (1.0 / math.sqrt(2.0 * math.pi))
    return values * cumulative, cumulative + values * density


def dot_nn(left, right):
    return lax.dot_general(left, right, (((1,), (0,)), ((), ())), preferred_element_type=F32)


def dot_nt(left, right):
    return lax.dot_general(left, right, (((1,), (1,)), ((), ())), preferred_element_type=F32)


def dot_tn(left, right):
    return lax.dot_general(left, right, (((0,), (0,)), ((), ())), preferred_element_type=F32)


def thirds(value):
    first = value.astype(BF16)
    rest = value - first.astype(F32)
    second = rest.astype(BF16)
    return first, second, (rest - second.astype(F32)).astype(BF16)


class HeadView:
    def __init__(self, head, far, refs, head_dim, other_segment, own=True):
        half = refs["q"].shape[-1] // 2
        same = lax.rem(head, 2)
        same = same if far else 1 - same
        self.half = half
        self.rows = pl.ds(pl.multiple_of(head * head_dim, 16), head_dim)
        self.same = pl.ds(pl.multiple_of(same * half, LANES), half)
        self.other = pl.ds(pl.multiple_of((1 - same) * half, LANES), half)
        self.devices = refs["k"].shape[0] if own else 0
        self.head = head
        self.far = far
        self.own = own
        self.other_segment = other_segment
        extras = []
        if own:
            extras += [
                refs["same"][head] if far else refs["plain"][same],
                refs["plain"][1 - same],
            ]
        if other_segment:
            extras.append(refs["far"][head])
        self.extra = jnp.concatenate(extras, axis=1)

    def gathered(self, own_ref, far_ref):
        found = [own_ref[d, self.rows, self.same] for d in range(self.devices)]
        found += [own_ref[d, self.rows, self.other] for d in range(self.devices)]
        if self.other_segment:
            found += [far_ref[d, self.rows, :] for d in range(far_ref.shape[0])]
        return jnp.concatenate(found, axis=1)

    def spread(self, value, own_ref, far_ref, before_ref=None):
        half = self.half
        for d in range(self.devices):
            for lanes, at in ((self.same, d), (self.other, self.devices + d)):
                part = value[:, at * half : (at + 1) * half]
                if before_ref is not None:
                    part = part + before_ref[d, self.rows, lanes].astype(F32)
                own_ref[d, self.rows, lanes] = part.astype(BF16)
        if self.other_segment:
            for d in range(far_ref.shape[0]):
                at = 2 * self.devices + d
                far_ref[d, self.rows, :] = value[:, at * half : (at + 1) * half].astype(BF16)


def with_self(scores, own, first):
    half = scores.shape[1]
    if first >= half:
        return scores
    eye = lax.broadcasted_iota(jnp.int32, (LANES, LANES), 0) == lax.broadcasted_iota(
        jnp.int32, (LANES, LANES), 1
    )
    bands = []
    for row in range(0, min(scores.shape[0], half - first), LANES):
        at = first + row
        band = scores[row : row + LANES]
        here = jnp.where(eye, own[:, at : at + LANES], band[:, at : at + LANES])
        sides = [band[:, :at]] if at else []
        sides.append(here)
        if at + LANES < half:
            sides.append(band[:, at + LANES :])
        bands.append(jnp.concatenate(sides, axis=1))
    if half - first < scores.shape[0]:
        bands.append(scores[half - first :])
    return jnp.concatenate(bands, axis=0)


def head_scores(view, refs, keys, head_dim, constant):
    scale = head_dim ** (-0.5) * math.log2(math.e)
    scaled = refs["q"][view.rows, view.same].astype(F32) * scale
    high = scaled.astype(BF16)
    low = (scaled - high.astype(F32)).astype(BF16)
    half = view.half
    if view.far:
        extra = refs["query"][view.head]
        own = refs["self"][view.head]
    else:
        row = lax.broadcasted_iota(jnp.int32, (EXTRA, half), 0)
        extra = jnp.where(row == LIVE, 1.0, 0.0).astype(BF16)
        own = jnp.zeros((1, half), F32)
    if view.own:
        own = own + jnp.sum(scaled * keys[:, :half].astype(F32), axis=0, keepdims=True)
    if constant is not None:
        row = lax.broadcasted_iota(jnp.int32, (EXTRA, half), 0)
        filled = extra.astype(F32)
        for i, part in enumerate(thirds(constant)):
            filled = jnp.where(row == FIXED + i, part.astype(F32), filled)
        extra = filled.astype(BF16)
        own = own + constant
    left = jnp.concatenate([keys, keys, view.extra], axis=0)
    right = jnp.concatenate([high, low, extra], axis=0)

    def scores(at):
        product = dot_tn(left[:, at : at + PIECE], right)
        return with_self(product, own, at) if view.own else product

    return scores


def softmax_parts(parts, values, known):
    highest = functools.reduce(
        jnp.maximum, [jnp.max(part, axis=0, keepdims=True) for part in parts]
    )
    if known is not None:
        highest = jnp.maximum(highest, known[0])
    mixed, total = 0.0, 0.0
    at = 0
    for part in parts:
        weights = jnp.exp2(part - highest)
        total += jnp.sum(weights, axis=0, keepdims=True)
        mixed += dot_nn(values[:, at : at + part.shape[0]], weights.astype(BF16))
        at += part.shape[0]
    if known is not None:
        share = jnp.exp2(known[0] - highest)
        total += share
        mixed += known[1] * share
    return mixed * (1.0 / total), highest + jnp.log2(total)


def own_kernel(head_dim, names, count, *refs):
    o_ref, part_ref, t_ref = refs[len(names) :]
    refs = dict(zip(names, refs))

    @pl.loop(0, count, unroll=UNROLL)
    def _(head):
        for far in (True, False):
            view = HeadView(head, far, refs, head_dim, False)
            keys = view.gathered(refs["k"], None)
            values = view.gathered(refs["v"], None)
            scores = head_scores(view, refs, keys, head_dim, None)
            parts = [scores(at) for at in range(0, keys.shape[1], PIECE)]
            mixed, total_log = softmax_parts(parts, values, None)
            if far:
                part_ref[view.rows, :] = mixed
            else:
                o_ref[view.rows, view.same] = mixed.astype(BF16)
            t_ref[head, :, view.same] = total_log


def far_kernel(head_dim, names, count, *refs):
    o_ref, t_ref = refs[len(names) :]
    refs = dict(zip(names, refs))
    o_ref[...] = refs["o"][...]
    t_ref[...] = refs["t"][...]

    @pl.loop(0, count, unroll=UNROLL)
    def _(head):
        view = HeadView(head, True, refs, head_dim, True, own=False)
        keys = view.gathered(None, refs["kx"])
        values = view.gathered(None, refs["vx"])
        scores = head_scores(view, refs, keys, head_dim, None)
        parts = [scores(at) for at in range(0, keys.shape[1], PIECE)]
        known = (refs["t"][head, :, view.same], refs["part"][view.rows, :])
        mixed, total_log = softmax_parts(parts, values, known)
        o_ref[view.rows, view.same] = mixed.astype(BF16)
        t_ref[head, :, view.same] = total_log


def backward_kernel(far, head_dim, names, count, *refs):
    results = refs[len(names) :]
    refs = dict(zip(names, refs))
    dq_ref, dk_ref, dv_ref = results[:3]
    dkx_ref, dvx_ref = results[3:] if far else (None, None)
    natural = head_dim ** (-0.5)
    if not far:
        dq_ref[...] = refs["dq"][...]

    @pl.loop(0, count, unroll=UNROLL)
    def _(head):
        view = HeadView(head, far, refs, head_dim, far)
        keys = view.gathered(refs["k"], refs.get("kx"))
        values = view.gathered(refs["v"], refs.get("vx"))
        queries = refs["q"][view.rows, view.same]
        upstream = refs["g"][view.rows, view.same]
        mixed = refs["o"][view.rows, view.same]
        total_log = refs["t"][head, :, view.same]
        scores = head_scores(view, refs, keys, head_dim, -total_log)
        inner = -jnp.sum(upstream.astype(F32) * mixed.astype(F32), axis=0, keepdims=True)
        row = lax.broadcasted_iota(jnp.int32, (16, view.half), 0)
        filled = jnp.zeros((16, view.half), F32)
        for i, part in enumerate(thirds(inner)):
            filled = jnp.where(row == i, part.astype(F32), filled)
        row = lax.broadcasted_iota(jnp.int32, (16, keys.shape[1]), 0)
        ones = jnp.where(row < 3, 1.0, 0.0).astype(BF16)
        left = jnp.concatenate([values, ones], axis=0)
        right = jnp.concatenate([upstream, filled.astype(BF16)], axis=0)
        query_grad, key_parts, value_parts = 0.0, [], []
        for at in range(0, keys.shape[1], PIECE):
            span = slice(at, at + PIECE)
            part = scores(at)
            prob_grad = dot_tn(left[:, span], right)
            probs = jnp.exp2(part)
            score_grad = (probs * prob_grad).astype(BF16)
            value_parts.append(dot_nt(upstream, probs.astype(BF16)))
            key_parts.append(dot_nt(queries, score_grad) * natural)
            query_grad += dot_nn(keys[:, span], score_grad)
        query_grad *= natural
        value_grad = jnp.concatenate(value_parts, axis=1)
        key_grad = jnp.concatenate(key_parts, axis=1)
        dq_ref[view.rows, view.same] = query_grad.astype(BF16)
        view.spread(value_grad, dv_ref, dvx_ref, refs.get("dv"))
        view.spread(key_grad, dk_ref, dkx_ref, refs.get("dk"))


def whole_spec(shape):
    zeros = (0,) * len(shape)
    return pl.BlockSpec(shape, lambda *_: zeros)


def like(*members):
    return [jax.ShapeDtypeStruct(m.shape, m.dtype) for m in members]


def attention_call(kernel, name, ins, outs, pairs, matmuls):
    width, rows = ins["q"].shape
    return pl.pallas_call(
        functools.partial(kernel, width // HEADS, tuple(ins), HEADS),
        in_specs=[pl.BlockSpec(memory_space=pltpu.VMEM)] * len(ins),
        out_specs=[pl.BlockSpec(memory_space=pltpu.VMEM)] * len(outs),
        out_shape=outs,
        compiler_params=pltpu.CompilerParams(vmem_limit_bytes=VMEM_LIMIT),
        cost_estimate=pl.CostEstimate(
            flops=2 * matmuls * HEADS * pairs * LANES,
            transcendentals=HEADS * pairs,
            bytes_accessed=8 * rows * width,
        ),
        name=name,
    )(*ins.values())


def attend_own(q, k, v, extras):
    width, rows = q.shape
    ins = dict(q=q, k=k, v=v, **{n: extras[n] for n in ("plain", "same", "query", "self")})
    outs = like(q) + [
        jax.ShapeDtypeStruct((width, rows // 2), F32),
        jax.ShapeDtypeStruct((HEADS, 1, rows), F32),
    ]
    return attention_call(own_kernel, "attend_own", ins, outs, rows * rows * k.shape[0], 2)


def attend_far(q, kx, vx, extras, o, part, t):
    rows = q.shape[1]
    ins = dict(q=q, kx=kx, vx=vx, o=o, part=part, t=t)
    ins |= {n: extras[n] for n in ("far", "query", "self")}
    return attention_call(far_kernel, "attend_far", ins, like(o, t), rows * rows * kx.shape[0] // 4, 2)


def attend_far_back(q, k, v, kx, vx, extras, o, g, t):
    rows = q.shape[1]
    ins = dict(q=q, k=k, v=v, kx=kx, vx=vx, o=o, g=g, t=t, **extras)
    pairs = rows * rows * k.shape[0] // 2 + rows * rows * kx.shape[0] // 4
    kernel = functools.partial(backward_kernel, True)
    return attention_call(kernel, "attend_far_back", ins, like(q, k, v, kx, vx), pairs, 5)


def attend_own_back(q, k, v, extras, o, g, t, dq, dk, dv):
    rows = q.shape[1]
    ins = dict(q=q, k=k, v=v, o=o, g=g, t=t, dq=dq, dk=dk, dv=dv, plain=extras["plain"])
    kernel = functools.partial(backward_kernel, False)
    return attention_call(
        kernel, "attend_own_back", ins, like(q, k, v), rows * rows * k.shape[0] // 2, 5
    )


def residue_rows(block):
    order = [2 * i + parity for parity in range(2) for i in range(RESIDUES // 2)]
    return [
        (i * block, pl.ds(residue, block, stride=RESIDUES)) for i, residue in enumerate(order)
    ]


def stripes(rows, width):
    return pltpu.VMEM((width // LANES, rows, LANES), F32)


def fill_stripes(ref, value):
    for c in range(ref.shape[0]):
        ref[c] = value[:, c * LANES : (c + 1) * LANES]


def read_stripes(ref, rows):
    return jnp.concatenate([ref[c, rows, :] for c in range(ref.shape[0])], axis=1)


def write_stripes(ref, rows, value):
    for c in range(ref.shape[0]):
        ref[c, rows, :] = value[:, c * LANES : (c + 1) * LANES]


def place_pieces(spot, pieces, full, depth, columns):
    outer, near, core, branch = spot[0], spot[1], spot[2], spot[3]
    for index, piece in enumerate(pieces):
        group, other_core = index % 2, index // 2
        rounds, width = piece.shape[2], piece.shape[4]
        for one in range(2):
            for two in range(2):
                far_branch, far_near = (one, two) if group == 0 else (two, one)
                offset = 0 if group == 0 else columns - width
                column = jnp.bitwise_xor(branch, far_branch) * columns + offset
                lanes = pl.ds(pl.multiple_of(column, LANES), width)
                for step in range(rounds):
                    shard = (
                        lax.rem(outer - step + rounds, rounds) * 4
                        + jnp.bitwise_xor(near, far_near) * 2
                        + jnp.bitwise_xor(core, other_core)
                    )
                    row = pl.multiple_of(shard * depth, 16)
                    full[pl.ds(row, depth), lanes] = piece[one, two, step]


def project_kernel(head_dim, placed, *refs):
    tokens_ref, norm_ref, bias_ref = refs[:3]
    outs, wide_ref, hidden_ref = refs[-10:-2], refs[-2], refs[-1]
    full_ref, ordered_ref, turned_ref = outs[:3]
    rows, width = tokens_ref.shape
    block = rows // RESIDUES
    if placed is None:
        full_ref[...] = refs[3][...]
    else:
        place_pieces(refs[3], refs[4:8], full_ref, *placed)
    fill_stripes(wide_ref, tokens_ref[...].astype(F32))
    gain, shift = norm_ref[0:1], norm_ref[1:2]
    for first, natural in residue_rows(block):
        span = slice(first, first + block)
        values = read_stripes(wide_ref, natural)
        ordered_ref[span] = values.astype(BF16)
        hidden_ref[span] = (standardize(values)[0] * gain + shift).astype(BF16)
    turned_ref[...] = hidden_ref[...].T
    ones = jnp.where(lax.broadcasted_iota(jnp.int32, (16, LANES), 0) == 0, 1.0, 0.0).astype(BF16)
    odd = lax.rem(lax.div(lax.broadcasted_iota(jnp.int32, (width, 1), 0), head_dim), 2) == 1
    half = rows // 2
    for i in range(3):
        product = dot_tn(full_ref[:, i * width : (i + 1) * width], turned_ref[...])
        if i != 1:
            at = i // 2 * width
            column = dot_tn(bias_ref[:, at : at + width], ones)
            product += jnp.concatenate([column] * (rows // LANES), axis=1)
        low = product.astype(BF16)
        outs[3 + i][...] = low
        if i:
            outs[5 + i][...] = jnp.where(odd, low[:, half:], low[:, :half])


def project(tokens, norms, bias, full, pieces, spot, placed, head_dim):
    rows, width = tokens.shape
    ins = [tokens, norms, bias] + ([full] if placed is None else [spot, *pieces])
    specs = [pl.BlockSpec(memory_space=pltpu.VMEM)] * len(ins)
    if placed is not None:
        specs[3] = pl.BlockSpec(memory_space=pltpu.SMEM)
    turned = jax.ShapeDtypeStruct((width, rows), BF16)
    part = jax.ShapeDtypeStruct((width, rows // 2), BF16)
    outs = [
        jax.ShapeDtypeStruct((width, 3 * width), BF16), jax.ShapeDtypeStruct((rows, width), BF16),
        turned, turned, turned, turned, part, part,
    ]
    return pl.pallas_call(
        functools.partial(project_kernel, head_dim, placed),
        in_specs=specs,
        out_specs=[pl.BlockSpec(memory_space=pltpu.VMEM)] * len(outs),
        out_shape=outs,
        scratch_shapes=[stripes(rows, width), pltpu.VMEM((rows, width), BF16)],
        compiler_params=pltpu.CompilerParams(vmem_limit_bytes=VMEM_LIMIT),
        cost_estimate=pl.CostEstimate(
            flops=6 * rows * width * width,
            transcendentals=0,
            bytes_accessed=12 * width * width + 16 * rows * width,
        ),
        name="project",
    )(*ins)


def finish_kernel(weight_ref, grad_ref, tokens_ref, middle_ref, norm_ref, sums_ref, wide_ref, out_ref, table_ref, natural_ref):
    step, count = pl.program_id(0), pl.num_programs(0)
    tile, width = tokens_ref.shape
    block = out_ref.shape[0] // RESIDUES

    @pl.when(step == 0)
    def _():
        table_ref[...] = jnp.zeros_like(table_ref)
        table_ref[4:8] = sums_ref[...]
        for i in range(wide_ref.shape[1] // width):
            table_ref[8 + i : 9 + i] = wide_ref[:, i * width : (i + 1) * width]

    grad = dot_nn(weight_ref[...], grad_ref[...]).T
    normed, inverse = standardize(tokens_ref[...].astype(F32))
    table_ref[0:1] += jnp.sum(grad * normed, axis=0, keepdims=True)
    table_ref[1:2] += jnp.sum(grad, axis=0, keepdims=True)
    ones = jnp.ones((16, tile), BF16)
    table_ref[2:3] += dot_nt(ones, grad_ref[:width])[0:1]
    table_ref[3:4] += dot_nt(ones, grad_ref[2 * width :])[0:1]
    total = middle_ref[...] + norm_back(grad, normed, inverse, norm_ref[0:1])
    many = tile // block
    half = RESIDUES // 2
    for i in range(many):
        place = step * many + i
        residue = 2 * lax.rem(place, half) + lax.div(place, half)
        natural = pl.ds(residue, block, stride=RESIDUES)
        write_stripes(natural_ref, natural, total[i * block : (i + 1) * block])

    @pl.when(step == count - 1)
    def _():
        out_ref[...] = read_stripes(natural_ref, slice(None))


def finish(weight, grad, tokens, middle, norms, sums, wide):
    rows, width = tokens.shape
    tile = min(rows, 512)
    narrow_spec = pl.BlockSpec((tile, width), lambda r: (r, 0))
    once = pl.BlockSpec(memory_space=pltpu.VMEM)
    return pl.pallas_call(
        finish_kernel,
        grid=(rows // tile,),
        in_specs=[
            once, pl.BlockSpec((grad.shape[0], tile), lambda r: (0, r)), narrow_spec, narrow_spec,
            once, once, once,
        ],
        out_specs=[once, once],
        out_shape=[
            jax.ShapeDtypeStruct((rows, width), F32),
            jax.ShapeDtypeStruct((16, width), F32),
        ],
        scratch_shapes=[stripes(rows, width)],
        compiler_params=pltpu.CompilerParams(vmem_limit_bytes=VMEM_LIMIT),
        cost_estimate=pl.CostEstimate(
            flops=6 * rows * width * width,
            transcendentals=0,
            bytes_accessed=6 * width * width + 16 * rows * width,
        ),
        name="finish",
    )(weight, grad, tokens, middle, norms, sums, wide)


def feed_forward_kernel(blocks, *refs):
    tokens_ref, attended_ref, natural_ref, small_ref, wide_ref, packed_ref = refs[:6]
    output_ref, grad_ref, mixed_ref, sums_ref, wide_sums_ref, grads_ref = refs[6:12]
    reduce_w, expand_w, output_w, natural_scr, active_scr, expanded_scr = refs[12:18]
    cotangent_scr, hidden_scr, low_scr, in_sems, out_sems = refs[18:]
    tile, width = tokens_ref.shape
    cut, depth = reduce_w.shape[1], output_w.shape[1]
    step, count = pl.program_id(0), pl.num_programs(0)
    block = natural_ref.shape[0] // RESIDUES
    halves, columns = packed_ref.shape[1], packed_ref.shape[3]
    local = blocks // halves * width // columns

    def arrival(index, y, at, size, target):
        return pltpu.make_async_copy(
            packed_ref.at[:, y, pl.ds(at, size)], target, in_sems.at[index]
        )

    def arrivals(first=0, last=None):
        found = []
        for y in range(halves):
            lanes = pl.ds(y * columns, columns)
            found.append((y, cut + local * depth, depth, output_w.at[:, :, lanes]))
        for y in range(halves):
            for i in range(local):
                at = (y * local + i) * columns
                target = expand_w.at[at // width, :, :, pl.ds(at % width, columns)]
                found.append((y, cut + i * depth, depth, target))
        for y in range(halves):
            found.append((y, 0, cut, reduce_w.at[:, :, pl.ds(y * columns, columns)]))
        indices = range(len(found))[first:last]
        return [arrival(i, *found[i]) for i in indices]

    def await_first(first, last):
        @pl.when(step == 0)
        def _():
            for copy in arrivals(first, last):
                copy.wait()

    @pl.when(step == 0)
    def _():
        for copy in arrivals():
            copy.start()
        fill_stripes(natural_scr, natural_ref[...].astype(F32))
        sums_ref[...] = jnp.zeros_like(sums_ref)
        wide_sums_ref[...] = jnp.zeros_like(wide_sums_ref)

    many, half = tile // block, RESIDUES // 2
    strided = []
    for i in range(many):
        place = step * many + i
        residue = 2 * lax.rem(place, half) + lax.div(place, half)
        strided.append(pl.ds(residue, block, stride=RESIDUES))
    here = pl.ds(pl.multiple_of(step * tile, tile), tile)
    bias_output, gain, shift, bias_reduce = (small_ref[i : i + 1] for i in range(4))
    upstream = jnp.concatenate([read_stripes(natural_scr, natural) for natural in strided], axis=0)
    cotangent = upstream.astype(BF16)
    cotangent_scr[here] = cotangent
    await_first(0, halves)
    project = output_w[...].reshape(width, width)
    middle = tokens_ref[...].astype(F32) + dot_tn(attended_ref[:, here], project) + bias_output
    normed, inverse = standardize(middle)
    hidden = (normed * gain + shift).astype(BF16)
    hidden_scr[here] = hidden
    output = middle + bias_reduce
    hidden_grad = jnp.zeros(middle.shape, F32)
    await_first(halves, halves + halves * local + halves)
    shrink_all = reduce_w[...].reshape(blocks * width, width)
    for i in range(blocks):
        span = slice(i * width, (i + 1) * width)
        grow = expand_w[i].reshape(width, width)
        shrink = shrink_all[span]
        active, slope = gelu_pair(dot_nn(hidden, grow) + wide_ref[:, span])
        active = active.astype(BF16)
        active_scr[i, here] = active
        output += dot_nn(active, shrink)
        expanded = (dot_nt(cotangent, shrink) * slope).astype(BF16)
        expanded_scr[i, here] = expanded
        wide_sums_ref[:, span] += jnp.sum(expanded.astype(F32), axis=0, keepdims=True)
        hidden_grad += dot_nt(expanded, grow)
    for i, natural in enumerate(strided):
        write_stripes(natural_scr, natural, output[i * block : (i + 1) * block])
    middle_grad = upstream + norm_back(hidden_grad, normed, inverse, gain)
    grad_ref[...] = middle_grad
    low = middle_grad.astype(BF16)
    low_scr[here] = low
    mixed_ref[...] = dot_nt(project, low).astype(BF16)
    for i, part in enumerate((hidden_grad * normed, hidden_grad, middle_grad, upstream)):
        sums_ref[i : i + 1] += jnp.sum(part, axis=0, keepdims=True)

    @pl.when(step == count - 1)
    def _():
        output_ref[...] = read_stripes(natural_scr, slice(None)).astype(BF16)
        copies = []

        def leave(source, target):
            copies.append(pltpu.make_async_copy(source, target, out_sems.at[len(copies)]))
            copies[-1].start()

        for i in range(blocks):
            product = dot_tn(active_scr[i], cotangent_scr[...]).astype(BF16)
            if cut <= width:
                shards = slice(i * width // cut, (i + 1) * width // cut)
                reduce_w[shards] = product.reshape(-1, cut, width)
                leave(reduce_w.at[shards], grads_ref.at[shards, pl.ds(0, cut)])
            else:
                span = pl.ds(i * width, width)
                reduce_w[0, span] = product
                leave(reduce_w.at[:, span], grads_ref.at[:, span])
        for i in range(blocks):
            product = dot_tn(hidden_scr[...], expanded_scr[i]).astype(BF16)
            expand_w[i] = product.reshape(-1, depth, width)
            leave(expand_w.at[i], grads_ref.at[:, pl.ds(cut + i * depth, depth)])
        product = dot_nn(attended_ref[...], low_scr[...]).astype(BF16)
        output_w[...] = product.reshape(-1, depth, width)
        leave(output_w, grads_ref.at[:, pl.ds(cut + blocks * depth, depth)])
        for copy in copies:
            copy.wait()


def feed_forward(tokens, attended, cotangent, small, wide, packed):
    rows, width = tokens.shape
    ff = wide.shape[1]
    blocks = ff // width
    shards, halves = packed.shape[:2]
    tile = min(rows, 512)
    narrow_spec = pl.BlockSpec((tile, width), lambda r: (r, 0))
    turned_spec = pl.BlockSpec((width, tile), lambda r: (0, r))
    once = pl.BlockSpec(memory_space=pltpu.VMEM)
    rows_scr = pltpu.VMEM((rows, width), BF16)
    wide_scr = pltpu.VMEM((blocks, rows, width), BF16)
    return pl.pallas_call(
        functools.partial(feed_forward_kernel, blocks),
        grid=(rows // tile,),
        in_specs=[narrow_spec, once, once, once, once, pl.BlockSpec(memory_space=pl.ANY)],
        out_specs=[once, narrow_spec, turned_spec, once, once, pl.BlockSpec(memory_space=pl.ANY)],
        out_shape=[
            jax.ShapeDtypeStruct((rows, width), BF16),
            jax.ShapeDtypeStruct((rows, width), F32),
            jax.ShapeDtypeStruct((width, rows), BF16),
            jax.ShapeDtypeStruct((4, width), F32),
            jax.ShapeDtypeStruct((1, ff), F32),
            jax.ShapeDtypeStruct((shards, (2 * ff + width) // shards, width), BF16),
        ],
        scratch_shapes=[
            pltpu.VMEM((shards, ff // shards, width), BF16),
            pltpu.VMEM((blocks, shards, width // shards, width), BF16),
            pltpu.VMEM((shards, width // shards, width), BF16),
            stripes(rows, width),
            wide_scr,
            wide_scr,
            rows_scr,
            rows_scr,
            rows_scr,
            pltpu.SemaphoreType.DMA((2 * halves + blocks * halves,)),
            pltpu.SemaphoreType.DMA((2 * blocks + 1,)),
        ],
        compiler_params=pltpu.CompilerParams(vmem_limit_bytes=FEED_FORWARD_VMEM),
        cost_estimate=pl.CostEstimate(
            flops=2 * rows * width * (6 * ff + 3 * width),
            transcendentals=2 * rows * ff,
            bytes_accessed=4 * packed.size + 20 * rows * width,
        ),
        name="feed_forward",
    )(tokens, attended, cotangent, small, wide, packed)


def level_table():
    head = np.arange(HEADS)[:, None]
    residue = 2 * np.arange(RESIDUES // 2)[None, :] + head % 2
    return sum((residue % 2**b == head % 2**b).astype(int) for b in range(1, BRANCHES))


def log_rows(times):
    parts = np.log2(times).astype(np.float32)
    rows = []
    for _ in range(3):
        low = parts.astype(ml_dtypes.bfloat16)
        rows.append(low)
        parts = parts - low.astype(np.float32)
    return np.stack(rows, axis=2).reshape(times.shape[0], -1, times.shape[2])


def attention_extras(rows, own_starts, far_starts, own_count, far_count, same):
    half, block = rows // 2, rows // RESIDUES
    levels = level_table()
    level = np.arange(1, BRANCHES)[None, :, None]
    lower = np.minimum(level, levels[:, None, :])

    def repeat(table, devices):
        return np.tile(np.repeat(table, block, axis=-1), devices)

    rank = np.arange(half)
    place = [(rank % block) * RESIDUES + 2 * (rank // block) + parity for parity in range(2)]

    def liveness(starts, count, allowed):
        live = [
            jnp.stack([(start + jnp.asarray(place[p]) < count) & allowed for p in range(2)])
            for start in starts
        ]
        return jnp.where(jnp.concatenate(live, axis=1), 0.0, NEGATIVE).astype(BF16)

    def built(times, live):
        count, _, keys = times.shape
        fixed = np.zeros((count, EXTRA, keys), ml_dtypes.bfloat16)
        fixed[:, TIMES:LIVE] = times
        fixed[:, FIXED : FIXED + 3] = 1
        row = np.arange(EXTRA)[None, :, None]
        return jnp.where(row == LIVE, live[:, None], jnp.asarray(fixed))

    own_live = liveness(own_starts, own_count, True)
    far_live = liveness(far_starts, far_count, same)
    by_head = np.arange(HEADS) % 2
    none = np.zeros((2, LIVE, half * len(own_starts)), ml_dtypes.bfloat16)

    def per_head(live):
        return jnp.where(by_head[:, None] == 1, live[1], live[0])

    query = np.zeros((HEADS, EXTRA, half), ml_dtypes.bfloat16)
    spread = np.repeat(levels, block, axis=1)
    for one in range(1, BRANCHES):
        query[:, 3 * (one - 1) : 3 * one] = (spread == one)[:, None, :]
    query[:, LIVE] = 1
    return {
        "plain": built(none, own_live),
        "same": built(repeat(log_rows(1.0 + lower), len(own_starts)), per_head(own_live)),
        "far": built(repeat(log_rows(lower), len(far_starts)), per_head(far_live)),
        "query": jnp.asarray(query),
        "self": jnp.asarray(np.log2(1.0 + spread).astype(np.float32))[:, None],
    }


def half_of(table, odd):
    half = table.shape[-1] // 2
    return jnp.where(odd, table[..., half:], table[..., :half])


def add_half(total, part, odd):
    part = part.astype(F32)
    both = jnp.concatenate([jnp.where(odd, 0.0, part), jnp.where(odd, part, 0.0)], axis=-1)
    return total.astype(F32) + both


def swap_pairs(value):
    return lax.ppermute(value, "branch", [(0, 1), (1, 0)])


def gather_columns(shard, branches):
    if branches != 2:
        return lax.all_gather(shard, "branch", axis=shard.ndim - 1, tiled=True)
    other = swap_pairs(shard)
    first = lax.axis_index("branch") == 0
    return jnp.concatenate(
        [jnp.where(first, shard, other), jnp.where(first, other, shard)], axis=-1
    )


def scatter_columns(total, branches):
    if branches != 2:
        return lax.psum_scatter(
            total, "branch", scatter_dimension=total.ndim - 1, tiled=True
        ).astype(F32)
    half = total.shape[-1] // 2
    at = lax.axis_index("branch")
    keep = lax.dynamic_slice_in_dim(total, at * half, half, total.ndim - 1)
    away = lax.dynamic_slice_in_dim(total, (1 - at) * half, half, total.ndim - 1)
    return keep.astype(F32) + swap_pairs(away).astype(F32)


def weight_sum(partial, branches):
    low = lax.psum_scatter(partial, "slides", scatter_dimension=0, tiled=True)
    return scatter_columns(low, branches)


def pack_rows(reduce_part, expand_part, output_part):
    width = output_part.shape[-1]
    blocks = expand_part.shape[-1] // width
    return jnp.concatenate(
        [reduce_part]
        + [expand_part[..., i * width : (i + 1) * width] for i in range(blocks)]
        + [output_part],
        axis=-2,
    )


def unpack_rows(packed, width, ff):
    blocks = ff // width
    depth = packed.shape[-2] // (2 * blocks + 1)
    cut = blocks * depth
    expand = [packed[..., cut + i * depth : cut + (i + 1) * depth, :] for i in range(blocks)]
    return packed[..., :cut, :], jnp.concatenate(expand, axis=-1), packed[..., 2 * cut :, :]


def join_columns(own, other):
    first = lax.axis_index("branch") == 0
    return jnp.concatenate(
        [jnp.where(first, own, other), jnp.where(first, other, own)], axis=-1
    )


def pack_kernel(reduce_ref, expand_ref, output_ref, packed_ref):
    cut, width = reduce_ref.shape
    depth = output_ref.shape[0]
    packed_ref[:cut] = reduce_ref[...]
    blocks = expand_ref.shape[1] // width
    for i in range(blocks):
        packed_ref[cut + i * depth : cut + (i + 1) * depth] = expand_ref[:, i * width : (i + 1) * width]
    packed_ref[cut + blocks * depth :] = output_ref[...]


def gather_packed(reduce_weight, expand_weight, output_weight, branches):
    size = lax.axis_size("slides")
    depth, columns = output_weight.shape
    aligned = branches == 2 and depth % 16 == 0 and columns % LANES == 0
    if aligned:
        rows = reduce_weight.shape[0] + depth + expand_weight.size // columns
        shard = pl.pallas_call(
            pack_kernel,
            out_shape=jax.ShapeDtypeStruct((rows, columns), BF16),
            name="pack",
        )(reduce_weight, expand_weight, output_weight)
    else:
        shard = pack_rows(reduce_weight, expand_weight, output_weight)
    packed = lax.all_gather(shard, ("slides", "branch"), axis=0, tiled=False)
    packed = packed.reshape(size, branches, *shard.shape)
    if aligned:
        return packed
    ff = size * reduce_weight.shape[0]
    parts = unpack_rows(packed, columns, ff // branches)
    parts = [m.transpose(0, 2, 1, 3).reshape(1, -1, branches * m.shape[-1]) for m in parts]
    return pack_rows(*parts)[None]


def gather_vectors(vectors, branches, rows_of):
    cuts = np.cumsum([0] + [m.shape[0] for m in vectors])
    if branches != 2:
        table = lax.all_gather(jnp.concatenate(vectors), "branch", axis=0, tiled=False)
        return [table[:, a:b].reshape(1, -1) for a, b in zip(cuts, cuts[1:])]
    own, other = rows_of
    columns = own.shape[1]
    first = lax.axis_index("branch") == 0
    halves = [jnp.where(first, own, other), jnp.where(first, other, own)]
    at = cuts // columns
    return [
        jnp.concatenate(
            [half[row : row + 1] for half in halves for row in range(at[i], at[i + 1])], axis=1
        )
        for i in range(len(vectors))
    ]


def sum_packed(packed, width, ff):
    size = lax.axis_size("slides")
    if packed.shape[0] != size:
        parts = unpack_rows(packed, width, ff)
        packed = pack_rows(*(m.reshape(size, -1, m.shape[-1]) for m in parts))
    rows = packed.shape[1]
    return lax.psum_scatter(
        packed.reshape(size * rows, width), "slides", scatter_dimension=0, tiled=True
    )


def branch_half(low, index, width, ff):
    reduce_part, expand_part, output_part = unpack_rows(low, width, ff)
    columns = width // 2
    grown = lax.dynamic_slice_in_dim(expand_part, index * (ff // 2), ff // 2, 1)
    pieces = [
        lax.dynamic_slice_in_dim(part, index * columns, columns, 1)
        for part in (reduce_part, output_part)
    ]
    pieces += [grown[:, i : i + columns] for i in range(0, ff // 2, columns)]
    return jnp.concatenate(pieces, axis=0)


def unpack_half(total, depth, cut):
    tail = [total[row : row + depth] for row in range(cut + depth, total.shape[0], depth)]
    return total[:cut], jnp.concatenate(tail, axis=1), total[cut : cut + depth]


def flip(value, bit):
    return lax.ppermute(value, "slides", [(i, i ^ bit) for i in range(lax.axis_size("slides"))])


def shifted(value, step):
    size = lax.axis_size("slides")
    return lax.ppermute(value, "slides", [(i, (i + 4 * step) % size) for i in range(size)])


def gather_pieces(shard, small):
    size = lax.axis_size("slides")
    depth, columns = shard.shape
    held = [shard] + [shifted(shard, step) for step in range(1, size // 4)]
    half = columns // 2 // LANES * LANES
    first = jnp.stack([m[:, :half] for m in held])
    second = jnp.stack([m[:, half:] for m in held])
    first, second = jnp.stack([first, flip(first, 2)]), jnp.stack([second, swap_pairs(second)])
    first, second, small = lax.optimization_barrier((first, second, small))
    other = swap_pairs(small)
    first, second = jnp.stack([first, swap_pairs(first)]), jnp.stack([second, flip(second, 2)])
    pieces = (first, second, flip(first, 1), flip(second, 1))
    slide = lax.axis_index("slides")
    spot = jnp.stack(
        [
            lax.div(slide, 4),
            lax.rem(lax.div(slide, 2), 2),
            lax.rem(slide, 2),
            lax.axis_index("branch"),
        ]
    )
    return pieces, spot.astype(jnp.int32), other


def pick(table, index, axis):
    return lax.dynamic_index_in_dim(table, index, axis, keepdims=False)


def split_kernel(core_ref, left_ref, right_ref, keep_ref, send_ref, product_ref):
    product_ref[...] = dot_nt(left_ref[...], right_ref[...]).astype(BF16).reshape(product_ref.shape)
    core = core_ref[0]
    for pair in range(product_ref.shape[0] // 2):
        at = (0, pair // 2, pair % 2)
        keep_ref[at] = product_ref[2 * pair + core]
        send_ref[at] = product_ref[2 * pair + 1 - core]


def split_product(left, right, core):
    size = lax.axis_size("slides")
    features, rows = left.shape
    depth, columns = features // size, right.shape[0] // 2
    step = columns
    wide = columns // step
    block = pl.BlockSpec((1, size // 4, 2, depth, step), lambda j: (j // wide, 0, 0, 0, j % wide))
    return pl.pallas_call(
        split_kernel,
        grid=(2 * wide,),
        in_specs=[
            pl.BlockSpec(memory_space=pltpu.SMEM),
            whole_spec(left.shape),
            pl.BlockSpec((step, rows), lambda j: (j, 0)),
        ],
        out_specs=[block, block],
        out_shape=[jax.ShapeDtypeStruct((2, size // 4, 2, depth, columns), BF16)] * 2,
        scratch_shapes=[pltpu.VMEM((size, depth, step), BF16)],
        compiler_params=pltpu.CompilerParams(vmem_limit_bytes=VMEM_LIMIT),
        cost_estimate=pl.CostEstimate(
            flops=4 * rows * features * columns,
            transcendentals=0,
            bytes_accessed=2 * (left.size + right.size + 2 * features * columns),
        ),
        name="joint_gradient",
    )(core.reshape(1), left, right)


def sum_tree(kept, sent, table_of, packed, near, outer, at):
    rounds = kept.shape[1]

    def both(one, two):
        return (one.astype(F32) + two.astype(F32)).astype(BF16)

    arrived = flip(sent, 1)
    table = table_of()
    table += flip(table, 1)
    total = both(kept, arrived)
    low, high = total[:, : rounds // 2], total[:, rounds // 2 :]
    away, off, table = lax.optimization_barrier(
        (pick(low, 1 - at, 0), pick(high, 1 - near, 2), table)
    )
    low, high = both(pick(low, at, 0), swap_pairs(away)), both(pick(high, near, 2), flip(off, 2))
    table += swap_pairs(table)
    away, off, table = lax.optimization_barrier(
        (pick(low, 1 - near, 1), pick(high, 1 - at, 0), table)
    )
    low, high = both(pick(low, near, 1), flip(away, 2)), both(pick(high, at, 0), swap_pairs(off))
    table += flip(table, 2)
    joined = jnp.concatenate([low, high], axis=0)
    total = pick(joined, outer, 0).astype(F32)
    sends = [pick(joined, lax.rem(outer + step, rounds), 0) for step in range(1, rounds)]
    sends, table, packed = lax.optimization_barrier((sends, table, packed))
    result = table
    for step, part in enumerate(sends):
        total += shifted(part, step + 1).astype(F32)
        result += shifted(table, step + 1)
    return total, result, swap_pairs(packed)


def on_device(
    tokens,
    cotangent,
    first_gain,
    first_shift,
    joint_weight,
    joint_bias,
    output_weight,
    output_bias,
    second_gain,
    second_shift,
    expand_weight,
    expand_bias,
    reduce_weight,
    reduce_bias,
    block_owner,
    tile_count,
):
    rows, width = tokens.shape
    branches = lax.axis_size("branch")
    head_dim = width // HEADS
    block = rows // RESIDUES
    mates = SEG_BASE // rows
    at = lax.axis_index("branch")
    segment = lax.div(at, mates)
    within = at - segment * mates
    odd = ((np.arange(width) // head_dim) % 2 == 1)[:, None]

    parameters = (
        first_gain, first_shift, joint_bias, output_bias,
        second_gain, second_shift, expand_bias, reduce_bias,
    )
    packed_weights = gather_packed(reduce_weight, expand_weight, output_weight, branches)
    depth = joint_weight.shape[0]
    slides = lax.axis_size("slides")
    trees = branches == 2 and slides % 8 == 0 and depth % 16 == 0
    if trees:
        small = jnp.concatenate([m.reshape(-1, width // 2) for m in parameters], axis=0)
        pieces, spot, other = gather_pieces(joint_weight, small)
        vectors = gather_vectors(parameters, branches, (small, other))
        joint_full, placed = None, joint_weight.shape
    else:
        joint_full = lax.all_gather(
            gather_columns(joint_weight, branches), "slides", axis=0, tiled=True
        )
        vectors = gather_vectors(parameters, branches, None)
        pieces, spot, placed = (), None, None
    bias_joint = jnp.pad(vectors[2], ((0, 15), (0, 0)))
    gain_one, shift_one, _, bias_output, gain_two, shift_two, bias_expand, bias_reduce = (
        m.astype(F32) for m in vectors
    )
    norms = jnp.concatenate([gain_one, shift_one], axis=0)

    owners = block_owner.reshape(-1)
    counts = tile_count.reshape(-1)
    own_count = jnp.where(segment == 0, counts[0], counts[1])
    far_count = jnp.where(segment == 0, counts[1], counts[0])
    own_starts = [lax.rem(within + d, mates) * rows for d in range(mates)]
    far_starts = [d * rows for d in range(mates)]
    extras = attention_extras(
        rows, own_starts, far_starts, own_count, far_count, owners[0] == owners[1]
    )

    joint_full, tokens_low, hidden_turned, q, k, v, k_half, v_half = project(
        tokens, norms, bias_joint, joint_full, pieces, spot, placed, head_dim
    )
    if mates == 1 and branches == 2:
        k_own, v_own = k[None], v[None]
        k_far, v_far = swap_pairs(k_half)[None], swap_pairs(v_half)[None]
    else:
        own_at = [segment * mates + lax.rem(within + d, mates) for d in range(mates)]
        far_at = [(1 - segment) * mates + d for d in range(mates)]

        def chosen(table, indices):
            whole = lax.all_gather(table, "branch", axis=0)
            return jnp.stack([lax.dynamic_index_in_dim(whole, d, 0, False) for d in indices])

        k_own, v_own = chosen(k, own_at), chosen(v, own_at)
        k_far, v_far = chosen(k_half, far_at), chosen(v_half, far_at)
    attended, part, total_log = attend_own(q, k_own, v_own, extras)
    attended, total_log = attend_far(q, k_far, v_far, extras, attended, part, total_log)
    ff = bias_expand.shape[1]
    small = jnp.concatenate([bias_output, gain_two, shift_two, bias_reduce], axis=0)
    output, middle_grad, mixed_grad, sums, wide_sums, packed_grads = feed_forward(
        tokens_low, attended, cotangent, small, bias_expand, packed_weights
    )
    mixed_grad, packed_grads = lax.optimization_barrier((mixed_grad, packed_grads))
    low_sums = sum_packed(packed_grads, width, ff)

    dq, dk_first, dv_first, dk_far, dv_far = attend_far_back(
        q, k_own, v_own, k_far, v_far, extras, attended, mixed_grad, total_log
    )
    dq, dk_own, dv_own = attend_own_back(
        q, k_own, v_own, extras, attended, mixed_grad, total_log, dq, dk_first, dv_first
    )
    if mates == 1 and branches == 2:
        key_sum = add_half(dk_own[0], swap_pairs(dk_far[0]), odd)
        value_sum = add_half(dv_own[0], swap_pairs(dv_far[0]), odd)
    else:

        def spread(own, far):
            canvas = jnp.zeros((branches, width, rows), BF16)
            for d, index in enumerate(own_at):
                canvas = lax.dynamic_update_index_in_dim(canvas, own[d], index, 0)
            for d, index in enumerate(far_at):
                full = add_half(jnp.zeros((width, rows), F32), far[d], odd).astype(BF16)
                canvas = lax.dynamic_update_index_in_dim(canvas, full, index, 0)
            return lax.psum_scatter(canvas, "branch", scatter_dimension=0, tiled=True)[0]

        key_sum = spread(dk_own, dk_far)
        value_sum = spread(dv_own, dv_far)
    value_low = value_sum.astype(BF16)
    joint_grad = jnp.concatenate([dq, key_sum.astype(BF16), value_low], axis=0)
    found = []

    def table_of():
        found.extend(
            finish(joint_full, joint_grad, tokens_low, middle_grad, norms, sums, wide_sums)
        )
        return found[1]

    if trees:
        slide = lax.axis_index("slides")
        kept, sent = split_product(hidden_turned, joint_grad, lax.rem(slide, 2))
        joint_sum, table, arrived = sum_tree(
            kept, sent, table_of, branch_half(low_sums, 1 - at, width, ff),
            lax.rem(lax.div(slide, 2), 2), lax.div(slide, 4), at,
        )
        halves = branch_half(low_sums, at, width, ff).astype(F32) + arrived.astype(F32)
        reduce_sum, expand_sum, output_sum = unpack_half(
            halves, output_weight.shape[0], reduce_weight.shape[0]
        )
    else:
        joint_sum = weight_sum(dot_nt(hidden_turned, joint_grad).astype(BF16), branches)
        table = lax.psum(table_of(), ("slides", "branch"))
        reduce_sum, expand_sum, output_sum = (
            scatter_columns(part, branches) for part in unpack_rows(low_sums, width, ff)
        )
    tokens_grad = found[0]
    mine = []
    row = 0
    for count in (1, 1, 2, 1, 1, 1, 1, ff // width):
        whole = table[row : row + count].reshape(-1)
        share = count * width // branches
        mine.append(lax.dynamic_slice_in_dim(whole, at * share, share))
        row += count
    first_gain_sum, first_shift_sum, joint_bias_sum, second_gain_sum = mine[:4]
    second_shift_sum, output_bias_sum, reduce_bias_sum, expand_bias_sum = mine[4:]
    return (
        output,
        tokens_grad,
        first_gain_sum,
        first_shift_sum,
        joint_sum,
        joint_bias_sum,
        output_sum,
        output_bias_sum,
        second_gain_sum,
        second_shift_sum,
        expand_sum,
        expand_bias_sum,
        reduce_sum,
        reduce_bias_sum,
    )


def solution(mesh):
    rows = P(("slides", "branch"), None)
    matrix = P("slides", "branch")
    vector = P("branch")
    placed = (
        rows, rows, vector, vector, matrix, vector, matrix, vector,
        vector, vector, matrix, vector, matrix, vector, P("slides", None), P("slides", None),
    )
    given = (
        rows, rows, vector, vector, matrix, vector, matrix, vector,
        vector, vector, matrix, vector, matrix, vector,
    )
    return jax.shard_map(on_device, mesh=mesh, in_specs=placed, out_specs=given, check_vma=False)
```

```python
import functools
import math

import jax
import jax.numpy as jnp
import ml_dtypes
import numpy as np
from jax import lax
from jax.experimental import pallas as pl
from jax.experimental.pallas import tpu as pltpu
from jax.sharding import PartitionSpec as P

HEADS = 16
SEG_BASE = 1024
BRANCHES = 5
RESIDUES = 2 ** (BRANCHES - 1)
EPSILON = 1e-05
NEGATIVE = -1e30
LANES = 128
EXTRA = 32
TIMES, LIVE, FIXED = 0, 12, 13
UNROLL = 2
PIECE = 512
VMEM_LIMIT = 60 * 1024 * 1024

BF16 = jnp.bfloat16
F32 = jnp.float32


def standardize(values):
    centred = values - jnp.mean(values, axis=-1, keepdims=True)
    inverse = lax.rsqrt(jnp.mean(centred * centred, axis=-1, keepdims=True) + EPSILON)
    return (centred * inverse, inverse)


def norm_back(upstream, normed, inverse, gain):
    scaled = upstream * gain
    return inverse * (
        scaled
        - jnp.mean(scaled, axis=-1, keepdims=True)
        - normed * jnp.mean(scaled * normed, axis=-1, keepdims=True)
    )


def gelu_pair(values):
    cumulative = 0.5 * (1.0 + lax.erf(values * (1.0 / math.sqrt(2.0))))
    density = jnp.exp(-0.5 * values * values) * (1.0 / math.sqrt(2.0 * math.pi))
    return values * cumulative, cumulative + values * density


def dot_nn(left, right):
    return lax.dot_general(left, right, (((1,), (0,)), ((), ())), preferred_element_type=F32)


def dot_nt(left, right):
    return lax.dot_general(left, right, (((1,), (1,)), ((), ())), preferred_element_type=F32)


def dot_tn(left, right):
    return lax.dot_general(left, right, (((0,), (0,)), ((), ())), preferred_element_type=F32)


def thirds(value):
    first = value.astype(BF16)
    rest = value - first.astype(F32)
    second = rest.astype(BF16)
    return first, second, (rest - second.astype(F32)).astype(BF16)


class HeadView:
    def __init__(self, head, far, refs, head_dim, other_segment, own=True):
        half = refs["q"].shape[-1] // 2
        same = lax.rem(head, 2)
        same = same if far else 1 - same
        self.half = half
        self.rows = pl.ds(pl.multiple_of(head * head_dim, 16), head_dim)
        self.same = pl.ds(pl.multiple_of(same * half, LANES), half)
        self.other = pl.ds(pl.multiple_of((1 - same) * half, LANES), half)
        self.devices = refs["k"].shape[0] if own else 0
        self.head = head
        self.far = far
        self.own = own
        self.other_segment = other_segment
        extras = []
        if own:
            extras += [
                refs["same"][head] if far else refs["plain"][same],
                refs["plain"][1 - same],
            ]
        if other_segment:
            extras.append(refs["far"][head])
        self.extra = jnp.concatenate(extras, axis=1)

    def gathered(self, own_ref, far_ref):
        found = [own_ref[d, self.rows, self.same] for d in range(self.devices)]
        found += [own_ref[d, self.rows, self.other] for d in range(self.devices)]
        if self.other_segment:
            found += [far_ref[d, self.rows, :] for d in range(far_ref.shape[0])]
        return jnp.concatenate(found, axis=1)

    def spread(self, value, own_ref, far_ref, before_ref=None):
        half = self.half
        for d in range(self.devices):
            for lanes, at in ((self.same, d), (self.other, self.devices + d)):
                part = value[:, at * half : (at + 1) * half]
                if before_ref is not None:
                    part = part + before_ref[d, self.rows, lanes].astype(F32)
                own_ref[d, self.rows, lanes] = part.astype(BF16)
        if self.other_segment:
            for d in range(far_ref.shape[0]):
                at = 2 * self.devices + d
                far_ref[d, self.rows, :] = value[:, at * half : (at + 1) * half].astype(BF16)


def with_self(scores, own, first):
    half = scores.shape[1]
    if first >= half:
        return scores
    eye = lax.broadcasted_iota(jnp.int32, (LANES, LANES), 0) == lax.broadcasted_iota(
        jnp.int32, (LANES, LANES), 1
    )
    bands = []
    for row in range(0, min(scores.shape[0], half - first), LANES):
        at = first + row
        band = scores[row : row + LANES]
        here = jnp.where(eye, own[:, at : at + LANES], band[:, at : at + LANES])
        sides = [band[:, :at]] if at else []
        sides.append(here)
        if at + LANES < half:
            sides.append(band[:, at + LANES :])
        bands.append(jnp.concatenate(sides, axis=1))
    if half - first < scores.shape[0]:
        bands.append(scores[half - first :])
    return jnp.concatenate(bands, axis=0)


def head_scores(view, refs, keys, head_dim, constant):
    scale = head_dim ** (-0.5) * math.log2(math.e)
    scaled = refs["q"][view.rows, view.same].astype(F32) * scale
    high = scaled.astype(BF16)
    low = (scaled - high.astype(F32)).astype(BF16)
    half = view.half
    if view.far:
        extra = refs["query"][view.head]
        own = refs["self"][view.head]
    else:
        row = lax.broadcasted_iota(jnp.int32, (EXTRA, half), 0)
        extra = jnp.where(row == LIVE, 1.0, 0.0).astype(BF16)
        own = jnp.zeros((1, half), F32)
    if view.own:
        own = own + jnp.sum(scaled * keys[:, :half].astype(F32), axis=0, keepdims=True)
    if constant is not None:
        row = lax.broadcasted_iota(jnp.int32, (EXTRA, half), 0)
        filled = extra.astype(F32)
        for i, part in enumerate(thirds(constant)):
            filled = jnp.where(row == FIXED + i, part.astype(F32), filled)
        extra = filled.astype(BF16)
        own = own + constant
    left = jnp.concatenate([keys, keys, view.extra], axis=0)
    right = jnp.concatenate([high, low, extra], axis=0)

    def scores(at):
        product = dot_tn(left[:, at : at + PIECE], right)
        return with_self(product, own, at) if view.own else product

    return scores


def softmax_parts(parts, values, known):
    highest = functools.reduce(
        jnp.maximum, [jnp.max(part, axis=0, keepdims=True) for part in parts]
    )
    if known is not None:
        highest = jnp.maximum(highest, known[0])
    mixed, total = 0.0, 0.0
    at = 0
    for part in parts:
        weights = jnp.exp2(part - highest)
        total += jnp.sum(weights, axis=0, keepdims=True)
        mixed += dot_nn(values[:, at : at + part.shape[0]], weights.astype(BF16))
        at += part.shape[0]
    if known is not None:
        share = jnp.exp2(known[0] - highest)
        total += share
        mixed += known[1] * share
    return mixed * (1.0 / total), highest + jnp.log2(total)


def own_kernel(head_dim, names, count, *refs):
    o_ref, part_ref, t_ref = refs[len(names) :]
    refs = dict(zip(names, refs))

    @pl.loop(0, count, unroll=UNROLL)
    def _(head):
        for far in (True, False):
            view = HeadView(head, far, refs, head_dim, False)
            keys = view.gathered(refs["k"], None)
            values = view.gathered(refs["v"], None)
            scores = head_scores(view, refs, keys, head_dim, None)
            parts = [scores(at) for at in range(0, keys.shape[1], PIECE)]
            mixed, total_log = softmax_parts(parts, values, None)
            if far:
                part_ref[view.rows, :] = mixed
            else:
                o_ref[view.rows, view.same] = mixed.astype(BF16)
            t_ref[head, :, view.same] = total_log


def far_kernel(head_dim, names, count, *refs):
    o_ref, t_ref = refs[len(names) :]
    refs = dict(zip(names, refs))
    o_ref[...] = refs["o"][...]
    t_ref[...] = refs["t"][...]

    @pl.loop(0, count, unroll=UNROLL)
    def _(head):
        view = HeadView(head, True, refs, head_dim, True, own=False)
        keys = view.gathered(None, refs["kx"])
        values = view.gathered(None, refs["vx"])
        scores = head_scores(view, refs, keys, head_dim, None)
        parts = [scores(at) for at in range(0, keys.shape[1], PIECE)]
        known = (refs["t"][head, :, view.same], refs["part"][view.rows, :])
        mixed, total_log = softmax_parts(parts, values, known)
        o_ref[view.rows, view.same] = mixed.astype(BF16)
        t_ref[head, :, view.same] = total_log


def backward_kernel(far, head_dim, names, count, *refs):
    results = refs[len(names) :]
    refs = dict(zip(names, refs))
    dq_ref, dk_ref, dv_ref = results[:3]
    dkx_ref, dvx_ref = results[3:] if far else (None, None)
    natural = head_dim ** (-0.5)
    if not far:
        dq_ref[...] = refs["dq"][...]

    @pl.loop(0, count, unroll=UNROLL)
    def _(head):
        view = HeadView(head, far, refs, head_dim, far)
        keys = view.gathered(refs["k"], refs.get("kx"))
        values = view.gathered(refs["v"], refs.get("vx"))
        queries = refs["q"][view.rows, view.same]
        upstream = refs["g"][view.rows, view.same]
        mixed = refs["o"][view.rows, view.same]
        total_log = refs["t"][head, :, view.same]
        scores = head_scores(view, refs, keys, head_dim, -total_log)
        inner = -jnp.sum(upstream.astype(F32) * mixed.astype(F32), axis=0, keepdims=True)
        row = lax.broadcasted_iota(jnp.int32, (16, view.half), 0)
        filled = jnp.zeros((16, view.half), F32)
        for i, part in enumerate(thirds(inner)):
            filled = jnp.where(row == i, part.astype(F32), filled)
        row = lax.broadcasted_iota(jnp.int32, (16, keys.shape[1]), 0)
        ones = jnp.where(row < 3, 1.0, 0.0).astype(BF16)
        left = jnp.concatenate([values, ones], axis=0)
        right = jnp.concatenate([upstream, filled.astype(BF16)], axis=0)
        query_grad, key_parts, value_parts = 0.0, [], []
        for at in range(0, keys.shape[1], PIECE):
            span = slice(at, at + PIECE)
            part = scores(at)
            prob_grad = dot_tn(left[:, span], right)
            probs = jnp.exp2(part)
            score_grad = (probs * prob_grad).astype(BF16)
            value_parts.append(dot_nt(upstream, probs.astype(BF16)))
            key_parts.append(dot_nt(queries, score_grad) * natural)
            query_grad += dot_nn(keys[:, span], score_grad)
        query_grad *= natural
        value_grad = jnp.concatenate(value_parts, axis=1)
        key_grad = jnp.concatenate(key_parts, axis=1)
        dq_ref[view.rows, view.same] = query_grad.astype(BF16)
        view.spread(value_grad, dv_ref, dvx_ref, refs.get("dv"))
        view.spread(key_grad, dk_ref, dkx_ref, refs.get("dk"))


def whole_spec(shape):
    zeros = (0,) * len(shape)
    return pl.BlockSpec(shape, lambda *_: zeros)


def like(*members):
    return [jax.ShapeDtypeStruct(m.shape, m.dtype) for m in members]


def attention_call(kernel, name, ins, outs, pairs, matmuls):
    width, rows = ins["q"].shape
    return pl.pallas_call(
        functools.partial(kernel, width // HEADS, tuple(ins), HEADS),
        in_specs=[pl.BlockSpec(memory_space=pltpu.VMEM)] * len(ins),
        out_specs=[pl.BlockSpec(memory_space=pltpu.VMEM)] * len(outs),
        out_shape=outs,
        compiler_params=pltpu.CompilerParams(vmem_limit_bytes=VMEM_LIMIT),
        cost_estimate=pl.CostEstimate(
            flops=2 * matmuls * HEADS * pairs * LANES,
            transcendentals=HEADS * pairs,
            bytes_accessed=8 * rows * width,
        ),
        name=name,
    )(*ins.values())


def attend_own(q, k, v, extras):
    width, rows = q.shape
    ins = dict(q=q, k=k, v=v, **{n: extras[n] for n in ("plain", "same", "query", "self")})
    outs = like(q) + [
        jax.ShapeDtypeStruct((width, rows // 2), F32),
        jax.ShapeDtypeStruct((HEADS, 1, rows), F32),
    ]
    return attention_call(own_kernel, "attend_own", ins, outs, rows * rows * k.shape[0], 2)


def attend_far(q, kx, vx, extras, o, part, t):
    rows = q.shape[1]
    ins = dict(q=q, kx=kx, vx=vx, o=o, part=part, t=t)
    ins |= {n: extras[n] for n in ("far", "query", "self")}
    return attention_call(far_kernel, "attend_far", ins, like(o, t), rows * rows * kx.shape[0] // 4, 2)


def attend_far_back(q, k, v, kx, vx, extras, o, g, t):
    rows = q.shape[1]
    ins = dict(q=q, k=k, v=v, kx=kx, vx=vx, o=o, g=g, t=t, **extras)
    pairs = rows * rows * k.shape[0] // 2 + rows * rows * kx.shape[0] // 4
    kernel = functools.partial(backward_kernel, True)
    return attention_call(kernel, "attend_far_back", ins, like(q, k, v, kx, vx), pairs, 5)


def attend_own_back(q, k, v, extras, o, g, t, dq, dk, dv):
    rows = q.shape[1]
    ins = dict(q=q, k=k, v=v, o=o, g=g, t=t, dq=dq, dk=dk, dv=dv, plain=extras["plain"])
    kernel = functools.partial(backward_kernel, False)
    return attention_call(
        kernel, "attend_own_back", ins, like(q, k, v), rows * rows * k.shape[0] // 2, 5
    )


def residue_rows(block):
    order = [2 * i + parity for parity in range(2) for i in range(RESIDUES // 2)]
    return [
        (i * block, pl.ds(residue, block, stride=RESIDUES)) for i, residue in enumerate(order)
    ]


def stripes(rows, width):
    return pltpu.VMEM((width // LANES, rows, LANES), F32)


def fill_stripes(ref, value):
    for c in range(ref.shape[0]):
        ref[c] = value[:, c * LANES : (c + 1) * LANES]


def read_stripes(ref, rows):
    return jnp.concatenate([ref[c, rows, :] for c in range(ref.shape[0])], axis=1)


def write_stripes(ref, rows, value):
    for c in range(ref.shape[0]):
        ref[c, rows, :] = value[:, c * LANES : (c + 1) * LANES]


def place_pieces(spot, pieces, full, depth, columns):
    outer, near, core, branch = spot[0], spot[1], spot[2], spot[3]
    for index, piece in enumerate(pieces):
        group, other_core = index % 2, index // 2
        rounds, width = piece.shape[2], piece.shape[4]
        for one in range(2):
            for two in range(2):
                far_branch, far_near = (one, two) if group == 0 else (two, one)
                offset = 0 if group == 0 else columns - width
                column = jnp.bitwise_xor(branch, far_branch) * columns + offset
                lanes = pl.ds(pl.multiple_of(column, LANES), width)
                for step in range(rounds):
                    shard = (
                        lax.rem(outer - step + rounds, rounds) * 4
                        + jnp.bitwise_xor(near, far_near) * 2
                        + jnp.bitwise_xor(core, other_core)
                    )
                    row = pl.multiple_of(shard * depth, 16)
                    full[pl.ds(row, depth), lanes] = piece[one, two, step]


def project_kernel(head_dim, placed, *refs):
    tokens_ref, norm_ref, bias_ref = refs[:3]
    outs, wide_ref, hidden_ref = refs[-10:-2], refs[-2], refs[-1]
    full_ref, ordered_ref, turned_ref = outs[:3]
    rows, width = tokens_ref.shape
    block = rows // RESIDUES
    if placed is None:
        full_ref[...] = refs[3][...]
    else:
        place_pieces(refs[3], refs[4:8], full_ref, *placed)
    fill_stripes(wide_ref, tokens_ref[...].astype(F32))
    gain, shift = norm_ref[0:1], norm_ref[1:2]
    for first, natural in residue_rows(block):
        span = slice(first, first + block)
        values = read_stripes(wide_ref, natural)
        ordered_ref[span] = values.astype(BF16)
        hidden_ref[span] = (standardize(values)[0] * gain + shift).astype(BF16)
    turned_ref[...] = hidden_ref[...].T
    ones = jnp.where(lax.broadcasted_iota(jnp.int32, (16, LANES), 0) == 0, 1.0, 0.0).astype(BF16)
    odd = lax.rem(lax.div(lax.broadcasted_iota(jnp.int32, (width, 1), 0), head_dim), 2) == 1
    half = rows // 2
    for i in range(3):
        product = dot_tn(full_ref[:, i * width : (i + 1) * width], turned_ref[...])
        if i != 1:
            at = i // 2 * width
            column = dot_tn(bias_ref[:, at : at + width], ones)
            product += jnp.concatenate([column] * (rows // LANES), axis=1)
        low = product.astype(BF16)
        outs[3 + i][...] = low
        if i:
            outs[5 + i][...] = jnp.where(odd, low[:, half:], low[:, :half])


def project(tokens, norms, bias, full, pieces, spot, placed, head_dim):
    rows, width = tokens.shape
    ins = [tokens, norms, bias] + ([full] if placed is None else [spot, *pieces])
    specs = [pl.BlockSpec(memory_space=pltpu.VMEM)] * len(ins)
    if placed is not None:
        specs[3] = pl.BlockSpec(memory_space=pltpu.SMEM)
    turned = jax.ShapeDtypeStruct((width, rows), BF16)
    part = jax.ShapeDtypeStruct((width, rows // 2), BF16)
    outs = [
        jax.ShapeDtypeStruct((width, 3 * width), BF16), jax.ShapeDtypeStruct((rows, width), BF16),
        turned, turned, turned, turned, part, part,
    ]
    return pl.pallas_call(
        functools.partial(project_kernel, head_dim, placed),
        in_specs=specs,
        out_specs=[pl.BlockSpec(memory_space=pltpu.VMEM)] * len(outs),
        out_shape=outs,
        scratch_shapes=[stripes(rows, width), pltpu.VMEM((rows, width), BF16)],
        compiler_params=pltpu.CompilerParams(vmem_limit_bytes=VMEM_LIMIT),
        cost_estimate=pl.CostEstimate(
            flops=6 * rows * width * width,
            transcendentals=0,
            bytes_accessed=12 * width * width + 16 * rows * width,
        ),
        name="project",
    )(*ins)


def finish_kernel(weight_ref, grad_ref, tokens_ref, middle_ref, norm_ref, sums_ref, wide_ref, out_ref, table_ref, natural_ref):
    step, count = pl.program_id(0), pl.num_programs(0)
    tile, width = tokens_ref.shape
    block = out_ref.shape[0] // RESIDUES

    @pl.when(step == 0)
    def _():
        table_ref[...] = jnp.zeros_like(table_ref)
        table_ref[4:8] = sums_ref[...]
        for i in range(wide_ref.shape[1] // width):
            table_ref[8 + i : 9 + i] = wide_ref[:, i * width : (i + 1) * width]

    grad = dot_nn(weight_ref[...], grad_ref[...]).T
    normed, inverse = standardize(tokens_ref[...].astype(F32))
    table_ref[0:1] += jnp.sum(grad * normed, axis=0, keepdims=True)
    table_ref[1:2] += jnp.sum(grad, axis=0, keepdims=True)
    ones = jnp.ones((16, tile), BF16)
    table_ref[2:3] += dot_nt(ones, grad_ref[:width])[0:1]
    table_ref[3:4] += dot_nt(ones, grad_ref[2 * width :])[0:1]
    total = middle_ref[...] + norm_back(grad, normed, inverse, norm_ref[0:1])
    many = tile // block
    half = RESIDUES // 2
    for i in range(many):
        place = step * many + i
        residue = 2 * lax.rem(place, half) + lax.div(place, half)
        natural = pl.ds(residue, block, stride=RESIDUES)
        write_stripes(natural_ref, natural, total[i * block : (i + 1) * block])

    @pl.when(step == count - 1)
    def _():
        out_ref[...] = read_stripes(natural_ref, slice(None))


def finish(weight, grad, tokens, middle, norms, sums, wide):
    rows, width = tokens.shape
    tile = min(rows, 512)
    narrow_spec = pl.BlockSpec((tile, width), lambda r: (r, 0))
    once = pl.BlockSpec(memory_space=pltpu.VMEM)
    return pl.pallas_call(
        finish_kernel,
        grid=(rows // tile,),
        in_specs=[
            once, pl.BlockSpec((grad.shape[0], tile), lambda r: (0, r)), narrow_spec, narrow_spec,
            once, once, once,
        ],
        out_specs=[once, once],
        out_shape=[
            jax.ShapeDtypeStruct((rows, width), F32),
            jax.ShapeDtypeStruct((16, width), F32),
        ],
        scratch_shapes=[stripes(rows, width)],
        compiler_params=pltpu.CompilerParams(vmem_limit_bytes=VMEM_LIMIT),
        cost_estimate=pl.CostEstimate(
            flops=6 * rows * width * width,
            transcendentals=0,
            bytes_accessed=6 * width * width + 16 * rows * width,
        ),
        name="finish",
    )(weight, grad, tokens, middle, norms, sums, wide)


def feed_forward_kernel(blocks, *refs):
    tokens_ref, attended_ref, natural_ref, small_ref, wide_ref, packed_ref = refs[:6]
    output_ref, grad_ref, mixed_ref, sums_ref, wide_sums_ref, grads_ref = refs[6:12]
    reduce_w, expand_w, output_w, natural_scr, active_scr, expanded_scr = refs[12:18]
    cotangent_scr, hidden_scr, low_scr, in_sems, out_sems = refs[18:]
    tile, width = tokens_ref.shape
    cut, depth = reduce_w.shape[1], output_w.shape[1]
    step, count = pl.program_id(0), pl.num_programs(0)
    block = natural_ref.shape[0] // RESIDUES
    halves, columns = packed_ref.shape[1], packed_ref.shape[3]
    local = blocks // halves * width // columns

    def arrival(index, y, at, size, target):
        return pltpu.make_async_copy(
            packed_ref.at[:, y, pl.ds(at, size)], target, in_sems.at[index]
        )

    def arrivals(first=0, last=None):
        found = []
        for y in range(halves):
            lanes = pl.ds(y * columns, columns)
            found.append((y, cut + local * depth, depth, output_w.at[:, :, lanes]))
        for y in range(halves):
            for i in range(local):
                at = (y * local + i) * columns
                target = expand_w.at[at // width, :, :, pl.ds(at % width, columns)]
                found.append((y, cut + i * depth, depth, target))
        for y in range(halves):
            found.append((y, 0, cut, reduce_w.at[:, :, pl.ds(y * columns, columns)]))
        indices = range(len(found))[first:last]
        return [arrival(i, *found[i]) for i in indices]

    def await_first(first, last):
        @pl.when(step == 0)
        def _():
            for copy in arrivals(first, last):
                copy.wait()

    @pl.when(step == 0)
    def _():
        for copy in arrivals():
            copy.start()
        fill_stripes(natural_scr, natural_ref[...].astype(F32))
        sums_ref[...] = jnp.zeros_like(sums_ref)
        wide_sums_ref[...] = jnp.zeros_like(wide_sums_ref)

    many, half = tile // block, RESIDUES // 2
    strided = []
    for i in range(many):
        place = step * many + i
        residue = 2 * lax.rem(place, half) + lax.div(place, half)
        strided.append(pl.ds(residue, block, stride=RESIDUES))
    here = pl.ds(pl.multiple_of(step * tile, tile), tile)
    bias_output, gain, shift, bias_reduce = (small_ref[i : i + 1] for i in range(4))
    upstream = jnp.concatenate([read_stripes(natural_scr, natural) for natural in strided], axis=0)
    cotangent = upstream.astype(BF16)
    cotangent_scr[here] = cotangent
    await_first(0, halves)
    project = output_w[...].reshape(width, width)
    middle = tokens_ref[...].astype(F32) + dot_tn(attended_ref[:, here], project) + bias_output
    normed, inverse = standardize(middle)
    hidden = (normed * gain + shift).astype(BF16)
    hidden_scr[here] = hidden
    output = middle + bias_reduce
    hidden_grad = jnp.zeros(middle.shape, F32)
    await_first(halves, halves + halves * local + halves)
    shrink_all = reduce_w[...].reshape(blocks * width, width)
    for i in range(blocks):
        span = slice(i * width, (i + 1) * width)
        grow = expand_w[i].reshape(width, width)
        shrink = shrink_all[span]
        active, slope = gelu_pair(dot_nn(hidden, grow) + wide_ref[:, span])
        active = active.astype(BF16)
        active_scr[i, here] = active
        output += dot_nn(active, shrink)
        expanded = (dot_nt(cotangent, shrink) * slope).astype(BF16)
        expanded_scr[i, here] = expanded
        wide_sums_ref[:, span] += jnp.sum(expanded.astype(F32), axis=0, keepdims=True)
        hidden_grad += dot_nt(expanded, grow)
    for i, natural in enumerate(strided):
        write_stripes(natural_scr, natural, output[i * block : (i + 1) * block])
    middle_grad = upstream + norm_back(hidden_grad, normed, inverse, gain)
    grad_ref[...] = middle_grad
    low = middle_grad.astype(BF16)
    low_scr[here] = low
    mixed_ref[...] = dot_nt(project, low).astype(BF16)
    for i, part in enumerate((hidden_grad * normed, hidden_grad, middle_grad, upstream)):
        sums_ref[i : i + 1] += jnp.sum(part, axis=0, keepdims=True)

    @pl.when(step == count - 1)
    def _():
        output_ref[...] = read_stripes(natural_scr, slice(None)).astype(BF16)
        copies = []

        def leave(source, target):
            copies.append(pltpu.make_async_copy(source, target, out_sems.at[len(copies)]))
            copies[-1].start()

        for i in range(blocks):
            product = dot_tn(active_scr[i], cotangent_scr[...]).astype(BF16)
            if cut <= width:
                shards = slice(i * width // cut, (i + 1) * width // cut)
                reduce_w[shards] = product.reshape(-1, cut, width)
                leave(reduce_w.at[shards], grads_ref.at[shards, pl.ds(0, cut)])
            else:
                span = pl.ds(i * width, width)
                reduce_w[0, span] = product
                leave(reduce_w.at[:, span], grads_ref.at[:, span])
        for i in range(blocks):
            product = dot_tn(hidden_scr[...], expanded_scr[i]).astype(BF16)
            expand_w[i] = product.reshape(-1, depth, width)
            leave(expand_w.at[i], grads_ref.at[:, pl.ds(cut + i * depth, depth)])
        product = dot_nn(attended_ref[...], low_scr[...]).astype(BF16)
        output_w[...] = product.reshape(-1, depth, width)
        leave(output_w, grads_ref.at[:, pl.ds(cut + blocks * depth, depth)])
        for copy in copies:
            copy.wait()


def feed_forward(tokens, attended, cotangent, small, wide, packed):
    rows, width = tokens.shape
    ff = wide.shape[1]
    blocks = ff // width
    shards, halves = packed.shape[:2]
    tile = min(rows, 256)
    narrow_spec = pl.BlockSpec((tile, width), lambda r: (r, 0))
    turned_spec = pl.BlockSpec((width, tile), lambda r: (0, r))
    once = pl.BlockSpec(memory_space=pltpu.VMEM)
    rows_scr = pltpu.VMEM((rows, width), BF16)
    wide_scr = pltpu.VMEM((blocks, rows, width), BF16)
    return pl.pallas_call(
        functools.partial(feed_forward_kernel, blocks),
        grid=(rows // tile,),
        in_specs=[narrow_spec, once, once, once, once, pl.BlockSpec(memory_space=pl.ANY)],
        out_specs=[once, narrow_spec, turned_spec, once, once, pl.BlockSpec(memory_space=pl.ANY)],
        out_shape=[
            jax.ShapeDtypeStruct((rows, width), BF16),
            jax.ShapeDtypeStruct((rows, width), F32),
            jax.ShapeDtypeStruct((width, rows), BF16),
            jax.ShapeDtypeStruct((4, width), F32),
            jax.ShapeDtypeStruct((1, ff), F32),
            jax.ShapeDtypeStruct((shards, (2 * ff + width) // shards, width), BF16),
        ],
        scratch_shapes=[
            pltpu.VMEM((shards, ff // shards, width), BF16),
            pltpu.VMEM((blocks, shards, width // shards, width), BF16),
            pltpu.VMEM((shards, width // shards, width), BF16),
            stripes(rows, width),
            wide_scr,
            wide_scr,
            rows_scr,
            rows_scr,
            rows_scr,
            pltpu.SemaphoreType.DMA((2 * halves + blocks * halves,)),
            pltpu.SemaphoreType.DMA((2 * blocks + 1,)),
        ],
        compiler_params=pltpu.CompilerParams(vmem_limit_bytes=VMEM_LIMIT),
        cost_estimate=pl.CostEstimate(
            flops=2 * rows * width * (6 * ff + 3 * width),
            transcendentals=2 * rows * ff,
            bytes_accessed=4 * packed.size + 20 * rows * width,
        ),
        name="feed_forward",
    )(tokens, attended, cotangent, small, wide, packed)


def level_table():
    head = np.arange(HEADS)[:, None]
    residue = 2 * np.arange(RESIDUES // 2)[None, :] + head % 2
    return sum((residue % 2**b == head % 2**b).astype(int) for b in range(1, BRANCHES))


def log_rows(times):
    parts = np.log2(times).astype(np.float32)
    rows = []
    for _ in range(3):
        low = parts.astype(ml_dtypes.bfloat16)
        rows.append(low)
        parts = parts - low.astype(np.float32)
    return np.stack(rows, axis=2).reshape(times.shape[0], -1, times.shape[2])


def attention_extras(rows, own_starts, far_starts, own_count, far_count, same):
    half, block = rows // 2, rows // RESIDUES
    levels = level_table()
    level = np.arange(1, BRANCHES)[None, :, None]
    lower = np.minimum(level, levels[:, None, :])

    def repeat(table, devices):
        return np.tile(np.repeat(table, block, axis=-1), devices)

    rank = np.arange(half)
    place = [(rank % block) * RESIDUES + 2 * (rank // block) + parity for parity in range(2)]

    def liveness(starts, count, allowed):
        live = [
            jnp.stack([(start + jnp.asarray(place[p]) < count) & allowed for p in range(2)])
            for start in starts
        ]
        return jnp.where(jnp.concatenate(live, axis=1), 0.0, NEGATIVE).astype(BF16)

    def built(times, live):
        count, _, keys = times.shape
        fixed = np.zeros((count, EXTRA, keys), ml_dtypes.bfloat16)
        fixed[:, TIMES:LIVE] = times
        fixed[:, FIXED : FIXED + 3] = 1
        row = np.arange(EXTRA)[None, :, None]
        return jnp.where(row == LIVE, live[:, None], jnp.asarray(fixed))

    own_live = liveness(own_starts, own_count, True)
    far_live = liveness(far_starts, far_count, same)
    by_head = np.arange(HEADS) % 2
    none = np.zeros((2, LIVE, half * len(own_starts)), ml_dtypes.bfloat16)

    def per_head(live):
        return jnp.where(by_head[:, None] == 1, live[1], live[0])

    query = np.zeros((HEADS, EXTRA, half), ml_dtypes.bfloat16)
    spread = np.repeat(levels, block, axis=1)
    for one in range(1, BRANCHES):
        query[:, 3 * (one - 1) : 3 * one] = (spread == one)[:, None, :]
    query[:, LIVE] = 1
    return {
        "plain": built(none, own_live),
        "same": built(repeat(log_rows(1.0 + lower), len(own_starts)), per_head(own_live)),
        "far": built(repeat(log_rows(lower), len(far_starts)), per_head(far_live)),
        "query": jnp.asarray(query),
        "self": jnp.asarray(np.log2(1.0 + spread).astype(np.float32))[:, None],
    }


def half_of(table, odd):
    half = table.shape[-1] // 2
    return jnp.where(odd, table[..., half:], table[..., :half])


def add_half(total, part, odd):
    part = part.astype(F32)
    both = jnp.concatenate([jnp.where(odd, 0.0, part), jnp.where(odd, part, 0.0)], axis=-1)
    return total.astype(F32) + both


def swap_pairs(value):
    return lax.ppermute(value, "branch", [(0, 1), (1, 0)])


def gather_columns(shard, branches):
    if branches != 2:
        return lax.all_gather(shard, "branch", axis=shard.ndim - 1, tiled=True)
    other = swap_pairs(shard)
    first = lax.axis_index("branch") == 0
    return jnp.concatenate(
        [jnp.where(first, shard, other), jnp.where(first, other, shard)], axis=-1
    )


def scatter_columns(total, branches):
    if branches != 2:
        return lax.psum_scatter(
            total, "branch", scatter_dimension=total.ndim - 1, tiled=True
        ).astype(F32)
    half = total.shape[-1] // 2
    at = lax.axis_index("branch")
    keep = lax.dynamic_slice_in_dim(total, at * half, half, total.ndim - 1)
    away = lax.dynamic_slice_in_dim(total, (1 - at) * half, half, total.ndim - 1)
    return keep.astype(F32) + swap_pairs(away).astype(F32)


def weight_sum(partial, branches):
    low = lax.psum_scatter(partial, "slides", scatter_dimension=0, tiled=True)
    return scatter_columns(low, branches)


def pack_rows(reduce_part, expand_part, output_part):
    width = output_part.shape[-1]
    blocks = expand_part.shape[-1] // width
    return jnp.concatenate(
        [reduce_part]
        + [expand_part[..., i * width : (i + 1) * width] for i in range(blocks)]
        + [output_part],
        axis=-2,
    )


def unpack_rows(packed, width, ff):
    blocks = ff // width
    depth = packed.shape[-2] // (2 * blocks + 1)
    cut = blocks * depth
    expand = [packed[..., cut + i * depth : cut + (i + 1) * depth, :] for i in range(blocks)]
    return packed[..., :cut, :], jnp.concatenate(expand, axis=-1), packed[..., 2 * cut :, :]


def join_columns(own, other):
    first = lax.axis_index("branch") == 0
    return jnp.concatenate(
        [jnp.where(first, own, other), jnp.where(first, other, own)], axis=-1
    )


def pack_kernel(reduce_ref, expand_ref, output_ref, packed_ref):
    cut, width = reduce_ref.shape
    depth = output_ref.shape[0]
    packed_ref[:cut] = reduce_ref[...]
    blocks = expand_ref.shape[1] // width
    for i in range(blocks):
        packed_ref[cut + i * depth : cut + (i + 1) * depth] = expand_ref[:, i * width : (i + 1) * width]
    packed_ref[cut + blocks * depth :] = output_ref[...]


def join_kernel(cut, depth, at_ref, own_ref, other_ref, joined_ref):
    columns = own_ref.shape[1]
    blocks = (own_ref.shape[0] - cut) // depth - 1

    def put(halves):
        for y, half in enumerate(halves):
            lanes = slice(y * columns, (y + 1) * columns)
            joined_ref[:cut, lanes] = half[:cut]
            joined_ref[cut + blocks * depth :, lanes] = half[cut + blocks * depth :]
            for i in range(blocks):
                row, lane = divmod((y * blocks + i) * columns, 2 * columns)
                target = cut + row * depth
                source = cut + i * depth
                joined_ref[target : target + depth, lane : lane + columns] = half[
                    source : source + depth
                ]

    @pl.when(at_ref[0] == 0)
    def _():
        put((own_ref, other_ref))

    @pl.when(at_ref[0] != 0)
    def _():
        put((other_ref, own_ref))


def gather_packed(reduce_weight, expand_weight, output_weight, first_transfers, branches):
    size = lax.axis_size("slides")
    depth, columns = output_weight.shape
    aligned = branches == 2 and depth % 16 == 0 and columns % LANES == 0
    if aligned:
        rows = reduce_weight.shape[0] + depth + expand_weight.size // columns
        shard = pl.pallas_call(
            pack_kernel,
            out_shape=jax.ShapeDtypeStruct((rows, columns), BF16),
            name="pack",
        )(reduce_weight, expand_weight, output_weight)
    else:
        shard = pack_rows(reduce_weight, expand_weight, output_weight)
    if aligned:
        at = lax.axis_index("branch").reshape(1)
        other, first_transfers = lax.optimization_barrier((swap_pairs(shard), first_transfers))
        shard = pl.pallas_call(
            functools.partial(join_kernel, reduce_weight.shape[0], depth),
            in_specs=[pl.BlockSpec(memory_space=pltpu.SMEM)]
            + [pl.BlockSpec(memory_space=pltpu.VMEM)] * 2,
            out_shape=jax.ShapeDtypeStruct((rows, 2 * columns), BF16),
            name="join",
        )(at, shard, other)
        return lax.all_gather(shard, "slides", axis=0, tiled=False)[:, None], first_transfers
    packed = lax.all_gather(shard, ("slides", "branch"), axis=0, tiled=False)
    packed = packed.reshape(size, branches, *shard.shape)
    ff = size * reduce_weight.shape[0]
    parts = unpack_rows(packed, columns, ff // branches)
    parts = [m.transpose(0, 2, 1, 3).reshape(1, -1, branches * m.shape[-1]) for m in parts]
    return pack_rows(*parts)[None], first_transfers


def gather_vectors(vectors, branches, rows_of):
    cuts = np.cumsum([0] + [m.shape[0] for m in vectors])
    if branches != 2:
        table = lax.all_gather(jnp.concatenate(vectors), "branch", axis=0, tiled=False)
        return [table[:, a:b].reshape(1, -1) for a, b in zip(cuts, cuts[1:])]
    own, other = rows_of
    columns = own.shape[1]
    first = lax.axis_index("branch") == 0
    halves = [jnp.where(first, own, other), jnp.where(first, other, own)]
    at = cuts // columns
    return [
        jnp.concatenate(
            [half[row : row + 1] for half in halves for row in range(at[i], at[i + 1])], axis=1
        )
        for i in range(len(vectors))
    ]


def sum_packed(packed, width, ff):
    size = lax.axis_size("slides")
    if packed.shape[0] != size:
        parts = unpack_rows(packed, width, ff)
        packed = pack_rows(*(m.reshape(size, -1, m.shape[-1]) for m in parts))
    rows = packed.shape[1]
    return lax.psum_scatter(
        packed.reshape(size * rows, width), "slides", scatter_dimension=0, tiled=True
    )


def branch_half(low, index, width, ff):
    reduce_part, expand_part, output_part = unpack_rows(low, width, ff)
    columns = width // 2
    grown = lax.dynamic_slice_in_dim(expand_part, index * (ff // 2), ff // 2, 1)
    pieces = [
        lax.dynamic_slice_in_dim(part, index * columns, columns, 1)
        for part in (reduce_part, output_part)
    ]
    pieces += [grown[:, i : i + columns] for i in range(0, ff // 2, columns)]
    return jnp.concatenate(pieces, axis=0)


def unpack_half(total, depth, cut):
    tail = [total[row : row + depth] for row in range(cut + depth, total.shape[0], depth)]
    return total[:cut], jnp.concatenate(tail, axis=1), total[cut : cut + depth]


def flip(value, bit):
    return lax.ppermute(value, "slides", [(i, i ^ bit) for i in range(lax.axis_size("slides"))])


def shifted(value, step):
    size = lax.axis_size("slides")
    return lax.ppermute(value, "slides", [(i, (i + 4 * step) % size) for i in range(size)])


def gather_pieces(held, later):
    half = held[0].shape[1] // 2 // LANES * LANES
    first = jnp.stack([m[:, :half] for m in held])
    second = jnp.stack([m[:, half:] for m in held])
    first, second = jnp.stack([first, flip(first, 2)]), jnp.stack([second, swap_pairs(second)])
    first, second, later = lax.optimization_barrier((first, second, later))
    other = swap_pairs(later[0])
    first, second = jnp.stack([first, swap_pairs(first)]), jnp.stack([second, flip(second, 2)])
    pieces = (first, second, flip(first, 1), flip(second, 1))
    slide = lax.axis_index("slides")
    spot = jnp.stack(
        [
            lax.div(slide, 4),
            lax.rem(lax.div(slide, 2), 2),
            lax.rem(slide, 2),
            lax.axis_index("branch"),
        ]
    )
    return pieces, spot.astype(jnp.int32), other, later


def pick(table, index, axis):
    return lax.dynamic_index_in_dim(table, index, axis, keepdims=False)


def split_kernel(core_ref, left_ref, right_ref, keep_ref, send_ref, product_ref):
    product_ref[...] = dot_nt(left_ref[...], right_ref[...]).astype(BF16).reshape(product_ref.shape)
    core = core_ref[0]
    for pair in range(product_ref.shape[0] // 2):
        at = (0, pair // 2, pair % 2)
        keep_ref[at] = product_ref[2 * pair + core]
        send_ref[at] = product_ref[2 * pair + 1 - core]


def split_product(left, right, core):
    size = lax.axis_size("slides")
    features, rows = left.shape
    depth, columns = features // size, right.shape[0] // 2
    step = columns
    wide = columns // step
    block = pl.BlockSpec((1, size // 4, 2, depth, step), lambda j: (j // wide, 0, 0, 0, j % wide))
    return pl.pallas_call(
        split_kernel,
        grid=(2 * wide,),
        in_specs=[
            pl.BlockSpec(memory_space=pltpu.SMEM),
            whole_spec(left.shape),
            pl.BlockSpec((step, rows), lambda j: (j, 0)),
        ],
        out_specs=[block, block],
        out_shape=[jax.ShapeDtypeStruct((2, size // 4, 2, depth, columns), BF16)] * 2,
        scratch_shapes=[pltpu.VMEM((size, depth, step), BF16)],
        compiler_params=pltpu.CompilerParams(vmem_limit_bytes=VMEM_LIMIT),
        cost_estimate=pl.CostEstimate(
            flops=4 * rows * features * columns,
            transcendentals=0,
            bytes_accessed=2 * (left.size + right.size + 2 * features * columns),
        ),
        name="joint_gradient",
    )(core.reshape(1), left, right)


def deal_kernel(spans, at_ref, *refs):
    tables, outs = refs[: -len(spans)], refs[-len(spans) :]
    total = sum((table[...] for table in tables[1:]), tables[0][...])
    width = total.shape[1]

    def put(index):
        for (row, count), out in zip(spans, outs):
            if count == 1:
                out[...] = total[row, index * width // 2 : (index + 1) * width // 2]
            else:
                for i in range(count // 2):
                    at = row + index * count // 2 + i
                    out[i * width : (i + 1) * width] = total[at]

    @pl.when(at_ref[0] == 0)
    def _():
        put(0)

    @pl.when(at_ref[0] != 0)
    def _():
        put(1)


def deal(tables, spans, at):
    width = tables[0].shape[1]
    return pl.pallas_call(
        functools.partial(deal_kernel, spans),
        in_specs=[pl.BlockSpec(memory_space=pltpu.SMEM)]
        + [pl.BlockSpec(memory_space=pltpu.VMEM)] * len(tables),
        out_shape=[jax.ShapeDtypeStruct((count * width // 2,), F32) for _, count in spans],
        name="deal",
    )(at.reshape(1), *tables)


def sum_tree(kept, sent, table_of, gate, near, outer, at):
    rounds = kept.shape[1]

    def both(one, two):
        return (one.astype(F32) + two.astype(F32)).astype(BF16)

    total = both(kept, flip(sent, 1))
    low, high = total[:, : rounds // 2], total[:, rounds // 2 :]
    away, off, gate = lax.optimization_barrier(
        (pick(low, 1 - at, 0), pick(high, 1 - near, 2), gate)
    )
    away, off = swap_pairs(away), flip(off, 2)
    table = table_of(gate)
    low, high = both(pick(low, at, 0), away), both(pick(high, near, 2), off)
    away, off, table = lax.optimization_barrier(
        (pick(low, 1 - near, 1), pick(high, 1 - at, 0), table)
    )
    low, high = both(pick(low, near, 1), flip(away, 2)), both(pick(high, at, 0), swap_pairs(off))
    table += flip(table, 1)
    table += swap_pairs(table)
    joined = jnp.concatenate([low, high], axis=0)
    total = pick(joined, outer, 0).astype(F32)
    sends = [pick(joined, lax.rem(outer + step, rounds), 0) for step in range(1, rounds)]
    sends, table = lax.optimization_barrier((sends, table))
    for step, part in enumerate(sends):
        total += shifted(part, step + 1).astype(F32)
    table += flip(table, 2)
    return total, [table] + [shifted(table, step) for step in range(1, rounds)]


def on_device(
    tokens,
    cotangent,
    first_gain,
    first_shift,
    joint_weight,
    joint_bias,
    output_weight,
    output_bias,
    second_gain,
    second_shift,
    expand_weight,
    expand_bias,
    reduce_weight,
    reduce_bias,
    block_owner,
    tile_count,
):
    rows, width = tokens.shape
    branches = lax.axis_size("branch")
    head_dim = width // HEADS
    block = rows // RESIDUES
    mates = SEG_BASE // rows
    at = lax.axis_index("branch")
    segment = lax.div(at, mates)
    within = at - segment * mates
    odd = ((np.arange(width) // head_dim) % 2 == 1)[:, None]

    parameters = (
        first_gain, first_shift, joint_bias, output_bias,
        second_gain, second_shift, expand_bias, reduce_bias,
    )
    depth = joint_weight.shape[0]
    slides = lax.axis_size("slides")
    trees = branches == 2 and slides % 8 == 0 and depth % 16 == 0
    held = [joint_weight]
    if trees:
        held += [shifted(joint_weight, step) for step in range(1, slides // 4)]
    packed_weights, held = gather_packed(
        reduce_weight, expand_weight, output_weight, held, branches
    )
    if trees:
        small = jnp.concatenate([m.reshape(-1, width // 2) for m in parameters], axis=0)
        pieces, spot, other, (small, block_owner, tile_count) = gather_pieces(
            held, (small, block_owner, tile_count)
        )
        vectors = gather_vectors(parameters, branches, (small, other))
        joint_full, placed = None, joint_weight.shape
    else:
        joint_full = lax.all_gather(
            gather_columns(joint_weight, branches), "slides", axis=0, tiled=True
        )
        vectors = gather_vectors(parameters, branches, None)
        pieces, spot, placed = (), None, None
    bias_joint = jnp.pad(vectors[2], ((0, 15), (0, 0)))
    gain_one, shift_one, _, bias_output, gain_two, shift_two, bias_expand, bias_reduce = (
        m.astype(F32) for m in vectors
    )
    norms = jnp.concatenate([gain_one, shift_one], axis=0)

    owners = block_owner.reshape(-1)
    counts = tile_count.reshape(-1)
    own_count = jnp.where(segment == 0, counts[0], counts[1])
    far_count = jnp.where(segment == 0, counts[1], counts[0])
    own_starts = [lax.rem(within + d, mates) * rows for d in range(mates)]
    far_starts = [d * rows for d in range(mates)]
    extras = attention_extras(
        rows, own_starts, far_starts, own_count, far_count, owners[0] == owners[1]
    )

    joint_full, tokens_low, hidden_turned, q, k, v, k_half, v_half = project(
        tokens, norms, bias_joint, joint_full, pieces, spot, placed, head_dim
    )
    if mates == 1 and branches == 2:
        k_own, v_own = k[None], v[None]
        k_far, v_far = swap_pairs(k_half)[None], swap_pairs(v_half)[None]
    else:
        own_at = [segment * mates + lax.rem(within + d, mates) for d in range(mates)]
        far_at = [(1 - segment) * mates + d for d in range(mates)]

        def chosen(table, indices):
            whole = lax.all_gather(table, "branch", axis=0)
            return jnp.stack([lax.dynamic_index_in_dim(whole, d, 0, False) for d in indices])

        k_own, v_own = chosen(k, own_at), chosen(v, own_at)
        k_far, v_far = chosen(k_half, far_at), chosen(v_half, far_at)
    attended, part, total_log = attend_own(q, k_own, v_own, extras)
    attended, total_log = attend_far(q, k_far, v_far, extras, attended, part, total_log)
    ff = bias_expand.shape[1]
    small = jnp.concatenate([bias_output, gain_two, shift_two, bias_reduce], axis=0)
    output, middle_grad, mixed_grad, sums, wide_sums, packed_grads = feed_forward(
        tokens_low, attended, cotangent, small, bias_expand, packed_weights
    )
    mixed_grad, packed_grads = lax.optimization_barrier((mixed_grad, packed_grads))
    low_sums = sum_packed(packed_grads, width, ff)

    dq, dk_first, dv_first, dk_far, dv_far = attend_far_back(
        q, k_own, v_own, k_far, v_far, extras, attended, mixed_grad, total_log
    )
    dq, dk_own, dv_own = attend_own_back(
        q, k_own, v_own, extras, attended, mixed_grad, total_log, dq, dk_first, dv_first
    )
    if mates == 1 and branches == 2:
        key_sum = add_half(dk_own[0], swap_pairs(dk_far[0]), odd)
        value_sum = add_half(dv_own[0], swap_pairs(dv_far[0]), odd)
    else:

        def spread(own, far):
            canvas = jnp.zeros((branches, width, rows), BF16)
            for d, index in enumerate(own_at):
                canvas = lax.dynamic_update_index_in_dim(canvas, own[d], index, 0)
            for d, index in enumerate(far_at):
                full = add_half(jnp.zeros((width, rows), F32), far[d], odd).astype(BF16)
                canvas = lax.dynamic_update_index_in_dim(canvas, full, index, 0)
            return lax.psum_scatter(canvas, "branch", scatter_dimension=0, tiled=True)[0]

        key_sum = spread(dk_own, dk_far)
        value_sum = spread(dv_own, dv_far)
    value_low = value_sum.astype(BF16)
    joint_grad = jnp.concatenate([dq, key_sum.astype(BF16), value_low], axis=0)
    found = []

    def table_of(grad):
        found.extend(finish(joint_full, joint_grad, tokens_low, grad, norms, sums, wide_sums))
        return found[1]

    sizes = (1, 1, 2, 1, 1, 1, 1, ff // width)
    starts = np.cumsum((0,) + sizes)
    if trees:
        slide = lax.axis_index("slides")
        kept, sent = split_product(hidden_turned, joint_grad, lax.rem(slide, 2))
        joint_sum, tables = sum_tree(
            kept, sent, table_of, middle_grad, lax.rem(lax.div(slide, 2), 2), lax.div(slide, 4), at
        )
        arrived = swap_pairs(branch_half(low_sums, 1 - at, width, ff))
        halves = branch_half(low_sums, at, width, ff).astype(F32) + arrived.astype(F32)
        reduce_sum, expand_sum, output_sum = unpack_half(
            halves, output_weight.shape[0], reduce_weight.shape[0]
        )
        mine = deal(tables, tuple((int(a), n) for a, n in zip(starts, sizes)), at)
    else:
        joint_sum = weight_sum(dot_nt(hidden_turned, joint_grad).astype(BF16), branches)
        table = lax.psum(table_of(middle_grad), ("slides", "branch"))
        reduce_sum, expand_sum, output_sum = (
            scatter_columns(part, branches) for part in unpack_rows(low_sums, width, ff)
        )
        mine = []
        for row, count in zip(starts, sizes):
            share = count * width // branches
            whole = table[row : row + count].reshape(-1)
            mine.append(lax.dynamic_slice_in_dim(whole, at * share, share))
    tokens_grad = found[0]
    first_gain_sum, first_shift_sum, joint_bias_sum, second_gain_sum = mine[:4]
    second_shift_sum, output_bias_sum, reduce_bias_sum, expand_bias_sum = mine[4:]
    return (
        output,
        tokens_grad,
        first_gain_sum,
        first_shift_sum,
        joint_sum,
        joint_bias_sum,
        output_sum,
        output_bias_sum,
        second_gain_sum,
        second_shift_sum,
        expand_sum,
        expand_bias_sum,
        reduce_sum,
        reduce_bias_sum,
    )


def solution(mesh):
    rows = P(("slides", "branch"), None)
    matrix = P("slides", "branch")
    vector = P("branch")
    placed = (
        rows, rows, vector, vector, matrix, vector, matrix, vector,
        vector, vector, matrix, vector, matrix, vector, P("slides", None), P("slides", None),
    )
    given = (
        rows, rows, vector, vector, matrix, vector, matrix, vector,
        vector, vector, matrix, vector, matrix, vector,
    )
    return jax.shard_map(on_device, mesh=mesh, in_specs=placed, out_specs=given, check_vma=False)
```

```python
import functools
import math

import jax
import jax.numpy as jnp
import ml_dtypes
import numpy as np
from jax import lax
from jax.experimental import pallas as pl
from jax.experimental.pallas import tpu as pltpu
from jax.sharding import PartitionSpec as P

HEADS = 16
SEG_BASE = 1024
BRANCHES = 5
RESIDUES = 2 ** (BRANCHES - 1)
EPSILON = 1e-05
NEGATIVE = -1e30
LANES = 128
EXTRA = 32
TIMES, LIVE, FIXED = 0, 12, 13
UNROLL = 4
OWN_UNROLL = 2
PIECE = 512
VMEM_LIMIT = 60 * 1024 * 1024

BF16 = jnp.bfloat16
F32 = jnp.float32


def standardize(values):
    centred = values - jnp.mean(values, axis=-1, keepdims=True)
    inverse = lax.rsqrt(jnp.mean(centred * centred, axis=-1, keepdims=True) + EPSILON)
    return (centred * inverse, inverse)


def norm_back(upstream, normed, inverse, gain):
    scaled = upstream * gain
    return inverse * (
        scaled
        - jnp.mean(scaled, axis=-1, keepdims=True)
        - normed * jnp.mean(scaled * normed, axis=-1, keepdims=True)
    )


def gelu_pair(values):
    cumulative = 0.5 * (1.0 + lax.erf(values * (1.0 / math.sqrt(2.0))))
    density = jnp.exp(-0.5 * values * values) * (1.0 / math.sqrt(2.0 * math.pi))
    return values * cumulative, cumulative + values * density


def dot_nn(left, right):
    return lax.dot_general(left, right, (((1,), (0,)), ((), ())), preferred_element_type=F32)


def dot_nt(left, right):
    return lax.dot_general(left, right, (((1,), (1,)), ((), ())), preferred_element_type=F32)


def dot_tn(left, right):
    return lax.dot_general(left, right, (((0,), (0,)), ((), ())), preferred_element_type=F32)


def thirds(value):
    first = value.astype(BF16)
    rest = value - first.astype(F32)
    second = rest.astype(BF16)
    return first, second, (rest - second.astype(F32)).astype(BF16)


class HeadView:
    def __init__(self, head, far, refs, head_dim, other_segment, own=True):
        half = refs["q"].shape[-1] // 2
        same = lax.rem(head, 2)
        same = same if far else 1 - same
        self.half = half
        self.rows = pl.ds(pl.multiple_of(head * head_dim, 16), head_dim)
        self.same = pl.ds(pl.multiple_of(same * half, LANES), half)
        self.other = pl.ds(pl.multiple_of((1 - same) * half, LANES), half)
        self.devices = refs["k"].shape[0] if own else 0
        self.head = head
        self.far = far
        self.own = own
        self.other_segment = other_segment
        extras = []
        if own:
            extras += [
                refs["same"][head] if far else refs["plain"][same],
                refs["plain"][1 - same],
            ]
        if other_segment:
            extras.append(refs["far"][head])
        self.extra = jnp.concatenate(extras, axis=1)

    def gathered(self, own_ref, far_ref):
        found = [own_ref[d, self.rows, self.same] for d in range(self.devices)]
        found += [own_ref[d, self.rows, self.other] for d in range(self.devices)]
        if self.other_segment:
            found += [far_ref[d, self.rows, :] for d in range(far_ref.shape[0])]
        return jnp.concatenate(found, axis=1)


def with_self(scores, own, first):
    half = scores.shape[1]
    if first >= half:
        return scores
    eye = lax.broadcasted_iota(jnp.int32, (LANES, LANES), 0) == lax.broadcasted_iota(
        jnp.int32, (LANES, LANES), 1
    )
    bands = []
    for row in range(0, min(scores.shape[0], half - first), LANES):
        at = first + row
        band = scores[row : row + LANES]
        here = jnp.where(eye, own[:, at : at + LANES], band[:, at : at + LANES])
        sides = [band[:, :at]] if at else []
        sides.append(here)
        if at + LANES < half:
            sides.append(band[:, at + LANES :])
        bands.append(jnp.concatenate(sides, axis=1))
    if half - first < scores.shape[0]:
        bands.append(scores[half - first :])
    return jnp.concatenate(bands, axis=0)


def head_scores(view, refs, keys, head_dim, constant):
    scale = head_dim ** (-0.5) * math.log2(math.e)
    scaled = refs["q"][view.rows, view.same].astype(F32) * scale
    high = scaled.astype(BF16)
    low = (scaled - high.astype(F32)).astype(BF16)
    half = view.half
    if view.far:
        extra = refs["query"][view.head]
        own = refs["self"][view.head]
    else:
        row = lax.broadcasted_iota(jnp.int32, (EXTRA, half), 0)
        extra = jnp.where(row == LIVE, 1.0, 0.0).astype(BF16)
        own = jnp.zeros((1, half), F32)
    if view.own:
        own = own + jnp.sum(scaled * keys[:, :half].astype(F32), axis=0, keepdims=True)
    if constant is not None:
        row = lax.broadcasted_iota(jnp.int32, (EXTRA, half), 0)
        filled = extra.astype(F32)
        for i, part in enumerate(thirds(constant)):
            filled = jnp.where(row == FIXED + i, part.astype(F32), filled)
        extra = filled.astype(BF16)
        own = own + constant
    left = jnp.concatenate([keys, keys, view.extra], axis=0)
    right = jnp.concatenate([high, low, extra], axis=0)

    def scores(at):
        product = dot_tn(left[:, at : at + PIECE], right)
        return with_self(product, own, at) if view.own else product

    return scores


def softmax_parts(parts, values, known):
    highest = functools.reduce(
        jnp.maximum, [jnp.max(part, axis=0, keepdims=True) for part in parts]
    )
    if known is not None:
        highest = jnp.maximum(highest, known[0])
    mixed, total = 0.0, 0.0
    at = 0
    for part in parts:
        weights = jnp.exp2(part - highest)
        total += jnp.sum(weights, axis=0, keepdims=True)
        mixed += dot_nn(values[:, at : at + part.shape[0]], weights.astype(BF16))
        at += part.shape[0]
    if known is not None:
        share = jnp.exp2(known[0] - highest)
        total += share
        mixed += known[1] * share
    return mixed * (1.0 / total), highest + jnp.log2(total)


def own_kernel(head_dim, names, count, *refs):
    o_ref, part_ref, t_ref = refs[len(names) :]
    refs = dict(zip(names, refs))

    @pl.loop(0, count, unroll=UNROLL)
    def _(head):
        for far in (True, False):
            view = HeadView(head, far, refs, head_dim, False)
            keys = view.gathered(refs["k"], None)
            values = view.gathered(refs["v"], None)
            scores = head_scores(view, refs, keys, head_dim, None)
            parts = [scores(at) for at in range(0, keys.shape[1], PIECE)]
            mixed, total_log = softmax_parts(parts, values, None)
            if far:
                part_ref[view.rows, :] = mixed
            else:
                o_ref[view.rows, view.same] = mixed.astype(BF16)
            t_ref[head, :, view.same] = total_log


def far_kernel(head_dim, names, count, *refs):
    o_ref, t_ref = refs[len(names) :]
    refs = dict(zip(names, refs))
    o_ref[...] = refs["o"][...]
    t_ref[...] = refs["t"][...]

    @pl.loop(0, count, unroll=UNROLL)
    def _(head):
        view = HeadView(head, True, refs, head_dim, True, own=False)
        keys = view.gathered(None, refs["kx"])
        values = view.gathered(None, refs["vx"])
        scores = head_scores(view, refs, keys, head_dim, None)
        parts = [scores(at) for at in range(0, keys.shape[1], PIECE)]
        known = (refs["t"][head, :, view.same], refs["part"][view.rows, :])
        mixed, total_log = softmax_parts(parts, values, known)
        o_ref[view.rows, view.same] = mixed.astype(BF16)
        t_ref[head, :, view.same] = total_log


def head_gradients(view, refs, head_dim):
    natural = head_dim ** (-0.5)
    keys = view.gathered(refs.get("k"), refs.get("kx"))
    values = view.gathered(refs.get("v"), refs.get("vx"))
    queries = refs["q"][view.rows, view.same]
    upstream = refs["g"][view.rows, view.same]
    mixed = refs["o"][view.rows, view.same]
    scores = head_scores(view, refs, keys, head_dim, -refs["t"][view.head, :, view.same])
    inner = -jnp.sum(upstream.astype(F32) * mixed.astype(F32), axis=0, keepdims=True)
    row = lax.broadcasted_iota(jnp.int32, (16, view.half), 0)
    filled = jnp.zeros((16, view.half), F32)
    for i, part in enumerate(thirds(inner)):
        filled = jnp.where(row == i, part.astype(F32), filled)
    row = lax.broadcasted_iota(jnp.int32, (16, keys.shape[1]), 0)
    ones = jnp.where(row < 3, 1.0, 0.0).astype(BF16)
    left = jnp.concatenate([values, ones], axis=0)
    right = jnp.concatenate([upstream, filled.astype(BF16)], axis=0)
    query_grad, key_parts, value_parts = 0.0, [], []
    for at in range(0, keys.shape[1], PIECE):
        span = slice(at, at + PIECE)
        part = scores(at)
        prob_grad = dot_tn(left[:, span], right)
        probs = jnp.exp2(part)
        score_grad = (probs * prob_grad).astype(BF16)
        value_parts.append(dot_nt(upstream, probs.astype(BF16)))
        key_parts.append(dot_nt(queries, score_grad) * natural)
        query_grad += dot_nn(keys[:, span], score_grad)
    return query_grad, jnp.concatenate(key_parts, axis=1), jnp.concatenate(value_parts, axis=1)


def far_back_kernel(head_dim, names, count, *refs):
    part_ref, dkx_ref, dvx_ref = refs[len(names) :]
    refs = dict(zip(names, refs))

    @pl.loop(0, count, unroll=UNROLL)
    def _(head):
        view = HeadView(head, True, refs, head_dim, True, own=False)
        query_grad, key_grad, value_grad = head_gradients(view, refs, head_dim)
        part_ref[view.rows, :] = query_grad
        for d in range(dkx_ref.shape[0]):
            lanes = slice(d * view.half, (d + 1) * view.half)
            dkx_ref[d, view.rows, :] = key_grad[:, lanes].astype(BF16)
            dvx_ref[d, view.rows, :] = value_grad[:, lanes].astype(BF16)


def own_back_kernel(head_dim, names, count, *refs):
    dq_ref, dk_ref, dv_ref = refs[len(names) :]
    refs = dict(zip(names, refs))
    natural = head_dim ** (-0.5)

    @pl.loop(0, count, unroll=OWN_UNROLL)
    def _(head):
        totals = None
        for far in (False, True):
            view = HeadView(head, far, refs, head_dim, False)
            query_grad, *grads = head_gradients(view, refs, head_dim)
            if far:
                query_grad += refs["part"][view.rows, :]
            dq_ref[view.rows, view.same] = (query_grad * natural).astype(BF16)
            if far:
                grads = [one + two for one, two in zip(grads, totals)]
            cut = view.devices * view.half
            totals = [jnp.concatenate([m[:, cut:], m[:, :cut]], axis=1) for m in grads]
        for total, ref in zip(grads, (dk_ref, dv_ref)):
            for d in range(view.devices):
                for lanes, at in ((view.same, d), (view.other, view.devices + d)):
                    part = total[:, at * view.half : (at + 1) * view.half]
                    ref[d, view.rows, lanes] = part.astype(BF16)


def whole_spec(shape):
    zeros = (0,) * len(shape)
    return pl.BlockSpec(shape, lambda *_: zeros)


def like(*members):
    return [jax.ShapeDtypeStruct(m.shape, m.dtype) for m in members]


def attention_call(kernel, name, ins, outs, pairs, matmuls):
    width, rows = ins["q"].shape
    return pl.pallas_call(
        functools.partial(kernel, width // HEADS, tuple(ins), HEADS),
        in_specs=[pl.BlockSpec(memory_space=pltpu.VMEM)] * len(ins),
        out_specs=[pl.BlockSpec(memory_space=pltpu.VMEM)] * len(outs),
        out_shape=outs,
        compiler_params=pltpu.CompilerParams(vmem_limit_bytes=VMEM_LIMIT),
        cost_estimate=pl.CostEstimate(
            flops=2 * matmuls * HEADS * pairs * LANES,
            transcendentals=HEADS * pairs,
            bytes_accessed=8 * rows * width,
        ),
        name=name,
    )(*ins.values())


def attend_own(q, k, v, extras):
    width, rows = q.shape
    ins = dict(q=q, k=k, v=v, **{n: extras[n] for n in ("plain", "same", "query", "self")})
    outs = like(q) + [
        jax.ShapeDtypeStruct((width, rows // 2), F32),
        jax.ShapeDtypeStruct((HEADS, 1, rows), F32),
    ]
    return attention_call(own_kernel, "attend_own", ins, outs, rows * rows * k.shape[0], 2)


def attend_far(q, kx, vx, extras, o, part, t):
    rows = q.shape[1]
    ins = dict(q=q, kx=kx, vx=vx, o=o, part=part, t=t)
    ins |= {n: extras[n] for n in ("far", "query", "self")}
    return attention_call(far_kernel, "attend_far", ins, like(o, t), rows * rows * kx.shape[0] // 4, 2)


def attend_far_back(q, kx, vx, extras, o, g, t):
    width, rows = q.shape
    ins = dict(q=q, kx=kx, vx=vx, o=o, g=g, t=t)
    ins |= {n: extras[n] for n in ("far", "query", "self")}
    outs = [jax.ShapeDtypeStruct((width, rows // 2), F32)] + like(kx, vx)
    pairs = rows * rows * kx.shape[0] // 4
    return attention_call(far_back_kernel, "attend_far_back", ins, outs, pairs, 5)


def attend_own_back(q, k, v, extras, o, g, t, part):
    rows = q.shape[1]
    ins = dict(q=q, k=k, v=v, o=o, g=g, t=t, part=part)
    ins |= {n: extras[n] for n in ("plain", "same", "query", "self")}
    pairs = rows * rows * k.shape[0]
    return attention_call(own_back_kernel, "attend_own_back", ins, like(q, k, v), pairs, 5)


def residue_rows(block):
    order = [2 * i + parity for parity in range(2) for i in range(RESIDUES // 2)]
    return [
        (i * block, pl.ds(residue, block, stride=RESIDUES)) for i, residue in enumerate(order)
    ]


def stripes(rows, width):
    return pltpu.VMEM((width // LANES, rows, LANES), F32)


def fill_stripes(ref, value):
    for c in range(ref.shape[0]):
        ref[c] = value[:, c * LANES : (c + 1) * LANES]


def read_stripes(ref, rows):
    return jnp.concatenate([ref[c, rows, :] for c in range(ref.shape[0])], axis=1)


def write_stripes(ref, rows, value):
    for c in range(ref.shape[0]):
        ref[c, rows, :] = value[:, c * LANES : (c + 1) * LANES]


def place_pieces(spot, pieces, full, depth, columns):
    outer, near, core, branch = spot[0], spot[1], spot[2], spot[3]
    for index, piece in enumerate(pieces):
        group, other_core = index % 2, index // 2
        rounds, width = piece.shape[2], piece.shape[4]
        for one in range(2):
            for two in range(2):
                far_branch, far_near = (one, two) if group == 0 else (two, one)
                offset = 0 if group == 0 else columns - width
                column = jnp.bitwise_xor(branch, far_branch) * columns + offset
                lanes = pl.ds(pl.multiple_of(column, LANES), width)
                for step in range(rounds):
                    shard = (
                        lax.rem(outer - step + rounds, rounds) * 4
                        + jnp.bitwise_xor(near, far_near) * 2
                        + jnp.bitwise_xor(core, other_core)
                    )
                    row = pl.multiple_of(shard * depth, 16)
                    full[pl.ds(row, depth), lanes] = piece[one, two, step]


def project_kernel(head_dim, placed, *refs):
    tokens_ref, norm_ref, bias_ref = refs[:3]
    outs, wide_ref, hidden_ref = refs[-10:-2], refs[-2], refs[-1]
    full_ref, ordered_ref, turned_ref = outs[:3]
    rows, width = tokens_ref.shape
    block = rows // RESIDUES
    if placed is None:
        full_ref[...] = refs[3][...]
    else:
        place_pieces(refs[3], refs[4:8], full_ref, *placed)
    fill_stripes(wide_ref, tokens_ref[...].astype(F32))
    gain, shift = norm_ref[0:1], norm_ref[1:2]
    for first, natural in residue_rows(block):
        span = slice(first, first + block)
        values = read_stripes(wide_ref, natural)
        ordered_ref[span] = values.astype(BF16)
        hidden_ref[span] = (standardize(values)[0] * gain + shift).astype(BF16)
    turned_ref[...] = hidden_ref[...].T
    ones = jnp.where(lax.broadcasted_iota(jnp.int32, (16, LANES), 0) == 0, 1.0, 0.0).astype(BF16)
    odd = lax.rem(lax.div(lax.broadcasted_iota(jnp.int32, (width, 1), 0), head_dim), 2) == 1
    half = rows // 2
    for i in range(3):
        product = dot_tn(full_ref[:, i * width : (i + 1) * width], turned_ref[...])
        if i != 1:
            at = i // 2 * width
            column = dot_tn(bias_ref[:, at : at + width], ones)
            product += jnp.concatenate([column] * (rows // LANES), axis=1)
        low = product.astype(BF16)
        outs[3 + i][...] = low
        if i:
            outs[5 + i][...] = jnp.where(odd, low[:, half:], low[:, :half])


def project(tokens, norms, bias, full, pieces, spot, placed, head_dim):
    rows, width = tokens.shape
    ins = [tokens, norms, bias] + ([full] if placed is None else [spot, *pieces])
    specs = [pl.BlockSpec(memory_space=pltpu.VMEM)] * len(ins)
    if placed is not None:
        specs[3] = pl.BlockSpec(memory_space=pltpu.SMEM)
    turned = jax.ShapeDtypeStruct((width, rows), BF16)
    part = jax.ShapeDtypeStruct((width, rows // 2), BF16)
    outs = [
        jax.ShapeDtypeStruct((width, 3 * width), BF16), jax.ShapeDtypeStruct((rows, width), BF16),
        turned, turned, turned, turned, part, part,
    ]
    return pl.pallas_call(
        functools.partial(project_kernel, head_dim, placed),
        in_specs=specs,
        out_specs=[pl.BlockSpec(memory_space=pltpu.VMEM)] * len(outs),
        out_shape=outs,
        scratch_shapes=[stripes(rows, width), pltpu.VMEM((rows, width), BF16)],
        compiler_params=pltpu.CompilerParams(vmem_limit_bytes=VMEM_LIMIT),
        cost_estimate=pl.CostEstimate(
            flops=6 * rows * width * width,
            transcendentals=0,
            bytes_accessed=12 * width * width + 16 * rows * width,
        ),
        name="project",
    )(*ins)


def finish_kernel(weight_ref, grad_ref, tokens_ref, middle_ref, norm_ref, sums_ref, wide_ref, out_ref, table_ref, natural_ref):
    step, count = pl.program_id(0), pl.num_programs(0)
    tile, width = tokens_ref.shape
    block = out_ref.shape[0] // RESIDUES

    @pl.when(step == 0)
    def _():
        table_ref[...] = jnp.zeros_like(table_ref)
        table_ref[4:8] = sums_ref[...]
        for i in range(wide_ref.shape[1] // width):
            table_ref[8 + i : 9 + i] = wide_ref[:, i * width : (i + 1) * width]

    grad = dot_nn(weight_ref[...], grad_ref[...]).T
    normed, inverse = standardize(tokens_ref[...].astype(F32))
    table_ref[0:1] += jnp.sum(grad * normed, axis=0, keepdims=True)
    table_ref[1:2] += jnp.sum(grad, axis=0, keepdims=True)
    ones = jnp.ones((16, tile), BF16)
    table_ref[2:3] += dot_nt(ones, grad_ref[:width])[0:1]
    table_ref[3:4] += dot_nt(ones, grad_ref[2 * width :])[0:1]
    total = middle_ref[...] + norm_back(grad, normed, inverse, norm_ref[0:1])
    many = tile // block
    half = RESIDUES // 2
    for i in range(many):
        place = step * many + i
        residue = 2 * lax.rem(place, half) + lax.div(place, half)
        natural = pl.ds(residue, block, stride=RESIDUES)
        write_stripes(natural_ref, natural, total[i * block : (i + 1) * block])

    @pl.when(step == count - 1)
    def _():
        out_ref[...] = read_stripes(natural_ref, slice(None))


def finish(weight, grad, tokens, middle, norms, sums, wide):
    rows, width = tokens.shape
    tile = min(rows, 512)
    narrow_spec = pl.BlockSpec((tile, width), lambda r: (r, 0))
    once = pl.BlockSpec(memory_space=pltpu.VMEM)
    return pl.pallas_call(
        finish_kernel,
        grid=(rows // tile,),
        in_specs=[
            once, pl.BlockSpec((grad.shape[0], tile), lambda r: (0, r)), narrow_spec, narrow_spec,
            once, once, once,
        ],
        out_specs=[once, once],
        out_shape=[
            jax.ShapeDtypeStruct((rows, width), F32),
            jax.ShapeDtypeStruct((16, width), F32),
        ],
        scratch_shapes=[stripes(rows, width)],
        compiler_params=pltpu.CompilerParams(vmem_limit_bytes=VMEM_LIMIT),
        cost_estimate=pl.CostEstimate(
            flops=6 * rows * width * width,
            transcendentals=0,
            bytes_accessed=6 * width * width + 16 * rows * width,
        ),
        name="finish",
    )(weight, grad, tokens, middle, norms, sums, wide)


def feed_forward_kernel(blocks, *refs):
    tokens_ref, attended_ref, natural_ref, small_ref, wide_ref, packed_ref = refs[:6]
    output_ref, grad_ref, mixed_ref, sums_ref, wide_sums_ref, grads_ref = refs[6:12]
    reduce_w, expand_w, output_w, natural_scr, active_scr, expanded_scr = refs[12:18]
    cotangent_scr, hidden_scr, low_scr, in_sems, out_sems = refs[18:]
    tile, width = tokens_ref.shape
    cut, depth = reduce_w.shape[1], output_w.shape[1]
    step, count = pl.program_id(0), pl.num_programs(0)
    block = natural_ref.shape[0] // RESIDUES
    halves, columns = packed_ref.shape[1], packed_ref.shape[3]
    local = blocks // halves * width // columns

    def arrival(index, y, at, size, target):
        return pltpu.make_async_copy(
            packed_ref.at[:, y, pl.ds(at, size)], target, in_sems.at[index]
        )

    def arrivals(first=0, last=None):
        found = []
        for y in range(halves):
            lanes = pl.ds(y * columns, columns)
            found.append((y, cut + local * depth, depth, output_w.at[:, :, lanes]))
        for y in range(halves):
            for i in range(local):
                at = (y * local + i) * columns
                target = expand_w.at[at // width, :, :, pl.ds(at % width, columns)]
                found.append((y, cut + i * depth, depth, target))
        for y in range(halves):
            found.append((y, 0, cut, reduce_w.at[:, :, pl.ds(y * columns, columns)]))
        indices = range(len(found))[first:last]
        return [arrival(i, *found[i]) for i in indices]

    def await_first(first, last):
        @pl.when(step == 0)
        def _():
            for copy in arrivals(first, last):
                copy.wait()

    @pl.when(step == 0)
    def _():
        for copy in arrivals():
            copy.start()
        fill_stripes(natural_scr, natural_ref[...].astype(F32))
        sums_ref[...] = jnp.zeros_like(sums_ref)
        wide_sums_ref[...] = jnp.zeros_like(wide_sums_ref)

    many, half = tile // block, RESIDUES // 2
    strided = []
    for i in range(many):
        place = step * many + i
        residue = 2 * lax.rem(place, half) + lax.div(place, half)
        strided.append(pl.ds(residue, block, stride=RESIDUES))
    here = pl.ds(pl.multiple_of(step * tile, tile), tile)
    bias_output, gain, shift, bias_reduce = (small_ref[i : i + 1] for i in range(4))
    upstream = jnp.concatenate([read_stripes(natural_scr, natural) for natural in strided], axis=0)
    cotangent = upstream.astype(BF16)
    cotangent_scr[here] = cotangent
    await_first(0, halves)
    project = output_w[...].reshape(width, width)
    middle = tokens_ref[...].astype(F32) + dot_tn(attended_ref[:, here], project) + bias_output
    normed, inverse = standardize(middle)
    hidden = (normed * gain + shift).astype(BF16)
    hidden_scr[here] = hidden
    output = middle + bias_reduce
    hidden_grad = jnp.zeros(middle.shape, F32)
    await_first(halves, halves + halves * local + halves)
    shrink_all = reduce_w[...].reshape(blocks * width, width)
    for i in range(blocks):
        span = slice(i * width, (i + 1) * width)
        grow = expand_w[i].reshape(width, width)
        shrink = shrink_all[span]
        active, slope = gelu_pair(dot_nn(hidden, grow) + wide_ref[:, span])
        active = active.astype(BF16)
        active_scr[i, here] = active
        output += dot_nn(active, shrink)
        expanded = (dot_nt(cotangent, shrink) * slope).astype(BF16)
        expanded_scr[i, here] = expanded
        wide_sums_ref[:, span] += jnp.sum(expanded.astype(F32), axis=0, keepdims=True)
        hidden_grad += dot_nt(expanded, grow)
    for i, natural in enumerate(strided):
        write_stripes(natural_scr, natural, output[i * block : (i + 1) * block])
    middle_grad = upstream + norm_back(hidden_grad, normed, inverse, gain)
    grad_ref[...] = middle_grad
    low = middle_grad.astype(BF16)
    low_scr[here] = low
    mixed_ref[...] = dot_nt(project, low).astype(BF16)
    for i, part in enumerate((hidden_grad * normed, hidden_grad, middle_grad, upstream)):
        sums_ref[i : i + 1] += jnp.sum(part, axis=0, keepdims=True)

    @pl.when(step == count - 1)
    def _():
        output_ref[...] = read_stripes(natural_scr, slice(None)).astype(BF16)
        copies = []

        def leave(source, target):
            copies.append(pltpu.make_async_copy(source, target, out_sems.at[len(copies)]))
            copies[-1].start()

        for i in range(blocks):
            product = dot_tn(active_scr[i], cotangent_scr[...]).astype(BF16)
            if cut <= width:
                shards = slice(i * width // cut, (i + 1) * width // cut)
                reduce_w[shards] = product.reshape(-1, cut, width)
                leave(reduce_w.at[shards], grads_ref.at[shards, pl.ds(0, cut)])
            else:
                span = pl.ds(i * width, width)
                reduce_w[0, span] = product
                leave(reduce_w.at[:, span], grads_ref.at[:, span])
        for i in range(blocks):
            product = dot_tn(hidden_scr[...], expanded_scr[i]).astype(BF16)
            expand_w[i] = product.reshape(-1, depth, width)
            leave(expand_w.at[i], grads_ref.at[:, pl.ds(cut + i * depth, depth)])
        product = dot_nn(attended_ref[...], low_scr[...]).astype(BF16)
        output_w[...] = product.reshape(-1, depth, width)
        leave(output_w, grads_ref.at[:, pl.ds(cut + blocks * depth, depth)])
        for copy in copies:
            copy.wait()


def feed_forward(tokens, attended, cotangent, small, wide, packed):
    rows, width = tokens.shape
    ff = wide.shape[1]
    blocks = ff // width
    shards, halves = packed.shape[:2]
    tile = min(rows, 256)
    narrow_spec = pl.BlockSpec((tile, width), lambda r: (r, 0))
    turned_spec = pl.BlockSpec((width, tile), lambda r: (0, r))
    once = pl.BlockSpec(memory_space=pltpu.VMEM)
    rows_scr = pltpu.VMEM((rows, width), BF16)
    wide_scr = pltpu.VMEM((blocks, rows, width), BF16)
    return pl.pallas_call(
        functools.partial(feed_forward_kernel, blocks),
        grid=(rows // tile,),
        in_specs=[narrow_spec, once, once, once, once, pl.BlockSpec(memory_space=pl.ANY)],
        out_specs=[once, narrow_spec, turned_spec, once, once, pl.BlockSpec(memory_space=pl.ANY)],
        out_shape=[
            jax.ShapeDtypeStruct((rows, width), BF16),
            jax.ShapeDtypeStruct((rows, width), F32),
            jax.ShapeDtypeStruct((width, rows), BF16),
            jax.ShapeDtypeStruct((4, width), F32),
            jax.ShapeDtypeStruct((1, ff), F32),
            jax.ShapeDtypeStruct((shards, (2 * ff + width) // shards, width), BF16),
        ],
        scratch_shapes=[
            pltpu.VMEM((shards, ff // shards, width), BF16),
            pltpu.VMEM((blocks, shards, width // shards, width), BF16),
            pltpu.VMEM((shards, width // shards, width), BF16),
            stripes(rows, width),
            wide_scr,
            wide_scr,
            rows_scr,
            rows_scr,
            rows_scr,
            pltpu.SemaphoreType.DMA((2 * halves + blocks * halves,)),
            pltpu.SemaphoreType.DMA((2 * blocks + 1,)),
        ],
        compiler_params=pltpu.CompilerParams(vmem_limit_bytes=VMEM_LIMIT),
        cost_estimate=pl.CostEstimate(
            flops=2 * rows * width * (6 * ff + 3 * width),
            transcendentals=2 * rows * ff,
            bytes_accessed=4 * packed.size + 20 * rows * width,
        ),
        name="feed_forward",
    )(tokens, attended, cotangent, small, wide, packed)


def level_table():
    head = np.arange(HEADS)[:, None]
    residue = 2 * np.arange(RESIDUES // 2)[None, :] + head % 2
    return sum((residue % 2**b == head % 2**b).astype(int) for b in range(1, BRANCHES))


def log_rows(times):
    parts = np.log2(times).astype(np.float32)
    rows = []
    for _ in range(3):
        low = parts.astype(ml_dtypes.bfloat16)
        rows.append(low)
        parts = parts - low.astype(np.float32)
    return np.stack(rows, axis=2).reshape(times.shape[0], -1, times.shape[2])


def attention_extras(rows, own_starts, far_starts, own_count, far_count, same):
    half, block = rows // 2, rows // RESIDUES
    levels = level_table()
    level = np.arange(1, BRANCHES)[None, :, None]
    lower = np.minimum(level, levels[:, None, :])

    def repeat(table, devices):
        return np.tile(np.repeat(table, block, axis=-1), devices)

    rank = np.arange(half)
    place = [(rank % block) * RESIDUES + 2 * (rank // block) + parity for parity in range(2)]

    def liveness(starts, count, allowed):
        live = [
            jnp.stack([(start + jnp.asarray(place[p]) < count) & allowed for p in range(2)])
            for start in starts
        ]
        return jnp.where(jnp.concatenate(live, axis=1), 0.0, NEGATIVE).astype(BF16)

    def built(times, live):
        count, _, keys = times.shape
        fixed = np.zeros((count, EXTRA, keys), ml_dtypes.bfloat16)
        fixed[:, TIMES:LIVE] = times
        fixed[:, FIXED : FIXED + 3] = 1
        row = np.arange(EXTRA)[None, :, None]
        return jnp.where(row == LIVE, live[:, None], jnp.asarray(fixed))

    own_live = liveness(own_starts, own_count, True)
    far_live = liveness(far_starts, far_count, same)
    by_head = np.arange(HEADS) % 2
    none = np.zeros((2, LIVE, half * len(own_starts)), ml_dtypes.bfloat16)

    def per_head(live):
        return jnp.where(by_head[:, None] == 1, live[1], live[0])

    query = np.zeros((HEADS, EXTRA, half), ml_dtypes.bfloat16)
    spread = np.repeat(levels, block, axis=1)
    for one in range(1, BRANCHES):
        query[:, 3 * (one - 1) : 3 * one] = (spread == one)[:, None, :]
    query[:, LIVE] = 1
    return {
        "plain": built(none, own_live),
        "same": built(repeat(log_rows(1.0 + lower), len(own_starts)), per_head(own_live)),
        "far": built(repeat(log_rows(lower), len(far_starts)), per_head(far_live)),
        "query": jnp.asarray(query),
        "self": jnp.asarray(np.log2(1.0 + spread).astype(np.float32))[:, None],
    }


def half_of(table, odd):
    half = table.shape[-1] // 2
    return jnp.where(odd, table[..., half:], table[..., :half])


def add_half(total, part, odd):
    part = part.astype(F32)
    both = jnp.concatenate([jnp.where(odd, 0.0, part), jnp.where(odd, part, 0.0)], axis=-1)
    return total.astype(F32) + both


def swap_pairs(value):
    return lax.ppermute(value, "branch", [(0, 1), (1, 0)])


def gather_columns(shard, branches):
    if branches != 2:
        return lax.all_gather(shard, "branch", axis=shard.ndim - 1, tiled=True)
    other = swap_pairs(shard)
    first = lax.axis_index("branch") == 0
    return jnp.concatenate(
        [jnp.where(first, shard, other), jnp.where(first, other, shard)], axis=-1
    )


def scatter_columns(total, branches):
    if branches != 2:
        return lax.psum_scatter(
            total, "branch", scatter_dimension=total.ndim - 1, tiled=True
        ).astype(F32)
    half = total.shape[-1] // 2
    at = lax.axis_index("branch")
    keep = lax.dynamic_slice_in_dim(total, at * half, half, total.ndim - 1)
    away = lax.dynamic_slice_in_dim(total, (1 - at) * half, half, total.ndim - 1)
    return keep.astype(F32) + swap_pairs(away).astype(F32)


def weight_sum(partial, branches):
    low = lax.psum_scatter(partial, "slides", scatter_dimension=0, tiled=True)
    return scatter_columns(low, branches)


def pack_rows(reduce_part, expand_part, output_part):
    width = output_part.shape[-1]
    blocks = expand_part.shape[-1] // width
    return jnp.concatenate(
        [reduce_part]
        + [expand_part[..., i * width : (i + 1) * width] for i in range(blocks)]
        + [output_part],
        axis=-2,
    )


def unpack_rows(packed, width, ff):
    blocks = ff // width
    depth = packed.shape[-2] // (2 * blocks + 1)
    cut = blocks * depth
    expand = [packed[..., cut + i * depth : cut + (i + 1) * depth, :] for i in range(blocks)]
    return packed[..., :cut, :], jnp.concatenate(expand, axis=-1), packed[..., 2 * cut :, :]


def join_columns(own, other):
    first = lax.axis_index("branch") == 0
    return jnp.concatenate(
        [jnp.where(first, own, other), jnp.where(first, other, own)], axis=-1
    )


def pack_kernel(reduce_ref, expand_ref, output_ref, packed_ref):
    cut, width = reduce_ref.shape
    depth = output_ref.shape[0]
    packed_ref[:cut] = reduce_ref[...]
    blocks = expand_ref.shape[1] // width
    for i in range(blocks):
        packed_ref[cut + i * depth : cut + (i + 1) * depth] = expand_ref[:, i * width : (i + 1) * width]
    packed_ref[cut + blocks * depth :] = output_ref[...]


def join_kernel(cut, depth, at_ref, own_ref, other_ref, joined_ref):
    columns = own_ref.shape[1]
    blocks = (own_ref.shape[0] - cut) // depth - 1

    def put(halves):
        for y, half in enumerate(halves):
            lanes = slice(y * columns, (y + 1) * columns)
            joined_ref[:cut, lanes] = half[:cut]
            joined_ref[cut + blocks * depth :, lanes] = half[cut + blocks * depth :]
            for i in range(blocks):
                row, lane = divmod((y * blocks + i) * columns, 2 * columns)
                target = cut + row * depth
                source = cut + i * depth
                joined_ref[target : target + depth, lane : lane + columns] = half[
                    source : source + depth
                ]

    @pl.when(at_ref[0] == 0)
    def _():
        put((own_ref, other_ref))

    @pl.when(at_ref[0] != 0)
    def _():
        put((other_ref, own_ref))


def gather_packed(reduce_weight, expand_weight, output_weight, first_transfers, branches):
    size = lax.axis_size("slides")
    depth, columns = output_weight.shape
    aligned = branches == 2 and depth % 16 == 0 and columns % LANES == 0
    if aligned:
        rows = reduce_weight.shape[0] + depth + expand_weight.size // columns
        shard = pl.pallas_call(
            pack_kernel,
            out_shape=jax.ShapeDtypeStruct((rows, columns), BF16),
            name="pack",
        )(reduce_weight, expand_weight, output_weight)
    else:
        shard = pack_rows(reduce_weight, expand_weight, output_weight)
    if aligned:
        at = lax.axis_index("branch").reshape(1)
        other, first_transfers = lax.optimization_barrier((swap_pairs(shard), first_transfers))
        shard = pl.pallas_call(
            functools.partial(join_kernel, reduce_weight.shape[0], depth),
            in_specs=[pl.BlockSpec(memory_space=pltpu.SMEM)]
            + [pl.BlockSpec(memory_space=pltpu.VMEM)] * 2,
            out_shape=jax.ShapeDtypeStruct((rows, 2 * columns), BF16),
            name="join",
        )(at, shard, other)
        return lax.all_gather(shard, "slides", axis=0, tiled=False)[:, None], first_transfers
    packed = lax.all_gather(shard, ("slides", "branch"), axis=0, tiled=False)
    packed = packed.reshape(size, branches, *shard.shape)
    ff = size * reduce_weight.shape[0]
    parts = unpack_rows(packed, columns, ff // branches)
    parts = [m.transpose(0, 2, 1, 3).reshape(1, -1, branches * m.shape[-1]) for m in parts]
    return pack_rows(*parts)[None], first_transfers


def gather_vectors(vectors, branches, rows_of):
    cuts = np.cumsum([0] + [m.shape[0] for m in vectors])
    if branches != 2:
        table = lax.all_gather(jnp.concatenate(vectors), "branch", axis=0, tiled=False)
        return [table[:, a:b].reshape(1, -1) for a, b in zip(cuts, cuts[1:])]
    own, other = rows_of
    columns = own.shape[1]
    first = lax.axis_index("branch") == 0
    halves = [jnp.where(first, own, other), jnp.where(first, other, own)]
    at = cuts // columns
    return [
        jnp.concatenate(
            [half[row : row + 1] for half in halves for row in range(at[i], at[i + 1])], axis=1
        )
        for i in range(len(vectors))
    ]


def sum_packed(packed, width, ff):
    size = lax.axis_size("slides")
    if packed.shape[0] != size:
        parts = unpack_rows(packed, width, ff)
        packed = pack_rows(*(m.reshape(size, -1, m.shape[-1]) for m in parts))
    rows = packed.shape[1]
    return lax.psum_scatter(
        packed.reshape(size * rows, width), "slides", scatter_dimension=0, tiled=True
    )


def branch_half(low, index, width, ff):
    reduce_part, expand_part, output_part = unpack_rows(low, width, ff)
    columns = width // 2
    grown = lax.dynamic_slice_in_dim(expand_part, index * (ff // 2), ff // 2, 1)
    pieces = [
        lax.dynamic_slice_in_dim(part, index * columns, columns, 1)
        for part in (reduce_part, output_part)
    ]
    pieces += [grown[:, i : i + columns] for i in range(0, ff // 2, columns)]
    return jnp.concatenate(pieces, axis=0)


def unpack_half(total, depth, cut):
    tail = [total[row : row + depth] for row in range(cut + depth, total.shape[0], depth)]
    return total[:cut], jnp.concatenate(tail, axis=1), total[cut : cut + depth]


def flip(value, bit):
    return lax.ppermute(value, "slides", [(i, i ^ bit) for i in range(lax.axis_size("slides"))])


def shifted(value, step):
    size = lax.axis_size("slides")
    return lax.ppermute(value, "slides", [(i, (i + 4 * step) % size) for i in range(size)])


def gather_pieces(held, later):
    half = held[0].shape[1] // 2 // LANES * LANES
    first = jnp.stack([m[:, :half] for m in held])
    second = jnp.stack([m[:, half:] for m in held])
    first, second = jnp.stack([first, flip(first, 2)]), jnp.stack([second, swap_pairs(second)])
    first, second, later = lax.optimization_barrier((first, second, later))
    other = swap_pairs(later[0])
    first, second = jnp.stack([first, swap_pairs(first)]), jnp.stack([second, flip(second, 2)])
    pieces = (first, second, flip(first, 1), flip(second, 1))
    slide = lax.axis_index("slides")
    spot = jnp.stack(
        [
            lax.div(slide, 4),
            lax.rem(lax.div(slide, 2), 2),
            lax.rem(slide, 2),
            lax.axis_index("branch"),
        ]
    )
    return pieces, spot.astype(jnp.int32), other, later


def pick(table, index, axis):
    return lax.dynamic_index_in_dim(table, index, axis, keepdims=False)


def split_kernel(core_ref, left_ref, right_ref, keep_ref, send_ref, product_ref):
    product_ref[...] = dot_nt(left_ref[...], right_ref[...]).astype(BF16).reshape(product_ref.shape)
    core = core_ref[0]
    for pair in range(product_ref.shape[0] // 2):
        at = (0, pair // 2, pair % 2)
        keep_ref[at] = product_ref[2 * pair + core]
        send_ref[at] = product_ref[2 * pair + 1 - core]


def split_product(left, right, core):
    size = lax.axis_size("slides")
    features, rows = left.shape
    depth, columns = features // size, right.shape[0] // 2
    step = columns
    wide = columns // step
    block = pl.BlockSpec((1, size // 4, 2, depth, step), lambda j: (j // wide, 0, 0, 0, j % wide))
    return pl.pallas_call(
        split_kernel,
        grid=(2 * wide,),
        in_specs=[
            pl.BlockSpec(memory_space=pltpu.SMEM),
            whole_spec(left.shape),
            pl.BlockSpec((step, rows), lambda j: (j, 0)),
        ],
        out_specs=[block, block],
        out_shape=[jax.ShapeDtypeStruct((2, size // 4, 2, depth, columns), BF16)] * 2,
        scratch_shapes=[pltpu.VMEM((size, depth, step), BF16)],
        compiler_params=pltpu.CompilerParams(vmem_limit_bytes=VMEM_LIMIT),
        cost_estimate=pl.CostEstimate(
            flops=4 * rows * features * columns,
            transcendentals=0,
            bytes_accessed=2 * (left.size + right.size + 2 * features * columns),
        ),
        name="joint_gradient",
    )(core.reshape(1), left, right)


def deal_kernel(spans, at_ref, *refs):
    tables, outs = refs[: -len(spans)], refs[-len(spans) :]
    total = sum((table[...] for table in tables[1:]), tables[0][...])
    width = total.shape[1]

    def put(index):
        for (row, count), out in zip(spans, outs):
            if count == 1:
                out[...] = total[row, index * width // 2 : (index + 1) * width // 2]
            else:
                for i in range(count // 2):
                    at = row + index * count // 2 + i
                    out[i * width : (i + 1) * width] = total[at]

    @pl.when(at_ref[0] == 0)
    def _():
        put(0)

    @pl.when(at_ref[0] != 0)
    def _():
        put(1)


def deal(tables, spans, at):
    width = tables[0].shape[1]
    return pl.pallas_call(
        functools.partial(deal_kernel, spans),
        in_specs=[pl.BlockSpec(memory_space=pltpu.SMEM)]
        + [pl.BlockSpec(memory_space=pltpu.VMEM)] * len(tables),
        out_shape=[jax.ShapeDtypeStruct((count * width // 2,), F32) for _, count in spans],
        name="deal",
    )(at.reshape(1), *tables)


def sum_tree(kept, sent, table_of, gate, low_sums, near, outer, at):
    rounds = kept.shape[1]

    def both(one, two):
        return (one.astype(F32) + two.astype(F32)).astype(BF16)

    total = both(kept, flip(sent, 1))
    low, high = total[:, : rounds // 2], total[:, rounds // 2 :]
    away, off, gate = lax.optimization_barrier(
        (pick(low, 1 - at, 0), pick(high, 1 - near, 2), gate)
    )
    away, off = swap_pairs(away), flip(off, 2)
    table = table_of(gate)
    low, high = both(pick(low, at, 0), away), both(pick(high, near, 2), off)
    away, off, table = lax.optimization_barrier(
        (pick(low, 1 - near, 1), pick(high, 1 - at, 0), table)
    )
    low, high = both(pick(low, near, 1), flip(away, 2)), both(pick(high, at, 0), swap_pairs(off))
    table += flip(table, 1)
    table += swap_pairs(table)
    joined = jnp.concatenate([low, high], axis=0)
    total = pick(joined, outer, 0).astype(F32)
    sends = [pick(joined, lax.rem(outer + step, rounds), 0) for step in range(1, rounds)]
    sends, table = lax.optimization_barrier((sends, table))
    parts = [shifted(part, step + 1) for step, part in enumerate(sends)]
    table += flip(table, 2)
    parts[0], table, low_sums = lax.optimization_barrier((parts[0], table, low_sums))
    for part in parts:
        total += part.astype(F32)
    return total, [table] + [shifted(table, step) for step in range(1, rounds)], low_sums


def on_device(
    tokens,
    cotangent,
    first_gain,
    first_shift,
    joint_weight,
    joint_bias,
    output_weight,
    output_bias,
    second_gain,
    second_shift,
    expand_weight,
    expand_bias,
    reduce_weight,
    reduce_bias,
    block_owner,
    tile_count,
):
    rows, width = tokens.shape
    branches = lax.axis_size("branch")
    head_dim = width // HEADS
    block = rows // RESIDUES
    mates = SEG_BASE // rows
    at = lax.axis_index("branch")
    segment = lax.div(at, mates)
    within = at - segment * mates
    odd = ((np.arange(width) // head_dim) % 2 == 1)[:, None]

    parameters = (
        first_gain, first_shift, joint_bias, output_bias,
        second_gain, second_shift, expand_bias, reduce_bias,
    )
    depth = joint_weight.shape[0]
    slides = lax.axis_size("slides")
    trees = branches == 2 and slides % 8 == 0 and depth % 16 == 0
    held = [joint_weight]
    if trees:
        held += [shifted(joint_weight, step) for step in range(1, slides // 4)]
    packed_weights, held = gather_packed(
        reduce_weight, expand_weight, output_weight, held, branches
    )
    if trees:
        small = jnp.concatenate([m.reshape(-1, width // 2) for m in parameters], axis=0)
        pieces, spot, other, (small, block_owner, tile_count) = gather_pieces(
            held, (small, block_owner, tile_count)
        )
        vectors = gather_vectors(parameters, branches, (small, other))
        joint_full, placed = None, joint_weight.shape
    else:
        joint_full = lax.all_gather(
            gather_columns(joint_weight, branches), "slides", axis=0, tiled=True
        )
        vectors = gather_vectors(parameters, branches, None)
        pieces, spot, placed = (), None, None
    bias_joint = jnp.pad(vectors[2], ((0, 15), (0, 0)))
    gain_one, shift_one, _, bias_output, gain_two, shift_two, bias_expand, bias_reduce = (
        m.astype(F32) for m in vectors
    )
    norms = jnp.concatenate([gain_one, shift_one], axis=0)

    owners = block_owner.reshape(-1)
    counts = tile_count.reshape(-1)
    own_count = jnp.where(segment == 0, counts[0], counts[1])
    far_count = jnp.where(segment == 0, counts[1], counts[0])
    own_starts = [lax.rem(within + d, mates) * rows for d in range(mates)]
    far_starts = [d * rows for d in range(mates)]
    extras = attention_extras(
        rows, own_starts, far_starts, own_count, far_count, owners[0] == owners[1]
    )

    joint_full, tokens_low, hidden_turned, q, k, v, k_half, v_half = project(
        tokens, norms, bias_joint, joint_full, pieces, spot, placed, head_dim
    )
    if mates == 1 and branches == 2:
        k_own, v_own = k[None], v[None]
        k_far, v_far = swap_pairs(k_half)[None], swap_pairs(v_half)[None]
    else:
        own_at = [segment * mates + lax.rem(within + d, mates) for d in range(mates)]
        far_at = [(1 - segment) * mates + d for d in range(mates)]

        def chosen(table, indices):
            whole = lax.all_gather(table, "branch", axis=0)
            return jnp.stack([lax.dynamic_index_in_dim(whole, d, 0, False) for d in indices])

        k_own, v_own = chosen(k, own_at), chosen(v, own_at)
        k_far, v_far = chosen(k_half, far_at), chosen(v_half, far_at)
    attended, part, total_log = attend_own(q, k_own, v_own, extras)
    attended, total_log = attend_far(q, k_far, v_far, extras, attended, part, total_log)
    ff = bias_expand.shape[1]
    small = jnp.concatenate([bias_output, gain_two, shift_two, bias_reduce], axis=0)
    output, middle_grad, mixed_grad, sums, wide_sums, packed_grads = feed_forward(
        tokens_low, attended, cotangent, small, bias_expand, packed_weights
    )
    mixed_grad, packed_grads = lax.optimization_barrier((mixed_grad, packed_grads))
    low_sums = sum_packed(packed_grads, width, ff)

    part, dk_far, dv_far = attend_far_back(
        q, k_far, v_far, extras, attended, mixed_grad, total_log
    )
    dq, dk_own, dv_own = attend_own_back(
        q, k_own, v_own, extras, attended, mixed_grad, total_log, part
    )
    if mates == 1 and branches == 2:
        key_sum = add_half(dk_own[0], swap_pairs(dk_far[0]), odd)
        value_sum = add_half(dv_own[0], swap_pairs(dv_far[0]), odd)
    else:

        def spread(own, far):
            canvas = jnp.zeros((branches, width, rows), BF16)
            for d, index in enumerate(own_at):
                canvas = lax.dynamic_update_index_in_dim(canvas, own[d], index, 0)
            for d, index in enumerate(far_at):
                full = add_half(jnp.zeros((width, rows), F32), far[d], odd).astype(BF16)
                canvas = lax.dynamic_update_index_in_dim(canvas, full, index, 0)
            return lax.psum_scatter(canvas, "branch", scatter_dimension=0, tiled=True)[0]

        key_sum = spread(dk_own, dk_far)
        value_sum = spread(dv_own, dv_far)
    value_low = value_sum.astype(BF16)
    joint_grad = jnp.concatenate([dq, key_sum.astype(BF16), value_low], axis=0)
    found = []

    def table_of(grad):
        found.extend(finish(joint_full, joint_grad, tokens_low, grad, norms, sums, wide_sums))
        return found[1]

    sizes = (1, 1, 2, 1, 1, 1, 1, ff // width)
    starts = np.cumsum((0,) + sizes)
    if trees:
        slide = lax.axis_index("slides")
        kept, sent = split_product(hidden_turned, joint_grad, lax.rem(slide, 2))
        joint_sum, tables, low_sums = sum_tree(
            kept, sent, table_of, middle_grad, low_sums,
            lax.rem(lax.div(slide, 2), 2), lax.div(slide, 4), at,
        )
        arrived = swap_pairs(branch_half(low_sums, 1 - at, width, ff))
        halves = branch_half(low_sums, at, width, ff).astype(F32) + arrived.astype(F32)
        reduce_sum, expand_sum, output_sum = unpack_half(
            halves, output_weight.shape[0], reduce_weight.shape[0]
        )
        mine = deal(tables, tuple((int(a), n) for a, n in zip(starts, sizes)), at)
    else:
        joint_sum = weight_sum(dot_nt(hidden_turned, joint_grad).astype(BF16), branches)
        table = lax.psum(table_of(middle_grad), ("slides", "branch"))
        reduce_sum, expand_sum, output_sum = (
            scatter_columns(part, branches) for part in unpack_rows(low_sums, width, ff)
        )
        mine = []
        for row, count in zip(starts, sizes):
            share = count * width // branches
            whole = table[row : row + count].reshape(-1)
            mine.append(lax.dynamic_slice_in_dim(whole, at * share, share))
    tokens_grad = found[0]
    first_gain_sum, first_shift_sum, joint_bias_sum, second_gain_sum = mine[:4]
    second_shift_sum, output_bias_sum, reduce_bias_sum, expand_bias_sum = mine[4:]
    return (
        output,
        tokens_grad,
        first_gain_sum,
        first_shift_sum,
        joint_sum,
        joint_bias_sum,
        output_sum,
        output_bias_sum,
        second_gain_sum,
        second_shift_sum,
        expand_sum,
        expand_bias_sum,
        reduce_sum,
        reduce_bias_sum,
    )


def solution(mesh):
    rows = P(("slides", "branch"), None)
    matrix = P("slides", "branch")
    vector = P("branch")
    placed = (
        rows, rows, vector, vector, matrix, vector, matrix, vector,
        vector, vector, matrix, vector, matrix, vector, P("slides", None), P("slides", None),
    )
    given = (
        rows, rows, vector, vector, matrix, vector, matrix, vector,
        vector, vector, matrix, vector, matrix, vector,
    )
    return jax.shard_map(on_device, mesh=mesh, in_specs=placed, out_specs=given, check_vma=False)
```

```python
import functools
import math

import jax
import jax.numpy as jnp
import ml_dtypes
import numpy as np
from jax import lax
from jax.experimental import pallas as pl
from jax.experimental.pallas import tpu as pltpu
from jax.sharding import PartitionSpec as P

HEADS = 16
SEG_BASE = 1024
BRANCHES = 5
RESIDUES = 2 ** (BRANCHES - 1)
EPSILON = 1e-05
NEGATIVE = -1e30
LANES = 128
EXTRA = 32
TIMES, LIVE, FIXED = 0, 12, 13
UNROLL = 4
OWN_UNROLL = 2
PIECE = 512
VMEM_LIMIT = 60 * 1024 * 1024

BF16 = jnp.bfloat16
F32 = jnp.float32


def standardize(values):
    centred = values - jnp.mean(values, axis=-1, keepdims=True)
    inverse = lax.rsqrt(jnp.mean(centred * centred, axis=-1, keepdims=True) + EPSILON)
    return (centred * inverse, inverse)


def norm_back(upstream, normed, inverse, gain):
    scaled = upstream * gain
    return inverse * (
        scaled
        - jnp.mean(scaled, axis=-1, keepdims=True)
        - normed * jnp.mean(scaled * normed, axis=-1, keepdims=True)
    )


def gelu_pair(values):
    cumulative = 0.5 * (1.0 + lax.erf(values * (1.0 / math.sqrt(2.0))))
    density = jnp.exp(-0.5 * values * values) * (1.0 / math.sqrt(2.0 * math.pi))
    return values * cumulative, cumulative + values * density


def dot_nn(left, right):
    return lax.dot_general(left, right, (((1,), (0,)), ((), ())), preferred_element_type=F32)


def dot_nt(left, right):
    return lax.dot_general(left, right, (((1,), (1,)), ((), ())), preferred_element_type=F32)


def dot_tn(left, right):
    return lax.dot_general(left, right, (((0,), (0,)), ((), ())), preferred_element_type=F32)


def thirds(value):
    first = value.astype(BF16)
    rest = value - first.astype(F32)
    second = rest.astype(BF16)
    return first, second, (rest - second.astype(F32)).astype(BF16)


class HeadView:
    def __init__(self, head, far, refs, head_dim, other_segment, own=True):
        half = refs["q"].shape[-1] // 2
        same = lax.rem(head, 2)
        same = same if far else 1 - same
        self.half = half
        self.rows = pl.ds(pl.multiple_of(head * head_dim, 16), head_dim)
        self.same = pl.ds(pl.multiple_of(same * half, LANES), half)
        self.other = pl.ds(pl.multiple_of((1 - same) * half, LANES), half)
        self.devices = refs["k"].shape[0] if own else 0
        self.head = head
        self.far = far
        self.own = own
        self.other_segment = other_segment
        extras = []
        if own:
            extras += [
                refs["same"][head] if far else refs["plain"][same],
                refs["plain"][1 - same],
            ]
        if other_segment:
            extras.append(refs["far"][head])
        self.extra = jnp.concatenate(extras, axis=1)

    def gathered(self, own_ref, far_ref):
        found = [own_ref[d, self.rows, self.same] for d in range(self.devices)]
        found += [own_ref[d, self.rows, self.other] for d in range(self.devices)]
        if self.other_segment:
            found += [far_ref[d, self.rows, :] for d in range(far_ref.shape[0])]
        return jnp.concatenate(found, axis=1)


def with_self(scores, own, first):
    half = scores.shape[1]
    if first >= half:
        return scores
    eye = lax.broadcasted_iota(jnp.int32, (LANES, LANES), 0) == lax.broadcasted_iota(
        jnp.int32, (LANES, LANES), 1
    )
    bands = []
    for row in range(0, min(scores.shape[0], half - first), LANES):
        at = first + row
        band = scores[row : row + LANES]
        here = jnp.where(eye, own[:, at : at + LANES], band[:, at : at + LANES])
        sides = [band[:, :at]] if at else []
        sides.append(here)
        if at + LANES < half:
            sides.append(band[:, at + LANES :])
        bands.append(jnp.concatenate(sides, axis=1))
    if half - first < scores.shape[0]:
        bands.append(scores[half - first :])
    return jnp.concatenate(bands, axis=0)


def head_scores(view, refs, keys, head_dim, constant):
    scale = head_dim ** (-0.5) * math.log2(math.e)
    scaled = refs["q"][view.rows, view.same].astype(F32) * scale
    high = scaled.astype(BF16)
    low = (scaled - high.astype(F32)).astype(BF16)
    half = view.half
    if view.far:
        extra = refs["query"][view.head]
        own = refs["self"][view.head]
    else:
        row = lax.broadcasted_iota(jnp.int32, (EXTRA, half), 0)
        extra = jnp.where(row == LIVE, 1.0, 0.0).astype(BF16)
        own = jnp.zeros((1, half), F32)
    if view.own:
        own = own + jnp.sum(scaled * keys[:, :half].astype(F32), axis=0, keepdims=True)
    if constant is not None:
        row = lax.broadcasted_iota(jnp.int32, (EXTRA, half), 0)
        filled = extra.astype(F32)
        for i, part in enumerate(thirds(constant)):
            filled = jnp.where(row == FIXED + i, part.astype(F32), filled)
        extra = filled.astype(BF16)
        own = own + constant
    left = jnp.concatenate([keys, keys, view.extra], axis=0)
    right = jnp.concatenate([high, low, extra], axis=0)

    def scores(at):
        product = dot_tn(left[:, at : at + PIECE], right)
        return with_self(product, own, at) if view.own else product

    return scores


def softmax_parts(parts, values, known):
    highest = functools.reduce(
        jnp.maximum, [jnp.max(part, axis=0, keepdims=True) for part in parts]
    )
    if known is not None:
        highest = jnp.maximum(highest, known[0])
    mixed, total = 0.0, 0.0
    at = 0
    for part in parts:
        weights = jnp.exp2(part - highest)
        total += jnp.sum(weights, axis=0, keepdims=True)
        mixed += dot_nn(values[:, at : at + part.shape[0]], weights.astype(BF16))
        at += part.shape[0]
    if known is not None:
        share = jnp.exp2(known[0] - highest)
        total += share
        mixed += known[1] * share
    return mixed * (1.0 / total), highest + jnp.log2(total)


def own_kernel(head_dim, names, count, *refs):
    o_ref, part_ref, t_ref = refs[len(names) :]
    refs = dict(zip(names, refs))

    @pl.loop(0, count, unroll=UNROLL)
    def _(head):
        for far in (True, False):
            view = HeadView(head, far, refs, head_dim, False)
            keys = view.gathered(refs["k"], None)
            values = view.gathered(refs["v"], None)
            scores = head_scores(view, refs, keys, head_dim, None)
            parts = [scores(at) for at in range(0, keys.shape[1], PIECE)]
            mixed, total_log = softmax_parts(parts, values, None)
            if far:
                part_ref[view.rows, :] = mixed
            else:
                o_ref[view.rows, view.same] = mixed.astype(BF16)
            t_ref[head, :, view.same] = total_log


def far_kernel(head_dim, names, count, *refs):
    o_ref, t_ref = refs[len(names) :]
    refs = dict(zip(names, refs))
    o_ref[...] = refs["o"][...]
    t_ref[...] = refs["t"][...]

    @pl.loop(0, count, unroll=UNROLL)
    def _(head):
        view = HeadView(head, True, refs, head_dim, True, own=False)
        keys = view.gathered(None, refs["kx"])
        values = view.gathered(None, refs["vx"])
        scores = head_scores(view, refs, keys, head_dim, None)
        parts = [scores(at) for at in range(0, keys.shape[1], PIECE)]
        known = (refs["t"][head, :, view.same], refs["part"][view.rows, :])
        mixed, total_log = softmax_parts(parts, values, known)
        o_ref[view.rows, view.same] = mixed.astype(BF16)
        t_ref[head, :, view.same] = total_log


def head_gradients(view, refs, head_dim):
    natural = head_dim ** (-0.5)
    keys = view.gathered(refs.get("k"), refs.get("kx"))
    values = view.gathered(refs.get("v"), refs.get("vx"))
    queries = refs["q"][view.rows, view.same]
    upstream = refs["g"][view.rows, view.same]
    mixed = refs["o"][view.rows, view.same]
    scores = head_scores(view, refs, keys, head_dim, -refs["t"][view.head, :, view.same])
    inner = -jnp.sum(upstream.astype(F32) * mixed.astype(F32), axis=0, keepdims=True)
    row = lax.broadcasted_iota(jnp.int32, (16, view.half), 0)
    filled = jnp.zeros((16, view.half), F32)
    for i, part in enumerate(thirds(inner)):
        filled = jnp.where(row == i, part.astype(F32), filled)
    row = lax.broadcasted_iota(jnp.int32, (16, keys.shape[1]), 0)
    ones = jnp.where(row < 3, 1.0, 0.0).astype(BF16)
    left = jnp.concatenate([values, ones], axis=0)
    right = jnp.concatenate([upstream, filled.astype(BF16)], axis=0)
    query_grad, key_parts, value_parts = 0.0, [], []
    for at in range(0, keys.shape[1], PIECE):
        span = slice(at, at + PIECE)
        part = scores(at)
        prob_grad = dot_tn(left[:, span], right)
        probs = jnp.exp2(part)
        score_grad = (probs * prob_grad).astype(BF16)
        value_parts.append(dot_nt(upstream, probs.astype(BF16)))
        key_parts.append(dot_nt(queries, score_grad) * natural)
        query_grad += dot_nn(keys[:, span], score_grad)
    return query_grad, jnp.concatenate(key_parts, axis=1), jnp.concatenate(value_parts, axis=1)


def far_back_kernel(head_dim, names, count, *refs):
    part_ref, dkx_ref, dvx_ref = refs[len(names) :]
    refs = dict(zip(names, refs))

    @pl.loop(0, count, unroll=UNROLL)
    def _(head):
        view = HeadView(head, True, refs, head_dim, True, own=False)
        query_grad, key_grad, value_grad = head_gradients(view, refs, head_dim)
        part_ref[view.rows, :] = query_grad
        for d in range(dkx_ref.shape[0]):
            lanes = slice(d * view.half, (d + 1) * view.half)
            dkx_ref[d, view.rows, :] = key_grad[:, lanes].astype(BF16)
            dvx_ref[d, view.rows, :] = value_grad[:, lanes].astype(BF16)


def own_back_kernel(head_dim, names, count, *refs):
    dq_ref, dk_ref, dv_ref = refs[len(names) :]
    refs = dict(zip(names, refs))
    natural = head_dim ** (-0.5)

    @pl.loop(0, count, unroll=OWN_UNROLL)
    def _(head):
        totals = None
        for far in (False, True):
            view = HeadView(head, far, refs, head_dim, False)
            query_grad, *grads = head_gradients(view, refs, head_dim)
            if far:
                query_grad += refs["part"][view.rows, :]
            dq_ref[view.rows, view.same] = (query_grad * natural).astype(BF16)
            if far:
                grads = [one + two for one, two in zip(grads, totals)]
            cut = view.devices * view.half
            totals = [jnp.concatenate([m[:, cut:], m[:, :cut]], axis=1) for m in grads]
        for total, ref in zip(grads, (dk_ref, dv_ref)):
            for d in range(view.devices):
                for lanes, at in ((view.same, d), (view.other, view.devices + d)):
                    part = total[:, at * view.half : (at + 1) * view.half]
                    ref[d, view.rows, lanes] = part.astype(BF16)


def whole_spec(shape):
    zeros = (0,) * len(shape)
    return pl.BlockSpec(shape, lambda *_: zeros)


def like(*members):
    return [jax.ShapeDtypeStruct(m.shape, m.dtype) for m in members]


def attention_call(kernel, name, ins, outs, pairs, matmuls):
    width, rows = ins["q"].shape
    return pl.pallas_call(
        functools.partial(kernel, width // HEADS, tuple(ins), HEADS),
        in_specs=[pl.BlockSpec(memory_space=pltpu.VMEM)] * len(ins),
        out_specs=[pl.BlockSpec(memory_space=pltpu.VMEM)] * len(outs),
        out_shape=outs,
        compiler_params=pltpu.CompilerParams(vmem_limit_bytes=VMEM_LIMIT),
        cost_estimate=pl.CostEstimate(
            flops=2 * matmuls * HEADS * pairs * LANES,
            transcendentals=HEADS * pairs,
            bytes_accessed=8 * rows * width,
        ),
        name=name,
    )(*ins.values())


def attend_own(q, k, v, extras):
    width, rows = q.shape
    ins = dict(q=q, k=k, v=v, **{n: extras[n] for n in ("plain", "same", "query", "self")})
    outs = like(q) + [
        jax.ShapeDtypeStruct((width, rows // 2), F32),
        jax.ShapeDtypeStruct((HEADS, 1, rows), F32),
    ]
    return attention_call(own_kernel, "attend_own", ins, outs, rows * rows * k.shape[0], 2)


def attend_far(q, kx, vx, extras, o, part, t):
    rows = q.shape[1]
    ins = dict(q=q, kx=kx, vx=vx, o=o, part=part, t=t)
    ins |= {n: extras[n] for n in ("far", "query", "self")}
    return attention_call(far_kernel, "attend_far", ins, like(o, t), rows * rows * kx.shape[0] // 4, 2)


def attend_far_back(q, kx, vx, extras, o, g, t):
    width, rows = q.shape
    ins = dict(q=q, kx=kx, vx=vx, o=o, g=g, t=t)
    ins |= {n: extras[n] for n in ("far", "query", "self")}
    outs = [jax.ShapeDtypeStruct((width, rows // 2), F32)] + like(kx, vx)
    pairs = rows * rows * kx.shape[0] // 4
    return attention_call(far_back_kernel, "attend_far_back", ins, outs, pairs, 5)


def attend_own_back(q, k, v, extras, o, g, t, part):
    rows = q.shape[1]
    ins = dict(q=q, k=k, v=v, o=o, g=g, t=t, part=part)
    ins |= {n: extras[n] for n in ("plain", "same", "query", "self")}
    pairs = rows * rows * k.shape[0]
    return attention_call(own_back_kernel, "attend_own_back", ins, like(q, k, v), pairs, 5)


def residue_rows(block):
    order = [2 * i + parity for parity in range(2) for i in range(RESIDUES // 2)]
    return [
        (i * block, pl.ds(residue, block, stride=RESIDUES)) for i, residue in enumerate(order)
    ]


def stripes(rows, width):
    return pltpu.VMEM((width // LANES, rows, LANES), F32)


def fill_stripes(ref, value):
    for c in range(ref.shape[0]):
        ref[c] = value[:, c * LANES : (c + 1) * LANES]


def read_stripes(ref, rows):
    return jnp.concatenate([ref[c, rows, :] for c in range(ref.shape[0])], axis=1)


def write_stripes(ref, rows, value):
    for c in range(ref.shape[0]):
        ref[c, rows, :] = value[:, c * LANES : (c + 1) * LANES]


def place_pieces(spot, pieces, full, depth, columns):
    outer, near, core, branch = spot[0], spot[1], spot[2], spot[3]
    for index, piece in enumerate(pieces):
        group, other_core = index % 2, index // 2
        rounds, width = piece.shape[2], piece.shape[4]
        for one in range(2):
            for two in range(2):
                far_branch, far_near = (one, two) if group == 0 else (two, one)
                offset = 0 if group == 0 else columns - width
                column = jnp.bitwise_xor(branch, far_branch) * columns + offset
                lanes = pl.ds(pl.multiple_of(column, LANES), width)
                for step in range(rounds):
                    shard = (
                        lax.rem(outer - step + rounds, rounds) * 4
                        + jnp.bitwise_xor(near, far_near) * 2
                        + jnp.bitwise_xor(core, other_core)
                    )
                    row = pl.multiple_of(shard * depth, 16)
                    full[pl.ds(row, depth), lanes] = piece[one, two, step]


def project_kernel(head_dim, placed, *refs):
    tokens_ref, norm_ref, bias_ref = refs[:3]
    outs, wide_ref, hidden_ref = refs[-10:-2], refs[-2], refs[-1]
    full_ref, ordered_ref, turned_ref = outs[:3]
    rows, width = tokens_ref.shape
    block = rows // RESIDUES
    if placed is None:
        full_ref[...] = refs[3][...]
    else:
        place_pieces(refs[3], refs[4:8], full_ref, *placed)
    fill_stripes(wide_ref, tokens_ref[...].astype(F32))
    gain, shift = norm_ref[0:1], norm_ref[1:2]
    for first, natural in residue_rows(block):
        span = slice(first, first + block)
        values = read_stripes(wide_ref, natural)
        ordered_ref[span] = values.astype(BF16)
        hidden_ref[span] = (standardize(values)[0] * gain + shift).astype(BF16)
    turned_ref[...] = hidden_ref[...].T
    ones = jnp.where(lax.broadcasted_iota(jnp.int32, (16, LANES), 0) == 0, 1.0, 0.0).astype(BF16)
    odd = lax.rem(lax.div(lax.broadcasted_iota(jnp.int32, (width, 1), 0), head_dim), 2) == 1
    half = rows // 2
    for i in range(3):
        product = dot_tn(full_ref[:, i * width : (i + 1) * width], turned_ref[...])
        if i != 1:
            at = i // 2 * width
            column = dot_tn(bias_ref[:, at : at + width], ones)
            product += jnp.concatenate([column] * (rows // LANES), axis=1)
        low = product.astype(BF16)
        outs[3 + i][...] = low
        if i:
            outs[5 + i][...] = jnp.where(odd, low[:, half:], low[:, :half])


def project(tokens, norms, bias, full, pieces, spot, placed, head_dim):
    rows, width = tokens.shape
    ins = [tokens, norms, bias] + ([full] if placed is None else [spot, *pieces])
    specs = [pl.BlockSpec(memory_space=pltpu.VMEM)] * len(ins)
    if placed is not None:
        specs[3] = pl.BlockSpec(memory_space=pltpu.SMEM)
    turned = jax.ShapeDtypeStruct((width, rows), BF16)
    part = jax.ShapeDtypeStruct((width, rows // 2), BF16)
    outs = [
        jax.ShapeDtypeStruct((width, 3 * width), BF16), jax.ShapeDtypeStruct((rows, width), BF16),
        turned, turned, turned, turned, part, part,
    ]
    return pl.pallas_call(
        functools.partial(project_kernel, head_dim, placed),
        in_specs=specs,
        out_specs=[pl.BlockSpec(memory_space=pltpu.VMEM)] * len(outs),
        out_shape=outs,
        scratch_shapes=[stripes(rows, width), pltpu.VMEM((rows, width), BF16)],
        compiler_params=pltpu.CompilerParams(vmem_limit_bytes=VMEM_LIMIT),
        cost_estimate=pl.CostEstimate(
            flops=6 * rows * width * width,
            transcendentals=0,
            bytes_accessed=12 * width * width + 16 * rows * width,
        ),
        name="project",
    )(*ins)


def finish_kernel(weight_ref, grad_ref, tokens_ref, middle_ref, norm_ref, sums_ref, wide_ref, out_ref, table_ref, natural_ref):
    step, count = pl.program_id(0), pl.num_programs(0)
    tile, width = tokens_ref.shape
    block = out_ref.shape[0] // RESIDUES

    @pl.when(step == 0)
    def _():
        table_ref[...] = jnp.zeros_like(table_ref)
        table_ref[4:8] = sums_ref[...]
        for i in range(wide_ref.shape[1] // width):
            table_ref[8 + i : 9 + i] = wide_ref[:, i * width : (i + 1) * width]

    grad = dot_nn(weight_ref[...], grad_ref[...]).T
    normed, inverse = standardize(tokens_ref[...].astype(F32))
    table_ref[0:1] += jnp.sum(grad * normed, axis=0, keepdims=True)
    table_ref[1:2] += jnp.sum(grad, axis=0, keepdims=True)
    ones = jnp.ones((16, tile), BF16)
    table_ref[2:3] += dot_nt(ones, grad_ref[:width])[0:1]
    table_ref[3:4] += dot_nt(ones, grad_ref[2 * width :])[0:1]
    total = middle_ref[...] + norm_back(grad, normed, inverse, norm_ref[0:1])
    many = tile // block
    half = RESIDUES // 2
    for i in range(many):
        place = step * many + i
        residue = 2 * lax.rem(place, half) + lax.div(place, half)
        natural = pl.ds(residue, block, stride=RESIDUES)
        write_stripes(natural_ref, natural, total[i * block : (i + 1) * block])

    @pl.when(step == count - 1)
    def _():
        out_ref[...] = read_stripes(natural_ref, slice(None))


def finish(weight, grad, tokens, middle, norms, sums, wide):
    rows, width = tokens.shape
    tile = min(rows, 512)
    narrow_spec = pl.BlockSpec((tile, width), lambda r: (r, 0))
    once = pl.BlockSpec(memory_space=pltpu.VMEM)
    return pl.pallas_call(
        finish_kernel,
        grid=(rows // tile,),
        in_specs=[
            once, pl.BlockSpec((grad.shape[0], tile), lambda r: (0, r)), narrow_spec, narrow_spec,
            once, once, once,
        ],
        out_specs=[once, once],
        out_shape=[
            jax.ShapeDtypeStruct((rows, width), F32),
            jax.ShapeDtypeStruct((16, width), F32),
        ],
        scratch_shapes=[stripes(rows, width)],
        compiler_params=pltpu.CompilerParams(vmem_limit_bytes=VMEM_LIMIT),
        cost_estimate=pl.CostEstimate(
            flops=6 * rows * width * width,
            transcendentals=0,
            bytes_accessed=6 * width * width + 16 * rows * width,
        ),
        name="finish",
    )(weight, grad, tokens, middle, norms, sums, wide)


def feed_forward_kernel(blocks, *refs):
    tokens_ref, attended_ref, natural_ref, small_ref, wide_ref, packed_ref = refs[:6]
    output_ref, grad_ref, mixed_ref, sums_ref, wide_sums_ref, grads_ref = refs[6:12]
    reduce_w, expand_w, output_w, natural_scr, active_scr, expanded_scr = refs[12:18]
    cotangent_scr, hidden_scr, low_scr, in_sems, out_sems = refs[18:]
    tile, width = tokens_ref.shape
    cut, depth = reduce_w.shape[1], output_w.shape[1]
    step, count = pl.program_id(0), pl.num_programs(0)
    block = natural_ref.shape[0] // RESIDUES
    halves, columns = packed_ref.shape[1], packed_ref.shape[3]
    local = blocks // halves * width // columns

    def arrival(index, y, at, size, target):
        return pltpu.make_async_copy(
            packed_ref.at[:, y, pl.ds(at, size)], target, in_sems.at[index]
        )

    def arrivals(first=0, last=None):
        found = []
        for y in range(halves):
            lanes = pl.ds(y * columns, columns)
            found.append((y, cut + local * depth, depth, output_w.at[:, :, lanes]))
        for y in range(halves):
            for i in range(local):
                at = (y * local + i) * columns
                target = expand_w.at[at // width, :, :, pl.ds(at % width, columns)]
                found.append((y, cut + i * depth, depth, target))
        for y in range(halves):
            found.append((y, 0, cut, reduce_w.at[:, :, pl.ds(y * columns, columns)]))
        indices = range(len(found))[first:last]
        return [arrival(i, *found[i]) for i in indices]

    def await_first(first, last):
        @pl.when(step == 0)
        def _():
            for copy in arrivals(first, last):
                copy.wait()

    @pl.when(step == 0)
    def _():
        for copy in arrivals():
            copy.start()
        fill_stripes(natural_scr, natural_ref[...].astype(F32))
        sums_ref[...] = jnp.zeros_like(sums_ref)
        wide_sums_ref[...] = jnp.zeros_like(wide_sums_ref)

    many, half = tile // block, RESIDUES // 2
    strided = []
    for i in range(many):
        place = step * many + i
        residue = 2 * lax.rem(place, half) + lax.div(place, half)
        strided.append(pl.ds(residue, block, stride=RESIDUES))
    here = pl.ds(pl.multiple_of(step * tile, tile), tile)
    bias_output, gain, shift, bias_reduce = (small_ref[i : i + 1] for i in range(4))
    upstream = jnp.concatenate([read_stripes(natural_scr, natural) for natural in strided], axis=0)
    cotangent = upstream.astype(BF16)
    cotangent_scr[here] = cotangent
    await_first(0, halves)
    project = output_w[...].reshape(width, width)
    middle = tokens_ref[...].astype(F32) + dot_tn(attended_ref[:, here], project) + bias_output
    normed, inverse = standardize(middle)
    hidden = (normed * gain + shift).astype(BF16)
    hidden_scr[here] = hidden
    output = middle + bias_reduce
    hidden_grad = jnp.zeros(middle.shape, F32)
    await_first(halves, halves + halves * local + halves)
    shrink_all = reduce_w[...].reshape(blocks * width, width)
    for i in range(blocks):
        span = slice(i * width, (i + 1) * width)
        grow = expand_w[i].reshape(width, width)
        shrink = shrink_all[span]
        active, slope = gelu_pair(dot_nn(hidden, grow) + wide_ref[:, span])
        active = active.astype(BF16)
        active_scr[i, here] = active
        output += dot_nn(active, shrink)
        expanded = (dot_nt(cotangent, shrink) * slope).astype(BF16)
        expanded_scr[i, here] = expanded
        wide_sums_ref[:, span] += jnp.sum(expanded.astype(F32), axis=0, keepdims=True)
        hidden_grad += dot_nt(expanded, grow)
    for i, natural in enumerate(strided):
        write_stripes(natural_scr, natural, output[i * block : (i + 1) * block])
    middle_grad = upstream + norm_back(hidden_grad, normed, inverse, gain)
    grad_ref[...] = middle_grad
    low = middle_grad.astype(BF16)
    low_scr[here] = low
    mixed_ref[...] = dot_nt(project, low).astype(BF16)
    for i, part in enumerate((hidden_grad * normed, hidden_grad, middle_grad, upstream)):
        sums_ref[i : i + 1] += jnp.sum(part, axis=0, keepdims=True)

    @pl.when(step == count - 1)
    def _():
        output_ref[...] = read_stripes(natural_scr, slice(None)).astype(BF16)
        copies = []

        def leave(source, target):
            copies.append(pltpu.make_async_copy(source, target, out_sems.at[len(copies)]))
            copies[-1].start()

        for i in range(blocks):
            product = dot_tn(active_scr[i], cotangent_scr[...]).astype(BF16)
            if cut <= width:
                shards = slice(i * width // cut, (i + 1) * width // cut)
                reduce_w[shards] = product.reshape(-1, cut, width)
                leave(reduce_w.at[shards], grads_ref.at[shards, pl.ds(0, cut)])
            else:
                span = pl.ds(i * width, width)
                reduce_w[0, span] = product
                leave(reduce_w.at[:, span], grads_ref.at[:, span])
        for i in range(blocks):
            product = dot_tn(hidden_scr[...], expanded_scr[i]).astype(BF16)
            expand_w[i] = product.reshape(-1, depth, width)
            leave(expand_w.at[i], grads_ref.at[:, pl.ds(cut + i * depth, depth)])
        product = dot_nn(attended_ref[...], low_scr[...]).astype(BF16)
        output_w[...] = product.reshape(-1, depth, width)
        leave(output_w, grads_ref.at[:, pl.ds(cut + blocks * depth, depth)])
        for copy in copies:
            copy.wait()


def feed_forward(tokens, attended, cotangent, small, wide, packed):
    rows, width = tokens.shape
    ff = wide.shape[1]
    blocks = ff // width
    shards, halves = packed.shape[:2]
    tile = min(rows, 256)
    narrow_spec = pl.BlockSpec((tile, width), lambda r: (r, 0))
    turned_spec = pl.BlockSpec((width, tile), lambda r: (0, r))
    once = pl.BlockSpec(memory_space=pltpu.VMEM)
    rows_scr = pltpu.VMEM((rows, width), BF16)
    wide_scr = pltpu.VMEM((blocks, rows, width), BF16)
    return pl.pallas_call(
        functools.partial(feed_forward_kernel, blocks),
        grid=(rows // tile,),
        in_specs=[narrow_spec, once, once, once, once, pl.BlockSpec(memory_space=pl.ANY)],
        out_specs=[once, narrow_spec, turned_spec, once, once, pl.BlockSpec(memory_space=pl.ANY)],
        out_shape=[
            jax.ShapeDtypeStruct((rows, width), BF16),
            jax.ShapeDtypeStruct((rows, width), F32),
            jax.ShapeDtypeStruct((width, rows), BF16),
            jax.ShapeDtypeStruct((4, width), F32),
            jax.ShapeDtypeStruct((1, ff), F32),
            jax.ShapeDtypeStruct((shards, (2 * ff + width) // shards, width), BF16),
        ],
        scratch_shapes=[
            pltpu.VMEM((shards, ff // shards, width), BF16),
            pltpu.VMEM((blocks, shards, width // shards, width), BF16),
            pltpu.VMEM((shards, width // shards, width), BF16),
            stripes(rows, width),
            wide_scr,
            wide_scr,
            rows_scr,
            rows_scr,
            rows_scr,
            pltpu.SemaphoreType.DMA((2 * halves + blocks * halves,)),
            pltpu.SemaphoreType.DMA((2 * blocks + 1,)),
        ],
        compiler_params=pltpu.CompilerParams(vmem_limit_bytes=VMEM_LIMIT),
        cost_estimate=pl.CostEstimate(
            flops=2 * rows * width * (6 * ff + 3 * width),
            transcendentals=2 * rows * ff,
            bytes_accessed=4 * packed.size + 20 * rows * width,
        ),
        name="feed_forward",
    )(tokens, attended, cotangent, small, wide, packed)


def level_table():
    head = np.arange(HEADS)[:, None]
    residue = 2 * np.arange(RESIDUES // 2)[None, :] + head % 2
    return sum((residue % 2**b == head % 2**b).astype(int) for b in range(1, BRANCHES))


def log_rows(times):
    parts = np.log2(times).astype(np.float32)
    rows = []
    for _ in range(3):
        low = parts.astype(ml_dtypes.bfloat16)
        rows.append(low)
        parts = parts - low.astype(np.float32)
    return np.stack(rows, axis=2).reshape(times.shape[0], -1, times.shape[2])


def attention_extras(rows, own_starts, far_starts, own_count, far_count, same):
    half, block = rows // 2, rows // RESIDUES
    levels = level_table()
    level = np.arange(1, BRANCHES)[None, :, None]
    lower = np.minimum(level, levels[:, None, :])

    def repeat(table, devices):
        return np.tile(np.repeat(table, block, axis=-1), devices)

    rank = np.arange(half)
    place = [(rank % block) * RESIDUES + 2 * (rank // block) + parity for parity in range(2)]

    def liveness(starts, count, allowed):
        live = [
            jnp.stack([(start + jnp.asarray(place[p]) < count) & allowed for p in range(2)])
            for start in starts
        ]
        return jnp.where(jnp.concatenate(live, axis=1), 0.0, NEGATIVE).astype(BF16)

    def built(times, live):
        count, _, keys = times.shape
        fixed = np.zeros((count, EXTRA, keys), ml_dtypes.bfloat16)
        fixed[:, TIMES:LIVE] = times
        fixed[:, FIXED : FIXED + 3] = 1
        row = np.arange(EXTRA)[None, :, None]
        return jnp.where(row == LIVE, live[:, None], jnp.asarray(fixed))

    own_live = liveness(own_starts, own_count, True)
    far_live = liveness(far_starts, far_count, same)
    by_head = np.arange(HEADS) % 2
    none = np.zeros((2, LIVE, half * len(own_starts)), ml_dtypes.bfloat16)

    def per_head(live):
        return jnp.where(by_head[:, None] == 1, live[1], live[0])

    query = np.zeros((HEADS, EXTRA, half), ml_dtypes.bfloat16)
    spread = np.repeat(levels, block, axis=1)
    for one in range(1, BRANCHES):
        query[:, 3 * (one - 1) : 3 * one] = (spread == one)[:, None, :]
    query[:, LIVE] = 1
    return {
        "plain": built(none, own_live),
        "same": built(repeat(log_rows(1.0 + lower), len(own_starts)), per_head(own_live)),
        "far": built(repeat(log_rows(lower), len(far_starts)), per_head(far_live)),
        "query": jnp.asarray(query),
        "self": jnp.asarray(np.log2(1.0 + spread).astype(np.float32))[:, None],
    }


def half_of(table, odd):
    half = table.shape[-1] // 2
    return jnp.where(odd, table[..., half:], table[..., :half])


def add_half(total, part, odd):
    part = part.astype(F32)
    both = jnp.concatenate([jnp.where(odd, 0.0, part), jnp.where(odd, part, 0.0)], axis=-1)
    return total.astype(F32) + both


def swap_pairs(value):
    return lax.ppermute(value, "branch", [(0, 1), (1, 0)])


def gather_columns(shard, branches):
    if branches != 2:
        return lax.all_gather(shard, "branch", axis=shard.ndim - 1, tiled=True)
    other = swap_pairs(shard)
    first = lax.axis_index("branch") == 0
    return jnp.concatenate(
        [jnp.where(first, shard, other), jnp.where(first, other, shard)], axis=-1
    )


def scatter_columns(total, branches):
    if branches != 2:
        return lax.psum_scatter(
            total, "branch", scatter_dimension=total.ndim - 1, tiled=True
        ).astype(F32)
    half = total.shape[-1] // 2
    at = lax.axis_index("branch")
    keep = lax.dynamic_slice_in_dim(total, at * half, half, total.ndim - 1)
    away = lax.dynamic_slice_in_dim(total, (1 - at) * half, half, total.ndim - 1)
    return keep.astype(F32) + swap_pairs(away).astype(F32)


def weight_sum(partial, branches):
    low = lax.psum_scatter(partial, "slides", scatter_dimension=0, tiled=True)
    return scatter_columns(low, branches)


def pack_rows(reduce_part, expand_part, output_part):
    width = output_part.shape[-1]
    blocks = expand_part.shape[-1] // width
    return jnp.concatenate(
        [reduce_part]
        + [expand_part[..., i * width : (i + 1) * width] for i in range(blocks)]
        + [output_part],
        axis=-2,
    )


def unpack_rows(packed, width, ff):
    blocks = ff // width
    depth = packed.shape[-2] // (2 * blocks + 1)
    cut = blocks * depth
    expand = [packed[..., cut + i * depth : cut + (i + 1) * depth, :] for i in range(blocks)]
    return packed[..., :cut, :], jnp.concatenate(expand, axis=-1), packed[..., 2 * cut :, :]


def join_columns(own, other):
    first = lax.axis_index("branch") == 0
    return jnp.concatenate(
        [jnp.where(first, own, other), jnp.where(first, other, own)], axis=-1
    )


def pack_kernel(reduce_ref, expand_ref, output_ref, packed_ref):
    cut, width = reduce_ref.shape
    depth = output_ref.shape[0]
    packed_ref[:cut] = reduce_ref[...]
    blocks = expand_ref.shape[1] // width
    for i in range(blocks):
        packed_ref[cut + i * depth : cut + (i + 1) * depth] = expand_ref[:, i * width : (i + 1) * width]
    packed_ref[cut + blocks * depth :] = output_ref[...]


def join_kernel(cut, depth, at_ref, own_ref, other_ref, joined_ref):
    columns = own_ref.shape[1]
    blocks = (own_ref.shape[0] - cut) // depth - 1

    def put(halves):
        for y, half in enumerate(halves):
            lanes = slice(y * columns, (y + 1) * columns)
            joined_ref[:cut, lanes] = half[:cut]
            joined_ref[cut + blocks * depth :, lanes] = half[cut + blocks * depth :]
            for i in range(blocks):
                row, lane = divmod((y * blocks + i) * columns, 2 * columns)
                target = cut + row * depth
                source = cut + i * depth
                joined_ref[target : target + depth, lane : lane + columns] = half[
                    source : source + depth
                ]

    @pl.when(at_ref[0] == 0)
    def _():
        put((own_ref, other_ref))

    @pl.when(at_ref[0] != 0)
    def _():
        put((other_ref, own_ref))


def gather_packed(reduce_weight, expand_weight, output_weight, first_transfers, branches):
    size = lax.axis_size("slides")
    depth, columns = output_weight.shape
    aligned = branches == 2 and depth % 16 == 0 and columns % LANES == 0
    if aligned:
        rows = reduce_weight.shape[0] + depth + expand_weight.size // columns
        shard = pl.pallas_call(
            pack_kernel,
            out_shape=jax.ShapeDtypeStruct((rows, columns), BF16),
            name="pack",
        )(reduce_weight, expand_weight, output_weight)
    else:
        shard = pack_rows(reduce_weight, expand_weight, output_weight)
    if aligned:
        at = lax.axis_index("branch").reshape(1)
        other, first_transfers = lax.optimization_barrier((swap_pairs(shard), first_transfers))
        shard = pl.pallas_call(
            functools.partial(join_kernel, reduce_weight.shape[0], depth),
            in_specs=[pl.BlockSpec(memory_space=pltpu.SMEM)]
            + [pl.BlockSpec(memory_space=pltpu.VMEM)] * 2,
            out_shape=jax.ShapeDtypeStruct((rows, 2 * columns), BF16),
            name="join",
        )(at, shard, other)
        return lax.all_gather(shard, "slides", axis=0, tiled=False)[:, None], first_transfers
    packed = lax.all_gather(shard, ("slides", "branch"), axis=0, tiled=False)
    packed = packed.reshape(size, branches, *shard.shape)
    ff = size * reduce_weight.shape[0]
    parts = unpack_rows(packed, columns, ff // branches)
    parts = [m.transpose(0, 2, 1, 3).reshape(1, -1, branches * m.shape[-1]) for m in parts]
    return pack_rows(*parts)[None], first_transfers


def gather_vectors(vectors, branches, rows_of):
    cuts = np.cumsum([0] + [m.shape[0] for m in vectors])
    if branches != 2:
        table = lax.all_gather(jnp.concatenate(vectors), "branch", axis=0, tiled=False)
        return [table[:, a:b].reshape(1, -1) for a, b in zip(cuts, cuts[1:])]
    own, other = rows_of
    columns = own.shape[1]
    first = lax.axis_index("branch") == 0
    halves = [jnp.where(first, own, other), jnp.where(first, other, own)]
    at = cuts // columns
    return [
        jnp.concatenate(
            [half[row : row + 1] for half in halves for row in range(at[i], at[i + 1])], axis=1
        )
        for i in range(len(vectors))
    ]


def sum_packed(packed, width, ff):
    size = lax.axis_size("slides")
    if packed.shape[0] != size:
        parts = unpack_rows(packed, width, ff)
        packed = pack_rows(*(m.reshape(size, -1, m.shape[-1]) for m in parts))
    rows = packed.shape[1]
    return lax.psum_scatter(
        packed.reshape(size * rows, width), "slides", scatter_dimension=0, tiled=True
    )


def branch_half(low, index, width, ff):
    reduce_part, expand_part, output_part = unpack_rows(low, width, ff)
    columns = width // 2
    grown = lax.dynamic_slice_in_dim(expand_part, index * (ff // 2), ff // 2, 1)
    pieces = [
        lax.dynamic_slice_in_dim(part, index * columns, columns, 1)
        for part in (reduce_part, output_part)
    ]
    pieces += [grown[:, i : i + columns] for i in range(0, ff // 2, columns)]
    return jnp.concatenate(pieces, axis=0)


def unpack_half(total, depth, cut):
    tail = [total[row : row + depth] for row in range(cut + depth, total.shape[0], depth)]
    return total[:cut], jnp.concatenate(tail, axis=1), total[cut : cut + depth]


def flip(value, bit):
    return lax.ppermute(value, "slides", [(i, i ^ bit) for i in range(lax.axis_size("slides"))])


def shifted(value, step):
    size = lax.axis_size("slides")
    return lax.ppermute(value, "slides", [(i, (i + 4 * step) % size) for i in range(size)])


def gather_pieces(held, later):
    half = held[0].shape[1] // 2 // LANES * LANES
    first = jnp.stack([m[:, :half] for m in held])
    second = jnp.stack([m[:, half:] for m in held])
    first, second = jnp.stack([first, flip(first, 2)]), jnp.stack([second, swap_pairs(second)])
    first, second, later = lax.optimization_barrier((first, second, later))
    other = swap_pairs(later[0])
    first, second = jnp.stack([first, swap_pairs(first)]), jnp.stack([second, flip(second, 2)])
    pieces = (first, second, flip(first, 1), flip(second, 1))
    slide = lax.axis_index("slides")
    spot = jnp.stack(
        [
            lax.div(slide, 4),
            lax.rem(lax.div(slide, 2), 2),
            lax.rem(slide, 2),
            lax.axis_index("branch"),
        ]
    )
    return pieces, spot.astype(jnp.int32), other, later


def pick(table, index, axis):
    return lax.dynamic_index_in_dim(table, index, axis, keepdims=False)


def split_kernel(core_ref, left_ref, right_ref, keep_ref, send_ref, product_ref):
    product_ref[...] = dot_nt(left_ref[...], right_ref[...]).astype(BF16).reshape(product_ref.shape)
    core = core_ref[0]
    for pair in range(product_ref.shape[0] // 2):
        at = (0, pair // 2, pair % 2)
        keep_ref[at] = product_ref[2 * pair + core]
        send_ref[at] = product_ref[2 * pair + 1 - core]


def split_product(left, right, core):
    size = lax.axis_size("slides")
    features, rows = left.shape
    depth, columns = features // size, right.shape[0] // 2
    step = columns
    wide = columns // step
    block = pl.BlockSpec((1, size // 4, 2, depth, step), lambda j: (j // wide, 0, 0, 0, j % wide))
    return pl.pallas_call(
        split_kernel,
        grid=(2 * wide,),
        in_specs=[
            pl.BlockSpec(memory_space=pltpu.SMEM),
            whole_spec(left.shape),
            pl.BlockSpec((step, rows), lambda j: (j, 0)),
        ],
        out_specs=[block, block],
        out_shape=[jax.ShapeDtypeStruct((2, size // 4, 2, depth, columns), BF16)] * 2,
        scratch_shapes=[pltpu.VMEM((size, depth, step), BF16)],
        compiler_params=pltpu.CompilerParams(vmem_limit_bytes=VMEM_LIMIT),
        cost_estimate=pl.CostEstimate(
            flops=4 * rows * features * columns,
            transcendentals=0,
            bytes_accessed=2 * (left.size + right.size + 2 * features * columns),
        ),
        name="joint_gradient",
    )(core.reshape(1), left, right)


def deal_kernel(spans, at_ref, *refs):
    tables, outs = refs[: -len(spans)], refs[-len(spans) :]
    total = sum((table[...] for table in tables[1:]), tables[0][...])
    width = total.shape[1]

    def put(index):
        for (row, count), out in zip(spans, outs):
            if count == 1:
                out[...] = total[row, index * width // 2 : (index + 1) * width // 2]
            else:
                for i in range(count // 2):
                    at = row + index * count // 2 + i
                    out[i * width : (i + 1) * width] = total[at]

    @pl.when(at_ref[0] == 0)
    def _():
        put(0)

    @pl.when(at_ref[0] != 0)
    def _():
        put(1)


def deal(tables, spans, at):
    width = tables[0].shape[1]
    return pl.pallas_call(
        functools.partial(deal_kernel, spans),
        in_specs=[pl.BlockSpec(memory_space=pltpu.SMEM)]
        + [pl.BlockSpec(memory_space=pltpu.VMEM)] * len(tables),
        out_shape=[jax.ShapeDtypeStruct((count * width // 2,), F32) for _, count in spans],
        name="deal",
    )(at.reshape(1), *tables)


def sum_tree(kept, sent, table_of, gate, low_sums, near, outer, at):
    rounds = kept.shape[1]

    def both(one, two):
        return (one.astype(F32) + two.astype(F32)).astype(BF16)

    total = both(kept, flip(sent, 1))
    low, high = total[:, : rounds // 2], total[:, rounds // 2 :]
    away, off, gate = lax.optimization_barrier(
        (pick(low, 1 - at, 0), pick(high, 1 - near, 2), gate)
    )
    away, off = swap_pairs(away), flip(off, 2)
    table = table_of(gate)
    low, high = both(pick(low, at, 0), away), both(pick(high, near, 2), off)
    away, off, table = lax.optimization_barrier(
        (pick(low, 1 - near, 1), pick(high, 1 - at, 0), table)
    )
    low, high = both(pick(low, near, 1), flip(away, 2)), both(pick(high, at, 0), swap_pairs(off))
    table += flip(table, 1)
    table += swap_pairs(table)
    joined = jnp.concatenate([low, high], axis=0)
    total = pick(joined, outer, 0).astype(F32)
    sends = [pick(joined, lax.rem(outer + step, rounds), 0) for step in range(1, rounds)]
    sends, table = lax.optimization_barrier((sends, table))
    parts = [shifted(part, step + 1) for step, part in enumerate(sends)]
    table += flip(table, 2)
    parts[0], table, low_sums = lax.optimization_barrier((parts[0], table, low_sums))
    for part in parts:
        total += part.astype(F32)
    bit = 4
    while bit < 4 * rounds:
        table += flip(table, bit)
        bit *= 2
    return total, table, low_sums


def on_device(
    tokens,
    cotangent,
    first_gain,
    first_shift,
    joint_weight,
    joint_bias,
    output_weight,
    output_bias,
    second_gain,
    second_shift,
    expand_weight,
    expand_bias,
    reduce_weight,
    reduce_bias,
    block_owner,
    tile_count,
):
    rows, width = tokens.shape
    branches = lax.axis_size("branch")
    head_dim = width // HEADS
    block = rows // RESIDUES
    mates = SEG_BASE // rows
    at = lax.axis_index("branch")
    segment = lax.div(at, mates)
    within = at - segment * mates
    odd = ((np.arange(width) // head_dim) % 2 == 1)[:, None]

    parameters = (
        first_gain, first_shift, joint_bias, output_bias,
        second_gain, second_shift, expand_bias, reduce_bias,
    )
    depth = joint_weight.shape[0]
    slides = lax.axis_size("slides")
    trees = branches == 2 and slides % 8 == 0 and slides & (slides - 1) == 0 and depth % 16 == 0
    held = [joint_weight]
    if trees:
        held += [shifted(joint_weight, step) for step in range(1, slides // 4)]
    packed_weights, held = gather_packed(
        reduce_weight, expand_weight, output_weight, held, branches
    )
    if trees:
        small = jnp.concatenate([m.reshape(-1, width // 2) for m in parameters], axis=0)
        pieces, spot, other, (small, block_owner, tile_count) = gather_pieces(
            held, (small, block_owner, tile_count)
        )
        vectors = gather_vectors(parameters, branches, (small, other))
        joint_full, placed = None, joint_weight.shape
    else:
        joint_full = lax.all_gather(
            gather_columns(joint_weight, branches), "slides", axis=0, tiled=True
        )
        vectors = gather_vectors(parameters, branches, None)
        pieces, spot, placed = (), None, None
    bias_joint = jnp.pad(vectors[2], ((0, 15), (0, 0)))
    gain_one, shift_one, _, bias_output, gain_two, shift_two, bias_expand, bias_reduce = (
        m.astype(F32) for m in vectors
    )
    norms = jnp.concatenate([gain_one, shift_one], axis=0)

    owners = block_owner.reshape(-1)
    counts = tile_count.reshape(-1)
    own_count = jnp.where(segment == 0, counts[0], counts[1])
    far_count = jnp.where(segment == 0, counts[1], counts[0])
    own_starts = [lax.rem(within + d, mates) * rows for d in range(mates)]
    far_starts = [d * rows for d in range(mates)]
    extras = attention_extras(
        rows, own_starts, far_starts, own_count, far_count, owners[0] == owners[1]
    )

    joint_full, tokens_low, hidden_turned, q, k, v, k_half, v_half = project(
        tokens, norms, bias_joint, joint_full, pieces, spot, placed, head_dim
    )
    if mates == 1 and branches == 2:
        k_own, v_own = k[None], v[None]
        k_far, v_far = swap_pairs(k_half)[None], swap_pairs(v_half)[None]
    else:
        own_at = [segment * mates + lax.rem(within + d, mates) for d in range(mates)]
        far_at = [(1 - segment) * mates + d for d in range(mates)]

        def chosen(table, indices):
            whole = lax.all_gather(table, "branch", axis=0)
            return jnp.stack([lax.dynamic_index_in_dim(whole, d, 0, False) for d in indices])

        k_own, v_own = chosen(k, own_at), chosen(v, own_at)
        k_far, v_far = chosen(k_half, far_at), chosen(v_half, far_at)
    attended, part, total_log = attend_own(q, k_own, v_own, extras)
    attended, total_log = attend_far(q, k_far, v_far, extras, attended, part, total_log)
    ff = bias_expand.shape[1]
    small = jnp.concatenate([bias_output, gain_two, shift_two, bias_reduce], axis=0)
    output, middle_grad, mixed_grad, sums, wide_sums, packed_grads = feed_forward(
        tokens_low, attended, cotangent, small, bias_expand, packed_weights
    )
    mixed_grad, packed_grads = lax.optimization_barrier((mixed_grad, packed_grads))
    low_sums = sum_packed(packed_grads, width, ff)

    part, dk_far, dv_far = attend_far_back(
        q, k_far, v_far, extras, attended, mixed_grad, total_log
    )
    dq, dk_own, dv_own = attend_own_back(
        q, k_own, v_own, extras, attended, mixed_grad, total_log, part
    )
    if mates == 1 and branches == 2:
        key_sum = add_half(dk_own[0], swap_pairs(dk_far[0]), odd)
        value_sum = add_half(dv_own[0], swap_pairs(dv_far[0]), odd)
    else:

        def spread(own, far):
            canvas = jnp.zeros((branches, width, rows), BF16)
            for d, index in enumerate(own_at):
                canvas = lax.dynamic_update_index_in_dim(canvas, own[d], index, 0)
            for d, index in enumerate(far_at):
                full = add_half(jnp.zeros((width, rows), F32), far[d], odd).astype(BF16)
                canvas = lax.dynamic_update_index_in_dim(canvas, full, index, 0)
            return lax.psum_scatter(canvas, "branch", scatter_dimension=0, tiled=True)[0]

        key_sum = spread(dk_own, dk_far)
        value_sum = spread(dv_own, dv_far)
    value_low = value_sum.astype(BF16)
    joint_grad = jnp.concatenate([dq, key_sum.astype(BF16), value_low], axis=0)
    found = []

    def table_of(grad):
        found.extend(finish(joint_full, joint_grad, tokens_low, grad, norms, sums, wide_sums))
        return found[1]

    sizes = (1, 1, 2, 1, 1, 1, 1, ff // width)
    starts = np.cumsum((0,) + sizes)
    if trees:
        slide = lax.axis_index("slides")
        kept, sent = split_product(hidden_turned, joint_grad, lax.rem(slide, 2))
        joint_sum, table, low_sums = sum_tree(
            kept, sent, table_of, middle_grad, low_sums,
            lax.rem(lax.div(slide, 2), 2), lax.div(slide, 4), at,
        )
        arrived = swap_pairs(branch_half(low_sums, 1 - at, width, ff))
        halves = branch_half(low_sums, at, width, ff).astype(F32) + arrived.astype(F32)
        reduce_sum, expand_sum, output_sum = unpack_half(
            halves, output_weight.shape[0], reduce_weight.shape[0]
        )
        mine = deal([table], tuple((int(a), n) for a, n in zip(starts, sizes)), at)
    else:
        joint_sum = weight_sum(dot_nt(hidden_turned, joint_grad).astype(BF16), branches)
        table = lax.psum(table_of(middle_grad), ("slides", "branch"))
        reduce_sum, expand_sum, output_sum = (
            scatter_columns(part, branches) for part in unpack_rows(low_sums, width, ff)
        )
        mine = []
        for row, count in zip(starts, sizes):
            share = count * width // branches
            whole = table[row : row + count].reshape(-1)
            mine.append(lax.dynamic_slice_in_dim(whole, at * share, share))
    tokens_grad = found[0]
    first_gain_sum, first_shift_sum, joint_bias_sum, second_gain_sum = mine[:4]
    second_shift_sum, output_bias_sum, reduce_bias_sum, expand_bias_sum = mine[4:]
    return (
        output,
        tokens_grad,
        first_gain_sum,
        first_shift_sum,
        joint_sum,
        joint_bias_sum,
        output_sum,
        output_bias_sum,
        second_gain_sum,
        second_shift_sum,
        expand_sum,
        expand_bias_sum,
        reduce_sum,
        reduce_bias_sum,
    )


def solution(mesh):
    rows = P(("slides", "branch"), None)
    matrix = P("slides", "branch")
    vector = P("branch")
    placed = (
        rows, rows, vector, vector, matrix, vector, matrix, vector,
        vector, vector, matrix, vector, matrix, vector, P("slides", None), P("slides", None),
    )
    given = (
        rows, rows, vector, vector, matrix, vector, matrix, vector,
        vector, vector, matrix, vector, matrix, vector,
    )
    return jax.shard_map(on_device, mesh=mesh, in_specs=placed, out_specs=given, check_vma=False)
```

```python
import functools
import math

import jax
import jax.numpy as jnp
import ml_dtypes
import numpy as np
from jax import lax
from jax.experimental import pallas as pl
from jax.experimental.pallas import tpu as pltpu
from jax.sharding import PartitionSpec as P

HEADS = 16
SEG_BASE = 1024
BRANCHES = 5
RESIDUES = 2 ** (BRANCHES - 1)
EPSILON = 1e-05
NEGATIVE = -1e30
LANES = 128
EXTRA = 32
TIMES, LIVE, FIXED = 0, 12, 13
UNROLL = 4
OWN_UNROLL = 2
PIECE = 512
VMEM_LIMIT = 60 * 1024 * 1024

BF16 = jnp.bfloat16
F32 = jnp.float32


def standardize(values):
    centred = values - jnp.mean(values, axis=-1, keepdims=True)
    inverse = lax.rsqrt(jnp.mean(centred * centred, axis=-1, keepdims=True) + EPSILON)
    return (centred * inverse, inverse)


def norm_back(upstream, normed, inverse, gain):
    scaled = upstream * gain
    return inverse * (
        scaled
        - jnp.mean(scaled, axis=-1, keepdims=True)
        - normed * jnp.mean(scaled * normed, axis=-1, keepdims=True)
    )


def gelu_pair(values):
    cumulative = 0.5 * (1.0 + lax.erf(values * (1.0 / math.sqrt(2.0))))
    density = jnp.exp(-0.5 * values * values) * (1.0 / math.sqrt(2.0 * math.pi))
    return values * cumulative, cumulative + values * density


def dot_nn(left, right):
    return lax.dot_general(left, right, (((1,), (0,)), ((), ())), preferred_element_type=F32)


def dot_nt(left, right):
    return lax.dot_general(left, right, (((1,), (1,)), ((), ())), preferred_element_type=F32)


def dot_tn(left, right):
    return lax.dot_general(left, right, (((0,), (0,)), ((), ())), preferred_element_type=F32)


def thirds(value):
    first = value.astype(BF16)
    rest = value - first.astype(F32)
    second = rest.astype(BF16)
    return first, second, (rest - second.astype(F32)).astype(BF16)


class HeadView:
    def __init__(self, head, far, refs, head_dim, other_segment, own=True):
        half = refs["q"].shape[-1] // 2
        same = lax.rem(head, 2)
        same = same if far else 1 - same
        self.half = half
        self.rows = pl.ds(pl.multiple_of(head * head_dim, 16), head_dim)
        self.same = pl.ds(pl.multiple_of(same * half, LANES), half)
        self.other = pl.ds(pl.multiple_of((1 - same) * half, LANES), half)
        self.devices = refs["k"].shape[0] if own else 0
        self.head = head
        self.far = far
        self.own = own
        self.other_segment = other_segment
        extras = []
        if own:
            extras += [
                refs["same"][head] if far else refs["plain"][same],
                refs["plain"][1 - same],
            ]
        if other_segment:
            extras.append(refs["far"][head])
        self.extra = jnp.concatenate(extras, axis=1)

    def gathered(self, own_ref, far_ref):
        found = [own_ref[d, self.rows, self.same] for d in range(self.devices)]
        found += [own_ref[d, self.rows, self.other] for d in range(self.devices)]
        if self.other_segment:
            found += [far_ref[d, self.rows, :] for d in range(far_ref.shape[0])]
        return jnp.concatenate(found, axis=1)


def with_self(scores, own, first):
    half = scores.shape[1]
    if first >= half:
        return scores
    eye = lax.broadcasted_iota(jnp.int32, (LANES, LANES), 0) == lax.broadcasted_iota(
        jnp.int32, (LANES, LANES), 1
    )
    bands = []
    for row in range(0, min(scores.shape[0], half - first), LANES):
        at = first + row
        band = scores[row : row + LANES]
        here = jnp.where(eye, own[:, at : at + LANES], band[:, at : at + LANES])
        sides = [band[:, :at]] if at else []
        sides.append(here)
        if at + LANES < half:
            sides.append(band[:, at + LANES :])
        bands.append(jnp.concatenate(sides, axis=1))
    if half - first < scores.shape[0]:
        bands.append(scores[half - first :])
    return jnp.concatenate(bands, axis=0)


def head_scores(view, refs, keys, head_dim, constant):
    scale = head_dim ** (-0.5) * math.log2(math.e)
    scaled = refs["q"][view.rows, view.same].astype(F32) * scale
    high = scaled.astype(BF16)
    low = (scaled - high.astype(F32)).astype(BF16)
    half = view.half
    if view.far:
        extra = refs["query"][view.head]
        own = refs["self"][view.head]
    else:
        row = lax.broadcasted_iota(jnp.int32, (EXTRA, half), 0)
        extra = jnp.where(row == LIVE, 1.0, 0.0).astype(BF16)
        own = jnp.zeros((1, half), F32)
    if view.own:
        own = own + jnp.sum(scaled * keys[:, :half].astype(F32), axis=0, keepdims=True)
    if constant is not None:
        row = lax.broadcasted_iota(jnp.int32, (EXTRA, half), 0)
        filled = extra.astype(F32)
        for i, part in enumerate(thirds(constant)):
            filled = jnp.where(row == FIXED + i, part.astype(F32), filled)
        extra = filled.astype(BF16)
        own = own + constant
    left = jnp.concatenate([keys, keys, view.extra], axis=0)
    right = jnp.concatenate([high, low, extra], axis=0)

    def scores(at):
        product = dot_tn(left[:, at : at + PIECE], right)
        return with_self(product, own, at) if view.own else product

    return scores


def softmax_parts(parts, values, known):
    highest = functools.reduce(
        jnp.maximum, [jnp.max(part, axis=0, keepdims=True) for part in parts]
    )
    if known is not None:
        highest = jnp.maximum(highest, known[0])
    mixed, total = 0.0, 0.0
    at = 0
    for part in parts:
        weights = jnp.exp2(part - highest)
        total += jnp.sum(weights, axis=0, keepdims=True)
        mixed += dot_nn(values[:, at : at + part.shape[0]], weights.astype(BF16))
        at += part.shape[0]
    if known is not None:
        share = jnp.exp2(known[0] - highest)
        total += share
        mixed += known[1] * share
    return mixed * (1.0 / total), highest + jnp.log2(total)


def own_kernel(head_dim, names, count, *refs):
    o_ref, part_ref, t_ref = refs[len(names) :]
    refs = dict(zip(names, refs))

    @pl.loop(0, count, unroll=UNROLL)
    def _(head):
        for far in (True, False):
            view = HeadView(head, far, refs, head_dim, False)
            keys = view.gathered(refs["k"], None)
            values = view.gathered(refs["v"], None)
            scores = head_scores(view, refs, keys, head_dim, None)
            parts = [scores(at) for at in range(0, keys.shape[1], PIECE)]
            mixed, total_log = softmax_parts(parts, values, None)
            if far:
                part_ref[view.rows, :] = mixed
            else:
                o_ref[view.rows, view.same] = mixed.astype(BF16)
            t_ref[head, :, view.same] = total_log


def far_kernel(head_dim, names, count, *refs):
    o_ref, t_ref = refs[len(names) :]
    refs = dict(zip(names, refs))
    o_ref[...] = refs["o"][...]
    t_ref[...] = refs["t"][...]

    @pl.loop(0, count, unroll=UNROLL)
    def _(head):
        view = HeadView(head, True, refs, head_dim, True, own=False)
        keys = view.gathered(None, refs["kx"])
        values = view.gathered(None, refs["vx"])
        scores = head_scores(view, refs, keys, head_dim, None)
        parts = [scores(at) for at in range(0, keys.shape[1], PIECE)]
        known = (refs["t"][head, :, view.same], refs["part"][view.rows, :])
        mixed, total_log = softmax_parts(parts, values, known)
        o_ref[view.rows, view.same] = mixed.astype(BF16)
        t_ref[head, :, view.same] = total_log


def head_gradients(view, refs, head_dim):
    natural = head_dim ** (-0.5)
    keys = view.gathered(refs.get("k"), refs.get("kx"))
    values = view.gathered(refs.get("v"), refs.get("vx"))
    queries = refs["q"][view.rows, view.same]
    upstream = refs["g"][view.rows, view.same]
    mixed = refs["o"][view.rows, view.same]
    scores = head_scores(view, refs, keys, head_dim, -refs["t"][view.head, :, view.same])
    inner = -jnp.sum(upstream.astype(F32) * mixed.astype(F32), axis=0, keepdims=True)
    row = lax.broadcasted_iota(jnp.int32, (16, view.half), 0)
    filled = jnp.zeros((16, view.half), F32)
    for i, part in enumerate(thirds(inner)):
        filled = jnp.where(row == i, part.astype(F32), filled)
    row = lax.broadcasted_iota(jnp.int32, (16, keys.shape[1]), 0)
    ones = jnp.where(row < 3, 1.0, 0.0).astype(BF16)
    left = jnp.concatenate([values, ones], axis=0)
    right = jnp.concatenate([upstream, filled.astype(BF16)], axis=0)
    query_grad, key_parts, value_parts = 0.0, [], []
    for at in range(0, keys.shape[1], PIECE):
        span = slice(at, at + PIECE)
        part = scores(at)
        prob_grad = dot_tn(left[:, span], right)
        probs = jnp.exp2(part)
        score_grad = (probs * prob_grad).astype(BF16)
        value_parts.append(dot_nt(upstream, probs.astype(BF16)))
        key_parts.append(dot_nt(queries, score_grad) * natural)
        query_grad += dot_nn(keys[:, span], score_grad)
    return query_grad, jnp.concatenate(key_parts, axis=1), jnp.concatenate(value_parts, axis=1)


def far_back_kernel(head_dim, names, count, *refs):
    part_ref, dkx_ref, dvx_ref = refs[len(names) :]
    refs = dict(zip(names, refs))

    @pl.loop(0, count, unroll=UNROLL)
    def _(head):
        view = HeadView(head, True, refs, head_dim, True, own=False)
        query_grad, key_grad, value_grad = head_gradients(view, refs, head_dim)
        part_ref[view.rows, :] = query_grad
        for d in range(dkx_ref.shape[0]):
            lanes = slice(d * view.half, (d + 1) * view.half)
            dkx_ref[d, view.rows, :] = key_grad[:, lanes].astype(BF16)
            dvx_ref[d, view.rows, :] = value_grad[:, lanes].astype(BF16)


def own_back_kernel(head_dim, names, count, *refs):
    dq_ref, dk_ref, dv_ref = refs[len(names) :]
    refs = dict(zip(names, refs))
    natural = head_dim ** (-0.5)

    @pl.loop(0, count, unroll=OWN_UNROLL)
    def _(head):
        totals = None
        for far in (False, True):
            view = HeadView(head, far, refs, head_dim, False)
            query_grad, *grads = head_gradients(view, refs, head_dim)
            if far:
                query_grad += refs["part"][view.rows, :]
            dq_ref[view.rows, view.same] = (query_grad * natural).astype(BF16)
            if far:
                grads = [one + two for one, two in zip(grads, totals)]
            cut = view.devices * view.half
            totals = [jnp.concatenate([m[:, cut:], m[:, :cut]], axis=1) for m in grads]
        for total, ref in zip(grads, (dk_ref, dv_ref)):
            for d in range(view.devices):
                for lanes, at in ((view.same, d), (view.other, view.devices + d)):
                    part = total[:, at * view.half : (at + 1) * view.half]
                    ref[d, view.rows, lanes] = part.astype(BF16)


def whole_spec(shape):
    zeros = (0,) * len(shape)
    return pl.BlockSpec(shape, lambda *_: zeros)


def like(*members):
    return [jax.ShapeDtypeStruct(m.shape, m.dtype) for m in members]


def attention_call(kernel, name, ins, outs, pairs, matmuls):
    width, rows = ins["q"].shape
    return pl.pallas_call(
        functools.partial(kernel, width // HEADS, tuple(ins), HEADS),
        in_specs=[pl.BlockSpec(memory_space=pltpu.VMEM)] * len(ins),
        out_specs=[pl.BlockSpec(memory_space=pltpu.VMEM)] * len(outs),
        out_shape=outs,
        compiler_params=pltpu.CompilerParams(vmem_limit_bytes=VMEM_LIMIT),
        cost_estimate=pl.CostEstimate(
            flops=2 * matmuls * HEADS * pairs * LANES,
            transcendentals=HEADS * pairs,
            bytes_accessed=8 * rows * width,
        ),
        name=name,
    )(*ins.values())


def attend_own(q, k, v, extras):
    width, rows = q.shape
    ins = dict(q=q, k=k, v=v, **{n: extras[n] for n in ("plain", "same", "query", "self")})
    outs = like(q) + [
        jax.ShapeDtypeStruct((width, rows // 2), F32),
        jax.ShapeDtypeStruct((HEADS, 1, rows), F32),
    ]
    return attention_call(own_kernel, "attend_own", ins, outs, rows * rows * k.shape[0], 2)


def attend_far(q, kx, vx, extras, o, part, t):
    rows = q.shape[1]
    ins = dict(q=q, kx=kx, vx=vx, o=o, part=part, t=t)
    ins |= {n: extras[n] for n in ("far", "query", "self")}
    return attention_call(far_kernel, "attend_far", ins, like(o, t), rows * rows * kx.shape[0] // 4, 2)


def attend_far_back(q, kx, vx, extras, o, g, t):
    width, rows = q.shape
    ins = dict(q=q, kx=kx, vx=vx, o=o, g=g, t=t)
    ins |= {n: extras[n] for n in ("far", "query", "self")}
    outs = [jax.ShapeDtypeStruct((width, rows // 2), F32)] + like(kx, vx)
    pairs = rows * rows * kx.shape[0] // 4
    return attention_call(far_back_kernel, "attend_far_back", ins, outs, pairs, 5)


def attend_own_back(q, k, v, extras, o, g, t, part):
    rows = q.shape[1]
    ins = dict(q=q, k=k, v=v, o=o, g=g, t=t, part=part)
    ins |= {n: extras[n] for n in ("plain", "same", "query", "self")}
    pairs = rows * rows * k.shape[0]
    return attention_call(own_back_kernel, "attend_own_back", ins, like(q, k, v), pairs, 5)


def residue_rows(block):
    order = [2 * i + parity for parity in range(2) for i in range(RESIDUES // 2)]
    return [
        (i * block, pl.ds(residue, block, stride=RESIDUES)) for i, residue in enumerate(order)
    ]


def stripes(rows, width):
    return pltpu.VMEM((width // LANES, rows, LANES), F32)


def fill_stripes(ref, value):
    for c in range(ref.shape[0]):
        ref[c] = value[:, c * LANES : (c + 1) * LANES]


def read_stripes(ref, rows):
    return jnp.concatenate([ref[c, rows, :] for c in range(ref.shape[0])], axis=1)


def write_stripes(ref, rows, value):
    for c in range(ref.shape[0]):
        ref[c, rows, :] = value[:, c * LANES : (c + 1) * LANES]


def place_pieces(spot, pieces, full, depth, columns):
    outer, near, core, branch = spot[0], spot[1], spot[2], spot[3]
    for index, piece in enumerate(pieces):
        group, other_core = index % 2, index // 2
        rounds, width = piece.shape[2], piece.shape[4]
        for one in range(2):
            for two in range(2):
                far_branch, far_near = (one, two) if group == 0 else (two, one)
                offset = 0 if group == 0 else columns - width
                column = jnp.bitwise_xor(branch, far_branch) * columns + offset
                lanes = pl.ds(pl.multiple_of(column, LANES), width)
                for step in range(rounds):
                    shard = (
                        lax.rem(outer - step + rounds, rounds) * 4
                        + jnp.bitwise_xor(near, far_near) * 2
                        + jnp.bitwise_xor(core, other_core)
                    )
                    row = pl.multiple_of(shard * depth, 16)
                    full[pl.ds(row, depth), lanes] = piece[one, two, step]


def project_kernel(head_dim, placed, count, *refs):
    tokens_ref, norm_ref, bias_ref = refs[:3]
    outs, held = refs[count : count + 8], refs[count + 8 : count + 16]
    wide_ref, hidden_ref, sems = refs[count + 16 :]
    full_ref, ordered_ref, turned_ref = held[:3]
    rows, width = tokens_ref.shape
    block = rows // RESIDUES
    copies = []

    def leave(index):
        copies.append(pltpu.make_async_copy(held[index], outs[index], sems.at[index]))
        copies[-1].start()

    if placed is None:
        full_ref[...] = refs[3][...]
    else:
        place_pieces(refs[3], refs[4:8], full_ref, *placed)
    leave(0)
    fill_stripes(wide_ref, tokens_ref[...].astype(F32))
    gain, shift = norm_ref[0:1], norm_ref[1:2]
    for first, natural in residue_rows(block):
        span = slice(first, first + block)
        values = read_stripes(wide_ref, natural)
        ordered_ref[span] = values.astype(BF16)
        hidden_ref[span] = (standardize(values)[0] * gain + shift).astype(BF16)
    leave(1)
    turned_ref[...] = hidden_ref[...].T
    leave(2)
    ones = jnp.where(lax.broadcasted_iota(jnp.int32, (16, LANES), 0) == 0, 1.0, 0.0).astype(BF16)
    odd = lax.rem(lax.div(lax.broadcasted_iota(jnp.int32, (width, 1), 0), head_dim), 2) == 1
    half = rows // 2
    for i in (1, 2, 0):
        product = dot_tn(full_ref[:, i * width : (i + 1) * width], turned_ref[...])
        if i != 1:
            at = i // 2 * width
            column = dot_tn(bias_ref[:, at : at + width], ones)
            product += jnp.concatenate([column] * (rows // LANES), axis=1)
        low = product.astype(BF16)
        held[3 + i][...] = low
        leave(3 + i)
        if i:
            held[5 + i][...] = jnp.where(odd, low[:, half:], low[:, :half])
            leave(5 + i)
    for copy in copies:
        copy.wait()


def project(tokens, norms, bias, full, pieces, spot, placed, head_dim):
    rows, width = tokens.shape
    ins = [tokens, norms, bias] + ([full] if placed is None else [spot, *pieces])
    specs = [pl.BlockSpec(memory_space=pltpu.VMEM)] * len(ins)
    if placed is not None:
        specs[3] = pl.BlockSpec(memory_space=pltpu.SMEM)
    turned = jax.ShapeDtypeStruct((width, rows), BF16)
    part = jax.ShapeDtypeStruct((width, rows // 2), BF16)
    outs = [
        jax.ShapeDtypeStruct((width, 3 * width), BF16), jax.ShapeDtypeStruct((rows, width), BF16),
        turned, turned, turned, turned, part, part,
    ]
    return pl.pallas_call(
        functools.partial(project_kernel, head_dim, placed, len(ins)),
        in_specs=specs,
        out_specs=[pl.BlockSpec(memory_space=pl.ANY)] * len(outs),
        out_shape=outs,
        scratch_shapes=[pltpu.VMEM(m.shape, m.dtype) for m in outs]
        + [
            stripes(rows, width),
            pltpu.VMEM((rows, width), BF16),
            pltpu.SemaphoreType.DMA((len(outs),)),
        ],
        compiler_params=pltpu.CompilerParams(vmem_limit_bytes=VMEM_LIMIT),
        cost_estimate=pl.CostEstimate(
            flops=6 * rows * width * width,
            transcendentals=0,
            bytes_accessed=12 * width * width + 16 * rows * width,
        ),
        name="project",
    )(*ins)


def finish_kernel(weight_ref, grad_ref, tokens_ref, middle_ref, norm_ref, sums_ref, wide_ref, out_ref, table_ref, natural_ref):
    step, count = pl.program_id(0), pl.num_programs(0)
    tile, width = tokens_ref.shape
    block = out_ref.shape[0] // RESIDUES

    @pl.when(step == 0)
    def _():
        table_ref[...] = jnp.zeros_like(table_ref)
        table_ref[4:8] = sums_ref[...]
        for i in range(wide_ref.shape[1] // width):
            table_ref[8 + i : 9 + i] = wide_ref[:, i * width : (i + 1) * width]

    grad = dot_nn(weight_ref[...], grad_ref[...]).T
    normed, inverse = standardize(tokens_ref[...].astype(F32))
    table_ref[0:1] += jnp.sum(grad * normed, axis=0, keepdims=True)
    table_ref[1:2] += jnp.sum(grad, axis=0, keepdims=True)
    ones = jnp.ones((16, tile), BF16)
    table_ref[2:3] += dot_nt(ones, grad_ref[:width])[0:1]
    table_ref[3:4] += dot_nt(ones, grad_ref[2 * width :])[0:1]
    total = middle_ref[...] + norm_back(grad, normed, inverse, norm_ref[0:1])
    many = tile // block
    half = RESIDUES // 2
    for i in range(many):
        place = step * many + i
        residue = 2 * lax.rem(place, half) + lax.div(place, half)
        natural = pl.ds(residue, block, stride=RESIDUES)
        write_stripes(natural_ref, natural, total[i * block : (i + 1) * block])

    @pl.when(step == count - 1)
    def _():
        out_ref[...] = read_stripes(natural_ref, slice(None))


def finish(weight, grad, tokens, middle, norms, sums, wide):
    rows, width = tokens.shape
    tile = min(rows, 256)
    narrow_spec = pl.BlockSpec((tile, width), lambda r: (r, 0))
    once = pl.BlockSpec(memory_space=pltpu.VMEM)
    return pl.pallas_call(
        finish_kernel,
        grid=(rows // tile,),
        in_specs=[
            once, pl.BlockSpec((grad.shape[0], tile), lambda r: (0, r)), narrow_spec, narrow_spec,
            once, once, once,
        ],
        out_specs=[once, once],
        out_shape=[
            jax.ShapeDtypeStruct((rows, width), F32),
            jax.ShapeDtypeStruct((16, width), F32),
        ],
        scratch_shapes=[stripes(rows, width)],
        compiler_params=pltpu.CompilerParams(vmem_limit_bytes=VMEM_LIMIT),
        cost_estimate=pl.CostEstimate(
            flops=6 * rows * width * width,
            transcendentals=0,
            bytes_accessed=6 * width * width + 16 * rows * width,
        ),
        name="finish",
    )(weight, grad, tokens, middle, norms, sums, wide)


def feed_forward_kernel(blocks, *refs):
    tokens_ref, attended_ref, natural_ref, small_ref, wide_ref, packed_ref = refs[:6]
    output_ref, grad_ref, mixed_ref, sums_ref, wide_sums_ref, grads_ref = refs[6:12]
    reduce_w, expand_w, output_w, natural_scr, active_scr, expanded_scr = refs[12:18]
    cotangent_scr, hidden_scr, low_scr, in_sems, out_sems = refs[18:]
    tile, width = tokens_ref.shape
    cut, depth = reduce_w.shape[1], output_w.shape[1]
    step, count = pl.program_id(0), pl.num_programs(0)
    block = natural_ref.shape[0] // RESIDUES
    halves, columns = packed_ref.shape[1], packed_ref.shape[3]
    local = blocks // halves * width // columns

    def arrival(index, y, at, size, target):
        return pltpu.make_async_copy(
            packed_ref.at[:, y, pl.ds(at, size)], target, in_sems.at[index]
        )

    def arrivals(first=0, last=None):
        found = []
        for y in range(halves):
            lanes = pl.ds(y * columns, columns)
            found.append((y, cut + local * depth, depth, output_w.at[:, :, lanes]))
        for y in range(halves):
            for i in range(local):
                at = (y * local + i) * columns
                target = expand_w.at[at // width, :, :, pl.ds(at % width, columns)]
                found.append((y, cut + i * depth, depth, target))
        for y in range(halves):
            found.append((y, 0, cut, reduce_w.at[:, :, pl.ds(y * columns, columns)]))
        indices = range(len(found))[first:last]
        return [arrival(i, *found[i]) for i in indices]

    def await_first(first, last):
        @pl.when(step == 0)
        def _():
            for copy in arrivals(first, last):
                copy.wait()

    @pl.when(step == 0)
    def _():
        for copy in arrivals():
            copy.start()
        fill_stripes(natural_scr, natural_ref[...].astype(F32))
        sums_ref[...] = jnp.zeros_like(sums_ref)
        wide_sums_ref[...] = jnp.zeros_like(wide_sums_ref)

    many, half = tile // block, RESIDUES // 2
    strided = []
    for i in range(many):
        place = step * many + i
        residue = 2 * lax.rem(place, half) + lax.div(place, half)
        strided.append(pl.ds(residue, block, stride=RESIDUES))
    here = pl.ds(pl.multiple_of(step * tile, tile), tile)
    bias_output, gain, shift, bias_reduce = (small_ref[i : i + 1] for i in range(4))
    upstream = jnp.concatenate([read_stripes(natural_scr, natural) for natural in strided], axis=0)
    cotangent = upstream.astype(BF16)
    cotangent_scr[here] = cotangent
    await_first(0, halves)
    project = output_w[...].reshape(width, width)
    middle = tokens_ref[...].astype(F32) + dot_tn(attended_ref[:, here], project) + bias_output
    normed, inverse = standardize(middle)
    hidden = (normed * gain + shift).astype(BF16)
    hidden_scr[here] = hidden
    output = middle + bias_reduce
    hidden_grad = jnp.zeros(middle.shape, F32)
    await_first(halves, halves + halves * local + halves)
    shrink_all = reduce_w[...].reshape(blocks * width, width)
    for i in range(blocks):
        span = slice(i * width, (i + 1) * width)
        grow = expand_w[i].reshape(width, width)
        shrink = shrink_all[span]
        active, slope = gelu_pair(dot_nn(hidden, grow) + wide_ref[:, span])
        active = active.astype(BF16)
        active_scr[i, here] = active
        output += dot_nn(active, shrink)
        expanded = (dot_nt(cotangent, shrink) * slope).astype(BF16)
        expanded_scr[i, here] = expanded
        wide_sums_ref[:, span] += jnp.sum(expanded.astype(F32), axis=0, keepdims=True)
        hidden_grad += dot_nt(expanded, grow)
    for i, natural in enumerate(strided):
        write_stripes(natural_scr, natural, output[i * block : (i + 1) * block])
    middle_grad = upstream + norm_back(hidden_grad, normed, inverse, gain)
    grad_ref[...] = middle_grad
    low = middle_grad.astype(BF16)
    low_scr[here] = low
    mixed_ref[...] = dot_nt(project, low).astype(BF16)
    for i, part in enumerate((hidden_grad * normed, hidden_grad, middle_grad, upstream)):
        sums_ref[i : i + 1] += jnp.sum(part, axis=0, keepdims=True)

    @pl.when(step == count - 1)
    def _():
        output_ref[...] = read_stripes(natural_scr, slice(None)).astype(BF16)
        copies = []

        def leave(source, target):
            copies.append(pltpu.make_async_copy(source, target, out_sems.at[len(copies)]))
            copies[-1].start()

        for i in range(blocks):
            product = dot_tn(active_scr[i], cotangent_scr[...]).astype(BF16)
            if cut <= width:
                shards = slice(i * width // cut, (i + 1) * width // cut)
                reduce_w[shards] = product.reshape(-1, cut, width)
                leave(reduce_w.at[shards], grads_ref.at[shards, pl.ds(0, cut)])
            else:
                span = pl.ds(i * width, width)
                reduce_w[0, span] = product
                leave(reduce_w.at[:, span], grads_ref.at[:, span])
        for i in range(blocks):
            product = dot_tn(hidden_scr[...], expanded_scr[i]).astype(BF16)
            expand_w[i] = product.reshape(-1, depth, width)
            leave(expand_w.at[i], grads_ref.at[:, pl.ds(cut + i * depth, depth)])
        product = dot_nn(attended_ref[...], low_scr[...]).astype(BF16)
        output_w[...] = product.reshape(-1, depth, width)
        leave(output_w, grads_ref.at[:, pl.ds(cut + blocks * depth, depth)])
        for copy in copies:
            copy.wait()


def feed_forward(tokens, attended, cotangent, small, wide, packed):
    rows, width = tokens.shape
    ff = wide.shape[1]
    blocks = ff // width
    shards, halves = packed.shape[:2]
    tile = min(rows, 256)
    narrow_spec = pl.BlockSpec((tile, width), lambda r: (r, 0))
    turned_spec = pl.BlockSpec((width, tile), lambda r: (0, r))
    once = pl.BlockSpec(memory_space=pltpu.VMEM)
    rows_scr = pltpu.VMEM((rows, width), BF16)
    wide_scr = pltpu.VMEM((blocks, rows, width), BF16)
    return pl.pallas_call(
        functools.partial(feed_forward_kernel, blocks),
        grid=(rows // tile,),
        in_specs=[narrow_spec, once, once, once, once, pl.BlockSpec(memory_space=pl.ANY)],
        out_specs=[once, narrow_spec, turned_spec, once, once, pl.BlockSpec(memory_space=pl.ANY)],
        out_shape=[
            jax.ShapeDtypeStruct((rows, width), BF16),
            jax.ShapeDtypeStruct((rows, width), F32),
            jax.ShapeDtypeStruct((width, rows), BF16),
            jax.ShapeDtypeStruct((4, width), F32),
            jax.ShapeDtypeStruct((1, ff), F32),
            jax.ShapeDtypeStruct((shards, (2 * ff + width) // shards, width), BF16),
        ],
        scratch_shapes=[
            pltpu.VMEM((shards, ff // shards, width), BF16),
            pltpu.VMEM((blocks, shards, width // shards, width), BF16),
            pltpu.VMEM((shards, width // shards, width), BF16),
            stripes(rows, width),
            wide_scr,
            wide_scr,
            rows_scr,
            rows_scr,
            rows_scr,
            pltpu.SemaphoreType.DMA((2 * halves + blocks * halves,)),
            pltpu.SemaphoreType.DMA((2 * blocks + 1,)),
        ],
        compiler_params=pltpu.CompilerParams(vmem_limit_bytes=VMEM_LIMIT),
        cost_estimate=pl.CostEstimate(
            flops=2 * rows * width * (6 * ff + 3 * width),
            transcendentals=2 * rows * ff,
            bytes_accessed=4 * packed.size + 20 * rows * width,
        ),
        name="feed_forward",
    )(tokens, attended, cotangent, small, wide, packed)


def level_table():
    head = np.arange(HEADS)[:, None]
    residue = 2 * np.arange(RESIDUES // 2)[None, :] + head % 2
    return sum((residue % 2**b == head % 2**b).astype(int) for b in range(1, BRANCHES))


def log_rows(times):
    parts = np.log2(times).astype(np.float32)
    rows = []
    for _ in range(3):
        low = parts.astype(ml_dtypes.bfloat16)
        rows.append(low)
        parts = parts - low.astype(np.float32)
    return np.stack(rows, axis=2).reshape(times.shape[0], -1, times.shape[2])


def attention_extras(rows, own_starts, far_starts, own_count, far_count, same):
    half, block = rows // 2, rows // RESIDUES
    levels = level_table()
    level = np.arange(1, BRANCHES)[None, :, None]
    lower = np.minimum(level, levels[:, None, :])

    def repeat(table, devices):
        return np.tile(np.repeat(table, block, axis=-1), devices)

    rank = np.arange(half)
    place = [(rank % block) * RESIDUES + 2 * (rank // block) + parity for parity in range(2)]

    def liveness(starts, count, allowed):
        live = [
            jnp.stack([(start + jnp.asarray(place[p]) < count) & allowed for p in range(2)])
            for start in starts
        ]
        return jnp.where(jnp.concatenate(live, axis=1), 0.0, NEGATIVE).astype(BF16)

    def built(times, live):
        count, _, keys = times.shape
        fixed = np.zeros((count, EXTRA, keys), ml_dtypes.bfloat16)
        fixed[:, TIMES:LIVE] = times
        fixed[:, FIXED : FIXED + 3] = 1
        row = np.arange(EXTRA)[None, :, None]
        return jnp.where(row == LIVE, live[:, None], jnp.asarray(fixed))

    own_live = liveness(own_starts, own_count, True)
    far_live = liveness(far_starts, far_count, same)
    by_head = np.arange(HEADS) % 2
    none = np.zeros((2, LIVE, half * len(own_starts)), ml_dtypes.bfloat16)

    def per_head(live):
        return jnp.where(by_head[:, None] == 1, live[1], live[0])

    query = np.zeros((HEADS, EXTRA, half), ml_dtypes.bfloat16)
    spread = np.repeat(levels, block, axis=1)
    for one in range(1, BRANCHES):
        query[:, 3 * (one - 1) : 3 * one] = (spread == one)[:, None, :]
    query[:, LIVE] = 1
    return {
        "plain": built(none, own_live),
        "same": built(repeat(log_rows(1.0 + lower), len(own_starts)), per_head(own_live)),
        "far": built(repeat(log_rows(lower), len(far_starts)), per_head(far_live)),
        "query": jnp.asarray(query),
        "self": jnp.asarray(np.log2(1.0 + spread).astype(np.float32))[:, None],
    }


def half_of(table, odd):
    half = table.shape[-1] // 2
    return jnp.where(odd, table[..., half:], table[..., :half])


def add_half(total, part, odd):
    part = part.astype(F32)
    both = jnp.concatenate([jnp.where(odd, 0.0, part), jnp.where(odd, part, 0.0)], axis=-1)
    return total.astype(F32) + both


def swap_pairs(value):
    return lax.ppermute(value, "branch", [(0, 1), (1, 0)])


def gather_columns(shard, branches):
    if branches != 2:
        return lax.all_gather(shard, "branch", axis=shard.ndim - 1, tiled=True)
    other = swap_pairs(shard)
    first = lax.axis_index("branch") == 0
    return jnp.concatenate(
        [jnp.where(first, shard, other), jnp.where(first, other, shard)], axis=-1
    )


def scatter_columns(total, branches):
    if branches != 2:
        return lax.psum_scatter(
            total, "branch", scatter_dimension=total.ndim - 1, tiled=True
        ).astype(F32)
    half = total.shape[-1] // 2
    at = lax.axis_index("branch")
    keep = lax.dynamic_slice_in_dim(total, at * half, half, total.ndim - 1)
    away = lax.dynamic_slice_in_dim(total, (1 - at) * half, half, total.ndim - 1)
    return keep.astype(F32) + swap_pairs(away).astype(F32)


def weight_sum(partial, branches):
    low = lax.psum_scatter(partial, "slides", scatter_dimension=0, tiled=True)
    return scatter_columns(low, branches)


def pack_rows(reduce_part, expand_part, output_part):
    width = output_part.shape[-1]
    blocks = expand_part.shape[-1] // width
    return jnp.concatenate(
        [reduce_part]
        + [expand_part[..., i * width : (i + 1) * width] for i in range(blocks)]
        + [output_part],
        axis=-2,
    )


def unpack_rows(packed, width, ff):
    blocks = ff // width
    depth = packed.shape[-2] // (2 * blocks + 1)
    cut = blocks * depth
    expand = [packed[..., cut + i * depth : cut + (i + 1) * depth, :] for i in range(blocks)]
    return packed[..., :cut, :], jnp.concatenate(expand, axis=-1), packed[..., 2 * cut :, :]


def join_columns(own, other):
    first = lax.axis_index("branch") == 0
    return jnp.concatenate(
        [jnp.where(first, own, other), jnp.where(first, other, own)], axis=-1
    )


def pack_kernel(reduce_ref, expand_ref, output_ref, packed_ref):
    cut, width = reduce_ref.shape
    depth = output_ref.shape[0]
    packed_ref[:cut] = reduce_ref[...]
    blocks = expand_ref.shape[1] // width
    for i in range(blocks):
        packed_ref[cut + i * depth : cut + (i + 1) * depth] = expand_ref[:, i * width : (i + 1) * width]
    packed_ref[cut + blocks * depth :] = output_ref[...]


def join_kernel(cut, depth, at_ref, own_ref, other_ref, joined_ref):
    columns = own_ref.shape[1]
    blocks = (own_ref.shape[0] - cut) // depth - 1

    def put(halves):
        for y, half in enumerate(halves):
            lanes = slice(y * columns, (y + 1) * columns)
            joined_ref[:cut, lanes] = half[:cut]
            joined_ref[cut + blocks * depth :, lanes] = half[cut + blocks * depth :]
            for i in range(blocks):
                row, lane = divmod((y * blocks + i) * columns, 2 * columns)
                target = cut + row * depth
                source = cut + i * depth
                joined_ref[target : target + depth, lane : lane + columns] = half[
                    source : source + depth
                ]

    @pl.when(at_ref[0] == 0)
    def _():
        put((own_ref, other_ref))

    @pl.when(at_ref[0] != 0)
    def _():
        put((other_ref, own_ref))


def gather_packed(reduce_weight, expand_weight, output_weight, first_transfers, branches):
    size = lax.axis_size("slides")
    depth, columns = output_weight.shape
    aligned = branches == 2 and depth % 16 == 0 and columns % LANES == 0
    if aligned:
        rows = reduce_weight.shape[0] + depth + expand_weight.size // columns
        shard = pl.pallas_call(
            pack_kernel,
            out_shape=jax.ShapeDtypeStruct((rows, columns), BF16),
            name="pack",
        )(reduce_weight, expand_weight, output_weight)
    else:
        shard = pack_rows(reduce_weight, expand_weight, output_weight)
    if aligned:
        at = lax.axis_index("branch").reshape(1)
        other, first_transfers = lax.optimization_barrier((swap_pairs(shard), first_transfers))
        shard = pl.pallas_call(
            functools.partial(join_kernel, reduce_weight.shape[0], depth),
            in_specs=[pl.BlockSpec(memory_space=pltpu.SMEM)]
            + [pl.BlockSpec(memory_space=pltpu.VMEM)] * 2,
            out_shape=jax.ShapeDtypeStruct((rows, 2 * columns), BF16),
            name="join",
        )(at, shard, other)
        return lax.all_gather(shard, "slides", axis=0, tiled=False)[:, None], first_transfers
    packed = lax.all_gather(shard, ("slides", "branch"), axis=0, tiled=False)
    packed = packed.reshape(size, branches, *shard.shape)
    ff = size * reduce_weight.shape[0]
    parts = unpack_rows(packed, columns, ff // branches)
    parts = [m.transpose(0, 2, 1, 3).reshape(1, -1, branches * m.shape[-1]) for m in parts]
    return pack_rows(*parts)[None], first_transfers


def gather_vectors(vectors, branches, rows_of):
    cuts = np.cumsum([0] + [m.shape[0] for m in vectors])
    if branches != 2:
        table = lax.all_gather(jnp.concatenate(vectors), "branch", axis=0, tiled=False)
        return [table[:, a:b].reshape(1, -1) for a, b in zip(cuts, cuts[1:])]
    own, other = rows_of
    columns = own.shape[1]
    first = lax.axis_index("branch") == 0
    halves = [jnp.where(first, own, other), jnp.where(first, other, own)]
    at = cuts // columns
    return [
        jnp.concatenate(
            [half[row : row + 1] for half in halves for row in range(at[i], at[i + 1])], axis=1
        )
        for i in range(len(vectors))
    ]


def sum_packed(packed, width, ff):
    size = lax.axis_size("slides")
    if packed.shape[0] != size:
        parts = unpack_rows(packed, width, ff)
        packed = pack_rows(*(m.reshape(size, -1, m.shape[-1]) for m in parts))
    rows = packed.shape[1]
    return lax.psum_scatter(
        packed.reshape(size * rows, width), "slides", scatter_dimension=0, tiled=True
    )


def branch_half(low, index, width, ff):
    reduce_part, expand_part, output_part = unpack_rows(low, width, ff)
    columns = width // 2
    grown = lax.dynamic_slice_in_dim(expand_part, index * (ff // 2), ff // 2, 1)
    pieces = [
        lax.dynamic_slice_in_dim(part, index * columns, columns, 1)
        for part in (reduce_part, output_part)
    ]
    pieces += [grown[:, i : i + columns] for i in range(0, ff // 2, columns)]
    return jnp.concatenate(pieces, axis=0)


def unpack_half(total, depth, cut):
    tail = [total[row : row + depth] for row in range(cut + depth, total.shape[0], depth)]
    return total[:cut], jnp.concatenate(tail, axis=1), total[cut : cut + depth]


def flip(value, bit):
    return lax.ppermute(value, "slides", [(i, i ^ bit) for i in range(lax.axis_size("slides"))])


def shifted(value, step):
    size = lax.axis_size("slides")
    return lax.ppermute(value, "slides", [(i, (i + 4 * step) % size) for i in range(size)])


def gather_pieces(held, later):
    half = held[0].shape[1] // 2 // LANES * LANES
    first = jnp.stack([m[:, :half] for m in held])
    second = jnp.stack([m[:, half:] for m in held])
    first, second = jnp.stack([first, flip(first, 2)]), jnp.stack([second, swap_pairs(second)])
    first, second, later = lax.optimization_barrier((first, second, later))
    other = swap_pairs(later[0])
    first, second = jnp.stack([first, swap_pairs(first)]), jnp.stack([second, flip(second, 2)])
    pieces = (first, second, flip(first, 1), flip(second, 1))
    slide = lax.axis_index("slides")
    spot = jnp.stack(
        [
            lax.div(slide, 4),
            lax.rem(lax.div(slide, 2), 2),
            lax.rem(slide, 2),
            lax.axis_index("branch"),
        ]
    )
    return pieces, spot.astype(jnp.int32), other, later


def pick(table, index, axis):
    return lax.dynamic_index_in_dim(table, index, axis, keepdims=False)


def split_kernel(core_ref, left_ref, right_ref, keep_ref, send_ref, product_ref):
    product_ref[...] = dot_nt(left_ref[...], right_ref[...]).astype(BF16).reshape(product_ref.shape)
    core = core_ref[0]
    for pair in range(product_ref.shape[0] // 2):
        at = (0, pair // 2, pair % 2)
        keep_ref[at] = product_ref[2 * pair + core]
        send_ref[at] = product_ref[2 * pair + 1 - core]


def split_product(left, right, core):
    size = lax.axis_size("slides")
    features, rows = left.shape
    depth, columns = features // size, right.shape[0] // 2
    step = columns
    wide = columns // step
    block = pl.BlockSpec((1, size // 4, 2, depth, step), lambda j: (j // wide, 0, 0, 0, j % wide))
    return pl.pallas_call(
        split_kernel,
        grid=(2 * wide,),
        in_specs=[
            pl.BlockSpec(memory_space=pltpu.SMEM),
            whole_spec(left.shape),
            pl.BlockSpec((step, rows), lambda j: (j, 0)),
        ],
        out_specs=[block, block],
        out_shape=[jax.ShapeDtypeStruct((2, size // 4, 2, depth, columns), BF16)] * 2,
        scratch_shapes=[pltpu.VMEM((size, depth, step), BF16)],
        compiler_params=pltpu.CompilerParams(vmem_limit_bytes=VMEM_LIMIT),
        cost_estimate=pl.CostEstimate(
            flops=4 * rows * features * columns,
            transcendentals=0,
            bytes_accessed=2 * (left.size + right.size + 2 * features * columns),
        ),
        name="joint_gradient",
    )(core.reshape(1), left, right)


def deal_kernel(spans, at_ref, *refs):
    tables, outs = refs[: -len(spans)], refs[-len(spans) :]
    total = sum((table[...] for table in tables[1:]), tables[0][...])
    width = total.shape[1]

    def put(index):
        for (row, count), out in zip(spans, outs):
            if count == 1:
                out[...] = total[row, index * width // 2 : (index + 1) * width // 2]
            else:
                for i in range(count // 2):
                    at = row + index * count // 2 + i
                    out[i * width : (i + 1) * width] = total[at]

    @pl.when(at_ref[0] == 0)
    def _():
        put(0)

    @pl.when(at_ref[0] != 0)
    def _():
        put(1)


def deal(tables, spans, at):
    width = tables[0].shape[1]
    return pl.pallas_call(
        functools.partial(deal_kernel, spans),
        in_specs=[pl.BlockSpec(memory_space=pltpu.SMEM)]
        + [pl.BlockSpec(memory_space=pltpu.VMEM)] * len(tables),
        out_shape=[jax.ShapeDtypeStruct((count * width // 2,), F32) for _, count in spans],
        name="deal",
    )(at.reshape(1), *tables)


def sum_tree(kept, sent, table_of, gate, low_sums, near, outer, at):
    rounds = kept.shape[1]

    def both(one, two):
        return (one.astype(F32) + two.astype(F32)).astype(BF16)

    total = both(kept, flip(sent, 1))
    low, high = total[:, : rounds // 2], total[:, rounds // 2 :]
    away, off, gate = lax.optimization_barrier(
        (pick(low, 1 - at, 0), pick(high, 1 - near, 2), gate)
    )
    away, off = swap_pairs(away), flip(off, 2)
    table = table_of(gate)
    low, high = both(pick(low, at, 0), away), both(pick(high, near, 2), off)
    away, off, table = lax.optimization_barrier(
        (pick(low, 1 - near, 1), pick(high, 1 - at, 0), table)
    )
    low, high = both(pick(low, near, 1), flip(away, 2)), both(pick(high, at, 0), swap_pairs(off))
    table += flip(table, 1)
    table += swap_pairs(table)
    joined = jnp.concatenate([low, high], axis=0)
    total = pick(joined, outer, 0).astype(F32)
    sends = [pick(joined, lax.rem(outer + step, rounds), 0) for step in range(1, rounds)]
    sends, table = lax.optimization_barrier((sends, table))
    parts = [shifted(part, step + 1) for step, part in enumerate(sends)]
    table += flip(table, 2)
    parts[0], table, low_sums = lax.optimization_barrier((parts[0], table, low_sums))
    for part in parts:
        total += part.astype(F32)
    bit = 4
    while bit < 4 * rounds:
        table += flip(table, bit)
        bit *= 2
    return total, table, low_sums


def on_device(
    tokens,
    cotangent,
    first_gain,
    first_shift,
    joint_weight,
    joint_bias,
    output_weight,
    output_bias,
    second_gain,
    second_shift,
    expand_weight,
    expand_bias,
    reduce_weight,
    reduce_bias,
    block_owner,
    tile_count,
):
    rows, width = tokens.shape
    branches = lax.axis_size("branch")
    head_dim = width // HEADS
    block = rows // RESIDUES
    mates = SEG_BASE // rows
    at = lax.axis_index("branch")
    segment = lax.div(at, mates)
    within = at - segment * mates
    odd = ((np.arange(width) // head_dim) % 2 == 1)[:, None]

    parameters = (
        first_gain, first_shift, joint_bias, output_bias,
        second_gain, second_shift, expand_bias, reduce_bias,
    )
    depth = joint_weight.shape[0]
    slides = lax.axis_size("slides")
    trees = branches == 2 and slides % 8 == 0 and slides & (slides - 1) == 0 and depth % 16 == 0
    held = [joint_weight]
    if trees:
        held += [shifted(joint_weight, step) for step in range(1, slides // 4)]
    packed_weights, held = gather_packed(
        reduce_weight, expand_weight, output_weight, held, branches
    )
    if trees:
        small = jnp.concatenate([m.reshape(-1, width // 2) for m in parameters], axis=0)
        pieces, spot, other, (small, block_owner, tile_count) = gather_pieces(
            held, (small, block_owner, tile_count)
        )
        vectors = gather_vectors(parameters, branches, (small, other))
        joint_full, placed = None, joint_weight.shape
    else:
        joint_full = lax.all_gather(
            gather_columns(joint_weight, branches), "slides", axis=0, tiled=True
        )
        vectors = gather_vectors(parameters, branches, None)
        pieces, spot, placed = (), None, None
    bias_joint = jnp.pad(vectors[2], ((0, 15), (0, 0)))
    gain_one, shift_one, _, bias_output, gain_two, shift_two, bias_expand, bias_reduce = (
        m.astype(F32) for m in vectors
    )
    norms = jnp.concatenate([gain_one, shift_one], axis=0)

    owners = block_owner.reshape(-1)
    counts = tile_count.reshape(-1)
    own_count = jnp.where(segment == 0, counts[0], counts[1])
    far_count = jnp.where(segment == 0, counts[1], counts[0])
    own_starts = [lax.rem(within + d, mates) * rows for d in range(mates)]
    far_starts = [d * rows for d in range(mates)]
    extras = attention_extras(
        rows, own_starts, far_starts, own_count, far_count, owners[0] == owners[1]
    )

    joint_full, tokens_low, hidden_turned, q, k, v, k_half, v_half = project(
        tokens, norms, bias_joint, joint_full, pieces, spot, placed, head_dim
    )
    if mates == 1 and branches == 2:
        k_own, v_own = k[None], v[None]
        k_far, v_far = swap_pairs(k_half)[None], swap_pairs(v_half)[None]
    else:
        own_at = [segment * mates + lax.rem(within + d, mates) for d in range(mates)]
        far_at = [(1 - segment) * mates + d for d in range(mates)]

        def chosen(table, indices):
            whole = lax.all_gather(table, "branch", axis=0)
            return jnp.stack([lax.dynamic_index_in_dim(whole, d, 0, False) for d in indices])

        k_own, v_own = chosen(k, own_at), chosen(v, own_at)
        k_far, v_far = chosen(k_half, far_at), chosen(v_half, far_at)
    attended, part, total_log = attend_own(q, k_own, v_own, extras)
    attended, total_log = attend_far(q, k_far, v_far, extras, attended, part, total_log)
    ff = bias_expand.shape[1]
    small = jnp.concatenate([bias_output, gain_two, shift_two, bias_reduce], axis=0)
    output, middle_grad, mixed_grad, sums, wide_sums, packed_grads = feed_forward(
        tokens_low, attended, cotangent, small, bias_expand, packed_weights
    )
    mixed_grad, packed_grads = lax.optimization_barrier((mixed_grad, packed_grads))
    low_sums = sum_packed(packed_grads, width, ff)

    part, dk_far, dv_far = attend_far_back(
        q, k_far, v_far, extras, attended, mixed_grad, total_log
    )
    dq, dk_own, dv_own = attend_own_back(
        q, k_own, v_own, extras, attended, mixed_grad, total_log, part
    )
    if mates == 1 and branches == 2:
        key_sum = add_half(dk_own[0], swap_pairs(dk_far[0]), odd)
        value_sum = add_half(dv_own[0], swap_pairs(dv_far[0]), odd)
    else:

        def spread(own, far):
            canvas = jnp.zeros((branches, width, rows), BF16)
            for d, index in enumerate(own_at):
                canvas = lax.dynamic_update_index_in_dim(canvas, own[d], index, 0)
            for d, index in enumerate(far_at):
                full = add_half(jnp.zeros((width, rows), F32), far[d], odd).astype(BF16)
                canvas = lax.dynamic_update_index_in_dim(canvas, full, index, 0)
            return lax.psum_scatter(canvas, "branch", scatter_dimension=0, tiled=True)[0]

        key_sum = spread(dk_own, dk_far)
        value_sum = spread(dv_own, dv_far)
    value_low = value_sum.astype(BF16)
    joint_grad = jnp.concatenate([dq, key_sum.astype(BF16), value_low], axis=0)
    found = []

    def table_of(grad):
        found.extend(finish(joint_full, joint_grad, tokens_low, grad, norms, sums, wide_sums))
        return found[1]

    sizes = (1, 1, 2, 1, 1, 1, 1, ff // width)
    starts = np.cumsum((0,) + sizes)
    if trees:
        slide = lax.axis_index("slides")
        kept, sent = split_product(hidden_turned, joint_grad, lax.rem(slide, 2))
        joint_sum, table, low_sums = sum_tree(
            kept, sent, table_of, middle_grad, low_sums,
            lax.rem(lax.div(slide, 2), 2), lax.div(slide, 4), at,
        )
        arrived = swap_pairs(branch_half(low_sums, 1 - at, width, ff))
        halves = branch_half(low_sums, at, width, ff).astype(F32) + arrived.astype(F32)
        reduce_sum, expand_sum, output_sum = unpack_half(
            halves, output_weight.shape[0], reduce_weight.shape[0]
        )
        mine = deal([table], tuple((int(a), n) for a, n in zip(starts, sizes)), at)
    else:
        joint_sum = weight_sum(dot_nt(hidden_turned, joint_grad).astype(BF16), branches)
        table = lax.psum(table_of(middle_grad), ("slides", "branch"))
        reduce_sum, expand_sum, output_sum = (
            scatter_columns(part, branches) for part in unpack_rows(low_sums, width, ff)
        )
        mine = []
        for row, count in zip(starts, sizes):
            share = count * width // branches
            whole = table[row : row + count].reshape(-1)
            mine.append(lax.dynamic_slice_in_dim(whole, at * share, share))
    tokens_grad = found[0]
    first_gain_sum, first_shift_sum, joint_bias_sum, second_gain_sum = mine[:4]
    second_shift_sum, output_bias_sum, reduce_bias_sum, expand_bias_sum = mine[4:]
    return (
        output,
        tokens_grad,
        first_gain_sum,
        first_shift_sum,
        joint_sum,
        joint_bias_sum,
        output_sum,
        output_bias_sum,
        second_gain_sum,
        second_shift_sum,
        expand_sum,
        expand_bias_sum,
        reduce_sum,
        reduce_bias_sum,
    )


def solution(mesh):
    rows = P(("slides", "branch"), None)
    matrix = P("slides", "branch")
    vector = P("branch")
    placed = (
        rows, rows, vector, vector, matrix, vector, matrix, vector,
        vector, vector, matrix, vector, matrix, vector, P("slides", None), P("slides", None),
    )
    given = (
        rows, rows, vector, vector, matrix, vector, matrix, vector,
        vector, vector, matrix, vector, matrix, vector,
    )
    return jax.shard_map(on_device, mesh=mesh, in_specs=placed, out_specs=given, check_vma=False)
```
